32 devices in a mesh: fsdp: 4 (over z), ctx: 4 (over x, core), tp: 2 (over y).
Axes of the slice: x: 2, y: 2, z: 4, core: 2. Of those that a mesh axis runs over, the one named last changes fastest.
Arguments:
- x_in: bfloat16 [8, 1024, 2048], P(None, ('fsdp', 'ctx')), may hold values from -6 to 6
- cotangent: bfloat16 [8, 1024, 2048], P(None, ('fsdp', 'ctx')), may hold values from -6 to 6
- lengths: int32 [8], replicated, may hold values from 128 to 1024, as said below
- adapter_ids: int32 [8], replicated, may hold values from 0 to 7
- w_qkv: bfloat16 [3, 2048, 2048], P(None, 'fsdp', 'tp'), may hold values from -0.125 to 0.125
- w_out: bfloat16 [2048, 2048], P('tp', 'fsdp'), may hold values from -2 to 2
- w_up: bfloat16 [2048, 8192], P('fsdp', 'tp'), may hold values from -0.125 to 0.125
- w_down: bfloat16 [8192, 2048], P('tp', 'fsdp'), may hold values from -0.0625 to 0.0625
- ln_gain: float32 [2, 2048], replicated, may hold values from 0.1 to 1.9
- ln_bias: float32 [2, 2048], replicated, may hold values from -1.5 to 1.5
- a_qkv: bfloat16 [3, 2048, 128], replicated, may hold values from -0.125 to 0.125
- b_qkv: bfloat16 [3, 128, 2048], P(None, None, 'tp'), may hold values from -0.5 to 0.5
- a_out: bfloat16 [2048, 128], P('tp'), may hold values from -2 to 2
- b_out: bfloat16 [128, 2048], replicated, may hold values from -0.5 to 0.5
- a_up: bfloat16 [2048, 128], replicated, may hold values from -0.125 to 0.125
- b_up: bfloat16 [128, 8192], P(None, 'tp'), may hold values from -0.5 to 0.5
- a_down: bfloat16 [8192, 128], P('tp'), may hold values from -0.0625 to 0.0625
- b_down: bfloat16 [128, 2048], replicated, may hold values from -0.5 to 0.5
Outputs:
- activations: bfloat16 [8, 1024, 2048], P(None, ('fsdp', 'ctx'))
- input_grad: bfloat16 [8, 1024, 2048], P(None, ('fsdp', 'ctx'))
- grad_a_qkv: float32 [3, 2048, 128], replicated
- grad_b_qkv: float32 [3, 128, 2048], P(None, None, 'tp')
- grad_a_out: float32 [2048, 128], P('tp')
- grad_b_out: float32 [128, 2048], replicated
- grad_a_up: float32 [2048, 128], replicated
- grad_b_up: float32 [128, 8192], P(None, 'tp')
- grad_a_down: float32 [8192, 128], P('tp')
- grad_b_down: float32 [128, 2048], replicated
The draws below stay inside these ranges and needn't reach their ends.
Inputs may be any that keep to these rules, and one draw needn't show every extreme that they name: `lengths`: each aligned block of 2 sequences holds at least one sequence of length 1024.
All inputs are finite; a program needn't handle non-finite values.
Results may differ from the reference program's by a relative error of at most 0.019.
Values may be sent and summed in bfloat16 or wider, within the bound.
A program may use at most 256 MiB of HBM per device.

```python
import math
import jax
import jax.numpy as jnp
from jax import lax

D = 2048
HEADS = 16
HEAD_DIM = 128
FF = 8192
RANK = 16
ADAPTERS = 8
L = 1024
S_DEV = 2
SEQS = 8
NR = 128


def draw_lengths(key, part):
    first_key, second_key = jax.random.split(key)
    base_lengths = jax.random.randint(first_key, (SEQS,), L // 8, L + 1)
    chosen_slot = jax.random.randint(second_key, (SEQS // S_DEV, 1), 0, S_DEV)
    full_mask = (jnp.arange(S_DEV)[None, :] == chosen_slot).reshape(SEQS)
    return jnp.where(full_mask, L, base_lengths).astype(jnp.int32)


def set_ends(entries, rng, least, largest):
    extent = entries.shape
    index_at = [jax.random.randint(jax.random.fold_in(rng, axis), (), 0, extent[axis]) for axis in range(len(extent))]
    entries = entries.at[tuple(index_at)].set(least)
    longest = extent.index(max(extent))
    index_at[longest] = (index_at[longest] + 1) % extent[longest]
    return entries.at[tuple(index_at)].set(largest)


def level_of(key, shape, shards, smallest, largest):
    def one(axis_at, blocks):
        draws = jax.random.uniform(jax.random.fold_in(jax.random.fold_in(key, 6), axis_at), (blocks,), jnp.float32, smallest / len(shards), largest / len(shards))
        return jnp.repeat(jnp.exp(draws), shape[axis_at] // blocks).reshape((-1,) + (1,) * (len(shape) - axis_at - 1))

    level = one(*shards[0])
    for cut in shards[1:]:
        level = level * one(*cut)
    return level


def gaussian(own_key, shape, scale, limit, cuts=(), held_as=jnp.bfloat16):
    factor_of = level_of(own_key, shape, cuts, -0.22, 0.18) if cuts else 1.0
    values = jax.random.normal(own_key, shape, jnp.float32) * scale * factor_of
    return jnp.minimum(jnp.maximum(values, -limit), limit).astype(held_as)


def setup_inputs(seed: int = 0) -> dict:
    seeds = jax.random.split(jax.random.key(seed), 19)
    return {
        "x_in": gaussian(seeds[0], (SEQS, L, D), 1.0, 6.0, ((1, 16),)),
        "cotangent": gaussian(seeds[1], (SEQS, L, D), 1.0, 6.0, ((1, 16),)),
        "lengths": draw_lengths(jax.random.fold_in(seeds[18], 71), 0),
        "adapter_ids": set_ends(jax.random.randint(seeds[3], (SEQS,), 0, ADAPTERS), jax.random.fold_in(seeds[3], 1), 0, ADAPTERS - 1).astype(jnp.int32),
        "w_qkv": gaussian(seeds[4], (3, D, D), D ** -0.5, 0.125, ((1, 4), (2, 2))),
        "w_out": gaussian(seeds[5], (D, D), (D * 4 // L) ** -0.5, 2.0, ((0, 2), (1, 4))),
        "w_up": gaussian(seeds[6], (D, FF), D ** -0.5, 0.125, ((0, 4), (1, 2))),
        "w_down": gaussian(seeds[7], (FF, D), FF ** -0.5, 0.0625, ((0, 2), (1, 4))),
        "ln_gain": jnp.clip(1.0 + 0.18 * jax.random.normal(seeds[8], (2, D), jnp.float32), 0.1, 1.9),
        "ln_bias": gaussian(seeds[9], (2, D), 0.3, 1.5, (), jnp.float32),
        "a_qkv": gaussian(seeds[10], (3, D, NR), D ** -0.5, 0.125),
        "b_qkv": gaussian(seeds[11], (3, NR, D), (10 * RANK) ** -0.5, 0.5, ((2, 2),)),
        "a_out": gaussian(seeds[12], (D, NR), (D * 4 // L) ** -0.5, 2.0, ((0, 2),)),
        "b_out": gaussian(seeds[13], (NR, D), (10 * RANK) ** -0.5, 0.5),
        "a_up": gaussian(seeds[14], (D, NR), D ** -0.5, 0.125),
        "b_up": gaussian(seeds[15], (NR, FF), (10 * RANK) ** -0.5, 0.5, ((1, 2),)),
        "a_down": gaussian(seeds[16], (FF, NR), FF ** -0.5, 0.0625, ((0, 2),)),
        "b_down": gaussian(seeds[17], (NR, D), (10 * RANK) ** -0.5, 0.5),
    }


@jax.custom_vjp
def low(v):
    return lax.optimization_barrier(v.astype(jnp.bfloat16)).astype(jnp.float32)

@jax.custom_vjp
def low_back(v):
    return v

def low_keep(v):
    return (low(v), None)

def low_pass(kept, grad):
    return (grad,)

def back_keep(v):
    return (v, None)

def back_low(kept, grad):
    return (low(grad),)
low.defvjp(low_keep, low_pass)
low_back.defvjp(back_keep, back_low)
NORM_EPS = 1e-06
GELU_COEF = 0.7978845608028654

def matmul_high(left_side, right_side):
    return jnp.einsum('...i,ij->...j', left_side, right_side, precision=lax.Precision.HIGHEST)

def norm_rows(values, gain_row, shift_row):
    center = values - lax.optimization_barrier(jnp.mean(values, axis=-1, keepdims=True))
    spread = lax.optimization_barrier(jnp.mean(center * center, axis=-1, keepdims=True))
    return center * lax.rsqrt(spread + NORM_EPS) * gain_row + shift_row

def gelu_tanh(values):
    return 0.5 * values * (1.0 + jnp.tanh(GELU_COEF * (values + 0.044715 * values * values * values)))

def attend_one(packed):
    queries, keys_all, values_all, usable = packed
    score_scale = 1.0 / math.sqrt(HEAD_DIM)
    scores = low_back(jnp.einsum('qhd,khd->hqk', queries, keys_all, precision=lax.Precision.HIGHEST) * score_scale)
    scores = jnp.where(usable[None, None, :], scores, -1e+30)
    attn_probs = jax.nn.softmax(scores, axis=-1)
    return jnp.einsum('hqk,khd->qhd', low(attn_probs), values_all, precision=lax.Precision.HIGHEST)

def group_forward(inputs, group_lengths, group_ids, frozen, adapters):
    w_qkv, w_out, w_up, w_down, ln_gain, ln_bias = frozen
    a_qkv, b_qkv, a_out, b_out, a_up, b_up, a_down, b_down = adapters
    picked = (group_ids[:, None] == jnp.arange(ADAPTERS)[None, :]).astype(jnp.float32)
    pick_cols = jnp.repeat(picked, RANK, axis=1)[:, None, :]

    def adapt(source, a_matrix):
        return low(low_back(matmul_high(source, a_matrix) * pick_cols))
    by_head = []
    for proj_index in range(3):
        adapt_part = adapt(inputs, a_qkv[proj_index])
        projection = low(low_back(matmul_high(inputs, w_qkv[proj_index]) + matmul_high(adapt_part, b_qkv[proj_index])))
        by_head.append(projection.reshape(inputs.shape[0], L, HEADS, HEAD_DIM))
    positions = jnp.arange(L)
    usable = positions[None, :] < group_lengths[:, None]
    context = lax.map(jax.checkpoint(attend_one), (by_head[0], by_head[1], by_head[2], usable))
    context = low(low_back(context.reshape(inputs.shape[0], L, D)))
    adapt_out = adapt(context, a_out)
    attn_branch = low_back(matmul_high(context, w_out) + matmul_high(adapt_out, b_out))
    hidden_one = norm_rows(inputs + attn_branch, ln_gain[0], ln_bias[0])
    hidden_low = low(hidden_one)
    adapt_up = adapt(hidden_low, a_up)
    pre_act = low_back(matmul_high(hidden_low, w_up) + matmul_high(adapt_up, b_up))
    gelu_out = low(gelu_tanh(pre_act))
    adapt_down = adapt(gelu_out, a_down)
    down_branch = low_back(matmul_high(gelu_out, w_down) + matmul_high(adapt_down, b_down))
    return norm_rows(hidden_one + down_branch, ln_gain[1], ln_bias[1])

def reference(x_in, cotangent, lengths, adapter_ids, w_qkv, w_out, w_up, w_down, ln_gain, ln_bias, a_qkv, b_qkv, a_out, b_out, a_up, b_up, a_down, b_down):
    frozen = tuple((weight.astype(jnp.float32) for weight in (w_qkv, w_out, w_up, w_down, ln_gain, ln_bias)))
    adapters = tuple((weight.astype(jnp.float32) for weight in (a_qkv, b_qkv, a_out, b_out, a_up, b_up, a_down, b_down)))
    groups = x_in.shape[0] // 4
    inputs = x_in.astype(jnp.float32).reshape(groups, 4, L, D)
    group_lengths = lengths.reshape(groups, 4)
    group_ids = adapter_ids.reshape(groups, 4)
    checked = jax.checkpoint(group_forward)

    def whole_layer(inputs_all, adapter_set):

        def scan_step(scan_carry, pieces):
            return (scan_carry, checked(pieces[0], pieces[1], pieces[2], frozen, adapter_set))
        carry_end, outputs = lax.scan(scan_step, jnp.zeros((), jnp.float32), (inputs_all, group_lengths, group_ids))
        return outputs
    layer_out, pull_back = jax.vjp(whole_layer, inputs, adapters)
    grad_in, grad_set = pull_back(cotangent.astype(jnp.float32).reshape(groups, 4, L, D))
    full_shape = x_in.shape
    return (layer_out.reshape(full_shape).astype(jnp.bfloat16), grad_in.reshape(full_shape).astype(jnp.bfloat16), grad_set[0], grad_set[1], grad_set[2], grad_set[3], grad_set[4], grad_set[5], grad_set[6], grad_set[7])
```

```python
import math

import jax
import jax.numpy as jnp
from jax import lax
from jax.experimental import pallas as pl
from jax.experimental.pallas import tpu as pltpu
from jax.sharding import PartitionSpec as P

HEAD_DIM = 128
RANK = 16
ADAPTERS = 8
NR = RANK * ADAPTERS
NORM_EPS = 1e-06
GELU_COEF = 0.7978845608028654
SCALE = 1.0 / math.sqrt(HEAD_DIM)
GROUPS = 2
F32 = jnp.float32
BF16 = jnp.bfloat16


def dot(left, right):
    return jnp.dot(left, right, preferred_element_type=F32)


def dot_nt(left, right):
    return lax.dot_general(left, right, (((1,), (1,)), ((), ())), preferred_element_type=F32)


def dot_tn(left, right):
    return lax.dot_general(left, right, (((0,), (0,)), ((), ())), preferred_element_type=F32)


def shift(block, axis, step):
    n = lax.axis_size(axis)
    return lax.ppermute(block, axis, [(i, (i + step) % n) for i in range(n)])


def swap(block, axis, mask):
    n = lax.axis_size(axis)
    return lax.ppermute(block, axis, [(i, i ^ mask) for i in range(n)])


def masks_of(n):
    out = []
    while n > 1:
        n //= 2
        out.append(n)
    return out


def spread(pieces, axis):
    for mask in masks_of(lax.axis_size(axis)):
        pieces = pieces + [swap(piece, axis, mask) for piece in pieces]
    return pieces


def offsets(n):
    out = [0]
    for mask in masks_of(n):
        out = out + [o ^ mask for o in out]
    return out


def fold(pieces, axis):
    for mask in reversed(masks_of(lax.axis_size(axis))):
        half = len(pieces) // 2
        got = [swap(piece, axis, mask) for piece in pieces[half:]]
        pieces = [
            (mine.astype(F32) + other.astype(F32)).astype(BF16)
            for mine, other in zip(pieces[:half], got)
        ]
    return pieces[0]


def both(part):
    low = part.astype(BF16)
    for mask in masks_of(lax.axis_size("tp")):
        total = low.astype(F32) + swap(low, "tp", mask).astype(F32)
        low = total.astype(BF16)
    return total


def attend_kernel(n_piece, q_ref, bias_ref, *refs):
    kv_refs, (out_ref, log_ref) = refs[:n_piece], refs[n_piece:]
    query = q_ref[0]
    loc = query.shape[0]
    scores = []
    for j in range(n_piece):
        bias = bias_ref[0, pl.ds(j * loc, loc), :]
        bias = jnp.concatenate([bias] * (loc // 128), axis=1)
        scores.append(dot_nt(kv_refs[j][0, 0], query) * SCALE + bias)
    top = scores[0].max(axis=0, keepdims=True)
    for s in scores[1:]:
        top = jnp.maximum(top, s.max(axis=0, keepdims=True))
    total = jnp.zeros_like(top)
    mixed = None
    for j in range(n_piece):
        probs = jnp.exp(scores[j] - top)
        total = total + probs.sum(axis=0, keepdims=True)
        term = dot_tn(kv_refs[j][1, 0], probs.astype(BF16))
        mixed = term if mixed is None else mixed + term
    out_ref[0] = (mixed / total).T.astype(BF16)
    log_ref[0, 0] = top + jnp.log(total)


def attend_back_kernel(n_piece, q_ref, bias_ref, g_ref, log_ref, *refs):
    kv_refs, dq_ref, dkv_refs = refs[:n_piece], refs[n_piece], refs[n_piece + 1 :]
    query = q_ref[0]
    grad = g_ref[0]
    log_total = log_ref[0, 0]
    loc = query.shape[0]
    probs, dprobs = [], []
    delta = jnp.zeros_like(log_total)
    for j in range(n_piece):
        bias = bias_ref[0, pl.ds(j * loc, loc), :]
        bias = jnp.concatenate([bias] * (loc // 128), axis=1)
        p = jnp.exp(dot_nt(kv_refs[j][0, 0], query) * SCALE + bias - log_total)
        dp = dot_nt(kv_refs[j][1, 0], grad)
        dkv_refs[j][1, 0] = dot(p.astype(BF16), grad).astype(BF16)
        delta = delta + (p * dp).sum(axis=0, keepdims=True)
        probs.append(p)
        dprobs.append(dp)
    dq = None
    for j in range(n_piece):
        ds = (probs[j] * (dprobs[j] - delta)).astype(BF16)
        dkv_refs[j][0, 0] = (dot(ds, query) * SCALE).astype(BF16)
        term = dot_tn(kv_refs[j][0, 0], ds)
        dq = term if dq is None else dq + term
    dq_ref[0] = (dq * SCALE).T.astype(BF16)


def attend_specs(n_seq, loc, n_piece):
    row = pl.BlockSpec((1, loc, HEAD_DIM), lambda s, h: (s, 0, h))
    bias = pl.BlockSpec((1, n_piece * loc, 128), lambda s, h: (s, 0, 0))
    pair = pl.BlockSpec((2, 1, loc, HEAD_DIM), lambda s, h: (0, s, 0, h))
    log = pl.BlockSpec((1, 1, 1, loc), lambda s, h: (s, h, 0, 0))
    return row, bias, pair, log


def attend(query, kv, bias):
    n_seq, loc, width = query.shape
    n_piece, heads = len(kv), width // HEAD_DIM
    row, bias_spec, pair, log = attend_specs(n_seq, loc, n_piece)
    return pl.pallas_call(
        lambda *refs: attend_kernel(n_piece, *refs),
        grid=(n_seq, heads),
        in_specs=[row, bias_spec] + [pair] * n_piece,
        out_specs=[row, log],
        out_shape=[
            jax.ShapeDtypeStruct(query.shape, BF16),
            jax.ShapeDtypeStruct((n_seq, heads, 1, loc), F32),
        ],
        compiler_params=pltpu.CompilerParams(vmem_limit_bytes=32 << 20),
        cost_estimate=pl.CostEstimate(
            flops=n_seq * heads * 4 * loc * loc * n_piece * HEAD_DIM * 4,
            bytes_accessed=2 * n_seq * loc * width * (2 + 2 * n_piece),
            transcendentals=n_seq * heads * loc * loc * n_piece,
        ),
    )(query, bias, *kv)


def attend_back(query, kv, bias, grad, log_total):
    n_seq, loc, width = query.shape
    n_piece, heads = len(kv), width // HEAD_DIM
    row, bias_spec, pair, log = attend_specs(n_seq, loc, n_piece)
    out = pl.pallas_call(
        lambda *refs: attend_back_kernel(n_piece, *refs),
        grid=(n_seq, heads),
        in_specs=[row, bias_spec, row, log] + [pair] * n_piece,
        out_specs=[row] + [pair] * n_piece,
        out_shape=[jax.ShapeDtypeStruct(query.shape, BF16)]
        + [jax.ShapeDtypeStruct(kv[0].shape, BF16)] * n_piece,
        compiler_params=pltpu.CompilerParams(vmem_limit_bytes=40 << 20),
        cost_estimate=pl.CostEstimate(
            flops=n_seq * heads * 10 * loc * loc * n_piece * HEAD_DIM * 4,
            bytes_accessed=2 * n_seq * loc * width * (3 + 4 * n_piece),
            transcendentals=n_seq * heads * loc * loc * n_piece,
        ),
    )(query, bias, grad, log_total, *kv)
    return out[0], list(out[1:])


def norm_parts(values):
    center = values - jnp.mean(values, axis=-1, keepdims=True)
    rstd = lax.rsqrt(jnp.mean(center * center, axis=-1, keepdims=True) + NORM_EPS)
    return center * rstd, rstd


def norm_back(hat, rstd, dhat):
    first = jnp.mean(dhat, axis=-1, keepdims=True)
    second = jnp.mean(dhat * hat, axis=-1, keepdims=True)
    return rstd * (dhat - first - hat * second)


def gelu_both(pre):
    square = pre * pre
    bent = jnp.tanh(GELU_COEF * (pre + 0.044715 * square * pre))
    out = 0.5 * pre * (1.0 + bent)
    slope = 0.5 * (1.0 + bent) + 0.5 * pre * (1.0 - bent * bent) * GELU_COEF * (
        1.0 + 3.0 * 0.044715 * square
    )
    return out.astype(BF16), slope.astype(BF16)


def local(
    x_in,
    cotangent,
    lengths,
    adapter_ids,
    w_qkv,
    w_out,
    w_up,
    w_down,
    ln_gain,
    ln_bias,
    a_qkv,
    b_qkv,
    a_out,
    b_out,
    a_up,
    b_up,
    a_down,
    b_down,
):
    n_ctx, n_fsdp = lax.axis_size("ctx"), lax.axis_size("fsdp")
    z, ct = lax.axis_index("fsdp"), lax.axis_index("ctx")
    seqs, piece, width = x_in.shape
    per = seqs // n_fsdp
    loc = n_fsdp * piece
    heads_width = w_qkv.shape[2]
    n_group = GROUPS if per % GROUPS == 0 else 1
    g_per = per // n_group
    g_rows = g_per * loc

    def take(array, start, size, axis=0):
        return lax.dynamic_slice_in_dim(array, start, size, axis)

    def put(array, block, *starts):
        return lax.dynamic_update_slice(array, block, starts)

    def deal(array, group):
        out = []
        for step in range(n_fsdp):
            to = lax.rem(z + step, n_fsdp)
            block = take(array, to * per + group * g_per, g_per)
            out.append(block if step == 0 else shift(block, "fsdp", step))
        return jnp.concatenate(out, axis=1)

    def undeal(rows, group_out):
        rows = rows.reshape(g_per, n_fsdp, piece, width)
        out = []
        for step in range(n_fsdp):
            block = rows[:, step]
            out.append(block if step == 0 else shift(block, "fsdp", -step))
        return out

    def gathered(shard, z_axis, full):
        size = shard.shape[0] // n_ctx
        mine = take(shard, ct * size, size)
        got = [shift(mine, "fsdp", step) for step in range(1, n_fsdp)]
        pieces = spread([jnp.stack(got)], "ctx")
        z_size = shard.shape[z_axis]
        full = put(full, shard, *((z * z_size, 0) if z_axis == 0 else (0, z * z_size)))
        for offset, block in zip(offsets(n_ctx), pieces):
            row = (ct ^ offset) * size
            for step in range(1, n_fsdp):
                start = lax.rem(z - step + n_fsdp, n_fsdp) * z_size
                at = (start + row, 0) if z_axis == 0 else (row, start)
                full = put(full, block[step - 1], *at)
        return full

    zero = jnp.zeros((), BF16)
    bands = [jnp.pad(b_qkv[j], ((0, 0), (j * heads_width, (2 - j) * heads_width))) for j in range(3)]
    qkv_base = jnp.pad(jnp.concatenate(bands, axis=0), ((width, 0), (0, 0)))
    qkv_shard = w_qkv.transpose(1, 0, 2).reshape(w_qkv.shape[1], 3 * heads_width)
    qkv_x = gathered(qkv_shard, 0, qkv_base)
    out_x = gathered(w_out, 1, jnp.pad(a_out, ((0, 0), (width, 0))))
    up_x = gathered(w_up, 0, jnp.pad(b_up, ((width, 0), (0, 0))))
    down_x = gathered(w_down, 1, jnp.pad(a_down, ((0, 0), (width, 0))))
    a_in = a_qkv.transpose(1, 0, 2).reshape(width, 3 * NR)

    my_lengths = take(lengths, z * per, per)
    my_ids = take(adapter_ids, z * per, per)
    picked = (my_ids[:, None] == jnp.arange(NR)[None, :] // RANK).astype(F32)
    steps = lax.rem(z - jnp.arange(n_fsdp) + n_fsdp, n_fsdp)
    ctx_of = ct ^ jnp.array(offsets(n_ctx))
    key_pos = (
        (steps[None, :, None] * n_ctx + ctx_of[:, None, None]) * piece
        + jnp.arange(piece)[None, None, :]
    ).reshape(-1)
    bias_all = jnp.where(key_pos[None, :] < my_lengths[:, None], 0.0, -1e30).astype(F32)
    bias_all = jnp.broadcast_to(bias_all[:, :, None], bias_all.shape + (128,))

    acts, ins = [], []
    early, late = [], []
    for group in range(n_group):
        pick = jnp.repeat(take(picked, group * g_per, g_per), loc, axis=0)
        pick3 = jnp.concatenate([pick] * 3, axis=1)
        bias = bias_all[group * g_per : (group + 1) * g_per]
        x_rows = deal(x_in, group).reshape(g_rows, width)
        grad_out = deal(cotangent, group).reshape(g_rows, width)

        def compact(codes, values, j=0):
            out = []
            for n in range(g_per):
                first = my_ids[group * g_per + n] * RANK + j * NR
                rows = slice(n * loc, (n + 1) * loc)
                out.append(dot_tn(take(codes[rows], first, RANK, 1), values[rows]).astype(BF16))
            return jnp.concatenate(out, axis=0)

        adapt_in = (dot(x_rows, a_in) * pick3).astype(BF16)
        proj = dot(jnp.concatenate([x_rows, adapt_in], axis=1), qkv_x).astype(BF16)
        query = proj[:, :heads_width].reshape(g_per, loc, heads_width)
        pair = jnp.stack([proj[:, heads_width : 2 * heads_width], proj[:, 2 * heads_width :]])
        kv = spread([pair.reshape(2, g_per, loc, heads_width)], "ctx")
        context, log_total = attend(query, kv, bias)
        ctx_rows = context.reshape(g_rows, heads_width)
        summed = both(dot(ctx_rows, out_x))
        adapt_out = (summed[:, width:] * pick).astype(BF16)
        hat1, rstd1 = norm_parts(x_rows.astype(F32) + summed[:, :width] + dot(adapt_out, b_out))
        hidden = hat1 * ln_gain[0] + ln_bias[0]
        hidden_low = hidden.astype(BF16)
        adapt_up = (dot(hidden_low, a_up) * pick).astype(BF16)
        gelu_out, slope = gelu_both(dot(jnp.concatenate([hidden_low, adapt_up], axis=1), up_x))
        summed = both(dot(gelu_out, down_x))
        adapt_down = (summed[:, width:] * pick).astype(BF16)
        hat2, rstd2 = norm_parts(hidden + summed[:, :width] + dot(adapt_down, b_down))
        layer_out = (hat2 * ln_gain[1] + ln_bias[1]).astype(BF16)
        acts.append(undeal(layer_out, group))

        dy2 = norm_back(hat2, rstd2, grad_out.astype(F32) * ln_gain[1])
        d_down = dy2.astype(BF16)
        dadapt_down = (dot_nt(d_down, b_down) * pick).astype(BF16)
        d_gelu = dot_nt(jnp.concatenate([d_down, dadapt_down], axis=1), down_x)
        d_pre = (d_gelu * slope.astype(F32)).astype(BF16)
        summed = both(dot_nt(d_pre, up_x))
        dadapt_up = (summed[:, width:] * pick).astype(BF16)
        dh1 = dy2 + summed[:, :width] + dot_nt(dadapt_up, a_up)
        dy1 = norm_back(hat1, rstd1, dh1 * ln_gain[0])
        d_attn = dy1.astype(BF16)
        dadapt_out = (dot_nt(d_attn, b_out) * pick).astype(BF16)
        d_context = dot_nt(jnp.concatenate([d_attn, dadapt_out], axis=1), out_x).astype(BF16)
        early.append(
            jnp.concatenate(
                [
                    compact(adapt_down, d_down),
                    compact(dadapt_down, gelu_out),
                    compact(adapt_up, d_pre),
                    compact(dadapt_up, hidden_low),
                    compact(adapt_out, d_attn),
                    compact(dadapt_out, ctx_rows),
                ],
                axis=1,
            )
        )
        d_query, d_kv = attend_back(
            query, kv, bias, d_context.reshape(g_per, loc, heads_width), log_total
        )
        d_pair = fold(d_kv, "ctx").reshape(2, g_rows, heads_width)
        d_proj = jnp.concatenate([d_query.reshape(g_rows, heads_width), d_pair[0], d_pair[1]], axis=1)
        summed = both(dot_nt(d_proj, qkv_x))
        dadapt_in = (summed[:, width:] * pick3).astype(BF16)
        d_x = (dy1 + summed[:, :width] + dot_nt(dadapt_in, a_in)).astype(BF16)
        ins.append(undeal(d_x, group))
        late.append(
            jnp.concatenate(
                [
                    compact(adapt_in, d_proj[:, j * heads_width : (j + 1) * heads_width], j)
                    for j in range(3)
                ]
                + [compact(dadapt_in, x_rows, j) for j in range(3)],
                axis=1,
            )
        )

    def assemble(parts):
        full = jnp.zeros((seqs, piece, width), BF16)
        for group, blocks in enumerate(parts):
            for step, block in enumerate(blocks):
                owner = lax.rem(z + step, n_fsdp)
                full = put(full, block, owner * per + group * g_per, 0, 0)
        return full

    codes = (adapter_ids[:, None] * RANK + jnp.arange(RANK)[None, :]).reshape(-1)
    chosen = (codes[:, None] == jnp.arange(NR)[None, :]).astype(BF16)

    def everywhere(parts):
        mine = jnp.concatenate(parts, axis=0)
        rows, columns = mine.shape
        size = columns // n_ctx
        blocks = [take(mine, (ct ^ offset) * size, size, 1) for offset in offsets(n_ctx)]
        own = fold(blocks, "ctx")
        got = jnp.stack([own] + [shift(own, "fsdp", step) for step in range(1, n_fsdp)])
        full = jnp.zeros((n_fsdp * rows, columns), BF16)
        for offset, block in zip(offsets(n_ctx), spread([got], "ctx")):
            for step in range(n_fsdp):
                owner = lax.rem(z - step + n_fsdp, n_fsdp)
                full = put(full, block[step], owner * rows, (ct ^ offset) * size)
        return full

    def split(full, sizes):
        out, at = [], 0
        for size in sizes:
            out.append(full[:, at : at + size])
            at += size
        return out

    units = w_up.shape[1]
    e = split(everywhere(early), [width, units, units, width, width, heads_width])
    l = split(everywhere(late), [heads_width] * 3 + [width] * 3)
    return (
        assemble(acts),
        assemble(ins),
        jnp.stack([dot_tn(l[3 + j], chosen) for j in range(3)]),
        jnp.stack([dot_tn(chosen, l[j]) for j in range(3)]),
        dot_tn(e[5], chosen),
        dot_tn(chosen, e[4]),
        dot_tn(e[3], chosen),
        dot_tn(chosen, e[2]),
        dot_tn(e[1], chosen),
        dot_tn(chosen, e[0]),
    )


def solution(mesh):
    rows = P(None, ("fsdp", "ctx"), None)
    return jax.shard_map(
        local,
        mesh=mesh,
        in_specs=(
            rows,
            rows,
            P(),
            P(),
            P(None, "fsdp", "tp"),
            P("tp", "fsdp"),
            P("fsdp", "tp"),
            P("tp", "fsdp"),
            P(),
            P(),
            P(),
            P(None, None, "tp"),
            P("tp", None),
            P(),
            P(),
            P(None, "tp"),
            P("tp", None),
            P(),
        ),
        out_specs=(
            rows,
            rows,
            P(),
            P(None, None, "tp"),
            P("tp", None),
            P(),
            P(),
            P(None, "tp"),
            P("tp", None),
            P(),
        ),
        check_vma=False,
    )
```

```python
import math

import jax
import jax.numpy as jnp
from jax import lax
from jax.experimental import pallas as pl
from jax.experimental.pallas import tpu as pltpu
from jax.sharding import PartitionSpec as P

HEAD_DIM = 128
RANK = 16
ADAPTERS = 8
NR = RANK * ADAPTERS
NORM_EPS = 1e-06
GELU_COEF = 0.7978845608028654
SCALE = 1.0 / math.sqrt(HEAD_DIM)
GROUPS = 2
F32 = jnp.float32
BF16 = jnp.bfloat16


def dot(left, right):
    return jnp.dot(left, right, preferred_element_type=F32)


def dot_nt(left, right):
    return lax.dot_general(left, right, (((1,), (1,)), ((), ())), preferred_element_type=F32)


def dot_tn(left, right):
    return lax.dot_general(left, right, (((0,), (0,)), ((), ())), preferred_element_type=F32)


def shift(block, axis, step):
    n = lax.axis_size(axis)
    return lax.ppermute(block, axis, [(i, (i + step) % n) for i in range(n)])


def swap(block, axis, mask):
    n = lax.axis_size(axis)
    return lax.ppermute(block, axis, [(i, i ^ mask) for i in range(n)])


def masks_of(n):
    out = []
    while n > 1:
        n //= 2
        out.append(n)
    return out


def spread(pieces, axis):
    for mask in masks_of(lax.axis_size(axis)):
        pieces = pieces + [swap(piece, axis, mask) for piece in pieces]
    return pieces


def offsets(n):
    out = [0]
    for mask in masks_of(n):
        out = out + [o ^ mask for o in out]
    return out


def fold(pieces, axis):
    for mask in reversed(masks_of(lax.axis_size(axis))):
        half = len(pieces) // 2
        got = [swap(piece, axis, mask) for piece in pieces[half:]]
        pieces = [
            (mine.astype(F32) + other.astype(F32)).astype(BF16)
            for mine, other in zip(pieces[:half], got)
        ]
    return pieces[0]


def both(part):
    low = part.astype(BF16)
    for mask in masks_of(lax.axis_size("tp")):
        total = low.astype(F32) + swap(low, "tp", mask).astype(F32)
        low = total.astype(BF16)
    return total


def attend_kernel(n_piece, q_ref, bias_ref, *refs):
    kv_refs, (out_ref, log_ref) = refs[:n_piece], refs[n_piece:]
    query = q_ref[0]
    loc = query.shape[0]
    scores = []
    for j in range(n_piece):
        bias = bias_ref[0, pl.ds(j * loc, loc), :]
        bias = jnp.concatenate([bias] * (loc // 128), axis=1)
        scores.append(dot_nt(kv_refs[j][0, 0], query) * SCALE + bias)
    top = scores[0].max(axis=0, keepdims=True)
    for s in scores[1:]:
        top = jnp.maximum(top, s.max(axis=0, keepdims=True))
    total = jnp.zeros_like(top)
    mixed = None
    for j in range(n_piece):
        probs = jnp.exp(scores[j] - top)
        total = total + probs.sum(axis=0, keepdims=True)
        term = dot_tn(kv_refs[j][1, 0], probs.astype(BF16))
        mixed = term if mixed is None else mixed + term
    out_ref[0] = (mixed / total).T.astype(BF16)
    log_ref[0, 0] = top + jnp.log(total)


def attend_back_kernel(n_piece, q_ref, bias_ref, g_ref, log_ref, *refs):
    kv_refs, dq_ref, dkv_refs = refs[:n_piece], refs[n_piece], refs[n_piece + 1 :]
    query = q_ref[0]
    grad = g_ref[0]
    log_total = log_ref[0, 0]
    loc = query.shape[0]
    probs, dprobs = [], []
    delta = jnp.zeros_like(log_total)
    for j in range(n_piece):
        bias = bias_ref[0, pl.ds(j * loc, loc), :]
        bias = jnp.concatenate([bias] * (loc // 128), axis=1)
        p = jnp.exp(dot_nt(kv_refs[j][0, 0], query) * SCALE + bias - log_total)
        dp = dot_nt(kv_refs[j][1, 0], grad)
        dkv_refs[j][1, 0] = dot(p.astype(BF16), grad).astype(BF16)
        delta = delta + (p * dp).sum(axis=0, keepdims=True)
        probs.append(p)
        dprobs.append(dp)
    dq = None
    for j in range(n_piece):
        ds = (probs[j] * (dprobs[j] - delta)).astype(BF16)
        dkv_refs[j][0, 0] = (dot(ds, query) * SCALE).astype(BF16)
        term = dot_tn(kv_refs[j][0, 0], ds)
        dq = term if dq is None else dq + term
    dq_ref[0] = (dq * SCALE).T.astype(BF16)


def attend_specs(n_seq, loc, n_piece, first):
    row = pl.BlockSpec((1, loc, HEAD_DIM), lambda s, h: (s, 0, h))
    bias = pl.BlockSpec((1, n_piece * loc, 128), lambda s, h: (s, 0, 0))
    pair = pl.BlockSpec((2, 1, loc, HEAD_DIM), lambda s, h: (0, s + first, 0, h))
    grads = pl.BlockSpec((2, 1, loc, HEAD_DIM), lambda s, h: (0, s, 0, h))
    log = pl.BlockSpec((1, 1, 1, loc), lambda s, h: (s, h, 0, 0))
    return row, bias, pair, log, grads


def attend(query, kv, bias, first):
    n_seq, loc, width = query.shape
    n_piece, heads = len(kv), width // HEAD_DIM
    row, bias_spec, pair, log, grads = attend_specs(n_seq, loc, n_piece, first)
    return pl.pallas_call(
        lambda *refs: attend_kernel(n_piece, *refs),
        grid=(n_seq, heads),
        in_specs=[row, bias_spec] + [pair] * n_piece,
        out_specs=[row, log],
        out_shape=[
            jax.ShapeDtypeStruct(query.shape, BF16),
            jax.ShapeDtypeStruct((n_seq, heads, 1, loc), F32),
        ],
        compiler_params=pltpu.CompilerParams(vmem_limit_bytes=32 << 20),
        cost_estimate=pl.CostEstimate(
            flops=n_seq * heads * 4 * loc * loc * n_piece * HEAD_DIM * 4,
            bytes_accessed=2 * n_seq * loc * width * (2 + 2 * n_piece),
            transcendentals=n_seq * heads * loc * loc * n_piece,
        ),
    )(query, bias, *kv)


def attend_back(query, kv, bias, grad, log_total, first):
    n_seq, loc, width = query.shape
    n_piece, heads = len(kv), width // HEAD_DIM
    row, bias_spec, pair, log, grads = attend_specs(n_seq, loc, n_piece, first)
    out = pl.pallas_call(
        lambda *refs: attend_back_kernel(n_piece, *refs),
        grid=(n_seq, heads),
        in_specs=[row, bias_spec, row, log] + [pair] * n_piece,
        out_specs=[row] + [grads] * n_piece,
        out_shape=[jax.ShapeDtypeStruct(query.shape, BF16)]
        + [jax.ShapeDtypeStruct((2, n_seq, loc, width), BF16)] * n_piece,
        compiler_params=pltpu.CompilerParams(vmem_limit_bytes=40 << 20),
        cost_estimate=pl.CostEstimate(
            flops=n_seq * heads * 10 * loc * loc * n_piece * HEAD_DIM * 4,
            bytes_accessed=2 * n_seq * loc * width * (3 + 4 * n_piece),
            transcendentals=n_seq * heads * loc * loc * n_piece,
        ),
    )(query, bias, grad, log_total, *kv)
    return out[0], list(out[1:])


def flip(ct, offset):
    mask = 1
    while mask <= offset:
        if offset & mask:
            ct = ct + mask - 2 * mask * lax.rem(ct // mask, 2)
        mask *= 2
    return ct


class Weight:
    def __init__(self, shard_at, whole_at):
        self.shard_at, self.whole_at = shard_at, whole_at


class Deal:
    def __init__(self, source_at, rows_at):
        self.source_at, self.rows_at = source_at, rows_at


class Pair:
    def __init__(self, slot_at):
        self.slot_at = slot_at


class Mover:
    def __init__(self, n_fsdp, n_ctx, send, recv):
        self.n_fsdp, self.n_ctx = n_fsdp, n_ctx
        self.z, self.ct = lax.axis_index("fsdp"), lax.axis_index("ctx")
        self.send, self.recv = send, recv
        self.used = 0
        self.open = []
        self.masks = masks_of(n_ctx)
        self.offsets = offsets(n_ctx)
        self.came, self.waiting = {}, {}

    def greet(self):
        barrier = pltpu.get_barrier_semaphore()
        others = [{"fsdp": lax.rem(self.z + s, self.n_fsdp)} for s in range(1, self.n_fsdp)]
        others += [{"ctx": flip(self.ct, mask)} for mask in self.masks]
        for other in others:
            pl.semaphore_signal(
                barrier, inc=1, device_id=other, device_id_type=pl.DeviceIdType.MESH
            )
        pl.semaphore_wait(barrier, len(others))

    def copy(self, source, target, device, at=None):
        if at is None:
            at = self.used
            self.used += 1
        return pltpu.make_async_remote_copy(
            src_ref=source,
            dst_ref=target,
            send_sem=self.send.at[at],
            recv_sem=self.recv.at[at],
            device_id=device,
            device_id_type=pl.DeviceIdType.MESH,
        )

    def go(self, source, target, device):
        copy = self.copy(source, target, device)
        copy.start()
        self.open.append((None, copy))
        return copy

    def along(self, item, owner, right, ok, source, slot):
        target = item.whole_at(owner, self.ct)
        device = {"fsdp": lax.rem(self.z + (1 if right else self.n_fsdp - 1), self.n_fsdp)}
        copy = self.copy(source, target, device, self.came[item] + slot - 1)
        pl.when(ok)(copy.start)
        self.open.append((ok, copy))

    def begin(self, item):
        if isinstance(item, Pair):
            self.waiting[item] = [[] for _ in self.masks]
            self.cast(item, item.slot_at, lambda k, level: item.slot_at(k + 2**level), 0, 0)
            return
        if isinstance(item, Weight):
            self.came[item] = self.used
            self.used += self.n_fsdp - 1
            source = item.shard_at(self.ct)
            self.along(item, self.z, True, self.z < self.n_fsdp - 1, source, 1)
            self.along(item, self.z, False, self.z > 0, source, self.n_fsdp - 1)
            return
        self.came[item] = [
            self.go(
                item.source_at(lax.rem(self.z + s, self.n_fsdp)),
                item.rows_at(s),
                {"fsdp": lax.rem(self.z + s, self.n_fsdp)},
            )
            for s in range(1, self.n_fsdp)
        ]

    def cast(self, item, source_at, target_at, k, first):
        for level in range(first, len(self.masks)):
            device = {"ctx": flip(self.ct, self.masks[level])}
            copy = self.go(source_at(k), target_at(k, level), device)
            self.waiting[item][level].append((copy, k + 2**level, source_at, target_at))

    def relay(self, item):
        if isinstance(item, Pair):
            return
        if isinstance(item, Deal):
            for copy in self.came[item]:
                copy.wait_recv()
            return
        self.waiting[item] = [[] for _ in self.masks]
        n = self.n_fsdp
        for i in range(n - 1):
            s = i // 2 + 1 if i % 2 == 0 else n - 1 - i // 2
            owner = lax.rem(self.z - s + n, n)
            here = item.whole_at(owner, self.ct)
            self.copy(here, here, {"fsdp": owner}, self.came[item] + s - 1).wait_recv()
            if s < n - 1:
                ok = (self.z >= s) & (self.z < n - 1)
                self.along(item, owner, True, ok, here, s + 1)
            if s > 1:
                ok = (self.z < s) & (self.z > 0)
                self.along(item, owner, False, ok, here, s - 1)

            def at(k, owner=owner):
                return item.whole_at(owner, flip(self.ct, self.offsets[k]))

            self.cast(item, at, lambda k, level, at=at: at(k), 0, 0)

    def finish(self, item, level):
        if isinstance(item, Deal):
            return
        for copy, k, source_at, target_at in self.waiting[item][level]:
            copy.wait_recv()
            self.cast(item, source_at, target_at, k, level + 1)

    def close(self):
        for ok, copy in self.open:
            if ok is None:
                copy.wait_send()
            else:
                pl.when(ok)(copy.wait_send)


def copies_of(items, n_fsdp, n_ctx):
    total = 0
    for item in items:
        total += {Weight: (n_fsdp - 1) * n_ctx, Deal: n_fsdp - 1, Pair: n_ctx - 1}[item]
    return total


def keep(stay, room, sems):
    out = []
    for k, (source, target) in enumerate(stay):
        first = pltpu.make_async_copy(source, room[k], sems.at[2 * k])
        first.start()
        out.append((first, pltpu.make_async_copy(room[k], target, sems.at[2 * k + 1])))
    return out


def move(make, kinds, inputs, outputs, n_fsdp, n_ctx, local_shapes, ident, ahead=2):
    n_in = len(inputs)
    n_copy = copies_of(kinds, n_fsdp, n_ctx)

    def kernel(*refs):
        ins, outs = refs[:n_in], refs[n_in : n_in + len(outputs)]
        send, recv, here = refs[n_in + len(outputs) : n_in + len(outputs) + 3]
        room = refs[n_in + len(outputs) + 3 :]
        mover = Mover(n_fsdp, n_ctx, send, recv)
        items, stay = make(ins, outs, mover.z)
        mover.greet()
        for item in items[:ahead]:
            mover.begin(item)
        kept = keep(stay, room, here)
        levels = len(mover.masks)
        for i in range(len(items) + levels):
            if i < len(items):
                mover.relay(items[i])
                if i + ahead < len(items):
                    mover.begin(items[i + ahead])
            if i == 0:
                for first, second in kept:
                    first.wait()
                    second.start()
            for level in range(levels):
                if 0 <= i - 1 - level < len(items):
                    mover.finish(items[i - 1 - level], level)
        for _, second in kept:
            second.wait()
        mover.close()

    return pl.pallas_call(
        kernel,
        in_specs=[pl.BlockSpec(memory_space=pl.ANY)] * n_in,
        out_specs=[pl.BlockSpec(memory_space=pl.ANY)] * len(outputs),
        out_shape=[jax.ShapeDtypeStruct(shape, BF16) for shape in outputs],
        scratch_shapes=[
            pltpu.SemaphoreType.DMA((n_copy,)),
            pltpu.SemaphoreType.DMA((n_copy,)),
            pltpu.SemaphoreType.DMA((2 * len(local_shapes),)),
        ]
        + [pltpu.VMEM(shape, BF16) for shape in local_shapes],
        compiler_params=pltpu.CompilerParams(
            collective_id=ident, has_side_effects=True, vmem_limit_bytes=32 << 20
        ),
    )(*inputs)


def norm_parts(values):
    center = values - jnp.mean(values, axis=-1, keepdims=True)
    rstd = lax.rsqrt(jnp.mean(center * center, axis=-1, keepdims=True) + NORM_EPS)
    return center * rstd, rstd


def norm_back(hat, rstd, dhat):
    first = jnp.mean(dhat, axis=-1, keepdims=True)
    second = jnp.mean(dhat * hat, axis=-1, keepdims=True)
    return rstd * (dhat - first - hat * second)


def gelu_both(pre):
    square = pre * pre
    bent = jnp.tanh(GELU_COEF * (pre + 0.044715 * square * pre))
    out = 0.5 * pre * (1.0 + bent)
    slope = 0.5 * (1.0 + bent) + 0.5 * pre * (1.0 - bent * bent) * GELU_COEF * (
        1.0 + 3.0 * 0.044715 * square
    )
    return out.astype(BF16), slope.astype(BF16)


def local(
    x_in,
    cotangent,
    lengths,
    adapter_ids,
    w_qkv,
    w_out,
    w_up,
    w_down,
    ln_gain,
    ln_bias,
    a_qkv,
    b_qkv,
    a_out,
    b_out,
    a_up,
    b_up,
    a_down,
    b_down,
):
    n_ctx, n_fsdp = lax.axis_size("ctx"), lax.axis_size("fsdp")
    z, ct = lax.axis_index("fsdp"), lax.axis_index("ctx")
    seqs, piece, width = x_in.shape
    per = seqs // n_fsdp
    loc = n_fsdp * piece
    heads_width = w_qkv.shape[2]
    n_group = GROUPS if per % GROUPS == 0 else 1
    g_per = per // n_group
    g_rows = g_per * loc

    def take(array, start, size, axis=0):
        return lax.dynamic_slice_in_dim(array, start, size, axis)

    def put(array, block, *starts):
        return lax.dynamic_update_slice(array, block, starts)

    def undeal(rows, group_out):
        rows = rows.reshape(g_per, n_fsdp, piece, width)
        out = []
        for step in range(n_fsdp):
            block = rows[:, step]
            out.append(block if step == 0 else shift(block, "fsdp", -step))
        return out

    units = w_up.shape[1]
    bands = [jnp.pad(b_qkv[j], ((0, 0), (j * heads_width, (2 - j) * heads_width))) for j in range(3)]
    qkv_foot = jnp.concatenate(bands, axis=0)
    rows_shape = (per, n_fsdp, piece, width)
    zq, zu = w_qkv.shape[1], w_up.shape[0]

    def first_items(ins, outs, z):
        x_ref, w_ref, foot_ref = ins
        rows_ref, whole_ref = outs

        def deal(g):
            return Deal(lambda to: x_ref.at[to * per + g], lambda s: rows_ref.at[g, s])

        def weight(j):
            size = zq // n_ctx
            columns = pl.ds(j * heads_width, heads_width)
            return Weight(
                lambda c: w_ref.at[j, pl.ds(pl.multiple_of(c * size, size), size)],
                lambda o, c: whole_ref.at[
                    pl.ds(pl.multiple_of(o * zq + c * size, size), size), columns
                ],
            )

        stay = [(x_ref.at[z * per + g], rows_ref.at[g, 0]) for g in range(per)]
        for j in range(3):
            own = whole_ref.at[
                pl.ds(pl.multiple_of(z * zq, zq), zq), pl.ds(j * heads_width, heads_width)
            ]
            stay.append((w_ref.at[j], own))
        stay.append((foot_ref, whole_ref.at[pl.ds(width, 3 * NR)]))
        items = [weight(0), deal(0), weight(1), weight(2)] + [deal(g) for g in range(1, per)]
        return items, stay

    x_all, qkv_x = move(
        first_items,
        [Weight] * 3 + [Deal] * per,
        (x_in, w_qkv, qkv_foot),
        (rows_shape, (width + 3 * NR, 3 * heads_width)),
        n_fsdp,
        n_ctx,
        ((piece, width),) * per + (w_qkv.shape[1:],) * 3 + (qkv_foot.shape,),
        0,
    )

    def second_items(ins, outs, z):
        kv_ref, cot_ref, wo_ref, wu_ref, wd_ref, ao_ref, bu_ref, ad_ref = ins
        slots, (rows_ref, out_ref, up_ref, down_ref) = outs[: n_ctx - 1], outs[n_ctx - 1 :]

        def ds(start, size):
            return pl.ds(pl.multiple_of(start, size), size)

        def deal(g):
            return Deal(lambda to: cot_ref.at[to * per + g], lambda s: rows_ref.at[g, s])

        zo = wo_ref.shape[1]
        so, su, sd = wo_ref.shape[0] // n_ctx, zu // n_ctx, wd_ref.shape[0] // n_ctx
        out_item = Weight(
            lambda c: wo_ref.at[ds(c * so, so)],
            lambda o, c: out_ref.at[ds(c * so, so), ds(o * zo, zo)],
        )

        def up_item(h):
            columns = pl.ds(h * (units // 2), units // 2)
            return Weight(
                lambda c: wu_ref.at[ds(c * su, su), columns],
                lambda o, c: up_ref.at[ds(o * zu + c * su, su), columns],
            )

        def down_item(h):
            half = sd // 2
            return Weight(
                lambda c: wd_ref.at[ds(c * sd + h * half, half)],
                lambda o, c: down_ref.at[ds(c * sd + h * half, half), ds(o * zo, zo)],
            )

        pair = Pair(lambda k: kv_ref if k == 0 else slots[k - 1])
        stay = [(cot_ref.at[z * per + g], rows_ref.at[g, 0]) for g in range(per)]
        stay += [
            (wo_ref, out_ref.at[:, ds(z * zo, zo)]),
            (wu_ref, up_ref.at[ds(z * zu, zu)]),
            (wd_ref, down_ref.at[:, ds(z * zo, zo)]),
            (ao_ref, out_ref.at[:, pl.ds(width, NR)]),
            (bu_ref, up_ref.at[pl.ds(width, NR)]),
            (ad_ref, down_ref.at[:, pl.ds(width, NR)]),
        ]
        items = [pair, out_item, up_item(0), up_item(1), down_item(0), down_item(1)]
        return items + [deal(g) for g in range(per)], stay

    a_in = a_qkv.transpose(1, 0, 2).reshape(width, 3 * NR)

    my_lengths = take(lengths, z * per, per)
    my_ids = take(adapter_ids, z * per, per)
    picked = (my_ids[:, None] == jnp.arange(NR)[None, :] // RANK).astype(F32)
    steps = lax.rem(z - jnp.arange(n_fsdp) + n_fsdp, n_fsdp)
    ctx_of = ct ^ jnp.array(offsets(n_ctx))
    key_pos = (
        (steps[None, :, None] * n_ctx + ctx_of[:, None, None]) * piece
        + jnp.arange(piece)[None, None, :]
    ).reshape(-1)
    bias_all = jnp.where(key_pos[None, :] < my_lengths[:, None], 0.0, -1e30).astype(F32)
    bias_all = jnp.broadcast_to(bias_all[:, :, None], bias_all.shape + (128,))

    pick_all = jnp.repeat(picked, loc, axis=0)
    x_flat = x_all.reshape(per * loc, width)
    adapt_all = (dot(x_flat, a_in) * jnp.concatenate([pick_all] * 3, axis=1)).astype(BF16)
    proj_all = dot(jnp.concatenate([x_flat, adapt_all], axis=1), qkv_x).astype(BF16)
    kv_own = jnp.stack([proj_all[:, heads_width : 2 * heads_width], proj_all[:, 2 * heads_width :]])
    kv_own = kv_own.reshape(2, per, loc, heads_width)
    moved = move(
        second_items,
        [Pair] + [Weight] * 5 + [Deal] * per,
        (kv_own, cotangent, w_out, w_up, w_down, a_out, b_up, a_down),
        ((2, per, loc, heads_width),) * (n_ctx - 1)
        + (
            rows_shape,
            (heads_width, width + NR),
            (width + NR, units),
            (units, width + NR),
        ),
        n_fsdp,
        n_ctx,
        ((piece, width),) * per
        + (w_out.shape, w_up.shape, w_down.shape, a_out.shape, b_up.shape, a_down.shape),
        1,
    )
    kv_all = [kv_own] + list(moved[: n_ctx - 1])
    cot_all, out_x, up_x, down_x = moved[n_ctx - 1 :]
    cot_flat = cot_all.reshape(per * loc, width)

    acts, ins = [], []
    early, late = [], []
    for group in range(n_group):
        mine = slice(group * g_rows, (group + 1) * g_rows)
        pick = jnp.repeat(take(picked, group * g_per, g_per), loc, axis=0)
        pick3 = jnp.concatenate([pick] * 3, axis=1)
        bias = bias_all[group * g_per : (group + 1) * g_per]
        x_rows = x_flat[mine]
        grad_out = cot_flat[mine]
        adapt_in = adapt_all[mine]
        query = proj_all[mine, :heads_width].reshape(g_per, loc, heads_width)
        first = group * g_per

        def compact(codes, values, j=0):
            out = []
            for n in range(g_per):
                first = my_ids[group * g_per + n] * RANK + j * NR
                rows = slice(n * loc, (n + 1) * loc)
                out.append(dot_tn(take(codes[rows], first, RANK, 1), values[rows]).astype(BF16))
            return jnp.concatenate(out, axis=0)

        context, log_total = attend(query, kv_all, bias, first)
        ctx_rows = context.reshape(g_rows, heads_width)
        summed = both(dot(ctx_rows, out_x))
        adapt_out = (summed[:, width:] * pick).astype(BF16)
        hat1, rstd1 = norm_parts(x_rows.astype(F32) + summed[:, :width] + dot(adapt_out, b_out))
        hidden = hat1 * ln_gain[0] + ln_bias[0]
        hidden_low = hidden.astype(BF16)
        adapt_up = (dot(hidden_low, a_up) * pick).astype(BF16)
        gelu_out, slope = gelu_both(dot(jnp.concatenate([hidden_low, adapt_up], axis=1), up_x))
        summed = both(dot(gelu_out, down_x))
        adapt_down = (summed[:, width:] * pick).astype(BF16)
        hat2, rstd2 = norm_parts(hidden + summed[:, :width] + dot(adapt_down, b_down))
        layer_out = (hat2 * ln_gain[1] + ln_bias[1]).astype(BF16)
        acts.append(undeal(layer_out, group))

        dy2 = norm_back(hat2, rstd2, grad_out.astype(F32) * ln_gain[1])
        d_down = dy2.astype(BF16)
        dadapt_down = (dot_nt(d_down, b_down) * pick).astype(BF16)
        d_gelu = dot_nt(jnp.concatenate([d_down, dadapt_down], axis=1), down_x)
        d_pre = (d_gelu * slope.astype(F32)).astype(BF16)
        summed = both(dot_nt(d_pre, up_x))
        dadapt_up = (summed[:, width:] * pick).astype(BF16)
        dh1 = dy2 + summed[:, :width] + dot_nt(dadapt_up, a_up)
        dy1 = norm_back(hat1, rstd1, dh1 * ln_gain[0])
        d_attn = dy1.astype(BF16)
        dadapt_out = (dot_nt(d_attn, b_out) * pick).astype(BF16)
        d_context = dot_nt(jnp.concatenate([d_attn, dadapt_out], axis=1), out_x).astype(BF16)
        early.append(
            jnp.concatenate(
                [
                    compact(adapt_down, d_down),
                    compact(dadapt_down, gelu_out),
                    compact(adapt_up, d_pre),
                    compact(dadapt_up, hidden_low),
                    compact(adapt_out, d_attn),
                    compact(dadapt_out, ctx_rows),
                ],
                axis=1,
            )
        )
        d_query, d_kv = attend_back(
            query, kv_all, bias, d_context.reshape(g_per, loc, heads_width), log_total, first
        )
        d_pair = fold(d_kv, "ctx").reshape(2, g_rows, heads_width)
        d_proj = jnp.concatenate([d_query.reshape(g_rows, heads_width), d_pair[0], d_pair[1]], axis=1)
        summed = both(dot_nt(d_proj, qkv_x))
        dadapt_in = (summed[:, width:] * pick3).astype(BF16)
        d_x = (dy1 + summed[:, :width] + dot_nt(dadapt_in, a_in)).astype(BF16)
        ins.append(undeal(d_x, group))
        late.append(
            jnp.concatenate(
                [
                    compact(adapt_in, d_proj[:, j * heads_width : (j + 1) * heads_width], j)
                    for j in range(3)
                ]
                + [compact(dadapt_in, x_rows, j) for j in range(3)],
                axis=1,
            )
        )

    def assemble(parts):
        full = jnp.zeros((seqs, piece, width), BF16)
        for group, blocks in enumerate(parts):
            for step, block in enumerate(blocks):
                owner = lax.rem(z + step, n_fsdp)
                full = put(full, block, owner * per + group * g_per, 0, 0)
        return full

    codes = (adapter_ids[:, None] * RANK + jnp.arange(RANK)[None, :]).reshape(-1)
    chosen = (codes[:, None] == jnp.arange(NR)[None, :]).astype(BF16)

    def everywhere(parts):
        mine = jnp.concatenate(parts, axis=0)
        rows, columns = mine.shape
        size = columns // n_ctx
        blocks = [take(mine, (ct ^ offset) * size, size, 1) for offset in offsets(n_ctx)]
        own = fold(blocks, "ctx")
        got = jnp.stack([own] + [shift(own, "fsdp", step) for step in range(1, n_fsdp)])
        full = jnp.zeros((n_fsdp * rows, columns), BF16)
        for offset, block in zip(offsets(n_ctx), spread([got], "ctx")):
            for step in range(n_fsdp):
                owner = lax.rem(z - step + n_fsdp, n_fsdp)
                full = put(full, block[step], owner * rows, (ct ^ offset) * size)
        return full

    def split(full, sizes):
        out, at = [], 0
        for size in sizes:
            out.append(full[:, at : at + size])
            at += size
        return out

    e = split(everywhere(early), [width, units, units, width, width, heads_width])
    l = split(everywhere(late), [heads_width] * 3 + [width] * 3)
    return (
        assemble(acts),
        assemble(ins),
        jnp.stack([dot_tn(l[3 + j], chosen) for j in range(3)]),
        jnp.stack([dot_tn(chosen, l[j]) for j in range(3)]),
        dot_tn(e[5], chosen),
        dot_tn(chosen, e[4]),
        dot_tn(e[3], chosen),
        dot_tn(chosen, e[2]),
        dot_tn(e[1], chosen),
        dot_tn(chosen, e[0]),
    )


def solution(mesh):
    rows = P(None, ("fsdp", "ctx"), None)
    return jax.shard_map(
        local,
        mesh=mesh,
        in_specs=(
            rows,
            rows,
            P(),
            P(),
            P(None, "fsdp", "tp"),
            P("tp", "fsdp"),
            P("fsdp", "tp"),
            P("tp", "fsdp"),
            P(),
            P(),
            P(),
            P(None, None, "tp"),
            P("tp", None),
            P(),
            P(),
            P(None, "tp"),
            P("tp", None),
            P(),
        ),
        out_specs=(
            rows,
            rows,
            P(),
            P(None, None, "tp"),
            P("tp", None),
            P(),
            P(),
            P(None, "tp"),
            P("tp", None),
            P(),
        ),
        check_vma=False,
    )
```

```python
import math

import jax
import jax.numpy as jnp
from jax import lax
from jax.experimental import pallas as pl
from jax.experimental.pallas import tpu as pltpu
from jax.sharding import PartitionSpec as P

HEAD_DIM = 128
RANK = 16
ADAPTERS = 8
NR = RANK * ADAPTERS
NORM_EPS = 1e-06
GELU_COEF = 0.7978845608028654
SCALE = 1.0 / math.sqrt(HEAD_DIM)
GROUPS = 2
F32 = jnp.float32
BF16 = jnp.bfloat16


def dot(left, right):
    return jnp.dot(left, right, preferred_element_type=F32)


def dot_nt(left, right):
    return lax.dot_general(left, right, (((1,), (1,)), ((), ())), preferred_element_type=F32)


def dot_tn(left, right):
    return lax.dot_general(left, right, (((0,), (0,)), ((), ())), preferred_element_type=F32)


def shift(block, axis, step):
    n = lax.axis_size(axis)
    return lax.ppermute(block, axis, [(i, (i + step) % n) for i in range(n)])


def swap(block, axis, mask):
    n = lax.axis_size(axis)
    return lax.ppermute(block, axis, [(i, i ^ mask) for i in range(n)])


def masks_of(n):
    out = []
    while n > 1:
        n //= 2
        out.append(n)
    return out


def spread(pieces, axis):
    for mask in masks_of(lax.axis_size(axis)):
        pieces = pieces + [swap(piece, axis, mask) for piece in pieces]
    return pieces


def offsets(n):
    out = [0]
    for mask in masks_of(n):
        out = out + [o ^ mask for o in out]
    return out


def fold(pieces, axis):
    for mask in reversed(masks_of(lax.axis_size(axis))):
        half = len(pieces) // 2
        got = [swap(piece, axis, mask) for piece in pieces[half:]]
        pieces = [
            (mine.astype(F32) + other.astype(F32)).astype(BF16)
            for mine, other in zip(pieces[:half], got)
        ]
    return pieces[0]


def both(low):
    for mask in masks_of(lax.axis_size("tp")):
        total = low.astype(F32) + swap(low, "tp", mask).astype(F32)
        low = total.astype(BF16)
    return total


def attend_kernel(n_piece, q_ref, bias_ref, *refs):
    kv_refs, (out_ref, log_ref) = refs[:n_piece], refs[n_piece:]
    query = q_ref[0]
    loc = query.shape[0]
    scores = []
    for j in range(n_piece):
        bias = bias_ref[0, pl.ds(j * loc, loc), :]
        bias = jnp.concatenate([bias] * (loc // 128), axis=1)
        scores.append(dot_nt(kv_refs[j][0, 0], query) * SCALE + bias)
    top = scores[0].max(axis=0, keepdims=True)
    for s in scores[1:]:
        top = jnp.maximum(top, s.max(axis=0, keepdims=True))
    total = jnp.zeros_like(top)
    mixed = None
    for j in range(n_piece):
        probs = jnp.exp(scores[j] - top)
        total = total + probs.sum(axis=0, keepdims=True)
        term = dot_tn(kv_refs[j][1, 0], probs.astype(BF16))
        mixed = term if mixed is None else mixed + term
    out_ref[0] = (mixed / total).T.astype(BF16)
    log_ref[0, 0] = top + jnp.log(total)


def attend_back_kernel(n_piece, q_ref, bias_ref, g_ref, log_ref, *refs):
    kv_refs, dq_ref, dkv_refs = refs[:n_piece], refs[n_piece], refs[n_piece + 1 :]
    query = q_ref[0]
    grad = g_ref[0]
    log_total = log_ref[0, 0]
    loc = query.shape[0]
    probs, dprobs = [], []
    delta = jnp.zeros_like(log_total)
    for j in range(n_piece):
        bias = bias_ref[0, pl.ds(j * loc, loc), :]
        bias = jnp.concatenate([bias] * (loc // 128), axis=1)
        p = jnp.exp(dot_nt(kv_refs[j][0, 0], query) * SCALE + bias - log_total)
        dp = dot_nt(kv_refs[j][1, 0], grad)
        dkv_refs[j][1, 0] = dot(p.astype(BF16), grad).astype(BF16)
        delta = delta + (p * dp).sum(axis=0, keepdims=True)
        probs.append(p)
        dprobs.append(dp)
    dq = None
    for j in range(n_piece):
        ds = (probs[j] * (dprobs[j] - delta)).astype(BF16)
        dkv_refs[j][0, 0] = (dot(ds, query) * SCALE).astype(BF16)
        term = dot_tn(kv_refs[j][0, 0], ds)
        dq = term if dq is None else dq + term
    dq_ref[0] = (dq * SCALE).T.astype(BF16)


def attend_specs(n_seq, loc, n_piece, first):
    row = pl.BlockSpec((1, loc, HEAD_DIM), lambda s, h: (s, 0, h))
    bias = pl.BlockSpec((1, n_piece * loc, 128), lambda s, h: (s, 0, 0))
    pair = pl.BlockSpec((2, 1, loc, HEAD_DIM), lambda s, h: (0, s + first, 0, h))
    grads = pl.BlockSpec((2, 1, loc, HEAD_DIM), lambda s, h: (0, s, 0, h))
    log = pl.BlockSpec((1, 1, 1, loc), lambda s, h: (s, h, 0, 0))
    return row, bias, pair, log, grads


def attend(query, kv, bias, first):
    n_seq, loc, width = query.shape
    n_piece, heads = len(kv), width // HEAD_DIM
    row, bias_spec, pair, log, grads = attend_specs(n_seq, loc, n_piece, first)
    return pl.pallas_call(
        lambda *refs: attend_kernel(n_piece, *refs),
        grid=(n_seq, heads),
        in_specs=[row, bias_spec] + [pair] * n_piece,
        out_specs=[row, log],
        out_shape=[
            jax.ShapeDtypeStruct(query.shape, BF16),
            jax.ShapeDtypeStruct((n_seq, heads, 1, loc), F32),
        ],
        compiler_params=pltpu.CompilerParams(vmem_limit_bytes=32 << 20),
        cost_estimate=pl.CostEstimate(
            flops=n_seq * heads * 4 * loc * loc * n_piece * HEAD_DIM * 4,
            bytes_accessed=2 * n_seq * loc * width * (2 + 2 * n_piece),
            transcendentals=n_seq * heads * loc * loc * n_piece,
        ),
    )(query, bias, *kv)


def attend_back(query, kv, bias, grad, log_total, first):
    n_seq, loc, width = query.shape
    n_piece, heads = len(kv), width // HEAD_DIM
    row, bias_spec, pair, log, grads = attend_specs(n_seq, loc, n_piece, first)
    out = pl.pallas_call(
        lambda *refs: attend_back_kernel(n_piece, *refs),
        grid=(n_seq, heads),
        in_specs=[row, bias_spec, row, log] + [pair] * n_piece,
        out_specs=[row] + [grads] * n_piece,
        out_shape=[jax.ShapeDtypeStruct(query.shape, BF16)]
        + [jax.ShapeDtypeStruct((2, n_seq, loc, width), BF16)] * n_piece,
        compiler_params=pltpu.CompilerParams(vmem_limit_bytes=40 << 20),
        cost_estimate=pl.CostEstimate(
            flops=n_seq * heads * 10 * loc * loc * n_piece * HEAD_DIM * 4,
            bytes_accessed=2 * n_seq * loc * width * (3 + 4 * n_piece),
            transcendentals=n_seq * heads * loc * loc * n_piece,
        ),
    )(query, bias, grad, log_total, *kv)
    return out[0], list(out[1:])


def flip(ct, offset):
    mask = 1
    while mask <= offset:
        if offset & mask:
            ct = ct + mask - 2 * mask * lax.rem(ct // mask, 2)
        mask *= 2
    return ct


class Weight:
    def __init__(self, shard_at, whole_at):
        self.shard_at, self.whole_at = shard_at, whole_at


class Deal:
    def __init__(self, source_at, rows_at):
        self.source_at, self.rows_at = source_at, rows_at


class Pair:
    def __init__(self, slot_at):
        self.slot_at = slot_at


class Mover:
    def __init__(self, n_fsdp, n_ctx, send, recv):
        self.n_fsdp, self.n_ctx = n_fsdp, n_ctx
        self.z, self.ct = lax.axis_index("fsdp"), lax.axis_index("ctx")
        self.send, self.recv = send, recv
        self.used = 0
        self.open = []
        self.masks = masks_of(n_ctx)
        self.offsets = offsets(n_ctx)
        self.came, self.waiting = {}, {}

    def greet(self):
        barrier = pltpu.get_barrier_semaphore()
        others = [{"fsdp": lax.rem(self.z + s, self.n_fsdp)} for s in range(1, self.n_fsdp)]
        others += [{"ctx": flip(self.ct, mask)} for mask in self.masks]
        for other in others:
            pl.semaphore_signal(
                barrier, inc=1, device_id=other, device_id_type=pl.DeviceIdType.MESH
            )
        pl.semaphore_wait(barrier, len(others))

    def copy(self, source, target, device, at=None):
        if at is None:
            at = self.used
            self.used += 1
        return pltpu.make_async_remote_copy(
            src_ref=source,
            dst_ref=target,
            send_sem=self.send.at[at],
            recv_sem=self.recv.at[at],
            device_id=device,
            device_id_type=pl.DeviceIdType.MESH,
        )

    def go(self, source, target, device):
        copy = self.copy(source, target, device)
        copy.start()
        self.open.append((None, copy))
        return copy

    def along(self, item, owner, right, ok, source, slot):
        target = item.whole_at(owner, self.ct)
        device = {"fsdp": lax.rem(self.z + (1 if right else self.n_fsdp - 1), self.n_fsdp)}
        copy = self.copy(source, target, device, self.came[item] + slot - 1)
        pl.when(ok)(copy.start)
        self.open.append((ok, copy))

    def begin(self, item):
        if isinstance(item, Pair):
            self.waiting[item] = [[] for _ in self.masks]
            self.cast(item, item.slot_at, lambda k, level: item.slot_at(k + 2**level), 0, 0)
            return
        if isinstance(item, Weight):
            self.came[item] = self.used
            self.used += self.n_fsdp - 1
            source = item.shard_at(self.ct)
            self.along(item, self.z, True, self.z < self.n_fsdp - 1, source, 1)
            self.along(item, self.z, False, self.z > 0, source, self.n_fsdp - 1)
            return
        self.came[item] = [
            self.go(
                item.source_at(lax.rem(self.z + s, self.n_fsdp)),
                item.rows_at(s),
                {"fsdp": lax.rem(self.z + s, self.n_fsdp)},
            )
            for s in range(1, self.n_fsdp)
        ]

    def cast(self, item, source_at, target_at, k, first):
        for level in range(first, len(self.masks)):
            device = {"ctx": flip(self.ct, self.masks[level])}
            copy = self.go(source_at(k), target_at(k, level), device)
            self.waiting[item][level].append((copy, k + 2**level, source_at, target_at))

    def relay(self, item):
        if isinstance(item, Pair):
            return
        if isinstance(item, Deal):
            for copy in self.came[item]:
                copy.wait_recv()
            return
        self.waiting[item] = [[] for _ in self.masks]
        n = self.n_fsdp
        for i in range(n - 1):
            s = i // 2 + 1 if i % 2 == 0 else n - 1 - i // 2
            owner = lax.rem(self.z - s + n, n)
            here = item.whole_at(owner, self.ct)
            self.copy(here, here, {"fsdp": owner}, self.came[item] + s - 1).wait_recv()
            if s < n - 1:
                ok = (self.z >= s) & (self.z < n - 1)
                self.along(item, owner, True, ok, here, s + 1)
            if s > 1:
                ok = (self.z < s) & (self.z > 0)
                self.along(item, owner, False, ok, here, s - 1)

            def at(k, owner=owner):
                return item.whole_at(owner, flip(self.ct, self.offsets[k]))

            self.cast(item, at, lambda k, level, at=at: at(k), 0, 0)

    def finish(self, item, level):
        if isinstance(item, Deal):
            return
        for copy, k, source_at, target_at in self.waiting[item][level]:
            copy.wait_recv()
            self.cast(item, source_at, target_at, k, level + 1)

    def close(self):
        for ok, copy in self.open:
            if ok is None:
                copy.wait_send()
            else:
                pl.when(ok)(copy.wait_send)


def copies_of(items, n_fsdp, n_ctx):
    total = 0
    for item in items:
        total += {Weight: (n_fsdp - 1) * n_ctx, Deal: n_fsdp - 1, Pair: n_ctx - 1}[item]
    return total


def keep(stay, room, sems):
    out = []
    for k, (source, target) in enumerate(stay):
        first = pltpu.make_async_copy(source, room[k], sems.at[2 * k])
        first.start()
        out.append((first, pltpu.make_async_copy(room[k], target, sems.at[2 * k + 1])))
    return out


def move(make, kinds, inputs, outputs, n_fsdp, n_ctx, local_shapes, ident, ahead=2, foot=None):
    n_in = len(inputs)
    n_copy = copies_of(kinds, n_fsdp, n_ctx)

    def kernel(*refs):
        ins, outs = refs[:n_in], refs[n_in : n_in + len(outputs)]
        send, recv, here = refs[n_in + len(outputs) : n_in + len(outputs) + 3]
        room = refs[n_in + len(outputs) + 3 :]
        if foot is not None:
            blocks_ref, ins = ins[-1], ins[:-1]
            strip = room[-1]
        mover = Mover(n_fsdp, n_ctx, send, recv)
        items, stay = make(ins, outs, mover.z)
        mover.greet()
        for item in items[:ahead]:
            mover.begin(item)
        kept = keep(stay, room, here)
        levels = len(mover.masks)
        for i in range(len(items) + levels):
            if i < len(items):
                mover.relay(items[i])
                if i + ahead < len(items):
                    mover.begin(items[i + ahead])
            if i == 0 and foot is not None:
                strip[...] = jnp.zeros_like(strip)
                high, wide = blocks_ref.shape[1:]
                for j in range(blocks_ref.shape[0]):
                    strip[j * high : (j + 1) * high, j * wide : (j + 1) * wide] = blocks_ref[j]
                set_foot = pltpu.make_async_copy(strip, foot[1](outs), here.at[2 * len(local_shapes)])
                set_foot.start()
                kept.append((None, set_foot))
            if i == 0:
                for first, second in kept:
                    if first is not None:
                        first.wait()
                        second.start()
            for level in range(levels):
                if 0 <= i - 1 - level < len(items):
                    mover.finish(items[i - 1 - level], level)
        for _, second in kept:
            second.wait()
        mover.close()

    spaces = [pl.BlockSpec(memory_space=pl.ANY)] * n_in
    room_shapes = list(local_shapes)
    if foot is not None:
        blocks = foot[0]
        inputs = inputs + (blocks,)
        n_in += 1
        spaces.append(pl.BlockSpec(memory_space=pltpu.VMEM))
        room_shapes.append((blocks.shape[0] * blocks.shape[1], blocks.shape[0] * blocks.shape[2]))
    return pl.pallas_call(
        kernel,
        in_specs=spaces,
        out_specs=[pl.BlockSpec(memory_space=pl.ANY)] * len(outputs),
        out_shape=[jax.ShapeDtypeStruct(shape, BF16) for shape in outputs],
        scratch_shapes=[
            pltpu.SemaphoreType.DMA((n_copy,)),
            pltpu.SemaphoreType.DMA((n_copy,)),
            pltpu.SemaphoreType.DMA((2 * len(local_shapes) + 1,)),
        ]
        + [pltpu.VMEM(shape, BF16) for shape in room_shapes],
        compiler_params=pltpu.CompilerParams(
            collective_id=ident, has_side_effects=True, vmem_limit_bytes=32 << 20
        ),
    )(*inputs)


def norm_parts(values):
    center = values - jnp.mean(values, axis=-1, keepdims=True)
    rstd = lax.rsqrt(jnp.mean(center * center, axis=-1, keepdims=True) + NORM_EPS)
    return center * rstd, rstd


def norm_back(hat, rstd, dhat):
    first = jnp.mean(dhat, axis=-1, keepdims=True)
    second = jnp.mean(dhat * hat, axis=-1, keepdims=True)
    return rstd * (dhat - first - hat * second)


def mm(left, right, nt, finish, tile, n_out=1, beside=None):
    rows, depth = left.shape
    columns = right.shape[0] if nt else right.shape[1]
    extra = [] if beside is None else [beside]
    sub = 128 if nt else tile

    def kernel(left_ref, right_ref, *refs):
        n_extra = len(extra)
        outs = refs[n_extra : n_extra + n_out]
        if nt:
            turned = refs[-1]

            @pl.when(pl.program_id(0) == 0)
            def _():
                turned[...] = left_ref[...].T

        for k in range(tile // sub):
            at = slice(k * sub, (k + 1) * sub)
            if nt:
                block = dot(right_ref[at, :], turned[...]).T
            else:
                block = dot(left_ref[...], right_ref[:, at])
            values = finish(block, *[ref[:, at] for ref in refs[:n_extra]])
            for ref, value in zip(outs, values):
                ref[:, at] = value

    part = pl.BlockSpec((rows, tile), lambda j: (0, j))
    out = pl.pallas_call(
        kernel,
        grid=(pl.cdiv(columns, tile),),
        in_specs=[
            pl.BlockSpec((rows, depth), lambda j: (0, 0)),
            pl.BlockSpec((tile, depth), lambda j: (j, 0))
            if nt
            else pl.BlockSpec((depth, tile), lambda j: (0, j)),
        ]
        + [part] * len(extra),
        out_specs=[part] * n_out,
        out_shape=[jax.ShapeDtypeStruct((rows, columns), BF16)] * n_out,
        scratch_shapes=[pltpu.VMEM((depth, rows), BF16)] if nt else [],
        compiler_params=pltpu.CompilerParams(vmem_limit_bytes=48 << 20),
        cost_estimate=pl.CostEstimate(
            flops=2 * rows * depth * columns,
            bytes_accessed=2 * (rows * depth + 2 * depth * columns + rows * columns * n_out),
            transcendentals=0,
        ),
    )(left, right, *extra)
    return out[0] if n_out == 1 else out


def compact(pairs, n_part):
    rows = pairs[0][0].shape[0]
    sizes = [values.shape[1] // n_part for _, values in pairs]
    total = sum(sizes)

    def kernel(*refs):
        out_ref = refs[-1]
        column = lax.broadcasted_iota(jnp.int32, (NR, RANK), 0)
        rank = lax.broadcasted_iota(jnp.int32, (NR, RANK), 1)
        used = jnp.where(lax.rem(column, RANK) == rank, 1.0, 0.0).astype(BF16)
        start = 0
        for i, size in enumerate(sizes):
            codes = dot(refs[2 * i][...], used).astype(BF16)
            block = dot_tn(codes, refs[2 * i + 1][...]).astype(BF16)
            for part in range(n_part):
                out_ref[part, :, start : start + size] = block[:, part * size : (part + 1) * size]
            start += size

    flat = [array for pair in pairs for array in pair]
    return pl.pallas_call(
        kernel,
        in_specs=[pl.BlockSpec(memory_space=pltpu.VMEM)] * len(flat),
        out_specs=pl.BlockSpec(memory_space=pltpu.VMEM),
        out_shape=jax.ShapeDtypeStruct((n_part, RANK, total), BF16),
        compiler_params=pltpu.CompilerParams(vmem_limit_bytes=40 << 20),
        cost_estimate=pl.CostEstimate(
            flops=2 * rows * RANK * total * n_part * 8,
            bytes_accessed=2 * rows * total * n_part,
            transcendentals=0,
        ),
    )(*flat)


def combine(pieces, chosen, shapes):
    n_part = len(pieces)
    n_fsdp, rows, columns = pieces[0].shape
    flat = []
    for i, shape in enumerate(shapes):
        for lead in range(shape[0] if len(shape) == 3 else 1):
            flat.append((i, lead if len(shape) == 3 else None, shape[-2:]))

    def kernel(chosen_ref, *refs):
        piece_refs, outs = refs[:n_part], refs[n_part:]
        z, ct = lax.axis_index("fsdp"), lax.axis_index("ctx")
        for k, offset in enumerate(offsets(n_part)):
            part = flip(ct, offset)
            ordered = jnp.concatenate(
                [piece_refs[k][lax.rem(z - a + n_fsdp, n_fsdp)] for a in range(n_fsdp)], axis=0
            )
            start = 0
            for i, lead, (high, wide) in flat:
                out_ref = outs[i] if lead is None else outs[i].at[lead]
                tall = wide == NR and high != NR
                size = (high if tall else wide) // n_part
                block = ordered[:, start : start + size]
                at = pl.ds(pl.multiple_of(part * size, size), size)
                if tall:
                    out_ref[at, :] = dot_tn(block, chosen_ref[...])
                else:
                    out_ref[:, at] = dot_tn(chosen_ref[...], block)
                start += size

    return pl.pallas_call(
        kernel,
        in_specs=[pl.BlockSpec(memory_space=pltpu.VMEM)] * (1 + n_part),
        out_specs=[pl.BlockSpec(memory_space=pltpu.VMEM)] * len(shapes),
        out_shape=[jax.ShapeDtypeStruct(shape, F32) for shape in shapes],
        compiler_params=pltpu.CompilerParams(vmem_limit_bytes=48 << 20),
        cost_estimate=pl.CostEstimate(
            flops=2 * NR * n_fsdp * rows * columns * n_part,
            bytes_accessed=2 * n_fsdp * rows * columns * n_part + 4 * NR * columns * n_part,
            transcendentals=0,
        ),
    )(chosen, *pieces)


def as_low(block):
    return (block.astype(BF16),)


def times(block, factor):
    return ((block * factor.astype(F32)).astype(BF16),)


def after(value, *first):
    return lax.optimization_barrier((value,) + first)[0]


def gelu_both(pre):
    square = pre * pre
    bent = jnp.tanh(GELU_COEF * (pre + 0.044715 * square * pre))
    out = 0.5 * pre * (1.0 + bent)
    slope = 0.5 * (1.0 + bent) + 0.5 * pre * (1.0 - bent * bent) * GELU_COEF * (
        1.0 + 3.0 * 0.044715 * square
    )
    return out.astype(BF16), slope.astype(BF16)


def local(
    x_in,
    cotangent,
    lengths,
    adapter_ids,
    w_qkv,
    w_out,
    w_up,
    w_down,
    ln_gain,
    ln_bias,
    a_qkv,
    b_qkv,
    a_out,
    b_out,
    a_up,
    b_up,
    a_down,
    b_down,
):
    n_ctx, n_fsdp = lax.axis_size("ctx"), lax.axis_size("fsdp")
    z, ct = lax.axis_index("fsdp"), lax.axis_index("ctx")
    seqs, piece, width = x_in.shape
    per = seqs // n_fsdp
    loc = n_fsdp * piece
    heads_width = w_qkv.shape[2]
    n_group = GROUPS if per % GROUPS == 0 else 1
    g_per = per // n_group
    g_rows = g_per * loc

    def take(array, start, size, axis=0):
        return lax.dynamic_slice_in_dim(array, start, size, axis)

    def put(array, block, *starts):
        return lax.dynamic_update_slice(array, block, starts)

    def undeal(rows, group_out):
        rows = rows.reshape(g_per, n_fsdp, piece, width)
        out = []
        for step in range(n_fsdp):
            block = rows[:, step]
            out.append(block if step == 0 else shift(block, "fsdp", -step))
        return out

    units = w_up.shape[1]
    rows_shape = (per, n_fsdp, piece, width)
    zq, zu = w_qkv.shape[1], w_up.shape[0]

    def first_items(ins, outs, z):
        x_ref, w_ref = ins
        rows_ref, whole_ref = outs

        def deal(g):
            return Deal(lambda to: x_ref.at[to * per + g], lambda s: rows_ref.at[g, s])

        def weight(j):
            size = zq // n_ctx
            columns = pl.ds(j * heads_width, heads_width)
            return Weight(
                lambda c: w_ref.at[j, pl.ds(pl.multiple_of(c * size, size), size)],
                lambda o, c: whole_ref.at[
                    pl.ds(pl.multiple_of(o * zq + c * size, size), size), columns
                ],
            )

        stay = [(x_ref.at[z * per + g], rows_ref.at[g, 0]) for g in range(per)]
        for j in range(3):
            own = whole_ref.at[
                pl.ds(pl.multiple_of(z * zq, zq), zq), pl.ds(j * heads_width, heads_width)
            ]
            stay.append((w_ref.at[j], own))
        items = [weight(j) for j in range(3)] + [deal(g) for g in range(per)]
        return items, stay

    x_all, qkv_x = move(
        first_items,
        [Weight] * 3 + [Deal] * per,
        (x_in, w_qkv),
        (rows_shape, (width + 3 * NR, 3 * heads_width)),
        n_fsdp,
        n_ctx,
        ((piece, width),) * per + (w_qkv.shape[1:],) * 3,
        0,
        foot=(b_qkv, lambda outs: outs[1].at[pl.ds(width, 3 * NR)]),
    )

    def second_items(ins, outs, z):
        kv_ref, cot_ref, wo_ref, wu_ref, wd_ref, ao_ref, bu_ref, ad_ref = ins
        slots, (rows_ref, out_ref, up_ref, down_ref) = outs[: n_ctx - 1], outs[n_ctx - 1 :]

        def ds(start, size):
            return pl.ds(pl.multiple_of(start, size), size)

        def deal(g):
            return Deal(lambda to: cot_ref.at[to * per + g], lambda s: rows_ref.at[g, s])

        zo = wo_ref.shape[1]
        so, su, sd = wo_ref.shape[0] // n_ctx, zu // n_ctx, wd_ref.shape[0] // n_ctx
        out_item = Weight(
            lambda c: wo_ref.at[ds(c * so, so)],
            lambda o, c: out_ref.at[ds(c * so, so), ds(o * zo, zo)],
        )

        def up_item(h):
            columns = pl.ds(h * (units // 2), units // 2)
            return Weight(
                lambda c: wu_ref.at[ds(c * su, su), columns],
                lambda o, c: up_ref.at[ds(o * zu + c * su, su), columns],
            )

        def down_item(h):
            half = sd // 2
            return Weight(
                lambda c: wd_ref.at[ds(c * sd + h * half, half)],
                lambda o, c: down_ref.at[ds(c * sd + h * half, half), ds(o * zo, zo)],
            )

        pair = Pair(lambda k: kv_ref if k == 0 else slots[k - 1])
        stay = [(cot_ref.at[z * per + g], rows_ref.at[g, 0]) for g in range(per)]
        stay += [
            (wo_ref, out_ref.at[:, ds(z * zo, zo)]),
            (wu_ref, up_ref.at[ds(z * zu, zu)]),
            (wd_ref, down_ref.at[:, ds(z * zo, zo)]),
            (ao_ref, out_ref.at[:, pl.ds(width, NR)]),
            (bu_ref, up_ref.at[pl.ds(width, NR)]),
            (ad_ref, down_ref.at[:, pl.ds(width, NR)]),
        ]
        items = [pair, out_item, up_item(0), up_item(1), down_item(0), down_item(1)]
        return items + [deal(g) for g in range(per)], stay

    a_in = a_qkv.transpose(1, 0, 2).reshape(width, 3 * NR)

    my_lengths = take(lengths, z * per, per)
    my_ids = take(adapter_ids, z * per, per)
    picked = (my_ids[:, None] == jnp.arange(NR)[None, :] // RANK).astype(F32)
    steps = lax.rem(z - jnp.arange(n_fsdp) + n_fsdp, n_fsdp)
    ctx_of = ct ^ jnp.array(offsets(n_ctx))
    key_pos = (
        (steps[None, :, None] * n_ctx + ctx_of[:, None, None]) * piece
        + jnp.arange(piece)[None, None, :]
    ).reshape(-1)
    bias_all = jnp.where(key_pos[None, :] < my_lengths[:, None], 0.0, -1e30).astype(F32)
    bias_all = jnp.broadcast_to(bias_all[:, :, None], bias_all.shape + (128,))

    pick_all = jnp.repeat(picked, loc, axis=0)
    x_flat = x_all.reshape(per * loc, width)
    adapt_all = (dot(x_flat, a_in) * jnp.concatenate([pick_all] * 3, axis=1)).astype(BF16)
    proj_all = mm(jnp.concatenate([x_flat, adapt_all], axis=1), qkv_x, False, as_low, 1024)
    kv_own = jnp.stack([proj_all[:, heads_width : 2 * heads_width], proj_all[:, 2 * heads_width :]])
    kv_own = kv_own.reshape(2, per, loc, heads_width)
    moved = move(
        second_items,
        [Pair] + [Weight] * 5 + [Deal] * per,
        (kv_own, cotangent, w_out, w_up, w_down, a_out, b_up, a_down),
        ((2, per, loc, heads_width),) * (n_ctx - 1)
        + (
            rows_shape,
            (heads_width, width + NR),
            (width + NR, units),
            (units, width + NR),
        ),
        n_fsdp,
        n_ctx,
        ((piece, width),) * per
        + (w_out.shape, w_up.shape, w_down.shape, a_out.shape, b_up.shape, a_down.shape),
        1,
    )
    kv_all = [kv_own] + list(moved[: n_ctx - 1])
    cot_all, out_x, up_x, down_x = moved[n_ctx - 1 :]
    cot_flat = cot_all.reshape(per * loc, width)

    groups = range(n_group)
    picks = [jnp.repeat(take(picked, g * g_per, g_per), loc, axis=0) for g in groups]
    biases = [bias_all[g * g_per : (g + 1) * g_per] for g in groups]
    part = [slice(g * g_rows, (g + 1) * g_rows) for g in groups]
    seq = [slice(n * loc, (n + 1) * loc) for n in range(g_per)]
    x_rows = [x_flat[part[g]] for g in groups]
    query = [proj_all[part[g], :heads_width].reshape(g_per, loc, heads_width) for g in groups]

    attended = [attend(query[g], kv_all, biases[g], g * g_per) for g in groups]
    ctx_rows = [attended[g][0].reshape(g_rows, heads_width) for g in groups]
    summed = [both(mm(ctx_rows[g], out_x, False, as_low, 768)) for g in groups]
    adapt_out, hat1, rstd1, hidden, hidden_low, adapt_up, gelu_out, slope = ([] for _ in range(8))
    for g in groups:
        adapt_out.append((summed[g][:, width:] * picks[g]).astype(BF16))
        y1 = x_rows[g].astype(F32) + summed[g][:, :width] + dot(adapt_out[g], b_out)
        parts = norm_parts(y1)
        hat1.append(parts[0])
        rstd1.append(parts[1])
        hidden.append(parts[0] * ln_gain[0] + ln_bias[0])
        hidden_low.append(hidden[g].astype(BF16))
        adapt_up.append((dot(hidden_low[g], a_up) * picks[g]).astype(BF16))
        wide = jnp.concatenate([hidden_low[g], adapt_up[g]], axis=1)
        pair = mm(wide, up_x, False, gelu_both, 1024, 2)
        gelu_out.append(pair[0])
        slope.append(pair[1])
    summed = [both(mm(gelu_out[g], down_x, False, as_low, 768)) for g in groups]
    adapt_down, acts, dy2, d_down, dadapt_down, d_pre = ([] for _ in range(6))
    for g in groups:
        adapt_down.append((summed[g][:, width:] * picks[g]).astype(BF16))
        hat2, rstd2 = norm_parts(hidden[g] + summed[g][:, :width] + dot(adapt_down[g], b_down))
        acts.append(undeal((hat2 * ln_gain[1] + ln_bias[1]).astype(BF16), g))
        dy2.append(norm_back(hat2, rstd2, cot_flat[part[g]].astype(F32) * ln_gain[1]))
        d_down.append(dy2[g].astype(BF16))
        dadapt_down.append((dot_nt(d_down[g], b_down) * picks[g]).astype(BF16))
        wide = jnp.concatenate([d_down[g], dadapt_down[g]], axis=1)
        d_pre.append(mm(wide, down_x, True, times, 1024, 1, slope[g]))
    summed = [both(mm(d_pre[g], up_x, True, as_low, 768)) for g in groups]
    dadapt_up, dy1, d_attn, dadapt_out, backs = ([] for _ in range(5))
    for g in groups:
        dadapt_up.append((summed[g][:, width:] * picks[g]).astype(BF16))
        dh1 = dy2[g] + summed[g][:, :width] + dot_nt(dadapt_up[g], a_up)
        dy1.append(norm_back(hat1[g], rstd1[g], dh1 * ln_gain[0]))
        d_attn.append(dy1[g].astype(BF16))
        dadapt_out.append((dot_nt(d_attn[g], b_out) * picks[g]).astype(BF16))
        wide = jnp.concatenate([d_attn[g], dadapt_out[g]], axis=1)
        d_context = mm(wide, out_x, True, as_low, 512).reshape(g_per, loc, heads_width)
        backs.append(
            attend_back(query[g], kv_all, biases[g], d_context, attended[g][1], g * g_per)
        )

    def gathered(parts):
        mine = jnp.concatenate(parts, axis=1)
        blocks = [
            lax.dynamic_index_in_dim(mine, ct ^ offset, 0, False) for offset in offsets(n_ctx)
        ]
        own = fold(blocks, "ctx")
        got = jnp.stack([own] + [shift(own, "fsdp", step) for step in range(1, n_fsdp)])
        return spread([got], "ctx")

    early_in = []
    for g in groups:
        pairs = (
            (adapt_down[g], d_down[g]),
            (dadapt_down[g], gelu_out[g]),
            (adapt_up[g], d_pre[g]),
            (dadapt_up[g], hidden_low[g]),
            (adapt_out[g], d_attn[g]),
            (dadapt_out[g], ctx_rows[g]),
        )
        early_in.append(pairs)
    early_in = after(early_in, backs[-1][0])
    early = gathered(
        [compact([(c[r], v[r]) for c, v in early_in[g]], n_ctx) for g in groups for r in seq]
    )

    d_proj, ins, late = [], [], []
    summed = []
    for g in groups:
        d_pair = fold(backs[g][1], "ctx").reshape(2, g_rows, heads_width)
        d_query = backs[g][0].reshape(g_rows, heads_width)
        d_proj.append(jnp.concatenate([d_query, d_pair[0], d_pair[1]], axis=1))
        summed.append(both(mm(d_proj[g], qkv_x, True, as_low, 640)))
    for g in groups:
        pick3 = jnp.concatenate([picks[g]] * 3, axis=1)
        dadapt_in = (summed[g][:, width:] * pick3).astype(BF16)
        d_x = (dy1[g] + summed[g][:, :width] + dot_nt(dadapt_in, a_in)).astype(BF16)
        ins.append(undeal(d_x, g))
        adapt_in = adapt_all[part[g]]
        for r in seq:
            pairs = []
            for j in range(3):
                codes = slice(j * NR, (j + 1) * NR)
                columns = slice(j * heads_width, (j + 1) * heads_width)
                pairs.append((adapt_in[r, codes], d_proj[g][r, columns]))
            for j in range(3):
                pairs.append((dadapt_in[r, j * NR : (j + 1) * NR], x_rows[g][r]))
            late.append(compact(pairs, n_ctx))
    late = gathered(late)

    def assemble(parts):
        full = jnp.zeros((seqs, piece, width), BF16)
        for group, blocks in enumerate(parts):
            for step, block in enumerate(blocks):
                owner = lax.rem(z + step, n_fsdp)
                full = put(full, block, owner * per + group * g_per, 0, 0)
        return full

    codes = (adapter_ids[:, None] * RANK + jnp.arange(RANK)[None, :]).reshape(-1)
    chosen = (codes[:, None] == jnp.arange(NR)[None, :]).astype(BF16)
    early, acts = after((early, acts), summed[-1])
    e = combine(
        early,
        chosen,
        [(NR, width), (units, NR), (NR, units), (width, NR), (NR, width), (heads_width, NR)],
    )
    l = combine(late, chosen, [(3, NR, heads_width), (3, width, NR)])
    return assemble(acts), assemble(ins), l[1], l[0], e[5], e[4], e[3], e[2], e[1], e[0]


def solution(mesh):
    rows = P(None, ("fsdp", "ctx"), None)
    return jax.shard_map(
        local,
        mesh=mesh,
        in_specs=(
            rows,
            rows,
            P(),
            P(),
            P(None, "fsdp", "tp"),
            P("tp", "fsdp"),
            P("fsdp", "tp"),
            P("tp", "fsdp"),
            P(),
            P(),
            P(),
            P(None, None, "tp"),
            P("tp", None),
            P(),
            P(),
            P(None, "tp"),
            P("tp", None),
            P(),
        ),
        out_specs=(
            rows,
            rows,
            P(),
            P(None, None, "tp"),
            P("tp", None),
            P(),
            P(),
            P(None, "tp"),
            P("tp", None),
            P(),
        ),
        check_vma=False,
    )
```

```python
import math

import jax
import jax.numpy as jnp
from jax import lax
from jax.experimental import pallas as pl
from jax.experimental.pallas import tpu as pltpu
from jax.sharding import PartitionSpec as P

HEAD_DIM = 128
RANK = 16
ADAPTERS = 8
NR = RANK * ADAPTERS
NORM_EPS = 1e-06
GELU_COEF = 0.7978845608028654
SCALE = 1.0 / math.sqrt(HEAD_DIM)
GROUPS = 2
F32 = jnp.float32
BF16 = jnp.bfloat16


def dot(left, right):
    return jnp.dot(left, right, preferred_element_type=F32)


def dot_nt(left, right):
    return lax.dot_general(left, right, (((1,), (1,)), ((), ())), preferred_element_type=F32)


def dot_tn(left, right):
    return lax.dot_general(left, right, (((0,), (0,)), ((), ())), preferred_element_type=F32)


def shift(block, axis, step):
    n = lax.axis_size(axis)
    return lax.ppermute(block, axis, [(i, (i + step) % n) for i in range(n)])


def swap(block, axis, mask):
    n = lax.axis_size(axis)
    return lax.ppermute(block, axis, [(i, i ^ mask) for i in range(n)])


def masks_of(n):
    out = []
    while n > 1:
        n //= 2
        out.append(n)
    return out


def spread(pieces, axis):
    for mask in masks_of(lax.axis_size(axis)):
        pieces = pieces + [swap(piece, axis, mask) for piece in pieces]
    return pieces


def offsets(n):
    out = [0]
    for mask in masks_of(n):
        out = out + [o ^ mask for o in out]
    return out


def fold(pieces, axis):
    for mask in reversed(masks_of(lax.axis_size(axis))):
        half = len(pieces) // 2
        got = [swap(piece, axis, mask) for piece in pieces[half:]]
        pieces = [
            (mine.astype(F32) + other.astype(F32)).astype(BF16)
            for mine, other in zip(pieces[:half], got)
        ]
    return pieces[0]


def both_in_turn(parts):
    lows, got = list(parts), None
    for mask in masks_of(lax.axis_size("tp")):
        got = [swap(low, "tp", mask) for low in lows]
        for g in range(len(lows) - 1):
            got[g] = after(got[g], *lows[g + 1 :])
        totals = [low.astype(F32) + other.astype(F32) for low, other in zip(lows, got)]
        lows = [total.astype(BF16) for total in totals]
    return totals


def attend_head(query, keys, values, biases):
    scores = [dot_nt(k, query) * SCALE + bias for k, bias in zip(keys, biases)]
    top = scores[0].max(axis=0, keepdims=True)
    for s in scores[1:]:
        top = jnp.maximum(top, s.max(axis=0, keepdims=True))
    total = jnp.zeros_like(top)
    mixed = None
    for s, v in zip(scores, values):
        probs = jnp.exp(s - top)
        total = total + probs.sum(axis=0, keepdims=True)
        term = dot_tn(v, probs.astype(BF16))
        mixed = term if mixed is None else mixed + term
    return (mixed / total).T.astype(BF16), top + jnp.log(total)


def attend_back_head(query, grad, log_total, keys, values, biases):
    probs, dprobs, dvalues = [], [], []
    delta = jnp.zeros_like(log_total)
    for k, v, bias in zip(keys, values, biases):
        p = jnp.exp(dot_nt(k, query) * SCALE + bias - log_total)
        dp = dot_nt(v, grad)
        dvalues.append(dot(p.astype(BF16), grad).astype(BF16))
        delta = delta + (p * dp).sum(axis=0, keepdims=True)
        probs.append(p)
        dprobs.append(dp)
    dquery, dkeys = None, []
    for k, p, dp in zip(keys, probs, dprobs):
        ds = (p * (dp - delta)).astype(BF16)
        dkeys.append((dot(ds, query) * SCALE).astype(BF16))
        term = dot_tn(k, ds)
        dquery = term if dquery is None else dquery + term
    return (dquery * SCALE).T.astype(BF16), dkeys, dvalues


def ds(start, size):
    return pl.ds(pl.multiple_of(start, size), size)


def flip(ct, offset):
    mask = 1
    while mask <= offset:
        if offset & mask:
            ct = ct + mask - 2 * mask * lax.rem(ct // mask, 2)
        mask *= 2
    return ct


class Weight:
    def __init__(self, shard_at, whole_at):
        self.shard_at, self.whole_at = shard_at, whole_at


class Deal:
    def __init__(self, source_at, rows_at):
        self.source_at, self.rows_at = source_at, rows_at


class Pair:
    def __init__(self, slot_at):
        self.slot_at = slot_at


class Mover:
    def __init__(self, n_fsdp, n_ctx, send, recv):
        self.n_fsdp, self.n_ctx = n_fsdp, n_ctx
        self.z, self.ct = lax.axis_index("fsdp"), lax.axis_index("ctx")
        self.send, self.recv = send, recv
        self.used = 0
        self.open = []
        self.masks = masks_of(n_ctx)
        self.offsets = offsets(n_ctx)
        self.came, self.waiting = {}, {}

    def greet(self, tp=False):
        barrier = pltpu.get_barrier_semaphore()
        others = [{"fsdp": lax.rem(self.z + s, self.n_fsdp)} for s in range(1, self.n_fsdp)]
        others += [{"ctx": flip(self.ct, mask)} for mask in self.masks]
        if tp:
            others.append({"tp": 1 - lax.axis_index("tp")})
        for other in others:
            pl.semaphore_signal(
                barrier, inc=1, device_id=other, device_id_type=pl.DeviceIdType.MESH
            )
        pl.semaphore_wait(barrier, len(others))

    def copy(self, source, target, device, at=None):
        if at is None:
            at = self.used
            self.used += 1
        return pltpu.make_async_remote_copy(
            src_ref=source,
            dst_ref=target,
            send_sem=self.send.at[at],
            recv_sem=self.recv.at[at],
            device_id=device,
            device_id_type=pl.DeviceIdType.MESH,
        )

    def go(self, source, target, device):
        copy = self.copy(source, target, device)
        copy.start()
        self.open.append((None, copy))
        return copy

    def along(self, item, owner, right, ok, source, slot):
        target = item.whole_at(owner, self.ct)
        device = {"fsdp": lax.rem(self.z + (1 if right else self.n_fsdp - 1), self.n_fsdp)}
        copy = self.copy(source, target, device, self.came[item] + slot - 1)
        pl.when(ok)(copy.start)
        self.open.append((ok, copy))

    def begin(self, item):
        if isinstance(item, Pair):
            self.waiting[item] = [[] for _ in self.masks]
            self.cast(item, item.slot_at, lambda k, level: item.slot_at(k + 2**level), 0, 0)
            return
        if isinstance(item, Weight):
            self.came[item] = self.used
            self.used += self.n_fsdp - 1
            source = item.shard_at(self.ct)
            self.along(item, self.z, True, self.z < self.n_fsdp - 1, source, 1)
            self.along(item, self.z, False, self.z > 0, source, self.n_fsdp - 1)
            return
        self.came[item] = [
            self.go(
                item.source_at(lax.rem(self.z + s, self.n_fsdp)),
                item.rows_at(s),
                {"fsdp": lax.rem(self.z + s, self.n_fsdp)},
            )
            for s in range(1, self.n_fsdp)
        ]

    def cast(self, item, source_at, target_at, k, first):
        for level in range(first, len(self.masks)):
            device = {"ctx": flip(self.ct, self.masks[level])}
            copy = self.go(source_at(k), target_at(k, level), device)
            self.waiting[item][level].append((copy, k + 2**level, source_at, target_at))

    def relay(self, item):
        if isinstance(item, Pair):
            return
        if isinstance(item, Deal):
            for copy in self.came[item]:
                copy.wait_recv()
            return
        self.waiting[item] = [[] for _ in self.masks]
        n = self.n_fsdp
        for i in range(n - 1):
            s = i // 2 + 1 if i % 2 == 0 else n - 1 - i // 2
            owner = lax.rem(self.z - s + n, n)
            here = item.whole_at(owner, self.ct)
            self.copy(here, here, {"fsdp": owner}, self.came[item] + s - 1).wait_recv()
            if s < n - 1:
                ok = (self.z >= s) & (self.z < n - 1)
                self.along(item, owner, True, ok, here, s + 1)
            if s > 1:
                ok = (self.z < s) & (self.z > 0)
                self.along(item, owner, False, ok, here, s - 1)

            def at(k, owner=owner):
                return item.whole_at(owner, flip(self.ct, self.offsets[k]))

            self.cast(item, at, lambda k, level, at=at: at(k), 0, 0)

    def finish(self, item, level):
        if isinstance(item, Deal):
            return
        for copy, k, source_at, target_at in self.waiting[item][level]:
            copy.wait_recv()
            self.cast(item, source_at, target_at, k, level + 1)

    def close(self):
        for ok, copy in self.open:
            if ok is None:
                copy.wait_send()
            else:
                pl.when(ok)(copy.wait_send)


def copies_of(items, n_fsdp, n_ctx):
    total = 0
    for item in items:
        total += {Weight: (n_fsdp - 1) * n_ctx, Deal: n_fsdp - 1, Pair: n_ctx - 1}[item]
    return total


def keep(stay, room, sems):
    out = []
    for k, (source, target) in enumerate(stay):
        first = pltpu.make_async_copy(source, room[k], sems.at[2 * k])
        first.start()
        out.append((first, pltpu.make_async_copy(room[k], target, sems.at[2 * k + 1])))
    return out


def move(make, kinds, inputs, outputs, n_fsdp, n_ctx, local_shapes, ident, ahead=2, foot=None):
    n_in = len(inputs)
    n_copy = copies_of(kinds, n_fsdp, n_ctx)

    def kernel(*refs):
        ins, outs = refs[:n_in], refs[n_in : n_in + len(outputs)]
        send, recv, here = refs[n_in + len(outputs) : n_in + len(outputs) + 3]
        room = refs[n_in + len(outputs) + 3 :]
        if foot is not None:
            blocks_ref, ins = ins[-1], ins[:-1]
            strip = room[-1]
        mover = Mover(n_fsdp, n_ctx, send, recv)
        items, stay = make(ins, outs, mover.z)
        mover.greet()
        for item in items[:ahead]:
            mover.begin(item)
        kept = keep(stay, room, here)
        levels = len(mover.masks)
        for i in range(len(items) + levels):
            if i < len(items):
                mover.relay(items[i])
                if i + ahead < len(items):
                    mover.begin(items[i + ahead])
            if i == 0 and foot is not None:
                strip[...] = jnp.zeros_like(strip)
                high, wide = blocks_ref.shape[1:]
                for j in range(blocks_ref.shape[0]):
                    strip[j * high : (j + 1) * high, j * wide : (j + 1) * wide] = blocks_ref[j]
                set_foot = pltpu.make_async_copy(strip, foot[1](outs), here.at[2 * len(local_shapes)])
                set_foot.start()
                kept.append((None, set_foot))
            if i == 0:
                for first, second in kept:
                    if first is not None:
                        first.wait()
                        second.start()
            for level in range(levels):
                if 0 <= i - 1 - level < len(items):
                    mover.finish(items[i - 1 - level], level)
        for _, second in kept:
            second.wait()
        mover.close()

    spaces = [pl.BlockSpec(memory_space=pl.ANY)] * n_in
    room_shapes = list(local_shapes)
    if foot is not None:
        blocks = foot[0]
        inputs = inputs + (blocks,)
        n_in += 1
        spaces.append(pl.BlockSpec(memory_space=pltpu.VMEM))
        room_shapes.append((blocks.shape[0] * blocks.shape[1], blocks.shape[0] * blocks.shape[2]))
    return pl.pallas_call(
        kernel,
        in_specs=spaces,
        out_specs=[pl.BlockSpec(memory_space=pl.ANY)] * len(outputs),
        out_shape=[jax.ShapeDtypeStruct(shape, BF16) for shape in outputs],
        scratch_shapes=[
            pltpu.SemaphoreType.DMA((n_copy,)),
            pltpu.SemaphoreType.DMA((n_copy,)),
            pltpu.SemaphoreType.DMA((2 * len(local_shapes) + 1,)),
        ]
        + [pltpu.VMEM(shape, BF16) for shape in room_shapes],
        compiler_params=pltpu.CompilerParams(
            collective_id=ident, has_side_effects=True, vmem_limit_bytes=32 << 20
        ),
    )(*inputs)


def forward_and_gather(query, kv_own, bias, shards, maps, n_fsdp, n_ctx):
    per, loc, width_here = query.shape
    cot, w_out, w_up, w_down = shards
    piece, width = cot.shape[1:]
    heads, units = width_here // HEAD_DIM, w_up.shape[1]
    zu, zo = w_up.shape[0], w_out.shape[1]
    so, su, sd = w_out.shape[0] // n_ctx, zu // n_ctx, w_down.shape[0] // n_ctx
    wide = width + NR
    stay_shapes = [(piece, width)] * per + [x.shape for x in (w_out, w_up, w_down) + maps]
    n_stay = len(stay_shapes)
    halves = 2
    n_copy = (n_fsdp - 1) * n_ctx * (1 + 2 * halves) + per * (n_fsdp - 1 + n_ctx - 1 + 1)

    def kernel(*refs):
        q_ref, bias_ref, kv_ref, cot_ref, wo_ref, wu_ref, wd_ref, ao_ref, bu_ref, ad_ref = refs[:10]
        slots = refs[10 : 9 + n_ctx]
        rows_ref, out_ref, up_ref, down_ref, ctx_ref, log_ref, part_ref, other_ref = refs[
            9 + n_ctx : 17 + n_ctx
        ]
        send, recv, here, load, kv_room, out_room = refs[17 + n_ctx : 23 + n_ctx]
        room = refs[23 + n_ctx :]
        mover = Mover(n_fsdp, n_ctx, send, recv)
        z = mover.z

        def deal(g):
            return Deal(lambda to: cot_ref.at[to * per + g], lambda s: rows_ref.at[g, s])

        def pair(g):
            return Pair(lambda k: kv_ref.at[:, g] if k == 0 else slots[k - 1].at[:, g])

        out_item = Weight(
            lambda c: wo_ref.at[ds(c * so, so)],
            lambda o, c: out_ref.at[ds(c * so, so), ds(o * zo, zo)],
        )

        def up_item(h):
            columns = pl.ds(h * (units // halves), units // halves)
            return Weight(
                lambda c: wu_ref.at[ds(c * su, su), columns],
                lambda o, c: up_ref.at[ds(o * zu + c * su, su), columns],
            )

        def down_item(h):
            size = sd // halves
            return Weight(
                lambda c: wd_ref.at[ds(c * sd + h * size, size)],
                lambda o, c: down_ref.at[ds(c * sd + h * size, size), ds(o * zo, zo)],
            )

        pairs = [pair(g) for g in range(per)]
        items = [out_item] + [up_item(h) for h in range(halves)]
        items += [down_item(h) for h in range(halves)] + [deal(g) for g in range(per)]
        stay = [(cot_ref.at[z * per + g], rows_ref.at[g, 0]) for g in range(per)]
        stay += [
            (wo_ref, out_ref.at[:, ds(z * zo, zo)]),
            (wu_ref, up_ref.at[ds(z * zu, zu)]),
            (wd_ref, down_ref.at[:, ds(z * zo, zo)]),
            (ao_ref, out_ref.at[:, pl.ds(width, NR)]),
            (bu_ref, up_ref.at[pl.ds(width, NR)]),
            (ad_ref, down_ref.at[:, pl.ds(width, NR)]),
        ]

        def attend(g):
            for level in range(len(mover.masks)):
                mover.finish(pairs[g], level)
            loads = []
            for k in range(n_ctx):
                copy = pltpu.make_async_copy(pairs[g].slot_at(k), kv_room.at[k], load.at[k])
                copy.start()
                loads.append(copy)
            for copy in loads:
                copy.wait()

            def one(h, carry):
                at = ds(h * HEAD_DIM, HEAD_DIM)
                biases = []
                for k in range(n_ctx):
                    block = bias_ref[g, k * loc : (k + 1) * loc, :]
                    biases.append(jnp.concatenate([block] * (loc // 128), axis=1))
                context, log = attend_head(
                    q_ref[g, :, at],
                    [kv_room[k, 0, :, at] for k in range(n_ctx)],
                    [kv_room[k, 1, :, at] for k in range(n_ctx)],
                    biases,
                )
                ctx_ref[g, :, at] = context
                log_ref[g, h] = log
                return carry

            lax.fori_loop(0, heads, one, 0)

        def project():
            copy = pltpu.make_async_copy(out_ref, out_room, load.at[n_ctx])
            copy.start()
            copy.wait()
            for g in range(per):
                for start in range(0, wide, 1024):
                    at = slice(start, min(start + 1024, wide))
                    part_ref[g, :, at] = dot(ctx_ref[g], out_room[:, at]).astype(BF16)
                swapped.append(
                    mover.go(
                        part_ref.at[g], other_ref.at[g], {"tp": 1 - lax.axis_index("tp")}
                    )
                )

        swapped = []
        tasks = {i: (lambda g=i: attend(g)) for i in range(per)}
        tasks[per] = project
        mover.greet(tp=True)
        for item in pairs + items[:2]:
            mover.begin(item)
        kept = keep(stay, room, here)
        levels = len(mover.masks)
        for i in range(len(items) + levels):
            if i < len(items):
                mover.relay(items[i])
                if i + 2 < len(items):
                    mover.begin(items[i + 2])
            if i == 0:
                for first, second in kept:
                    first.wait()
                    second.start()
            for level in range(levels):
                if 0 <= i - 1 - level < len(items):
                    mover.finish(items[i - 1 - level], level)
            if i == per:
                for _, second in kept:
                    second.wait()
            if i in tasks:
                tasks[i]()
        for copy in swapped:
            copy.wait_recv()
        mover.close()

    row = (per, loc, width_here)
    vmem, anywhere = pl.BlockSpec(memory_space=pltpu.VMEM), pl.BlockSpec(memory_space=pl.ANY)
    outputs = [(kv_own.shape, BF16, anywhere)] * (n_ctx - 1) + [
        ((per, n_fsdp, piece, width), BF16, anywhere),
        ((width_here, wide), BF16, anywhere),
        ((wide, units), BF16, anywhere),
        ((units, wide), BF16, anywhere),
        (row, BF16, vmem),
        ((per, heads, 1, loc), F32, vmem),
        ((per, loc, wide), BF16, vmem),
        ((per, loc, wide), BF16, anywhere),
    ]
    return pl.pallas_call(
        kernel,
        in_specs=[vmem, vmem] + [anywhere] * 8,
        out_specs=[space for _, _, space in outputs],
        out_shape=[jax.ShapeDtypeStruct(shape, dtype) for shape, dtype, _ in outputs],
        scratch_shapes=[
            pltpu.SemaphoreType.DMA((n_copy,)),
            pltpu.SemaphoreType.DMA((n_copy,)),
            pltpu.SemaphoreType.DMA((2 * n_stay,)),
            pltpu.SemaphoreType.DMA((n_ctx + 1,)),
            pltpu.VMEM((n_ctx, 2, loc, width_here), BF16),
            pltpu.VMEM((width_here, wide), BF16),
        ]
        + [pltpu.VMEM(shape, BF16) for shape in stay_shapes],
        compiler_params=pltpu.CompilerParams(
            collective_id=1, has_side_effects=True, vmem_limit_bytes=50 << 20
        ),
    )(query, bias, kv_own, cot, w_out, w_up, w_down, *maps)


def attend_back(query, kv_own, slots, bias, grad, log_total, acts, n_fsdp, n_ctx):
    per, loc, width_here = query.shape
    piece, width = acts.shape[2:]
    heads = width_here // HEAD_DIM
    cuts = 2
    high = heads // cuts
    columns = high * HEAD_DIM
    masks = masks_of(n_ctx)
    units = [(g, c) for g in range(per) for c in range(cuts)]
    n_copy = per * (n_fsdp - 1) + len(units) * (n_ctx - 1)

    def kernel(*refs):
        q_ref, bias_ref, g_ref, log_ref, acts_ref, kv_ref = refs[:6]
        slot_refs = refs[6 : 5 + n_ctx]
        dq_ref, dkv_ref, out_ref = refs[5 + n_ctx : 8 + n_ctx]
        send, recv, load, kv_room, own, came, act_room = refs[8 + n_ctx :]
        mover = Mover(n_fsdp, n_ctx, send, recv)
        z, ct = mover.z, mover.ct
        loads = []
        for g in range(per):
            loads.append([])
            for k in range(n_ctx):
                source = kv_ref if k == 0 else slot_refs[k - 1]
                copy = pltpu.make_async_copy(
                    source.at[:, g], kv_room.at[g, k], load.at[g * n_ctx + k]
                )
                copy.start()
                loads[g].append(copy)
        kept = []
        for g in range(per):
            at = per * n_ctx + 2 * g
            first = pltpu.make_async_copy(acts_ref.at[g, 0], act_room.at[g], load.at[at])
            first.start()
            second = pltpu.make_async_copy(
                act_room.at[g], out_ref.at[z * per + g], load.at[at + 1]
            )
            kept.append((first, second))
        mover.greet()
        dealt = []
        for g in range(per):
            for s in range(1, n_fsdp):
                to = lax.rem(z - s + n_fsdp, n_fsdp)
                dealt.append(
                    mover.go(acts_ref.at[g, s], out_ref.at[z * per + g], {"fsdp": to})
                )
        flying = {}

        def compute(u):
            g, c = units[u]
            if c == 0:
                for copy in loads[g]:
                    copy.wait()

            def one(h, carry):
                at = ds(c * columns + h * HEAD_DIM, HEAD_DIM)
                to = ds(h * HEAD_DIM, HEAD_DIM)
                biases = []
                for k in range(n_ctx):
                    block = bias_ref[g, k * loc : (k + 1) * loc, :]
                    biases.append(jnp.concatenate([block] * (loc // 128), axis=1))
                dquery, dkeys, dvalues = attend_back_head(
                    q_ref[g, :, at],
                    g_ref[g, :, at],
                    log_ref[g, c * high + h],
                    [kv_room[g, k, 0, :, at] for k in range(n_ctx)],
                    [kv_room[g, k, 1, :, at] for k in range(n_ctx)],
                    biases,
                )
                dq_ref[g, :, at] = dquery
                for k in range(n_ctx):
                    own[u, k, 0, :, to] = dkeys[k]
                    own[u, k, 1, :, to] = dvalues[k]
                return carry

            lax.fori_loop(0, high, one, 0)

        def hand(u, level):
            half = 2**level
            device = {"ctx": flip(ct, masks[level])}
            flying[u, level] = [
                mover.go(own.at[u, half + i], came.at[u, half - 1 + i], device) for i in range(half)
            ]

        def take_in(u, level):
            half = 2**level
            for i, copy in enumerate(flying[u, level]):
                copy.wait_recv()
                for j in range(2):
                    total = own[u, i, j].astype(F32) + came[u, half - 1 + i, j].astype(F32)
                    if level:
                        own[u, i, j] = total.astype(BF16)
                    else:
                        g, c = units[u]
                        dkv_ref[j, g, :, c * columns : (c + 1) * columns] = total.astype(BF16)

        last = len(masks) - 1
        for t in range(len(units) + last + 1):
            if t < len(units):
                compute(t)
                hand(t, last)
            if t == 0:
                for first, second in kept:
                    first.wait()
                    second.start()
            for k in range(last + 1):
                u, level = t - 1 - k, last - k
                if 0 <= u < len(units):
                    take_in(u, level)
                    if level:
                        hand(u, level - 1)
        for _, second in kept:
            second.wait()
        for copy in dealt:
            copy.wait_recv()
        mover.close()

    vmem, anywhere = pl.BlockSpec(memory_space=pltpu.VMEM), pl.BlockSpec(memory_space=pl.ANY)
    return pl.pallas_call(
        kernel,
        in_specs=[vmem] * 4 + [anywhere] * (1 + n_ctx),
        out_specs=[vmem, vmem, anywhere],
        out_shape=[
            jax.ShapeDtypeStruct(query.shape, BF16),
            jax.ShapeDtypeStruct(kv_own.shape, BF16),
            jax.ShapeDtypeStruct((per * n_fsdp, piece, width), BF16),
        ],
        scratch_shapes=[
            pltpu.SemaphoreType.DMA((n_copy,)),
            pltpu.SemaphoreType.DMA((n_copy,)),
            pltpu.SemaphoreType.DMA((per * (n_ctx + 2),)),
            pltpu.VMEM((per, n_ctx, 2, loc, width_here), BF16),
            pltpu.VMEM((len(units), n_ctx, 2, loc, columns), BF16),
            pltpu.VMEM((len(units), n_ctx - 1, 2, loc, columns), BF16),
            pltpu.VMEM((per, piece, width), BF16),
        ],
        compiler_params=pltpu.CompilerParams(
            collective_id=2, has_side_effects=True, vmem_limit_bytes=56 << 20
        ),
    )(query, bias, grad, log_total, acts, kv_own, *slots)


def norm_parts(values):
    center = values - jnp.mean(values, axis=-1, keepdims=True)
    rstd = lax.rsqrt(jnp.mean(center * center, axis=-1, keepdims=True) + NORM_EPS)
    return center * rstd, rstd


def norm_back(hat, rstd, dhat):
    first = jnp.mean(dhat, axis=-1, keepdims=True)
    second = jnp.mean(dhat * hat, axis=-1, keepdims=True)
    return rstd * (dhat - first - hat * second)


def mm(left, right, nt, finish, tile, n_out=1, beside=None):
    rows, depth = left.shape
    columns = right.shape[0] if nt else right.shape[1]
    extra = [] if beside is None else [beside]
    sub = 128 if nt else tile

    def kernel(left_ref, right_ref, *refs):
        n_extra = len(extra)
        outs = refs[n_extra : n_extra + n_out]
        if nt:
            turned = refs[-1]

            @pl.when(pl.program_id(0) == 0)
            def _():
                turned[...] = left_ref[...].T

        for k in range(tile // sub):
            at = slice(k * sub, (k + 1) * sub)
            if nt:
                block = dot(right_ref[at, :], turned[...]).T
            else:
                block = dot(left_ref[...], right_ref[:, at])
            values = finish(block, *[ref[:, at] for ref in refs[:n_extra]])
            for ref, value in zip(outs, values):
                ref[:, at] = value

    part = pl.BlockSpec((rows, tile), lambda j: (0, j))
    out = pl.pallas_call(
        kernel,
        grid=(pl.cdiv(columns, tile),),
        in_specs=[
            pl.BlockSpec((rows, depth), lambda j: (0, 0)),
            pl.BlockSpec((tile, depth), lambda j: (j, 0))
            if nt
            else pl.BlockSpec((depth, tile), lambda j: (0, j)),
        ]
        + [part] * len(extra),
        out_specs=[part] * n_out,
        out_shape=[jax.ShapeDtypeStruct((rows, columns), BF16)] * n_out,
        scratch_shapes=[pltpu.VMEM((depth, rows), BF16)] if nt else [],
        compiler_params=pltpu.CompilerParams(vmem_limit_bytes=48 << 20),
        cost_estimate=pl.CostEstimate(
            flops=2 * rows * depth * columns,
            bytes_accessed=2 * (rows * depth + 2 * depth * columns + rows * columns * n_out),
            transcendentals=0,
        ),
    )(left, right, *extra)
    return out[0] if n_out == 1 else out


def compact(pairs, n_part):
    rows = pairs[0][0].shape[0]
    sizes = [values.shape[1] // n_part for _, values in pairs]
    total = sum(sizes)

    def kernel(*refs):
        out_ref = refs[-1]
        column = lax.broadcasted_iota(jnp.int32, (NR, RANK), 0)
        rank = lax.broadcasted_iota(jnp.int32, (NR, RANK), 1)
        used = jnp.where(lax.rem(column, RANK) == rank, 1.0, 0.0).astype(BF16)
        start = 0
        for i, size in enumerate(sizes):
            codes = dot(refs[2 * i][...], used).astype(BF16)
            block = dot_tn(codes, refs[2 * i + 1][...]).astype(BF16)
            for part in range(n_part):
                out_ref[part, :, start : start + size] = block[:, part * size : (part + 1) * size]
            start += size

    flat = [array for pair in pairs for array in pair]
    return pl.pallas_call(
        kernel,
        in_specs=[pl.BlockSpec(memory_space=pltpu.VMEM)] * len(flat),
        out_specs=pl.BlockSpec(memory_space=pltpu.VMEM),
        out_shape=jax.ShapeDtypeStruct((n_part, RANK, total), BF16),
        compiler_params=pltpu.CompilerParams(vmem_limit_bytes=40 << 20),
        cost_estimate=pl.CostEstimate(
            flops=2 * rows * RANK * total * n_part * 8,
            bytes_accessed=2 * rows * total * n_part,
            transcendentals=0,
        ),
    )(*flat)


def combine(pieces, chosen, shapes):
    n_part = len(pieces)
    n_fsdp, rows, columns = pieces[0].shape
    flat = []
    for i, shape in enumerate(shapes):
        for lead in range(shape[0] if len(shape) == 3 else 1):
            flat.append((i, lead if len(shape) == 3 else None, shape[-2:]))

    def kernel(chosen_ref, *refs):
        piece_refs, outs = refs[:n_part], refs[n_part:]
        z, ct = lax.axis_index("fsdp"), lax.axis_index("ctx")
        for k, offset in enumerate(offsets(n_part)):
            part = flip(ct, offset)
            ordered = jnp.concatenate(
                [piece_refs[k][lax.rem(z - a + n_fsdp, n_fsdp)] for a in range(n_fsdp)], axis=0
            )
            start = 0
            for i, lead, (high, wide) in flat:
                out_ref = outs[i] if lead is None else outs[i].at[lead]
                tall = wide == NR and high != NR
                size = (high if tall else wide) // n_part
                block = ordered[:, start : start + size]
                at = pl.ds(pl.multiple_of(part * size, size), size)
                if tall:
                    out_ref[at, :] = dot_tn(block, chosen_ref[...])
                else:
                    out_ref[:, at] = dot_tn(chosen_ref[...], block)
                start += size

    return pl.pallas_call(
        kernel,
        in_specs=[pl.BlockSpec(memory_space=pltpu.VMEM)] * (1 + n_part),
        out_specs=[pl.BlockSpec(memory_space=pltpu.VMEM)] * len(shapes),
        out_shape=[jax.ShapeDtypeStruct(shape, F32) for shape in shapes],
        compiler_params=pltpu.CompilerParams(vmem_limit_bytes=48 << 20),
        cost_estimate=pl.CostEstimate(
            flops=2 * NR * n_fsdp * rows * columns * n_part,
            bytes_accessed=2 * n_fsdp * rows * columns * n_part + 4 * NR * columns * n_part,
            transcendentals=0,
        ),
    )(chosen, *pieces)


def as_low(block):
    return (block.astype(BF16),)


def times(block, factor):
    return ((block * factor.astype(F32)).astype(BF16),)


def after(value, *first):
    return lax.optimization_barrier((value,) + first)[0]


def gelu_both(pre):
    square = pre * pre
    bent = jnp.tanh(GELU_COEF * (pre + 0.044715 * square * pre))
    out = 0.5 * pre * (1.0 + bent)
    slope = 0.5 * (1.0 + bent) + 0.5 * pre * (1.0 - bent * bent) * GELU_COEF * (
        1.0 + 3.0 * 0.044715 * square
    )
    return out.astype(BF16), slope.astype(BF16)


def local(
    x_in,
    cotangent,
    lengths,
    adapter_ids,
    w_qkv,
    w_out,
    w_up,
    w_down,
    ln_gain,
    ln_bias,
    a_qkv,
    b_qkv,
    a_out,
    b_out,
    a_up,
    b_up,
    a_down,
    b_down,
):
    n_ctx, n_fsdp = lax.axis_size("ctx"), lax.axis_size("fsdp")
    z, ct = lax.axis_index("fsdp"), lax.axis_index("ctx")
    seqs, piece, width = x_in.shape
    per = seqs // n_fsdp
    loc = n_fsdp * piece
    heads_width = w_qkv.shape[2]
    n_group = GROUPS if per % GROUPS == 0 else 1
    g_per = per // n_group
    g_rows = g_per * loc

    def take(array, start, size, axis=0):
        return lax.dynamic_slice_in_dim(array, start, size, axis)

    def put(array, block, *starts):
        return lax.dynamic_update_slice(array, block, starts)

    def undeal(rows, group_out):
        rows = rows.reshape(g_per, n_fsdp, piece, width)
        out = []
        for step in range(n_fsdp):
            block = rows[:, step]
            out.append(block if step == 0 else shift(block, "fsdp", -step))
        return out

    units = w_up.shape[1]
    rows_shape = (per, n_fsdp, piece, width)
    zq, zu = w_qkv.shape[1], w_up.shape[0]

    def first_items(ins, outs, z):
        x_ref, w_ref = ins
        rows_ref, whole_ref = outs

        def deal(g):
            return Deal(lambda to: x_ref.at[to * per + g], lambda s: rows_ref.at[g, s])

        def weight(j):
            size = zq // n_ctx
            columns = pl.ds(j * heads_width, heads_width)
            return Weight(
                lambda c: w_ref.at[j, pl.ds(pl.multiple_of(c * size, size), size)],
                lambda o, c: whole_ref.at[
                    pl.ds(pl.multiple_of(o * zq + c * size, size), size), columns
                ],
            )

        stay = [(x_ref.at[z * per + g], rows_ref.at[g, 0]) for g in range(per)]
        for j in range(3):
            own = whole_ref.at[
                pl.ds(pl.multiple_of(z * zq, zq), zq), pl.ds(j * heads_width, heads_width)
            ]
            stay.append((w_ref.at[j], own))
        items = [weight(j) for j in range(3)] + [deal(g) for g in range(per)]
        return items, stay

    x_all, qkv_x = move(
        first_items,
        [Weight] * 3 + [Deal] * per,
        (x_in, w_qkv),
        (rows_shape, (width + 3 * NR, 3 * heads_width)),
        n_fsdp,
        n_ctx,
        ((piece, width),) * per + (w_qkv.shape[1:],) * 3,
        0,
        foot=(b_qkv, lambda outs: outs[1].at[pl.ds(width, 3 * NR)]),
    )

    a_in = a_qkv.transpose(1, 0, 2).reshape(width, 3 * NR)

    my_lengths = take(lengths, z * per, per)
    my_ids = take(adapter_ids, z * per, per)
    picked = (my_ids[:, None] == jnp.arange(NR)[None, :] // RANK).astype(F32)
    steps = lax.rem(z - jnp.arange(n_fsdp) + n_fsdp, n_fsdp)
    ctx_of = ct ^ jnp.array(offsets(n_ctx))
    key_pos = (
        (steps[None, :, None] * n_ctx + ctx_of[:, None, None]) * piece
        + jnp.arange(piece)[None, None, :]
    ).reshape(-1)
    bias_all = jnp.where(key_pos[None, :] < my_lengths[:, None], 0.0, -1e30).astype(F32)
    bias_all = jnp.broadcast_to(bias_all[:, :, None], bias_all.shape + (128,))

    pick_all = jnp.repeat(picked, loc, axis=0)
    x_flat = x_all.reshape(per * loc, width)
    adapt_all = (dot(x_flat, a_in) * jnp.concatenate([pick_all] * 3, axis=1)).astype(BF16)
    proj_all = mm(jnp.concatenate([x_flat, adapt_all], axis=1), qkv_x, False, as_low, 1024)
    kv_own = jnp.stack([proj_all[:, heads_width : 2 * heads_width], proj_all[:, 2 * heads_width :]])
    kv_own = kv_own.reshape(2, per, loc, heads_width)
    moved = forward_and_gather(
        proj_all[:, :heads_width].reshape(per, loc, heads_width),
        kv_own,
        bias_all,
        (cotangent, w_out, w_up, w_down),
        (a_out, b_up, a_down),
        n_fsdp,
        n_ctx,
    )
    kv_all = [kv_own] + list(moved[: n_ctx - 1])
    cot_all, out_x, up_x, down_x, context, log_total, part_out, other_out = moved[n_ctx - 1 :]
    cot_flat = cot_all.reshape(per * loc, width)

    groups = range(n_group)
    picks = [jnp.repeat(take(picked, g * g_per, g_per), loc, axis=0) for g in groups]
    part = [slice(g * g_rows, (g + 1) * g_rows) for g in groups]
    seq = [slice(n * loc, (n + 1) * loc) for n in range(g_per)]
    x_rows = [x_flat[part[g]] for g in groups]

    ctx_flat = context.reshape(per * loc, heads_width)
    ctx_rows = [ctx_flat[part[g]] for g in groups]
    summed = (part_out.astype(F32) + other_out.astype(F32)).reshape(per * loc, width + NR)
    summed = [summed[part[g]] for g in groups]
    adapt_out, hat1, rstd1, hidden, hidden_low, adapt_up, gelu_out, slope = ([] for _ in range(8))
    for g in groups:
        adapt_out.append((summed[g][:, width:] * picks[g]).astype(BF16))
        y1 = x_rows[g].astype(F32) + summed[g][:, :width] + dot(adapt_out[g], b_out)
        parts = norm_parts(y1)
        hat1.append(parts[0])
        rstd1.append(parts[1])
        hidden.append(parts[0] * ln_gain[0] + ln_bias[0])
        hidden_low.append(hidden[g].astype(BF16))
        adapt_up.append((dot(hidden_low[g], a_up) * picks[g]).astype(BF16))
        wide = jnp.concatenate([hidden_low[g], adapt_up[g]], axis=1)
        pair = mm(wide, up_x, False, gelu_both, 1024, 2)
        gelu_out.append(pair[0])
        slope.append(pair[1])
    summed = both_in_turn([mm(gelu_out[g], down_x, False, as_low, 768) for g in groups])
    adapt_down, acts, dy2, d_down, dadapt_down, d_pre = ([] for _ in range(6))
    for g in groups:
        adapt_down.append((summed[g][:, width:] * picks[g]).astype(BF16))
        hat2, rstd2 = norm_parts(hidden[g] + summed[g][:, :width] + dot(adapt_down[g], b_down))
        acts.append((hat2 * ln_gain[1] + ln_bias[1]).astype(BF16))
        dy2.append(norm_back(hat2, rstd2, cot_flat[part[g]].astype(F32) * ln_gain[1]))
        d_down.append(dy2[g].astype(BF16))
        dadapt_down.append((dot_nt(d_down[g], b_down) * picks[g]).astype(BF16))
        wide = jnp.concatenate([d_down[g], dadapt_down[g]], axis=1)
        d_pre.append(mm(wide, down_x, True, times, 1024, 1, slope[g]))
    summed = both_in_turn([mm(d_pre[g], up_x, True, as_low, 768) for g in groups])
    dadapt_up, dy1, d_attn, dadapt_out, backs = ([] for _ in range(5))
    for g in groups:
        dadapt_up.append((summed[g][:, width:] * picks[g]).astype(BF16))
        dh1 = dy2[g] + summed[g][:, :width] + dot_nt(dadapt_up[g], a_up)
        dy1.append(norm_back(hat1[g], rstd1[g], dh1 * ln_gain[0]))
        d_attn.append(dy1[g].astype(BF16))
        dadapt_out.append((dot_nt(d_attn[g], b_out) * picks[g]).astype(BF16))
        wide = jnp.concatenate([d_attn[g], dadapt_out[g]], axis=1)
        backs.append(mm(wide, out_x, True, as_low, 512).reshape(g_per, loc, heads_width))
    d_query, d_pair, activations = attend_back(
        proj_all[:, :heads_width].reshape(per, loc, heads_width),
        kv_own,
        kv_all[1:],
        bias_all,
        jnp.concatenate(backs, axis=0),
        log_total,
        jnp.concatenate(acts, axis=0).reshape(per, n_fsdp, piece, width),
        n_fsdp,
        n_ctx,
    )
    d_query = d_query.reshape(per * loc, heads_width)
    d_pair = d_pair.reshape(2, per * loc, heads_width)

    def gathered(parts):
        mine = jnp.concatenate(parts, axis=1)
        blocks = [
            lax.dynamic_index_in_dim(mine, ct ^ offset, 0, False) for offset in offsets(n_ctx)
        ]
        own = fold(blocks, "ctx")
        got = jnp.stack([own] + [shift(own, "fsdp", step) for step in range(1, n_fsdp)])
        return spread([got], "ctx")

    early_in = []
    for g in groups:
        pairs = (
            (adapt_down[g], d_down[g]),
            (dadapt_down[g], gelu_out[g]),
            (adapt_up[g], d_pre[g]),
            (dadapt_up[g], hidden_low[g]),
            (adapt_out[g], d_attn[g]),
            (dadapt_out[g], ctx_rows[g]),
        )
        early_in.append(pairs)
    early_in = after(early_in, d_query)
    early = gathered(
        [compact([(c[r], v[r]) for c, v in early_in[g]], n_ctx) for g in groups for r in seq]
    )

    ins, late = [], []
    d_proj = [
        jnp.concatenate([d_query[part[g]], d_pair[0, part[g]], d_pair[1, part[g]]], axis=1)
        for g in groups
    ]
    summed = both_in_turn([mm(d_proj[g], qkv_x, True, as_low, 640) for g in groups])
    for g in groups:
        pick3 = jnp.concatenate([picks[g]] * 3, axis=1)
        dadapt_in = (summed[g][:, width:] * pick3).astype(BF16)
        d_x = (dy1[g] + summed[g][:, :width] + dot_nt(dadapt_in, a_in)).astype(BF16)
        ins.append(undeal(d_x, g))
        adapt_in = adapt_all[part[g]]
        for r in seq:
            pairs = []
            for j in range(3):
                codes = slice(j * NR, (j + 1) * NR)
                columns = slice(j * heads_width, (j + 1) * heads_width)
                pairs.append((adapt_in[r, codes], d_proj[g][r, columns]))
            for j in range(3):
                pairs.append((dadapt_in[r, j * NR : (j + 1) * NR], x_rows[g][r]))
            late.append(compact(pairs, n_ctx))
    late = gathered(late)

    def assemble(parts):
        full = jnp.zeros((seqs, piece, width), BF16)
        for group, blocks in enumerate(parts):
            for step, block in enumerate(blocks):
                owner = lax.rem(z + step, n_fsdp)
                full = put(full, block, owner * per + group * g_per, 0, 0)
        return full

    codes = (adapter_ids[:, None] * RANK + jnp.arange(RANK)[None, :]).reshape(-1)
    chosen = (codes[:, None] == jnp.arange(NR)[None, :]).astype(BF16)
    early = after(early, summed[-1])
    e = combine(
        early,
        chosen,
        [(NR, width), (units, NR), (NR, units), (width, NR), (NR, width), (heads_width, NR)],
    )
    l = combine(late, chosen, [(3, NR, heads_width), (3, width, NR)])
    return activations, assemble(ins), l[1], l[0], e[5], e[4], e[3], e[2], e[1], e[0]


def solution(mesh):
    rows = P(None, ("fsdp", "ctx"), None)
    return jax.shard_map(
        local,
        mesh=mesh,
        in_specs=(
            rows,
            rows,
            P(),
            P(),
            P(None, "fsdp", "tp"),
            P("tp", "fsdp"),
            P("fsdp", "tp"),
            P("tp", "fsdp"),
            P(),
            P(),
            P(),
            P(None, None, "tp"),
            P("tp", None),
            P(),
            P(),
            P(None, "tp"),
            P("tp", None),
            P(),
        ),
        out_specs=(
            rows,
            rows,
            P(),
            P(None, None, "tp"),
            P("tp", None),
            P(),
            P(),
            P(None, "tp"),
            P("tp", None),
            P(),
        ),
        check_vma=False,
    )
```

```python
import math

import jax
import jax.numpy as jnp
from jax import lax
from jax.experimental import pallas as pl
from jax.experimental.pallas import tpu as pltpu
from jax.sharding import PartitionSpec as P

HEAD_DIM = 128
RANK = 16
ADAPTERS = 8
NR = RANK * ADAPTERS
NORM_EPS = 1e-06
GELU_COEF = 0.7978845608028654
SCALE = 1.0 / math.sqrt(HEAD_DIM)
GROUPS = 2
F32 = jnp.float32
BF16 = jnp.bfloat16


def dot(left, right):
    return jnp.dot(left, right, preferred_element_type=F32)


def dot_nt(left, right):
    return lax.dot_general(left, right, (((1,), (1,)), ((), ())), preferred_element_type=F32)


def dot_tn(left, right):
    return lax.dot_general(left, right, (((0,), (0,)), ((), ())), preferred_element_type=F32)


def shift(block, axis, step):
    n = lax.axis_size(axis)
    return lax.ppermute(block, axis, [(i, (i + step) % n) for i in range(n)])


def swap(block, axis, mask):
    n = lax.axis_size(axis)
    return lax.ppermute(block, axis, [(i, i ^ mask) for i in range(n)])


def masks_of(n):
    out = []
    while n > 1:
        n //= 2
        out.append(n)
    return out


def spread(pieces, axis):
    for mask in masks_of(lax.axis_size(axis)):
        pieces = pieces + [swap(piece, axis, mask) for piece in pieces]
    return pieces


def offsets(n):
    out = [0]
    for mask in masks_of(n):
        out = out + [o ^ mask for o in out]
    return out


def fold(pieces, axis):
    for mask in reversed(masks_of(lax.axis_size(axis))):
        half = len(pieces) // 2
        got = [swap(piece, axis, mask) for piece in pieces[half:]]
        pieces = [
            (mine.astype(F32) + other.astype(F32)).astype(BF16)
            for mine, other in zip(pieces[:half], got)
        ]
    return pieces[0]


def both_in_turn(parts):
    lows, got = list(parts), None
    for mask in masks_of(lax.axis_size("tp")):
        got = [swap(low, "tp", mask) for low in lows]
        for g in range(len(lows) - 1):
            got[g] = after(got[g], *lows[g + 1 :])
        totals = [low.astype(F32) + other.astype(F32) for low, other in zip(lows, got)]
        lows = [total.astype(BF16) for total in totals]
    return totals


def attend_head(query, keys, values, biases):
    scores = [dot_nt(k, query) * SCALE + bias for k, bias in zip(keys, biases)]
    top = scores[0].max(axis=0, keepdims=True)
    for s in scores[1:]:
        top = jnp.maximum(top, s.max(axis=0, keepdims=True))
    total = jnp.zeros_like(top)
    mixed = None
    for s, v in zip(scores, values):
        probs = jnp.exp(s - top)
        total = total + probs.sum(axis=0, keepdims=True)
        term = dot_tn(v, probs.astype(BF16))
        mixed = term if mixed is None else mixed + term
    return (mixed / total).T.astype(BF16), top + jnp.log(total)


def attend_back_head(query, grad, log_total, keys, values, biases):
    probs, dprobs, dvalues = [], [], []
    delta = jnp.zeros_like(log_total)
    for k, v, bias in zip(keys, values, biases):
        p = jnp.exp(dot_nt(k, query) * SCALE + bias - log_total)
        dp = dot_nt(v, grad)
        dvalues.append(dot(p.astype(BF16), grad).astype(BF16))
        delta = delta + (p * dp).sum(axis=0, keepdims=True)
        probs.append(p)
        dprobs.append(dp)
    dquery, dkeys = None, []
    for k, p, dp in zip(keys, probs, dprobs):
        ds = (p * (dp - delta)).astype(BF16)
        dkeys.append((dot(ds, query) * SCALE).astype(BF16))
        term = dot_tn(k, ds)
        dquery = term if dquery is None else dquery + term
    return (dquery * SCALE).T.astype(BF16), dkeys, dvalues


def ds(start, size):
    return pl.ds(pl.multiple_of(start, size), size)


def flip(ct, offset):
    mask = 1
    while mask <= offset:
        if offset & mask:
            ct = ct + mask - 2 * mask * lax.rem(ct // mask, 2)
        mask *= 2
    return ct


class Weight:
    def __init__(self, shard_at, whole_at):
        self.shard_at, self.whole_at = shard_at, whole_at


class Deal:
    def __init__(self, source_at, rows_at):
        self.source_at, self.rows_at = source_at, rows_at


class Pair:
    def __init__(self, slot_at):
        self.slot_at = slot_at


class Mover:
    def __init__(self, n_fsdp, n_ctx, send, recv):
        self.n_fsdp, self.n_ctx = n_fsdp, n_ctx
        self.z, self.ct = lax.axis_index("fsdp"), lax.axis_index("ctx")
        self.send, self.recv = send, recv
        self.used = 0
        self.open = []
        self.masks = masks_of(n_ctx)
        self.offsets = offsets(n_ctx)
        self.came, self.waiting = {}, {}

    def greet(self, tp=False):
        barrier = pltpu.get_barrier_semaphore()
        others = [{"fsdp": lax.rem(self.z + s, self.n_fsdp)} for s in range(1, self.n_fsdp)]
        others += [{"ctx": flip(self.ct, mask)} for mask in self.masks]
        if tp:
            others.append({"tp": 1 - lax.axis_index("tp")})
        for other in others:
            pl.semaphore_signal(
                barrier, inc=1, device_id=other, device_id_type=pl.DeviceIdType.MESH
            )
        pl.semaphore_wait(barrier, len(others))

    def copy(self, source, target, device, at=None):
        if at is None:
            at = self.used
            self.used += 1
        return pltpu.make_async_remote_copy(
            src_ref=source,
            dst_ref=target,
            send_sem=self.send.at[at],
            recv_sem=self.recv.at[at],
            device_id=device,
            device_id_type=pl.DeviceIdType.MESH,
        )

    def go(self, source, target, device):
        copy = self.copy(source, target, device)
        copy.start()
        self.open.append((None, copy))
        return copy

    def along(self, item, owner, right, ok, source, slot):
        target = item.whole_at(owner, self.ct)
        device = {"fsdp": lax.rem(self.z + (1 if right else self.n_fsdp - 1), self.n_fsdp)}
        copy = self.copy(source, target, device, self.came[item] + slot - 1)
        pl.when(ok)(copy.start)
        self.open.append((ok, copy))

    def begin(self, item):
        if isinstance(item, Pair):
            self.waiting[item] = [[] for _ in self.masks]
            self.cast(item, item.slot_at, lambda k, level: item.slot_at(k + 2**level), 0, 0)
            return
        if isinstance(item, Weight):
            self.came[item] = self.used
            self.used += self.n_fsdp - 1
            source = item.shard_at(self.ct)
            self.along(item, self.z, True, self.z < self.n_fsdp - 1, source, 1)
            self.along(item, self.z, False, self.z > 0, source, self.n_fsdp - 1)
            return
        self.came[item] = [
            self.go(
                item.source_at(lax.rem(self.z + s, self.n_fsdp)),
                item.rows_at(s),
                {"fsdp": lax.rem(self.z + s, self.n_fsdp)},
            )
            for s in range(1, self.n_fsdp)
        ]

    def cast(self, item, source_at, target_at, k, first):
        for level in range(first, len(self.masks)):
            device = {"ctx": flip(self.ct, self.masks[level])}
            copy = self.go(source_at(k), target_at(k, level), device)
            self.waiting[item][level].append((copy, k + 2**level, source_at, target_at))

    def relay(self, item):
        if isinstance(item, Pair):
            return
        if isinstance(item, Deal):
            for copy in self.came[item]:
                copy.wait_recv()
            return
        self.waiting[item] = [[] for _ in self.masks]
        n = self.n_fsdp
        for i in range(n - 1):
            s = i // 2 + 1 if i % 2 == 0 else n - 1 - i // 2
            owner = lax.rem(self.z - s + n, n)
            here = item.whole_at(owner, self.ct)
            self.copy(here, here, {"fsdp": owner}, self.came[item] + s - 1).wait_recv()
            if s < n - 1:
                ok = (self.z >= s) & (self.z < n - 1)
                self.along(item, owner, True, ok, here, s + 1)
            if s > 1:
                ok = (self.z < s) & (self.z > 0)
                self.along(item, owner, False, ok, here, s - 1)

            def at(k, owner=owner):
                return item.whole_at(owner, flip(self.ct, self.offsets[k]))

            self.cast(item, at, lambda k, level, at=at: at(k), 0, 0)

    def finish(self, item, level):
        if isinstance(item, Deal):
            return
        for copy, k, source_at, target_at in self.waiting[item][level]:
            copy.wait_recv()
            self.cast(item, source_at, target_at, k, level + 1)

    def close(self):
        for ok, copy in self.open:
            if ok is None:
                copy.wait_send()
            else:
                pl.when(ok)(copy.wait_send)


def copies_of(items, n_fsdp, n_ctx):
    total = 0
    for item in items:
        total += {Weight: (n_fsdp - 1) * n_ctx, Deal: n_fsdp - 1, Pair: n_ctx - 1}[item]
    return total


def keep(stay, room, sems):
    out = []
    for k, (source, target) in enumerate(stay):
        first = pltpu.make_async_copy(source, room[k], sems.at[2 * k])
        first.start()
        out.append((first, pltpu.make_async_copy(room[k], target, sems.at[2 * k + 1])))
    return out


def move(make, kinds, inputs, outputs, n_fsdp, n_ctx, local_shapes, ident, ahead=2, foot=None):
    n_in = len(inputs)
    n_copy = copies_of(kinds, n_fsdp, n_ctx)

    def kernel(*refs):
        ins, outs = refs[:n_in], refs[n_in : n_in + len(outputs)]
        send, recv, here = refs[n_in + len(outputs) : n_in + len(outputs) + 3]
        room = refs[n_in + len(outputs) + 3 :]
        if foot is not None:
            blocks_ref, ins = ins[-1], ins[:-1]
            strip = room[-1]
        mover = Mover(n_fsdp, n_ctx, send, recv)
        items, stay = make(ins, outs, mover.z)
        mover.greet()
        for item in items[:ahead]:
            mover.begin(item)
        kept = keep(stay, room, here)
        levels = len(mover.masks)
        for i in range(len(items) + levels):
            if i < len(items):
                mover.relay(items[i])
                if i + ahead < len(items):
                    mover.begin(items[i + ahead])
            if i == 0 and foot is not None:
                strip[...] = jnp.zeros_like(strip)
                high, wide = blocks_ref.shape[1:]
                for j in range(blocks_ref.shape[0]):
                    strip[j * high : (j + 1) * high, j * wide : (j + 1) * wide] = blocks_ref[j]
                set_foot = pltpu.make_async_copy(strip, foot[1](outs), here.at[2 * len(local_shapes)])
                set_foot.start()
                kept.append((None, set_foot))
            if i == 0:
                for first, second in kept:
                    if first is not None:
                        first.wait()
                        second.start()
            for level in range(levels):
                if 0 <= i - 1 - level < len(items):
                    mover.finish(items[i - 1 - level], level)
        for _, second in kept:
            second.wait()
        mover.close()

    spaces = [pl.BlockSpec(memory_space=pl.ANY)] * n_in
    room_shapes = list(local_shapes)
    if foot is not None:
        blocks = foot[0]
        inputs = inputs + (blocks,)
        n_in += 1
        spaces.append(pl.BlockSpec(memory_space=pltpu.VMEM))
        room_shapes.append((blocks.shape[0] * blocks.shape[1], blocks.shape[0] * blocks.shape[2]))
    return pl.pallas_call(
        kernel,
        in_specs=spaces,
        out_specs=[pl.BlockSpec(memory_space=pl.ANY)] * len(outputs),
        out_shape=[jax.ShapeDtypeStruct(shape, BF16) for shape in outputs],
        scratch_shapes=[
            pltpu.SemaphoreType.DMA((n_copy,)),
            pltpu.SemaphoreType.DMA((n_copy,)),
            pltpu.SemaphoreType.DMA((2 * len(local_shapes) + 1,)),
        ]
        + [pltpu.VMEM(shape, BF16) for shape in room_shapes],
        compiler_params=pltpu.CompilerParams(
            collective_id=ident, has_side_effects=True, vmem_limit_bytes=32 << 20
        ),
    )(*inputs)


def forward_and_gather(query, kv_own, bias, shards, maps, n_fsdp, n_ctx):
    per, loc, width_here = query.shape
    cot, w_out, w_up, w_down = shards
    piece, width = cot.shape[1:]
    heads, units = width_here // HEAD_DIM, w_up.shape[1]
    zu, zo = w_up.shape[0], w_out.shape[1]
    so, su, sd = w_out.shape[0] // n_ctx, zu // n_ctx, w_down.shape[0] // n_ctx
    wide = width + NR
    stay_shapes = [(piece, width)] * per + [x.shape for x in (w_out, w_up, w_down) + maps]
    n_stay = len(stay_shapes)
    halves = 2
    n_copy = (n_fsdp - 1) * n_ctx * (1 + 2 * halves) + per * (n_fsdp - 1 + n_ctx - 1 + 1)

    def kernel(*refs):
        q_ref, bias_ref, kv_ref, cot_ref, wo_ref, wu_ref, wd_ref, ao_ref, bu_ref, ad_ref = refs[:10]
        slots = refs[10 : 9 + n_ctx]
        rows_ref, out_ref, up_ref, down_ref, ctx_ref, log_ref, part_ref, other_ref = refs[
            9 + n_ctx : 17 + n_ctx
        ]
        send, recv, here, load, kv_room, out_room = refs[17 + n_ctx : 23 + n_ctx]
        room = refs[23 + n_ctx :]
        mover = Mover(n_fsdp, n_ctx, send, recv)
        z = mover.z

        def deal(g):
            return Deal(lambda to: cot_ref.at[to * per + g], lambda s: rows_ref.at[g, s])

        def pair(g):
            return Pair(lambda k: kv_ref.at[:, g] if k == 0 else slots[k - 1].at[:, g])

        out_item = Weight(
            lambda c: wo_ref.at[ds(c * so, so)],
            lambda o, c: out_ref.at[ds(c * so, so), ds(o * zo, zo)],
        )

        def up_item(h):
            columns = pl.ds(h * (units // halves), units // halves)
            return Weight(
                lambda c: wu_ref.at[ds(c * su, su), columns],
                lambda o, c: up_ref.at[ds(o * zu + c * su, su), columns],
            )

        def down_item(h):
            size = sd // halves
            return Weight(
                lambda c: wd_ref.at[ds(c * sd + h * size, size)],
                lambda o, c: down_ref.at[ds(c * sd + h * size, size), ds(o * zo, zo)],
            )

        pairs = [pair(g) for g in range(per)]
        items = [out_item] + [up_item(h) for h in range(halves)]
        items += [down_item(h) for h in range(halves)] + [deal(g) for g in range(per)]
        stay = [(cot_ref.at[z * per + g], rows_ref.at[g, 0]) for g in range(per)]
        stay += [
            (wo_ref, out_ref.at[:, ds(z * zo, zo)]),
            (wu_ref, up_ref.at[ds(z * zu, zu)]),
            (wd_ref, down_ref.at[:, ds(z * zo, zo)]),
            (ao_ref, out_ref.at[:, pl.ds(width, NR)]),
            (bu_ref, up_ref.at[pl.ds(width, NR)]),
            (ad_ref, down_ref.at[:, pl.ds(width, NR)]),
        ]

        def attend(g):
            for level in range(len(mover.masks)):
                mover.finish(pairs[g], level)
            loads = []
            for k in range(n_ctx):
                copy = pltpu.make_async_copy(pairs[g].slot_at(k), kv_room.at[k], load.at[k])
                copy.start()
                loads.append(copy)
            for copy in loads:
                copy.wait()

            def one(h, carry):
                at = ds(h * HEAD_DIM, HEAD_DIM)
                biases = []
                for k in range(n_ctx):
                    block = bias_ref[g, k * loc : (k + 1) * loc, :]
                    biases.append(jnp.concatenate([block] * (loc // 128), axis=1))
                context, log = attend_head(
                    q_ref[g, :, at],
                    [kv_room[k, 0, :, at] for k in range(n_ctx)],
                    [kv_room[k, 1, :, at] for k in range(n_ctx)],
                    biases,
                )
                ctx_ref[g, :, at] = context
                log_ref[g, h] = log
                return carry

            lax.fori_loop(0, heads, one, 0)

        def project():
            copy = pltpu.make_async_copy(out_ref, out_room, load.at[n_ctx])
            copy.start()
            copy.wait()
            for g in range(per):
                for start in range(0, wide, 1024):
                    at = slice(start, min(start + 1024, wide))
                    part_ref[g, :, at] = dot(ctx_ref[g], out_room[:, at]).astype(BF16)
                swapped.append(
                    mover.go(
                        part_ref.at[g], other_ref.at[g], {"tp": 1 - lax.axis_index("tp")}
                    )
                )

        swapped = []
        tasks = {i: (lambda g=i: attend(g)) for i in range(per)}
        tasks[per] = project
        mover.greet(tp=True)
        for item in pairs + items[:2]:
            mover.begin(item)
        kept = keep(stay, room, here)
        levels = len(mover.masks)
        for i in range(len(items) + levels):
            if i < len(items):
                mover.relay(items[i])
                if i + 2 < len(items):
                    mover.begin(items[i + 2])
            if i == 0:
                for first, second in kept:
                    first.wait()
                    second.start()
            for level in range(levels):
                if 0 <= i - 1 - level < len(items):
                    mover.finish(items[i - 1 - level], level)
            if i == per:
                for _, second in kept:
                    second.wait()
            if i in tasks:
                tasks[i]()
        for copy in swapped:
            copy.wait_recv()
        mover.close()

    row = (per, loc, width_here)
    vmem, anywhere = pl.BlockSpec(memory_space=pltpu.VMEM), pl.BlockSpec(memory_space=pl.ANY)
    outputs = [(kv_own.shape, BF16, anywhere)] * (n_ctx - 1) + [
        ((per, n_fsdp, piece, width), BF16, anywhere),
        ((width_here, wide), BF16, anywhere),
        ((wide, units), BF16, anywhere),
        ((units, wide), BF16, anywhere),
        (row, BF16, vmem),
        ((per, heads, 1, loc), F32, vmem),
        ((per, loc, wide), BF16, vmem),
        ((per, loc, wide), BF16, anywhere),
    ]
    return pl.pallas_call(
        kernel,
        in_specs=[vmem, vmem] + [anywhere] * 8,
        out_specs=[space for _, _, space in outputs],
        out_shape=[jax.ShapeDtypeStruct(shape, dtype) for shape, dtype, _ in outputs],
        scratch_shapes=[
            pltpu.SemaphoreType.DMA((n_copy,)),
            pltpu.SemaphoreType.DMA((n_copy,)),
            pltpu.SemaphoreType.DMA((2 * n_stay,)),
            pltpu.SemaphoreType.DMA((n_ctx + 1,)),
            pltpu.VMEM((n_ctx, 2, loc, width_here), BF16),
            pltpu.VMEM((width_here, wide), BF16),
        ]
        + [pltpu.VMEM(shape, BF16) for shape in stay_shapes],
        compiler_params=pltpu.CompilerParams(
            collective_id=1, has_side_effects=True, vmem_limit_bytes=50 << 20
        ),
    )(query, bias, kv_own, cot, w_out, w_up, w_down, *maps)


def attend_back(query, kv_own, slots, bias, grad, log_total, acts, n_fsdp, n_ctx):
    per, loc, width_here = query.shape
    piece, width = acts.shape[2:]
    heads = width_here // HEAD_DIM
    cuts = 2
    high = heads // cuts
    columns = high * HEAD_DIM
    masks = masks_of(n_ctx)
    units = [(g, c) for g in range(per) for c in range(cuts)]
    n_copy = per * (n_fsdp - 1) + len(units) * (n_ctx - 1)

    def kernel(*refs):
        q_ref, bias_ref, g_ref, log_ref, acts_ref, kv_ref = refs[:6]
        slot_refs = refs[6 : 5 + n_ctx]
        dq_ref, dkv_ref, out_ref = refs[5 + n_ctx : 8 + n_ctx]
        send, recv, load, kv_room, own, came, act_room = refs[8 + n_ctx :]
        mover = Mover(n_fsdp, n_ctx, send, recv)
        z, ct = mover.z, mover.ct
        loads = []
        for g in range(per):
            loads.append([])
            for k in range(n_ctx):
                source = kv_ref if k == 0 else slot_refs[k - 1]
                copy = pltpu.make_async_copy(
                    source.at[:, g], kv_room.at[g, k], load.at[g * n_ctx + k]
                )
                copy.start()
                loads[g].append(copy)
        kept = []
        for g in range(per):
            at = per * n_ctx + 2 * g
            first = pltpu.make_async_copy(acts_ref.at[g, 0], act_room.at[g], load.at[at])
            first.start()
            second = pltpu.make_async_copy(
                act_room.at[g], out_ref.at[z * per + g], load.at[at + 1]
            )
            kept.append((first, second))
        mover.greet()
        dealt = []
        for g in range(per):
            for s in range(1, n_fsdp):
                to = lax.rem(z - s + n_fsdp, n_fsdp)
                dealt.append(
                    mover.go(acts_ref.at[g, s], out_ref.at[z * per + g], {"fsdp": to})
                )
        flying = {}

        def compute(u):
            g, c = units[u]
            if c == 0:
                for copy in loads[g]:
                    copy.wait()

            def one(h, carry):
                at = ds(c * columns + h * HEAD_DIM, HEAD_DIM)
                to = ds(h * HEAD_DIM, HEAD_DIM)
                biases = []
                for k in range(n_ctx):
                    block = bias_ref[g, k * loc : (k + 1) * loc, :]
                    biases.append(jnp.concatenate([block] * (loc // 128), axis=1))
                dquery, dkeys, dvalues = attend_back_head(
                    q_ref[g, :, at],
                    g_ref[g, :, at],
                    log_ref[g, c * high + h],
                    [kv_room[g, k, 0, :, at] for k in range(n_ctx)],
                    [kv_room[g, k, 1, :, at] for k in range(n_ctx)],
                    biases,
                )
                dq_ref[g, :, at] = dquery
                for k in range(n_ctx):
                    own[u, k, 0, :, to] = dkeys[k]
                    own[u, k, 1, :, to] = dvalues[k]
                return carry

            lax.fori_loop(0, high, one, 0)

        def hand(u, level):
            half = 2**level
            device = {"ctx": flip(ct, masks[level])}
            flying[u, level] = [
                mover.go(own.at[u, half + i], came.at[u, half - 1 + i], device) for i in range(half)
            ]

        def take_in(u, level):
            half = 2**level
            for i, copy in enumerate(flying[u, level]):
                copy.wait_recv()
                for j in range(2):
                    total = own[u, i, j].astype(F32) + came[u, half - 1 + i, j].astype(F32)
                    if level:
                        own[u, i, j] = total.astype(BF16)
                    else:
                        g, c = units[u]
                        dkv_ref[j, g, :, c * columns : (c + 1) * columns] = total.astype(BF16)

        last = len(masks) - 1
        for t in range(len(units) + last + 1):
            if t < len(units):
                compute(t)
                hand(t, last)
            if t == 0:
                for first, second in kept:
                    first.wait()
                    second.start()
            for k in range(last + 1):
                u, level = t - 1 - k, last - k
                if 0 <= u < len(units):
                    take_in(u, level)
                    if level:
                        hand(u, level - 1)
        for _, second in kept:
            second.wait()
        for copy in dealt:
            copy.wait_recv()
        mover.close()

    vmem, anywhere = pl.BlockSpec(memory_space=pltpu.VMEM), pl.BlockSpec(memory_space=pl.ANY)
    return pl.pallas_call(
        kernel,
        in_specs=[vmem] * 4 + [anywhere] * (1 + n_ctx),
        out_specs=[vmem, vmem, anywhere],
        out_shape=[
            jax.ShapeDtypeStruct(query.shape, BF16),
            jax.ShapeDtypeStruct(kv_own.shape, BF16),
            jax.ShapeDtypeStruct((per * n_fsdp, piece, width), BF16),
        ],
        scratch_shapes=[
            pltpu.SemaphoreType.DMA((n_copy,)),
            pltpu.SemaphoreType.DMA((n_copy,)),
            pltpu.SemaphoreType.DMA((per * (n_ctx + 2),)),
            pltpu.VMEM((per, n_ctx, 2, loc, width_here), BF16),
            pltpu.VMEM((len(units), n_ctx, 2, loc, columns), BF16),
            pltpu.VMEM((len(units), n_ctx - 1, 2, loc, columns), BF16),
            pltpu.VMEM((per, piece, width), BF16),
        ],
        compiler_params=pltpu.CompilerParams(
            collective_id=2, has_side_effects=True, vmem_limit_bytes=56 << 20
        ),
    )(query, bias, grad, log_total, acts, kv_own, *slots)


class Ring:
    def __init__(self, room, sems, at, tile_at):
        self.room, self.sems, self.at, self.tile_at = room, sems, at, tile_at

    def copy(self, t):
        slot = lax.rem(t, 2)
        return pltpu.make_async_copy(
            self.tile_at(t), self.room.at[slot], self.sems.at[self.at + slot]
        )

    def prefetch(self):
        self.copy(0).start()
        self.copy(1).start()

    def run(self, n, body):
        def step(t, carry):
            self.copy(t).wait()
            body(t, self.room.at[lax.rem(t, 2)])

            @pl.when(t + 2 < n)
            def _():
                self.copy(t + 2).start()

            return carry

        lax.fori_loop(0, n, step, 0)


def norm_parts(values):
    center = values - jnp.mean(values, axis=-1, keepdims=True)
    rstd = lax.rsqrt(jnp.mean(center * center, axis=-1, keepdims=True) + NORM_EPS)
    return center * rstd, rstd


def norm_back(hat, rstd, dhat):
    first = jnp.mean(dhat, axis=-1, keepdims=True)
    second = jnp.mean(dhat * hat, axis=-1, keepdims=True)
    return rstd * (dhat - first - hat * second)


def gelu_both(pre):
    square = pre * pre
    bent = jnp.tanh(GELU_COEF * (pre + 0.044715 * square * pre))
    out = 0.5 * pre * (1.0 + bent)
    slope = 0.5 * (1.0 + bent) + 0.5 * pre * (1.0 - bent * bent) * GELU_COEF * (
        1.0 + 3.0 * 0.044715 * square
    )
    return out.astype(BF16), slope.astype(BF16)


def middle(x_all, part_out, other_out, cot_all, picked, gain, shift_by, weights, maps):
    per, loc, width = x_all.shape
    out_x, up_x, down_x = weights
    a_up, b_out, b_down, a_down, b_up = maps
    wide, units = up_x.shape
    width_here = out_x.shape[0]
    tile = 512
    chunk = 32
    n_wide = width // tile
    n_swap = n_wide + 1

    def kernel(*refs):
        pick_ref, gain_ref, shift_ref, a_up_ref, b_out_ref, b_down_ref, a_down_ref, b_up_ref = refs[:8]
        x_ref, first_ref, second_ref, cot_ref, out_ref, up_ref, down_ref = refs[8:15]
        h_out, gelu_out, acts_out, dd_out, dpre_out, dy1_out, da_out = refs[15:22]
        adapt_out_ref, adapt_down_ref, dadapt_up_ref, ctx_ref = refs[22:26]
        (send, recv, ring_sem, sems) = refs[26:30]
        (up_room, down_room, down_rows, up_rows) = refs[30:34]
        (stage, part, got, hat1, rstd1, keep32, slope, gelu, wide_v, turned, dpre_t) = refs[34:]
        partner = {"tp": 1 - lax.axis_index("tp")}

        up = Ring(up_room, ring_sem, 0, lambda t: up_ref.at[:, ds(t * tile, tile)])
        down = Ring(down_room, ring_sem, 2, lambda t: down_ref.at[:, ds(t * tile, tile)])
        down_r = Ring(down_rows, ring_sem, 4, lambda t: down_ref.at[ds(t * tile, tile)])
        up_r = Ring(up_rows, ring_sem, 6, lambda t: up_ref.at[ds(t * tile, tile)])
        out_r = Ring(down_rows, ring_sem, 4, lambda t: out_ref.at[ds(t * tile, tile)])

        busy = {}
        used = [0]

        def move(source, target, key):
            copy = pltpu.make_async_copy(source, target, sems.at[used[0]])
            used[0] += 1
            copy.start()
            busy.setdefault(key, []).append(copy)

        def free(*keys):
            for key in keys:
                for copy in busy.pop(key, []):
                    copy.wait()

        def swap_copy(turn, g, t, size):
            at = ds(t * tile, size)
            sem = (turn * per + g) * n_swap + t
            return pltpu.make_async_remote_copy(
                src_ref=part.at[g, :, at],
                dst_ref=got.at[turn, g, :, at],
                send_sem=send.at[sem],
                recv_sem=recv.at[sem],
                device_id=partner,
                device_id_type=pl.DeviceIdType.MESH,
            )

        def swapped(turn, g):
            for t in range(n_swap):
                copy = swap_copy(turn, g, t, tile if t < n_wide else NR)
                copy.wait_recv()
                copy.wait_send()

        def by_rows(body):
            def step(r, carry):
                body(pl.ds(pl.multiple_of(r * chunk, chunk), chunk))
                return carry

            lax.fori_loop(0, loc // chunk, step, 0)

        barrier = pltpu.get_barrier_semaphore()
        pl.semaphore_signal(
            barrier, inc=1, device_id=partner, device_id_type=pl.DeviceIdType.MESH
        )
        for g in range(per):
            move(x_ref.at[g], stage.at[g], ("stage", g))
            move(first_ref.at[g], part.at[g], ("part", g))
            move(second_ref.at[g], slope.at[g, :, pl.ds(0, wide)], ("slope", g))
        up.prefetch()
        down.prefetch()
        pl.semaphore_wait(barrier, 1)

        for g in range(per):
            free(("stage", g), ("part", g), ("slope", g), "wide", "gelu")
            pick = pick_ref[g]

            def first_norm(rows, g=g, pick=pick):
                total = part[g, rows, :].astype(F32) + slope[g, rows, :wide].astype(F32)
                code = (total[:, width:] * pick).astype(BF16)
                adapt_out_ref[g, rows, :] = code
                y1 = stage[g, rows, :].astype(F32) + total[:, :width] + dot(code, b_out_ref[...])
                hat, rstd = norm_parts(y1)
                hat1[g, rows, :] = hat
                rstd1[g, rows, :] = jnp.broadcast_to(rstd, (chunk, 128))
                low = (hat * gain_ref[0:1, :] + shift_ref[0:1, :]).astype(BF16)
                wide_v[rows, :width] = low
                wide_v[rows, width:] = (dot(low, a_up_ref[...]) * pick).astype(BF16)

            by_rows(first_norm)
            move(wide_v, h_out.at[g], "wide")
            move(cot_ref.at[g], stage.at[g], ("stage", g))

            def up_tile(t, room, g=g):
                at = ds(t * tile, tile)
                value, factor = gelu_both(dot(wide_v[...], room[...]))
                gelu[:, at] = value
                slope[g, :, at] = factor

            up.run(units // tile, up_tile)
            if g + 1 < per:
                up.prefetch()
            else:
                down_r.prefetch()
            move(gelu, gelu_out.at[g], "gelu")

            def down_tile(t, room, g=g):
                part[g, :, ds(t * tile, tile)] = dot(gelu[...], room[...]).astype(BF16)
                swap_copy(0, g, t, tile).start()

            down.run(n_wide, down_tile)
            if g + 1 < per:
                down.prefetch()
            else:
                up_r.prefetch()
            part[g, :, width:] = dot(gelu[...], a_down_ref[...]).astype(BF16)
            swap_copy(0, g, n_wide, NR).start()

        for g in range(per):
            swapped(0, g)
            free(("stage", g), "wide")
            pick = pick_ref[g]

            def second_norm(rows, g=g, pick=pick):
                total = part[g, rows, :].astype(F32) + got[0, g, rows, :].astype(F32)
                code = (total[:, width:] * pick).astype(BF16)
                adapt_down_ref[g, rows, :] = code
                hidden = hat1[g, rows, :] * gain_ref[0:1, :] + shift_ref[0:1, :]
                hat, rstd = norm_parts(hidden + total[:, :width] + dot(code, b_down_ref[...]))
                part[g, rows, :width] = (hat * gain_ref[1:2, :] + shift_ref[1:2, :]).astype(BF16)
                dy2 = norm_back(hat, rstd, stage[g, rows, :].astype(F32) * gain_ref[1:2, :])
                keep32[g, rows, :] = dy2
                low = dy2.astype(BF16)
                wide_v[rows, :width] = low
                wide_v[rows, width:] = (dot_nt(low, b_down_ref[...]) * pick).astype(BF16)

            by_rows(second_norm)
            move(part.at[g, :, pl.ds(0, width)], acts_out.at[g], ("part", g))
            move(wide_v, dd_out.at[g], "wide")
            turned[...] = wide_v[...].T

            def down_back(t, room, g=g):
                at = ds(t * tile, tile)
                block = dot(room[...], turned[...]).T
                low = (block * slope[g, :, at].astype(F32)).astype(BF16)
                slope[g, :, at] = low
                dpre_t[at, :] = low.T

            down_r.run(units // tile, down_back)
            (down_r if g + 1 < per else out_r).prefetch()
            move(slope.at[g], dpre_out.at[g], ("slope", g))
            free(("part", g))

            def up_back(t, room, g=g):
                part[g, :, ds(t * tile, tile)] = dot(room[...], dpre_t[...]).T.astype(BF16)
                swap_copy(1, g, t, tile).start()

            up_r.run(n_wide, up_back)
            if g + 1 < per:
                up_r.prefetch()
            part[g, :, width:] = dot(b_up_ref[...], dpre_t[...]).T.astype(BF16)
            swap_copy(1, g, n_wide, NR).start()

        for g in range(per):
            swapped(1, g)
            free("wide")
            pick = pick_ref[g]

            def first_back(rows, g=g, pick=pick):
                total = part[g, rows, :].astype(F32) + got[1, g, rows, :].astype(F32)
                code = (total[:, width:] * pick).astype(BF16)
                dadapt_up_ref[g, rows, :] = code
                dh1 = keep32[g, rows, :] + total[:, :width] + dot_nt(code, a_up_ref[...])
                rstd = rstd1[g, rows, 0:1]
                dy1 = norm_back(hat1[g, rows, :], rstd, dh1 * gain_ref[0:1, :])
                keep32[g, rows, :] = dy1
                low = dy1.astype(BF16)
                wide_v[rows, :width] = low
                wide_v[rows, width:] = (dot_nt(low, b_out_ref[...]) * pick).astype(BF16)

            by_rows(first_back)
            move(keep32.at[g], dy1_out.at[g], "dy1")
            move(wide_v, da_out.at[g], "wide")
            turned[...] = wide_v[...].T

            def out_back(t, room, g=g):
                ctx_ref[g, :, ds(t * tile, tile)] = dot(room[...], turned[...]).T.astype(BF16)

            out_r.run(width_here // tile, out_back)
            if g + 1 < per:
                out_r.prefetch()
        free(*list(busy))

    vmem, anywhere = pl.BlockSpec(memory_space=pltpu.VMEM), pl.BlockSpec(memory_space=pl.ANY)
    row = (per, loc)
    outputs = [
        (row + (wide,), BF16, anywhere),
        (row + (units,), BF16, anywhere),
        (row + (width,), BF16, anywhere),
        (row + (wide,), BF16, anywhere),
        (row + (units,), BF16, anywhere),
        (row + (width,), F32, anywhere),
        (row + (wide,), BF16, anywhere),
        (row + (NR,), BF16, vmem),
        (row + (NR,), BF16, vmem),
        (row + (NR,), BF16, vmem),
        (row + (width_here,), BF16, vmem),
    ]
    n_copy = 2 * per * n_swap
    return pl.pallas_call(
        kernel,
        in_specs=[vmem] * 8 + [anywhere] * 7,
        out_specs=[space for _, _, space in outputs],
        out_shape=[jax.ShapeDtypeStruct(shape, dtype) for shape, dtype, _ in outputs],
        scratch_shapes=[
            pltpu.SemaphoreType.DMA((n_copy,)),
            pltpu.SemaphoreType.DMA((n_copy,)),
            pltpu.SemaphoreType.DMA((8,)),
            pltpu.SemaphoreType.DMA((11 * per,)),
            pltpu.VMEM((2, wide, tile), BF16),
            pltpu.VMEM((2, units, tile), BF16),
            pltpu.VMEM((2, tile, wide), BF16),
            pltpu.VMEM((2, tile, units), BF16),
            pltpu.VMEM(row + (width,), BF16),
            pltpu.VMEM(row + (wide,), BF16),
            pltpu.VMEM((2,) + row + (wide,), BF16),
            pltpu.VMEM(row + (width,), F32),
            pltpu.VMEM(row + (128,), F32),
            pltpu.VMEM(row + (width,), F32),
            pltpu.VMEM(row + (units,), BF16),
            pltpu.VMEM((loc, units), BF16),
            pltpu.VMEM((loc, wide), BF16),
            pltpu.VMEM((wide, loc), BF16),
            pltpu.VMEM((units, loc), BF16),
        ],
        compiler_params=pltpu.CompilerParams(
            collective_id=3, has_side_effects=True, vmem_limit_bytes=62 << 20
        ),
    )(
        picked, gain, shift_by, a_up, b_out, b_down, a_down, b_up,
        x_all, part_out, other_out, cot_all, out_x, up_x, down_x,
    )


def mm(left, right, nt, finish, tile, n_out=1, beside=None):
    rows, depth = left.shape
    columns = right.shape[0] if nt else right.shape[1]
    extra = [] if beside is None else [beside]
    sub = 128 if nt else tile

    def kernel(left_ref, right_ref, *refs):
        n_extra = len(extra)
        outs = refs[n_extra : n_extra + n_out]
        if nt:
            turned = refs[-1]

            @pl.when(pl.program_id(0) == 0)
            def _():
                turned[...] = left_ref[...].T

        for k in range(tile // sub):
            at = slice(k * sub, (k + 1) * sub)
            if nt:
                block = dot(right_ref[at, :], turned[...]).T
            else:
                block = dot(left_ref[...], right_ref[:, at])
            values = finish(block, *[ref[:, at] for ref in refs[:n_extra]])
            for ref, value in zip(outs, values):
                ref[:, at] = value

    part = pl.BlockSpec((rows, tile), lambda j: (0, j))
    out = pl.pallas_call(
        kernel,
        grid=(pl.cdiv(columns, tile),),
        in_specs=[
            pl.BlockSpec((rows, depth), lambda j: (0, 0)),
            pl.BlockSpec((tile, depth), lambda j: (j, 0))
            if nt
            else pl.BlockSpec((depth, tile), lambda j: (0, j)),
        ]
        + [part] * len(extra),
        out_specs=[part] * n_out,
        out_shape=[jax.ShapeDtypeStruct((rows, columns), BF16)] * n_out,
        scratch_shapes=[pltpu.VMEM((depth, rows), BF16)] if nt else [],
        compiler_params=pltpu.CompilerParams(vmem_limit_bytes=48 << 20),
        cost_estimate=pl.CostEstimate(
            flops=2 * rows * depth * columns,
            bytes_accessed=2 * (rows * depth + 2 * depth * columns + rows * columns * n_out),
            transcendentals=0,
        ),
    )(left, right, *extra)
    return out[0] if n_out == 1 else out


def compact(arrays, pairs, n_part):
    per, loc = arrays[0].shape[:2]
    sizes = [values[2] // n_part for _, values in pairs]
    total = sum(sizes)

    def kernel(*refs):
        out_ref = refs[-1]
        column = lax.broadcasted_iota(jnp.int32, (NR, RANK), 0)
        rank = lax.broadcasted_iota(jnp.int32, (NR, RANK), 1)
        used = jnp.where(lax.rem(column, RANK) == rank, 1.0, 0.0).astype(BF16)
        start = 0
        for (codes, values), size in zip(pairs, sizes):
            code = refs[codes[0]][0, :, codes[1] : codes[1] + codes[2]]
            value = refs[values[0]][0, :, values[1] : values[1] + values[2]]
            block = dot_tn(dot(code, used).astype(BF16), value).astype(BF16)
            for part in range(n_part):
                out_ref[part, :, start : start + size] = block[:, part * size : (part + 1) * size]
            start += size

    return pl.pallas_call(
        kernel,
        grid=(per,),
        in_specs=[pl.BlockSpec((1,) + x.shape[1:], lambda n: (n, 0, 0)) for x in arrays],
        out_specs=pl.BlockSpec((n_part, RANK, total), lambda n: (0, n, 0)),
        out_shape=jax.ShapeDtypeStruct((n_part, per * RANK, total), BF16),
        compiler_params=pltpu.CompilerParams(vmem_limit_bytes=48 << 20),
        cost_estimate=pl.CostEstimate(
            flops=2 * per * loc * RANK * total * n_part * 8,
            bytes_accessed=2 * per * loc * total * n_part,
            transcendentals=0,
        ),
    )(*arrays)


def combine(pieces, chosen, shapes):
    n_part = len(pieces)
    n_fsdp, rows, columns = pieces[0].shape
    flat = []
    for i, shape in enumerate(shapes):
        for lead in range(shape[0] if len(shape) == 3 else 1):
            flat.append((i, lead if len(shape) == 3 else None, shape[-2:]))

    def kernel(chosen_ref, *refs):
        piece_refs, outs = refs[:n_part], refs[n_part:]
        z, ct = lax.axis_index("fsdp"), lax.axis_index("ctx")
        for k, offset in enumerate(offsets(n_part)):
            part = flip(ct, offset)
            ordered = jnp.concatenate(
                [piece_refs[k][lax.rem(z - a + n_fsdp, n_fsdp)] for a in range(n_fsdp)], axis=0
            )
            start = 0
            for i, lead, (high, wide) in flat:
                out_ref = outs[i] if lead is None else outs[i].at[lead]
                tall = wide == NR and high != NR
                size = (high if tall else wide) // n_part
                block = ordered[:, start : start + size]
                at = pl.ds(pl.multiple_of(part * size, size), size)
                if tall:
                    out_ref[at, :] = dot_tn(block, chosen_ref[...])
                else:
                    out_ref[:, at] = dot_tn(chosen_ref[...], block)
                start += size

    return pl.pallas_call(
        kernel,
        in_specs=[pl.BlockSpec(memory_space=pltpu.VMEM)] * (1 + n_part),
        out_specs=[pl.BlockSpec(memory_space=pltpu.VMEM)] * len(shapes),
        out_shape=[jax.ShapeDtypeStruct(shape, F32) for shape in shapes],
        compiler_params=pltpu.CompilerParams(vmem_limit_bytes=48 << 20),
        cost_estimate=pl.CostEstimate(
            flops=2 * NR * n_fsdp * rows * columns * n_part,
            bytes_accessed=2 * n_fsdp * rows * columns * n_part + 4 * NR * columns * n_part,
            transcendentals=0,
        ),
    )(chosen, *pieces)


def as_low(block):
    return (block.astype(BF16),)


def after(value, *first):
    return lax.optimization_barrier((value,) + first)[0]


def gelu_both(pre):
    square = pre * pre
    bent = jnp.tanh(GELU_COEF * (pre + 0.044715 * square * pre))
    out = 0.5 * pre * (1.0 + bent)
    slope = 0.5 * (1.0 + bent) + 0.5 * pre * (1.0 - bent * bent) * GELU_COEF * (
        1.0 + 3.0 * 0.044715 * square
    )
    return out.astype(BF16), slope.astype(BF16)


def local(
    x_in,
    cotangent,
    lengths,
    adapter_ids,
    w_qkv,
    w_out,
    w_up,
    w_down,
    ln_gain,
    ln_bias,
    a_qkv,
    b_qkv,
    a_out,
    b_out,
    a_up,
    b_up,
    a_down,
    b_down,
):
    n_ctx, n_fsdp = lax.axis_size("ctx"), lax.axis_size("fsdp")
    z, ct = lax.axis_index("fsdp"), lax.axis_index("ctx")
    seqs, piece, width = x_in.shape
    per = seqs // n_fsdp
    loc = n_fsdp * piece
    heads_width = w_qkv.shape[2]
    n_group = GROUPS if per % GROUPS == 0 else 1
    g_per = per // n_group
    g_rows = g_per * loc

    def take(array, start, size, axis=0):
        return lax.dynamic_slice_in_dim(array, start, size, axis)

    def put(array, block, *starts):
        return lax.dynamic_update_slice(array, block, starts)

    def undeal(rows, group_out):
        rows = rows.reshape(g_per, n_fsdp, piece, width)
        out = []
        for step in range(n_fsdp):
            block = rows[:, step]
            out.append(block if step == 0 else shift(block, "fsdp", -step))
        return out

    units = w_up.shape[1]
    rows_shape = (per, n_fsdp, piece, width)
    zq, zu = w_qkv.shape[1], w_up.shape[0]

    def first_items(ins, outs, z):
        x_ref, w_ref = ins
        rows_ref, whole_ref = outs

        def deal(g):
            return Deal(lambda to: x_ref.at[to * per + g], lambda s: rows_ref.at[g, s])

        def weight(j):
            size = zq // n_ctx
            columns = pl.ds(j * heads_width, heads_width)
            return Weight(
                lambda c: w_ref.at[j, pl.ds(pl.multiple_of(c * size, size), size)],
                lambda o, c: whole_ref.at[
                    pl.ds(pl.multiple_of(o * zq + c * size, size), size), columns
                ],
            )

        stay = [(x_ref.at[z * per + g], rows_ref.at[g, 0]) for g in range(per)]
        for j in range(3):
            own = whole_ref.at[
                pl.ds(pl.multiple_of(z * zq, zq), zq), pl.ds(j * heads_width, heads_width)
            ]
            stay.append((w_ref.at[j], own))
        items = [weight(j) for j in range(3)] + [deal(g) for g in range(per)]
        return items, stay

    x_all, qkv_x = move(
        first_items,
        [Weight] * 3 + [Deal] * per,
        (x_in, w_qkv),
        (rows_shape, (width + 3 * NR, 3 * heads_width)),
        n_fsdp,
        n_ctx,
        ((piece, width),) * per + (w_qkv.shape[1:],) * 3,
        0,
        foot=(b_qkv, lambda outs: outs[1].at[pl.ds(width, 3 * NR)]),
    )

    a_in = a_qkv.transpose(1, 0, 2).reshape(width, 3 * NR)

    my_lengths = take(lengths, z * per, per)
    my_ids = take(adapter_ids, z * per, per)
    picked = (my_ids[:, None] == jnp.arange(NR)[None, :] // RANK).astype(F32)
    steps = lax.rem(z - jnp.arange(n_fsdp) + n_fsdp, n_fsdp)
    ctx_of = ct ^ jnp.array(offsets(n_ctx))
    key_pos = (
        (steps[None, :, None] * n_ctx + ctx_of[:, None, None]) * piece
        + jnp.arange(piece)[None, None, :]
    ).reshape(-1)
    bias_all = jnp.where(key_pos[None, :] < my_lengths[:, None], 0.0, -1e30).astype(F32)
    bias_all = jnp.broadcast_to(bias_all[:, :, None], bias_all.shape + (128,))

    pick_all = jnp.repeat(picked, loc, axis=0)
    x_flat = x_all.reshape(per * loc, width)
    adapt_all = (dot(x_flat, a_in) * jnp.concatenate([pick_all] * 3, axis=1)).astype(BF16)
    proj_all = mm(jnp.concatenate([x_flat, adapt_all], axis=1), qkv_x, False, as_low, 1024)
    kv_own = jnp.stack([proj_all[:, heads_width : 2 * heads_width], proj_all[:, 2 * heads_width :]])
    kv_own = kv_own.reshape(2, per, loc, heads_width)
    moved = forward_and_gather(
        proj_all[:, :heads_width].reshape(per, loc, heads_width),
        kv_own,
        bias_all,
        (cotangent, w_out, w_up, w_down),
        (a_out, b_up, a_down),
        n_fsdp,
        n_ctx,
    )
    kv_all = [kv_own] + list(moved[: n_ctx - 1])
    cot_all, out_x, up_x, down_x, context, log_total, part_out, other_out = moved[n_ctx - 1 :]

    groups = range(n_group)
    picks = [jnp.repeat(take(picked, g * g_per, g_per), loc, axis=0) for g in groups]
    part = [slice(g * g_rows, (g + 1) * g_rows) for g in groups]
    x_rows = [x_flat[part[g]] for g in groups]

    (wide_h, gelu_out, acts, wide_d, d_pre, dy1, wide_a, adapt_out, adapt_down, dadapt_up, d_context) = middle(
        x_all.reshape(per, loc, width),
        part_out,
        other_out,
        cot_all.reshape(per, loc, width),
        picked[:, None, :],
        ln_gain,
        ln_bias,
        (out_x, up_x, down_x),
        (a_up, b_out, b_down, a_down, b_up),
    )
    d_query, d_pair, activations = attend_back(
        proj_all[:, :heads_width].reshape(per, loc, heads_width),
        kv_own,
        kv_all[1:],
        bias_all,
        d_context,
        log_total,
        acts.reshape(per, n_fsdp, piece, width),
        n_fsdp,
        n_ctx,
    )
    d_query = d_query.reshape(per * loc, heads_width)
    d_pair = d_pair.reshape(2, per * loc, heads_width)

    def gathered(mine):
        blocks = [
            lax.dynamic_index_in_dim(mine, ct ^ offset, 0, False) for offset in offsets(n_ctx)
        ]
        own = fold(blocks, "ctx")
        got = jnp.stack([own] + [shift(own, "fsdp", step) for step in range(1, n_fsdp)])
        return spread([got], "ctx")

    early_in = after(
        (adapt_down, wide_d, gelu_out, wide_h, d_pre, dadapt_up, adapt_out, wide_a, context),
        d_query,
    )
    code, row, unit = (0, NR), (0, width), (0, units)
    tail = (width, NR)
    early_pairs = [
        ((0,) + code, (1,) + row),
        ((1,) + tail, (2,) + unit),
        ((3,) + tail, (4,) + unit),
        ((5,) + code, (3,) + row),
        ((6,) + code, (7,) + row),
        ((7,) + tail, (8, 0, heads_width)),
    ]
    early = gathered(compact(early_in, early_pairs, n_ctx))

    dy1_flat = dy1.reshape(per * loc, width)
    ins, dadapt_all = [], []
    d_proj = [
        jnp.concatenate([d_query[part[g]], d_pair[0, part[g]], d_pair[1, part[g]]], axis=1)
        for g in groups
    ]
    summed = both_in_turn([mm(d_proj[g], qkv_x, True, as_low, 640) for g in groups])
    for g in groups:
        pick3 = jnp.concatenate([picks[g]] * 3, axis=1)
        dadapt_in = (summed[g][:, width:] * pick3).astype(BF16)
        d_x = (dy1_flat[part[g]] + summed[g][:, :width] + dot_nt(dadapt_in, a_in)).astype(BF16)
        ins.append(undeal(d_x, g))
        dadapt_all.append(dadapt_in)
    late_in = (
        adapt_all.reshape(per, loc, 3 * NR),
        jnp.concatenate(dadapt_all, axis=0).reshape(per, loc, 3 * NR),
        jnp.concatenate(d_proj, axis=0).reshape(per, loc, 3 * heads_width),
        x_flat.reshape(per, loc, width),
    )
    late_pairs = [
        ((0, j * NR, NR), (2, j * heads_width, heads_width)) for j in range(3)
    ] + [((1, j * NR, NR), (3,) + row) for j in range(3)]
    late = gathered(compact(late_in, late_pairs, n_ctx))

    def assemble(parts):
        full = jnp.zeros((seqs, piece, width), BF16)
        for group, blocks in enumerate(parts):
            for step, block in enumerate(blocks):
                owner = lax.rem(z + step, n_fsdp)
                full = put(full, block, owner * per + group * g_per, 0, 0)
        return full

    codes = (adapter_ids[:, None] * RANK + jnp.arange(RANK)[None, :]).reshape(-1)
    chosen = (codes[:, None] == jnp.arange(NR)[None, :]).astype(BF16)
    early = after(early, summed[-1])
    e = combine(
        early,
        chosen,
        [(NR, width), (units, NR), (NR, units), (width, NR), (NR, width), (heads_width, NR)],
    )
    l = combine(late, chosen, [(3, NR, heads_width), (3, width, NR)])
    return activations, assemble(ins), l[1], l[0], e[5], e[4], e[3], e[2], e[1], e[0]


def solution(mesh):
    rows = P(None, ("fsdp", "ctx"), None)
    return jax.shard_map(
        local,
        mesh=mesh,
        in_specs=(
            rows,
            rows,
            P(),
            P(),
            P(None, "fsdp", "tp"),
            P("tp", "fsdp"),
            P("fsdp", "tp"),
            P("tp", "fsdp"),
            P(),
            P(),
            P(),
            P(None, None, "tp"),
            P("tp", None),
            P(),
            P(),
            P(None, "tp"),
            P("tp", None),
            P(),
        ),
        out_specs=(
            rows,
            rows,
            P(),
            P(None, None, "tp"),
            P("tp", None),
            P(),
            P(),
            P(None, "tp"),
            P("tp", None),
            P(),
        ),
        check_vma=False,
    )
```

```python
import math

import jax
import jax.numpy as jnp
from jax import lax
from jax.experimental import pallas as pl
from jax.experimental.pallas import tpu as pltpu
from jax.sharding import PartitionSpec as P

HEAD_DIM = 128
RANK = 16
ADAPTERS = 8
NR = RANK * ADAPTERS
NORM_EPS = 1e-06
GELU_COEF = 0.7978845608028654
SCALE = 1.0 / math.sqrt(HEAD_DIM)
GROUPS = 2
F32 = jnp.float32
BF16 = jnp.bfloat16


def dot(left, right):
    return jnp.dot(left, right, preferred_element_type=F32)


def dot_nt(left, right):
    return lax.dot_general(left, right, (((1,), (1,)), ((), ())), preferred_element_type=F32)


def dot_tn(left, right):
    return lax.dot_general(left, right, (((0,), (0,)), ((), ())), preferred_element_type=F32)


def masks_of(n):
    out = []
    while n > 1:
        n //= 2
        out.append(n)
    return out


def offsets(n):
    out = [0]
    for mask in masks_of(n):
        out = out + [o ^ mask for o in out]
    return out


def attend_head(query, keys, values, biases):
    scores = [dot_nt(k, query) * SCALE + bias for k, bias in zip(keys, biases)]
    top = scores[0].max(axis=0, keepdims=True)
    for s in scores[1:]:
        top = jnp.maximum(top, s.max(axis=0, keepdims=True))
    total = jnp.zeros_like(top)
    mixed = None
    for s, v in zip(scores, values):
        probs = jnp.exp(s - top)
        total = total + probs.sum(axis=0, keepdims=True)
        term = dot_tn(v, probs.astype(BF16))
        mixed = term if mixed is None else mixed + term
    return (mixed / total).T.astype(BF16), top + jnp.log(total)


def attend_back_head(query, grad, log_total, keys, values, biases):
    probs, dprobs, dvalues = [], [], []
    delta = jnp.zeros_like(log_total)
    for k, v, bias in zip(keys, values, biases):
        p = jnp.exp(dot_nt(k, query) * SCALE + bias - log_total)
        dp = dot_nt(v, grad)
        dvalues.append(dot(p.astype(BF16), grad).astype(BF16))
        delta = delta + (p * dp).sum(axis=0, keepdims=True)
        probs.append(p)
        dprobs.append(dp)
    dquery, dkeys = None, []
    for k, p, dp in zip(keys, probs, dprobs):
        ds = (p * (dp - delta)).astype(BF16)
        dkeys.append((dot(ds, query) * SCALE).astype(BF16))
        term = dot_tn(k, ds)
        dquery = term if dquery is None else dquery + term
    return (dquery * SCALE).T.astype(BF16), dkeys, dvalues


def ds(start, size):
    return pl.ds(pl.multiple_of(start, size), size)


def flip(ct, offset):
    mask = 1
    while mask <= offset:
        if offset & mask:
            ct = ct + mask - 2 * mask * lax.rem(ct // mask, 2)
        mask *= 2
    return ct


class Weight:
    def __init__(self, shard_at, whole_at, own=None):
        self.shard_at, self.whole_at, self.own = shard_at, whole_at, own


class Deal:
    def __init__(self, source_at, rows_at):
        self.source_at, self.rows_at = source_at, rows_at


class Pair:
    def __init__(self, slot_at):
        self.slot_at = slot_at


class Mover:
    def __init__(self, n_fsdp, n_ctx, send, recv):
        self.n_fsdp, self.n_ctx = n_fsdp, n_ctx
        self.z, self.ct = lax.axis_index("fsdp"), lax.axis_index("ctx")
        self.send, self.recv = send, recv
        self.used = 0
        self.open = []
        self.masks = masks_of(n_ctx)
        self.offsets = offsets(n_ctx)
        self.came, self.waiting = {}, {}

    def greet(self, tp=False):
        barrier = pltpu.get_barrier_semaphore()
        others = [{"fsdp": lax.rem(self.z + s, self.n_fsdp)} for s in range(1, self.n_fsdp)]
        others += [{"ctx": flip(self.ct, mask)} for mask in self.masks]
        if tp:
            others.append({"tp": 1 - lax.axis_index("tp")})
        for other in others:
            pl.semaphore_signal(
                barrier, inc=1, device_id=other, device_id_type=pl.DeviceIdType.MESH
            )
        pl.semaphore_wait(barrier, len(others))

    def copy(self, source, target, device, at=None):
        if at is None:
            at = self.used
            self.used += 1
        return pltpu.make_async_remote_copy(
            src_ref=source,
            dst_ref=target,
            send_sem=self.send.at[at],
            recv_sem=self.recv.at[at],
            device_id=device,
            device_id_type=pl.DeviceIdType.MESH,
        )

    def go(self, source, target, device):
        copy = self.copy(source, target, device)
        copy.start()
        self.open.append((None, copy))
        return copy

    def along(self, item, owner, right, ok, source, slot):
        target = item.whole_at(owner, self.ct)
        device = {"fsdp": lax.rem(self.z + (1 if right else self.n_fsdp - 1), self.n_fsdp)}
        copy = self.copy(source, target, device, self.came[item] + slot - 1)
        pl.when(ok)(copy.start)
        self.open.append((ok, copy))

    def begin(self, item):
        if isinstance(item, Pair):
            self.waiting[item] = [[] for _ in self.masks]
            self.cast(item, item.slot_at, lambda k, level: item.slot_at(k + 2**level), 0, 0)
            return
        if isinstance(item, Weight):
            self.came[item] = self.used
            self.used += self.n_fsdp - 1
            source = item.shard_at(self.ct)
            self.along(item, self.z, True, self.z < self.n_fsdp - 1, source, 1)
            self.along(item, self.z, False, self.z > 0, source, self.n_fsdp - 1)
            return
        self.came[item] = [
            self.go(
                item.source_at(lax.rem(self.z + s, self.n_fsdp)),
                item.rows_at(s),
                {"fsdp": lax.rem(self.z + s, self.n_fsdp)},
            )
            for s in range(1, self.n_fsdp)
        ]

    def cast(self, item, source_at, target_at, k, first):
        for level in range(first, len(self.masks)):
            device = {"ctx": flip(self.ct, self.masks[level])}
            copy = self.go(source_at(k), target_at(k, level), device)
            self.waiting[item][level].append((copy, k + 2**level, source_at, target_at))

    def relay(self, item):
        if isinstance(item, Pair):
            return
        if isinstance(item, Deal):
            for copy in self.came[item]:
                copy.wait_recv()
            return
        self.waiting[item] = [[] for _ in self.masks]
        n = self.n_fsdp
        if item.own is not None:

            def mine(k):
                return item.own if k == 0 else item.whole_at(self.z, flip(self.ct, self.offsets[k]))

            def lands(k, level):
                return item.whole_at(self.z, flip(self.ct, self.offsets[k]))

            self.cast(item, mine, lands, 0, 0)
        for i in range(n - 1):
            s = i // 2 + 1 if i % 2 == 0 else n - 1 - i // 2
            owner = lax.rem(self.z - s + n, n)
            here = item.whole_at(owner, self.ct)
            self.copy(here, here, {"fsdp": owner}, self.came[item] + s - 1).wait_recv()
            if s < n - 1:
                ok = (self.z >= s) & (self.z < n - 1)
                self.along(item, owner, True, ok, here, s + 1)
            if s > 1:
                ok = (self.z < s) & (self.z > 0)
                self.along(item, owner, False, ok, here, s - 1)

            def at(k, owner=owner):
                return item.whole_at(owner, flip(self.ct, self.offsets[k]))

            self.cast(item, at, lambda k, level, at=at: at(k), 0, 0)

    def finish(self, item, level):
        if isinstance(item, Deal):
            return
        for copy, k, source_at, target_at in self.waiting[item][level]:
            copy.wait_recv()
            self.cast(item, source_at, target_at, k, level + 1)

    def close(self):
        for ok, copy in self.open:
            if ok is None:
                copy.wait_send()
            else:
                pl.when(ok)(copy.wait_send)


def copies_of(items, n_fsdp, n_ctx):
    total = 0
    for item in items:
        total += {Weight: (n_fsdp - 1) * n_ctx, Deal: n_fsdp - 1, Pair: n_ctx - 1}[item]
    return total


def keep(stay, room, sems):
    out = []
    for k, (source, target) in enumerate(stay):
        first = pltpu.make_async_copy(source, room[k], sems.at[2 * k])
        first.start()
        out.append((first, pltpu.make_async_copy(room[k], target, sems.at[2 * k + 1])))
    return out


def move(make, kinds, inputs, outputs, n_fsdp, n_ctx, local_shapes, ident, ahead=2, foot=None):
    n_in = len(inputs)
    n_copy = copies_of(kinds, n_fsdp, n_ctx)

    def kernel(*refs):
        ins, outs = refs[:n_in], refs[n_in : n_in + len(outputs)]
        send, recv, here = refs[n_in + len(outputs) : n_in + len(outputs) + 3]
        room = refs[n_in + len(outputs) + 3 :]
        if foot is not None:
            blocks_ref, ins = ins[-1], ins[:-1]
            strip = room[-1]
        mover = Mover(n_fsdp, n_ctx, send, recv)
        items, stay = make(ins, outs, mover.z)
        mover.greet()
        for item in items[:ahead]:
            mover.begin(item)
        kept = keep(stay, room, here)
        levels = len(mover.masks)
        for i in range(len(items) + levels):
            if i < len(items):
                mover.relay(items[i])
                if i + ahead < len(items):
                    mover.begin(items[i + ahead])
            if i == 0 and foot is not None:
                strip[...] = jnp.zeros_like(strip)
                high, wide = blocks_ref.shape[1:]
                for j in range(blocks_ref.shape[0]):
                    strip[j * high : (j + 1) * high, j * wide : (j + 1) * wide] = blocks_ref[j]
                set_foot = pltpu.make_async_copy(strip, foot[1](outs), here.at[2 * len(local_shapes)])
                set_foot.start()
                kept.append((None, set_foot))
            if i == 0:
                for first, second in kept:
                    if first is not None:
                        first.wait()
                        second.start()
            for level in range(levels):
                if 0 <= i - 1 - level < len(items):
                    mover.finish(items[i - 1 - level], level)
        for _, second in kept:
            second.wait()
        mover.close()

    spaces = [pl.BlockSpec(memory_space=pl.ANY)] * n_in
    room_shapes = list(local_shapes)
    if foot is not None:
        blocks = foot[0]
        inputs = inputs + (blocks,)
        n_in += 1
        spaces.append(pl.BlockSpec(memory_space=pltpu.VMEM))
        room_shapes.append((blocks.shape[0] * blocks.shape[1], blocks.shape[0] * blocks.shape[2]))
    return pl.pallas_call(
        kernel,
        in_specs=spaces,
        out_specs=[pl.BlockSpec(memory_space=pl.ANY)] * len(outputs),
        out_shape=[jax.ShapeDtypeStruct(shape, BF16) for shape in outputs],
        scratch_shapes=[
            pltpu.SemaphoreType.DMA((n_copy,)),
            pltpu.SemaphoreType.DMA((n_copy,)),
            pltpu.SemaphoreType.DMA((2 * len(local_shapes) + 1,)),
        ]
        + [pltpu.VMEM(shape, BF16) for shape in room_shapes],
        compiler_params=pltpu.CompilerParams(
            collective_id=ident, has_side_effects=True, vmem_limit_bytes=32 << 20
        ),
    )(*inputs)


def forward_and_gather(query, kv_own, bias, shards, maps, n_fsdp, n_ctx):
    per, loc, width_here = query.shape
    cot, w_out, w_up, w_down = shards
    piece, width = cot.shape[1:]
    heads, units = width_here // HEAD_DIM, w_up.shape[1]
    zu, zo = w_up.shape[0], w_out.shape[1]
    so, su, sd = w_out.shape[0] // n_ctx, zu // n_ctx, w_down.shape[0] // n_ctx
    wide = width + NR
    stay_shapes = [(piece, width)] * per + [x.shape for x in (w_out, w_up, w_down) + maps]
    n_stay = len(stay_shapes)
    halves = 2
    n_copy = (n_fsdp - 1) * n_ctx * (1 + 2 * halves) + per * (n_fsdp - 1 + n_ctx - 1 + 1)

    def kernel(*refs):
        q_ref, bias_ref, kv_ref, cot_ref, wo_ref, wu_ref, wd_ref, ao_ref, bu_ref, ad_ref = refs[:10]
        slots = refs[10 : 9 + n_ctx]
        rows_ref, out_ref, up_ref, down_ref, ctx_ref, log_ref, part_ref, other_ref = refs[
            9 + n_ctx : 17 + n_ctx
        ]
        send, recv, here, load, kv_room, out_room = refs[17 + n_ctx : 23 + n_ctx]
        room = refs[23 + n_ctx :]
        mover = Mover(n_fsdp, n_ctx, send, recv)
        z = mover.z

        def deal(g):
            return Deal(lambda to: cot_ref.at[to * per + g], lambda s: rows_ref.at[g, s])

        def pair(g):
            return Pair(lambda k: kv_ref.at[:, g] if k == 0 else slots[k - 1].at[:, g])

        out_item = Weight(
            lambda c: wo_ref.at[ds(c * so, so)],
            lambda o, c: out_ref.at[ds(c * so, so), ds(o * zo, zo)],
        )

        def up_item(h):
            columns = pl.ds(h * (units // halves), units // halves)
            return Weight(
                lambda c: wu_ref.at[ds(c * su, su), columns],
                lambda o, c: up_ref.at[ds(o * zu + c * su, su), columns],
            )

        def down_item(h):
            size = sd // halves
            return Weight(
                lambda c: wd_ref.at[ds(c * sd + h * size, size)],
                lambda o, c: down_ref.at[ds(c * sd + h * size, size), ds(o * zo, zo)],
            )

        pairs = [pair(g) for g in range(per)]
        items = [out_item] + [up_item(h) for h in range(halves)]
        items += [down_item(h) for h in range(halves)] + [deal(g) for g in range(per)]
        stay = [(cot_ref.at[z * per + g], rows_ref.at[g, 0]) for g in range(per)]
        stay += [
            (wo_ref, out_ref.at[:, ds(z * zo, zo)]),
            (wu_ref, up_ref.at[ds(z * zu, zu)]),
            (wd_ref, down_ref.at[:, ds(z * zo, zo)]),
            (ao_ref, out_ref.at[:, pl.ds(width, NR)]),
            (bu_ref, up_ref.at[pl.ds(width, NR)]),
            (ad_ref, down_ref.at[:, pl.ds(width, NR)]),
        ]

        def attend(g):
            for level in range(len(mover.masks)):
                mover.finish(pairs[g], level)
            loads = []
            for k in range(n_ctx):
                copy = pltpu.make_async_copy(pairs[g].slot_at(k), kv_room.at[k], load.at[k])
                copy.start()
                loads.append(copy)
            for copy in loads:
                copy.wait()

            def one(h, carry):
                at = ds(h * HEAD_DIM, HEAD_DIM)
                biases = []
                for k in range(n_ctx):
                    block = bias_ref[g, k * loc : (k + 1) * loc, :]
                    biases.append(jnp.concatenate([block] * (loc // 128), axis=1))
                context, log = attend_head(
                    q_ref[g, :, at],
                    [kv_room[k, 0, :, at] for k in range(n_ctx)],
                    [kv_room[k, 1, :, at] for k in range(n_ctx)],
                    biases,
                )
                ctx_ref[g, :, at] = context
                log_ref[g, h] = log
                return carry

            lax.fori_loop(0, heads, one, 0)

        def project():
            copy = pltpu.make_async_copy(out_ref, out_room, load.at[n_ctx])
            copy.start()
            copy.wait()
            for g in range(per):
                for start in range(0, wide, 1024):
                    at = slice(start, min(start + 1024, wide))
                    part_ref[g, :, at] = dot(ctx_ref[g], out_room[:, at]).astype(BF16)
                swapped.append(
                    mover.go(
                        part_ref.at[g], other_ref.at[g], {"tp": 1 - lax.axis_index("tp")}
                    )
                )

        swapped = []
        tasks = {i: (lambda g=i: attend(g)) for i in range(per)}
        tasks[per] = project
        mover.greet(tp=True)
        for item in pairs + items[:2]:
            mover.begin(item)
        kept = keep(stay, room, here)
        levels = len(mover.masks)
        for i in range(len(items) + levels):
            if i < len(items):
                mover.relay(items[i])
                if i + 2 < len(items):
                    mover.begin(items[i + 2])
            if i == 0:
                for first, second in kept:
                    first.wait()
                    second.start()
            for level in range(levels):
                if 0 <= i - 1 - level < len(items):
                    mover.finish(items[i - 1 - level], level)
            if i == per:
                for _, second in kept:
                    second.wait()
            if i in tasks:
                tasks[i]()
        for copy in swapped:
            copy.wait_recv()
        mover.close()

    row = (per, loc, width_here)
    vmem, anywhere = pl.BlockSpec(memory_space=pltpu.VMEM), pl.BlockSpec(memory_space=pl.ANY)
    outputs = [(kv_own.shape, BF16, anywhere)] * (n_ctx - 1) + [
        ((per, n_fsdp, piece, width), BF16, anywhere),
        ((width_here, wide), BF16, anywhere),
        ((wide, units), BF16, anywhere),
        ((units, wide), BF16, anywhere),
        (row, BF16, vmem),
        ((per, heads, 1, loc), F32, vmem),
        ((per, loc, wide), BF16, vmem),
        ((per, loc, wide), BF16, anywhere),
    ]
    return pl.pallas_call(
        kernel,
        in_specs=[vmem, vmem] + [anywhere] * 8,
        out_specs=[space for _, _, space in outputs],
        out_shape=[jax.ShapeDtypeStruct(shape, dtype) for shape, dtype, _ in outputs],
        scratch_shapes=[
            pltpu.SemaphoreType.DMA((n_copy,)),
            pltpu.SemaphoreType.DMA((n_copy,)),
            pltpu.SemaphoreType.DMA((2 * n_stay,)),
            pltpu.SemaphoreType.DMA((n_ctx + 1,)),
            pltpu.VMEM((n_ctx, 2, loc, width_here), BF16),
            pltpu.VMEM((width_here, wide), BF16),
        ]
        + [pltpu.VMEM(shape, BF16) for shape in stay_shapes],
        compiler_params=pltpu.CompilerParams(
            collective_id=1, has_side_effects=True, vmem_limit_bytes=50 << 20
        ),
    )(query, bias, kv_own, cot, w_out, w_up, w_down, *maps)


def attend_back(query, kv_own, slots, bias, grad, log_total, acts, n_fsdp, n_ctx):
    per, loc, width_here = query.shape
    piece, width = acts.shape[2:]
    heads = width_here // HEAD_DIM
    cuts = 4
    high = heads // cuts
    columns = high * HEAD_DIM
    masks = masks_of(n_ctx)
    units = [(g, c) for g in range(per) for c in range(cuts)]
    n_copy = per * (n_fsdp - 1) + len(units) * (n_ctx - 1)

    def kernel(*refs):
        q_ref, bias_ref, g_ref, log_ref, acts_ref, kv_ref = refs[:6]
        slot_refs = refs[6 : 5 + n_ctx]
        dq_ref, dkv_ref, out_ref = refs[5 + n_ctx : 8 + n_ctx]
        send, recv, load, kv_room, own, came, act_room = refs[8 + n_ctx :]
        mover = Mover(n_fsdp, n_ctx, send, recv)
        z, ct = mover.z, mover.ct
        loads = []
        for g in range(per):
            loads.append([])
            for k in range(n_ctx):
                source = kv_ref if k == 0 else slot_refs[k - 1]
                copy = pltpu.make_async_copy(
                    source.at[:, g], kv_room.at[g, k], load.at[g * n_ctx + k]
                )
                copy.start()
                loads[g].append(copy)
        kept = []
        for g in range(per):
            at = per * n_ctx + 2 * g
            first = pltpu.make_async_copy(acts_ref.at[g, 0], act_room.at[g], load.at[at])
            first.start()
            second = pltpu.make_async_copy(
                act_room.at[g], out_ref.at[z * per + g], load.at[at + 1]
            )
            kept.append((first, second))
        mover.greet()
        dealt = []
        for g in range(per):
            for s in range(1, n_fsdp):
                to = lax.rem(z - s + n_fsdp, n_fsdp)
                dealt.append(
                    mover.go(acts_ref.at[g, s], out_ref.at[z * per + g], {"fsdp": to})
                )
        flying = {}

        def compute(u):
            g, c = units[u]
            if c == 0:
                for copy in loads[g]:
                    copy.wait()

            def one(h, carry):
                at = ds(c * columns + h * HEAD_DIM, HEAD_DIM)
                to = ds(h * HEAD_DIM, HEAD_DIM)
                biases = []
                for k in range(n_ctx):
                    block = bias_ref[g, k * loc : (k + 1) * loc, :]
                    biases.append(jnp.concatenate([block] * (loc // 128), axis=1))
                dquery, dkeys, dvalues = attend_back_head(
                    q_ref[g, :, at],
                    g_ref[g, :, at],
                    log_ref[g, c * high + h],
                    [kv_room[g, k, 0, :, at] for k in range(n_ctx)],
                    [kv_room[g, k, 1, :, at] for k in range(n_ctx)],
                    biases,
                )
                dq_ref[g, :, at] = dquery
                for k in range(n_ctx):
                    own[u, k, 0, :, to] = dkeys[k]
                    own[u, k, 1, :, to] = dvalues[k]
                return carry

            lax.fori_loop(0, high, one, 0)

        def hand(u, level):
            half = 2**level
            device = {"ctx": flip(ct, masks[level])}
            flying[u, level] = [
                mover.go(own.at[u, half + i], came.at[u, half - 1 + i], device) for i in range(half)
            ]

        def take_in(u, level):
            half = 2**level
            for i, copy in enumerate(flying[u, level]):
                copy.wait_recv()
                for j in range(2):
                    total = own[u, i, j].astype(F32) + came[u, half - 1 + i, j].astype(F32)
                    if level:
                        own[u, i, j] = total.astype(BF16)
                    else:
                        g, c = units[u]
                        dkv_ref[j, g, :, c * columns : (c + 1) * columns] = total.astype(BF16)

        last = len(masks) - 1
        for t in range(len(units) + last + 1):
            if t < len(units):
                compute(t)
                hand(t, last)
            if t == 0:
                for first, second in kept:
                    first.wait()
                    second.start()
            for k in range(last + 1):
                u, level = t - 1 - k, last - k
                if 0 <= u < len(units):
                    take_in(u, level)
                    if level:
                        hand(u, level - 1)
        for _, second in kept:
            second.wait()
        for copy in dealt:
            copy.wait_recv()
        mover.close()

    vmem, anywhere = pl.BlockSpec(memory_space=pltpu.VMEM), pl.BlockSpec(memory_space=pl.ANY)
    return pl.pallas_call(
        kernel,
        in_specs=[vmem] * 4 + [anywhere] * (1 + n_ctx),
        out_specs=[vmem, vmem, anywhere],
        out_shape=[
            jax.ShapeDtypeStruct(query.shape, BF16),
            jax.ShapeDtypeStruct(kv_own.shape, BF16),
            jax.ShapeDtypeStruct((per * n_fsdp, piece, width), BF16),
        ],
        scratch_shapes=[
            pltpu.SemaphoreType.DMA((n_copy,)),
            pltpu.SemaphoreType.DMA((n_copy,)),
            pltpu.SemaphoreType.DMA((per * (n_ctx + 2),)),
            pltpu.VMEM((per, n_ctx, 2, loc, width_here), BF16),
            pltpu.VMEM((len(units), n_ctx, 2, loc, columns), BF16),
            pltpu.VMEM((len(units), n_ctx - 1, 2, loc, columns), BF16),
            pltpu.VMEM((per, piece, width), BF16),
        ],
        compiler_params=pltpu.CompilerParams(
            collective_id=2, has_side_effects=True, vmem_limit_bytes=56 << 20
        ),
    )(query, bias, grad, log_total, acts, kv_own, *slots)


class Ring:
    def __init__(self, room, sems, at, tile_at):
        self.room, self.sems, self.at, self.tile_at = room, sems, at, tile_at

    def copy(self, t):
        slot = lax.rem(t, 2)
        return pltpu.make_async_copy(
            self.tile_at(t), self.room.at[slot], self.sems.at[self.at + slot]
        )

    def prefetch(self):
        self.copy(0).start()
        self.copy(1).start()

    def run(self, n, body):
        def step(t, carry):
            self.copy(t).wait()
            body(t, self.room.at[lax.rem(t, 2)])

            @pl.when(t + 2 < n)
            def _():
                self.copy(t + 2).start()

            return carry

        lax.fori_loop(0, n, step, 0)


def norm_parts(values):
    center = values - jnp.mean(values, axis=-1, keepdims=True)
    rstd = lax.rsqrt(jnp.mean(center * center, axis=-1, keepdims=True) + NORM_EPS)
    return center * rstd, rstd


def norm_back(hat, rstd, dhat):
    first = jnp.mean(dhat, axis=-1, keepdims=True)
    second = jnp.mean(dhat * hat, axis=-1, keepdims=True)
    return rstd * (dhat - first - hat * second)


def gelu_both(pre):
    square = pre * pre
    bent = jnp.tanh(GELU_COEF * (pre + 0.044715 * square * pre))
    out = 0.5 * pre * (1.0 + bent)
    slope = 0.5 * (1.0 + bent) + 0.5 * pre * (1.0 - bent * bent) * GELU_COEF * (
        1.0 + 3.0 * 0.044715 * square
    )
    return out.astype(BF16), slope.astype(BF16)


def middle(x_all, part_out, other_out, cot_all, picked, gain, shift_by, weights, maps):
    per, loc, width = x_all.shape
    out_x, up_x, down_x = weights
    a_up, b_out, b_down, a_down, b_up = maps
    wide, units = up_x.shape
    width_here = out_x.shape[0]
    tile = 512
    chunk = 32
    n_wide = width // tile
    n_swap = n_wide + 1

    def kernel(*refs):
        pick_ref, gain_ref, shift_ref, a_up_ref, b_out_ref, b_down_ref, a_down_ref, b_up_ref = refs[:8]
        x_ref, first_ref, second_ref, cot_ref, out_ref, up_ref, down_ref = refs[8:15]
        h_out, gelu_out, acts_out, dd_out, dpre_out, dy1_out, da_out = refs[15:22]
        adapt_out_ref, adapt_down_ref, dadapt_up_ref, ctx_ref = refs[22:26]
        (send, recv, ring_sem, sems) = refs[26:30]
        (up_room, down_room, down_rows, up_rows) = refs[30:34]
        (stage, part, got, hat1, rstd1, keep32, slope, gelu, wide_v, turned, dpre_t) = refs[34:]
        partner = {"tp": 1 - lax.axis_index("tp")}

        up = Ring(up_room, ring_sem, 0, lambda t: up_ref.at[:, ds(t * tile, tile)])
        down = Ring(down_room, ring_sem, 2, lambda t: down_ref.at[:, ds(t * tile, tile)])
        down_r = Ring(down_rows, ring_sem, 4, lambda t: down_ref.at[ds(t * tile, tile)])
        up_r = Ring(up_rows, ring_sem, 6, lambda t: up_ref.at[ds(t * tile, tile)])
        out_r = Ring(down_rows, ring_sem, 4, lambda t: out_ref.at[ds(t * tile, tile)])

        busy = {}
        used = [0]

        def move(source, target, key):
            copy = pltpu.make_async_copy(source, target, sems.at[used[0]])
            used[0] += 1
            copy.start()
            busy.setdefault(key, []).append(copy)

        def free(*keys):
            for key in keys:
                for copy in busy.pop(key, []):
                    copy.wait()

        def swap_copy(turn, g, t, size):
            at = ds(t * tile, size)
            sem = (turn * per + g) * n_swap + t
            return pltpu.make_async_remote_copy(
                src_ref=part.at[g, :, at],
                dst_ref=got.at[turn, g, :, at],
                send_sem=send.at[sem],
                recv_sem=recv.at[sem],
                device_id=partner,
                device_id_type=pl.DeviceIdType.MESH,
            )

        def swapped(turn, g):
            for t in range(n_swap):
                copy = swap_copy(turn, g, t, tile if t < n_wide else NR)
                copy.wait_recv()
                copy.wait_send()

        def by_rows(body):
            def step(r, carry):
                body(pl.ds(pl.multiple_of(r * chunk, chunk), chunk))
                return carry

            lax.fori_loop(0, loc // chunk, step, 0)

        barrier = pltpu.get_barrier_semaphore()
        pl.semaphore_signal(
            barrier, inc=1, device_id=partner, device_id_type=pl.DeviceIdType.MESH
        )
        for g in range(per):
            move(x_ref.at[g], stage.at[g], ("stage", g))
            move(first_ref.at[g], part.at[g], ("part", g))
            move(second_ref.at[g], slope.at[g, :, pl.ds(0, wide)], ("slope", g))
        up.prefetch()
        down.prefetch()
        pl.semaphore_wait(barrier, 1)

        for g in range(per):
            free(("stage", g), ("part", g), ("slope", g), "wide", "gelu")
            pick = pick_ref[g]

            def first_norm(rows, g=g, pick=pick):
                total = part[g, rows, :].astype(F32) + slope[g, rows, :wide].astype(F32)
                code = (total[:, width:] * pick).astype(BF16)
                adapt_out_ref[g, rows, :] = code
                y1 = stage[g, rows, :].astype(F32) + total[:, :width] + dot(code, b_out_ref[...])
                hat, rstd = norm_parts(y1)
                hat1[g, rows, :] = hat
                rstd1[g, rows, :] = jnp.broadcast_to(rstd, (chunk, 128))
                low = (hat * gain_ref[0:1, :] + shift_ref[0:1, :]).astype(BF16)
                wide_v[rows, :width] = low
                wide_v[rows, width:] = (dot(low, a_up_ref[...]) * pick).astype(BF16)

            by_rows(first_norm)
            move(wide_v, h_out.at[g], "wide")
            move(cot_ref.at[g], stage.at[g], ("stage", g))

            def up_tile(t, room, g=g):
                at = ds(t * tile, tile)
                value, factor = gelu_both(dot(wide_v[...], room[...]))
                gelu[:, at] = value
                slope[g, :, at] = factor

            up.run(units // tile, up_tile)
            if g + 1 < per:
                up.prefetch()
            else:
                down_r.prefetch()
            move(gelu, gelu_out.at[g], "gelu")

            def down_tile(t, room, g=g):
                part[g, :, ds(t * tile, tile)] = dot(gelu[...], room[...]).astype(BF16)
                swap_copy(0, g, t, tile).start()

            down.run(n_wide, down_tile)
            if g + 1 < per:
                down.prefetch()
            else:
                up_r.prefetch()
            part[g, :, width:] = dot(gelu[...], a_down_ref[...]).astype(BF16)
            swap_copy(0, g, n_wide, NR).start()

        for g in range(per):
            swapped(0, g)
            free(("stage", g), "wide")
            pick = pick_ref[g]

            def second_norm(rows, g=g, pick=pick):
                total = part[g, rows, :].astype(F32) + got[0, g, rows, :].astype(F32)
                code = (total[:, width:] * pick).astype(BF16)
                adapt_down_ref[g, rows, :] = code
                hidden = hat1[g, rows, :] * gain_ref[0:1, :] + shift_ref[0:1, :]
                hat, rstd = norm_parts(hidden + total[:, :width] + dot(code, b_down_ref[...]))
                part[g, rows, :width] = (hat * gain_ref[1:2, :] + shift_ref[1:2, :]).astype(BF16)
                dy2 = norm_back(hat, rstd, stage[g, rows, :].astype(F32) * gain_ref[1:2, :])
                keep32[g, rows, :] = dy2
                low = dy2.astype(BF16)
                wide_v[rows, :width] = low
                wide_v[rows, width:] = (dot_nt(low, b_down_ref[...]) * pick).astype(BF16)

            by_rows(second_norm)
            move(part.at[g, :, pl.ds(0, width)], acts_out.at[g], ("part", g))
            move(wide_v, dd_out.at[g], "wide")
            turned[...] = wide_v[...].T

            def down_back(t, room, g=g):
                at = ds(t * tile, tile)
                block = dot(room[...], turned[...]).T
                low = (block * slope[g, :, at].astype(F32)).astype(BF16)
                slope[g, :, at] = low
                dpre_t[at, :] = low.T

            down_r.run(units // tile, down_back)
            (down_r if g + 1 < per else out_r).prefetch()
            move(slope.at[g], dpre_out.at[g], ("slope", g))
            free(("part", g))

            def up_back(t, room, g=g):
                part[g, :, ds(t * tile, tile)] = dot(room[...], dpre_t[...]).T.astype(BF16)
                swap_copy(1, g, t, tile).start()

            up_r.run(n_wide, up_back)
            if g + 1 < per:
                up_r.prefetch()
            part[g, :, width:] = dot(b_up_ref[...], dpre_t[...]).T.astype(BF16)
            swap_copy(1, g, n_wide, NR).start()

        for g in range(per):
            swapped(1, g)
            free("wide")
            pick = pick_ref[g]

            def first_back(rows, g=g, pick=pick):
                total = part[g, rows, :].astype(F32) + got[1, g, rows, :].astype(F32)
                code = (total[:, width:] * pick).astype(BF16)
                dadapt_up_ref[g, rows, :] = code
                dh1 = keep32[g, rows, :] + total[:, :width] + dot_nt(code, a_up_ref[...])
                rstd = rstd1[g, rows, 0:1]
                dy1 = norm_back(hat1[g, rows, :], rstd, dh1 * gain_ref[0:1, :])
                keep32[g, rows, :] = dy1
                low = dy1.astype(BF16)
                wide_v[rows, :width] = low
                wide_v[rows, width:] = (dot_nt(low, b_out_ref[...]) * pick).astype(BF16)

            by_rows(first_back)
            move(keep32.at[g], dy1_out.at[g], "dy1")
            move(wide_v, da_out.at[g], "wide")
            turned[...] = wide_v[...].T

            def out_back(t, room, g=g):
                ctx_ref[g, :, ds(t * tile, tile)] = dot(room[...], turned[...]).T.astype(BF16)

            out_r.run(width_here // tile, out_back)
            if g + 1 < per:
                out_r.prefetch()
        free(*list(busy))

    vmem, anywhere = pl.BlockSpec(memory_space=pltpu.VMEM), pl.BlockSpec(memory_space=pl.ANY)
    row = (per, loc)
    outputs = [
        (row + (wide,), BF16, anywhere),
        (row + (units,), BF16, anywhere),
        (row + (width,), BF16, anywhere),
        (row + (wide,), BF16, anywhere),
        (row + (units,), BF16, anywhere),
        (row + (width,), F32, anywhere),
        (row + (wide,), BF16, anywhere),
        (row + (NR,), BF16, vmem),
        (row + (NR,), BF16, vmem),
        (row + (NR,), BF16, vmem),
        (row + (width_here,), BF16, vmem),
    ]
    n_copy = 2 * per * n_swap
    return pl.pallas_call(
        kernel,
        in_specs=[vmem] * 8 + [anywhere] * 7,
        out_specs=[space for _, _, space in outputs],
        out_shape=[jax.ShapeDtypeStruct(shape, dtype) for shape, dtype, _ in outputs],
        scratch_shapes=[
            pltpu.SemaphoreType.DMA((n_copy,)),
            pltpu.SemaphoreType.DMA((n_copy,)),
            pltpu.SemaphoreType.DMA((8,)),
            pltpu.SemaphoreType.DMA((11 * per,)),
            pltpu.VMEM((2, wide, tile), BF16),
            pltpu.VMEM((2, units, tile), BF16),
            pltpu.VMEM((2, tile, wide), BF16),
            pltpu.VMEM((2, tile, units), BF16),
            pltpu.VMEM(row + (width,), BF16),
            pltpu.VMEM(row + (wide,), BF16),
            pltpu.VMEM((2,) + row + (wide,), BF16),
            pltpu.VMEM(row + (width,), F32),
            pltpu.VMEM(row + (128,), F32),
            pltpu.VMEM(row + (width,), F32),
            pltpu.VMEM(row + (units,), BF16),
            pltpu.VMEM((loc, units), BF16),
            pltpu.VMEM((loc, wide), BF16),
            pltpu.VMEM((wide, loc), BF16),
            pltpu.VMEM((units, loc), BF16),
        ],
        compiler_params=pltpu.CompilerParams(
            collective_id=3, has_side_effects=True, vmem_limit_bytes=62 << 20
        ),
    )(
        picked, gain, shift_by, a_up, b_out, b_down, a_down, b_up,
        x_all, part_out, other_out, cot_all, out_x, up_x, down_x,
    )


def mm(left, right, nt, finish, tile, n_out=1, beside=None):
    rows, depth = left.shape
    columns = right.shape[0] if nt else right.shape[1]
    extra = [] if beside is None else [beside]
    sub = 128 if nt else tile

    def kernel(left_ref, right_ref, *refs):
        n_extra = len(extra)
        outs = refs[n_extra : n_extra + n_out]
        if nt:
            turned = refs[-1]

            @pl.when(pl.program_id(0) == 0)
            def _():
                turned[...] = left_ref[...].T

        for k in range(tile // sub):
            at = slice(k * sub, (k + 1) * sub)
            if nt:
                block = dot(right_ref[at, :], turned[...]).T
            else:
                block = dot(left_ref[...], right_ref[:, at])
            values = finish(block, *[ref[:, at] for ref in refs[:n_extra]])
            for ref, value in zip(outs, values):
                ref[:, at] = value

    part = pl.BlockSpec((rows, tile), lambda j: (0, j))
    out = pl.pallas_call(
        kernel,
        grid=(pl.cdiv(columns, tile),),
        in_specs=[
            pl.BlockSpec((rows, depth), lambda j: (0, 0)),
            pl.BlockSpec((tile, depth), lambda j: (j, 0))
            if nt
            else pl.BlockSpec((depth, tile), lambda j: (0, j)),
        ]
        + [part] * len(extra),
        out_specs=[part] * n_out,
        out_shape=[jax.ShapeDtypeStruct((rows, columns), BF16)] * n_out,
        scratch_shapes=[pltpu.VMEM((depth, rows), BF16)] if nt else [],
        compiler_params=pltpu.CompilerParams(vmem_limit_bytes=48 << 20),
        cost_estimate=pl.CostEstimate(
            flops=2 * rows * depth * columns,
            bytes_accessed=2 * (rows * depth + 2 * depth * columns + rows * columns * n_out),
            transcendentals=0,
        ),
    )(left, right, *extra)
    return out[0] if n_out == 1 else out


def combine(pieces, chosen, shapes):
    n_part, n_fsdp = pieces.shape[:2]
    flat = []
    for i, shape in enumerate(shapes):
        for lead in range(shape[0] if len(shape) == 3 else 1):
            flat.append((i, lead if len(shape) == 3 else None, shape[-2:]))

    def kernel(chosen_ref, piece_ref, *outs):
        for part in range(n_part):
            ordered = jnp.concatenate([piece_ref[part, a] for a in range(n_fsdp)], axis=0)
            start = 0
            for i, lead, (high, wide) in flat:
                out_ref = outs[i] if lead is None else outs[i].at[lead]
                tall = wide == NR and high != NR
                size = (high if tall else wide) // n_part
                block = ordered[:, start : start + size]
                at = slice(part * size, (part + 1) * size)
                if tall:
                    out_ref[at, :] = dot_tn(block, chosen_ref[...])
                else:
                    out_ref[:, at] = dot_tn(chosen_ref[...], block)
                start += size

    vmem = pl.BlockSpec(memory_space=pltpu.VMEM)
    return pl.pallas_call(
        kernel,
        in_specs=[vmem, vmem],
        out_specs=[vmem] * len(shapes),
        out_shape=[jax.ShapeDtypeStruct(shape, F32) for shape in shapes],
        compiler_params=pltpu.CompilerParams(vmem_limit_bytes=48 << 20),
    )(chosen, pieces)


def last(d_query, d_pair, x_all, adapt_all, dy1, qkv_x, a_in, picked, early, pairs, n_fsdp, n_ctx):
    per, loc, width_here = d_query.shape
    piece, width = loc // n_fsdp, x_all.shape[2]
    depth = 3 * width_here
    foot = 3 * NR
    wide = width + foot
    tile, chunk = 512, 32
    n_wide = width // tile
    n_swap = n_wide + 1
    n_early = len(early)
    early_sizes = [values[2] // n_ctx for _, values in pairs] + [width_here // n_ctx] * 3
    late_sizes = [width // n_ctx] * 3
    gathers = 2
    n_copy = per * (n_fsdp - 1) + gathers * ((n_fsdp - 1) * n_ctx + 2 * (n_ctx - 1))

    def kernel(*refs):
        dq_ref, dkv_ref, x_ref, adapt_ref, a_ref, pick_ref = refs[:6]
        dy1_ref, w_ref = refs[6:8]
        early_refs = refs[8 : 8 + n_early]
        in_ref, early_out, late_out = refs[8 + n_early : 11 + n_early]
        send, recv, swap_send, swap_recv, ring_sem, sems = refs[11 + n_early : 17 + n_early]
        rows_room, foot_room, dy1_room, turned, part, got, codes_in, dx = refs[
            17 + n_early : 25 + n_early
        ]
        early_part, early_came, late_part, late_came = refs[25 + n_early : 29 + n_early]
        staged = refs[29 + n_early :]
        mover = Mover(n_fsdp, n_ctx, send, recv)
        z, ct, masks = mover.z, mover.ct, mover.masks
        partner = {"tp": 1 - lax.axis_index("tp")}
        ring = Ring(rows_room, ring_sem, 0, lambda t: w_ref.at[ds(t * tile, tile)])
        used = [0]

        def move(source, target):
            copy = pltpu.make_async_copy(source, target, sems.at[used[0]])
            used[0] += 1
            copy.start()
            return copy

        def swap_copy(g, t, size):
            at = ds(t * tile, tile) if size == tile else pl.ds(width, size)
            sem = g * n_swap + t
            return pltpu.make_async_remote_copy(
                src_ref=part.at[g, :, at],
                dst_ref=got.at[g, :, at],
                send_sem=swap_send.at[sem],
                recv_sem=swap_recv.at[sem],
                device_id=partner,
                device_id_type=pl.DeviceIdType.MESH,
            )

        def compact(out_ref, n, entries, sizes):
            column = lax.broadcasted_iota(jnp.int32, (NR, RANK), 0)
            rank = lax.broadcasted_iota(jnp.int32, (NR, RANK), 1)
            used_columns = jnp.where(lax.rem(column, RANK) == rank, 1.0, 0.0).astype(BF16)
            start = 0
            for (code, value), size in zip(entries, sizes):
                short = dot(code(), used_columns).astype(BF16)
                block = dot_tn(short, value()).astype(BF16)
                for k in range(n_ctx):
                    out_ref[k, n * RANK : (n + 1) * RANK, start : start + size] = block[
                        :, k * size : (k + 1) * size
                    ]
                start += size

        class Fold:
            def __init__(self, parts, came):
                self.parts, self.came, self.flying = parts, came, {}

            def at(self, k):
                return flip(ct, mover.offsets[k])

            def hand(self, level):
                half = 2**level
                self.flying[level] = [
                    mover.go(
                        self.parts.at[self.at(half + i)],
                        self.came.at[half - 1 + i],
                        {"ctx": flip(ct, masks[level])},
                    )
                    for i in range(half)
                ]

            def take(self, level):
                for i, copy in enumerate(self.flying[level]):
                    copy.wait_recv()
                    total = self.parts[self.at(i)].astype(F32) + self.came[2**level - 1 + i].astype(F32)
                    self.parts[self.at(i)] = total.astype(BF16)

        lasting = len(masks) - 1
        load_foot = move(w_ref.at[pl.ds(width, foot)], foot_room)
        ring.prefetch()
        loads = [move(ref, room) for ref, room in zip(early_refs, staged)]
        load_dy1 = move(dy1_ref, dy1_room)
        mover.greet(tp=True)
        folds = [Fold(early_part, early_came), Fold(late_part, late_came)]
        for g in range(per):
            turned[0:width_here, :] = dq_ref[g].T
            turned[width_here : 2 * width_here, :] = dkv_ref[0, g].T
            turned[2 * width_here :, :] = dkv_ref[1, g].T
            if g == 0:
                load_foot.wait()
            part[g, :, width:] = dot(foot_room[...], turned[...]).T.astype(BF16)
            swap_copy(g, n_wide, foot).start()

            def back(t, room, g=g):
                part[g, :, ds(t * tile, tile)] = dot(room[...], turned[...]).T.astype(BF16)
                swap_copy(g, t, tile).start()

            ring.run(n_wide, back)
            if g + 1 < per:
                ring.prefetch()
            if g == 0:
                for copy in loads:
                    copy.wait()
                for n in range(per):
                    entries = []
                    for (i, first, size), (j, start, count) in pairs:
                        entries.append(
                            (
                                lambda n=n, i=i, f=first, c=size: staged[i][n, :, f : f + c],
                                lambda n=n, i=j, f=start, c=count: staged[i][n, :, f : f + c],
                            )
                        )
                    values = [
                        lambda n=n: dq_ref[n],
                        lambda n=n: dkv_ref[0, n],
                        lambda n=n: dkv_ref[1, n],
                    ]
                    for j in range(3):
                        entries.append(
                            (lambda n=n, j=j: adapt_ref[n, :, j * NR : (j + 1) * NR], values[j])
                        )
                    compact(early_part, n, entries, early_sizes)
                folds[0].hand(lasting)
        for level in range(lasting, -1, -1):
            folds[0].take(level)
            if level:
                folds[0].hand(level - 1)

        def gather(parts, out_ref):
            own = parts.at[ct]
            kept.append(move(own, out_ref.at[ct, z]))
            item = Weight(lambda c: parts.at[c], lambda o, c: out_ref.at[c, o], own)
            mover.begin(item)
            return item

        kept = []
        first = gather(early_part, early_out)
        load_dy1.wait()
        dealt = []

        def finish_rows(g):
            for t in range(n_swap):
                copy = swap_copy(g, t, tile if t < n_wide else foot)
                copy.wait_recv()
                copy.wait_send()
            pick = jnp.concatenate([pick_ref[g]] * 3, axis=1)

            def step(r, carry):
                rows = ds(r * chunk, chunk)
                total = part[g, rows, :].astype(F32) + got[g, rows, :].astype(F32)
                code = (total[:, width:] * pick).astype(BF16)
                codes_in[g, rows, :] = code
                value = dy1_room[g, rows, :] + total[:, :width] + dot_nt(code, a_ref[...])
                dx[g, rows, :] = value.astype(BF16)
                return carry

            lax.fori_loop(0, loc // chunk, step, 0)
            kept.append(move(dx.at[g, pl.ds(0, piece)], in_ref.at[z * per + g]))
            for s in range(1, n_fsdp):
                to = lax.rem(z - s + n_fsdp, n_fsdp)
                dealt.append(
                    mover.go(
                        dx.at[g, pl.ds(s * piece, piece)], in_ref.at[z * per + g], {"fsdp": to}
                    )
                )

        for g in range(per):
            finish_rows(g)
            if g == 0:
                mover.relay(first)
        for n in range(per):
            entries = []
            for j in range(3):
                entries.append(
                    (
                        lambda n=n, j=j: codes_in[n, :, j * NR : (j + 1) * NR],
                        lambda n=n: x_ref[n],
                    )
                )
            compact(late_part, n, entries, late_sizes)
        folds[1].hand(lasting)
        for level in range(lasting, -1, -1):
            folds[1].take(level)
            if level:
                folds[1].hand(level - 1)
        second = gather(late_part, late_out)
        for level in range(len(masks)):
            mover.finish(first, level)
        mover.relay(second)
        for level in range(len(masks)):
            mover.finish(second, level)
        for copy in dealt:
            copy.wait_recv()
        for copy in kept:
            copy.wait()
        mover.close()

    vmem, anywhere = pl.BlockSpec(memory_space=pltpu.VMEM), pl.BlockSpec(memory_space=pl.ANY)
    parts = [(n_ctx, per * RANK, sum(early_sizes)), (n_ctx, per * RANK, sum(late_sizes))]
    rooms = [
        ((2, tile, depth), BF16),
        ((foot, depth), BF16),
        (dy1.shape, F32),
        ((depth, loc), BF16),
        ((per, loc, wide), BF16),
        ((per, loc, wide), BF16),
        ((per, loc, foot), BF16),
        ((per, loc, width), BF16),
    ]
    for shape in parts:
        rooms += [(shape, BF16), ((n_ctx - 1,) + shape[1:], BF16)]
    rooms += [(x.shape, BF16) for x in early]
    return pl.pallas_call(
        kernel,
        in_specs=[vmem] * 6 + [anywhere] * (2 + n_early),
        out_specs=[anywhere] * 3,
        out_shape=[jax.ShapeDtypeStruct((per * n_fsdp, piece, width), BF16)]
        + [jax.ShapeDtypeStruct((n_ctx, n_fsdp) + shape[1:], BF16) for shape in parts],
        scratch_shapes=[
            pltpu.SemaphoreType.DMA((n_copy,)),
            pltpu.SemaphoreType.DMA((n_copy,)),
            pltpu.SemaphoreType.DMA((per * n_swap,)),
            pltpu.SemaphoreType.DMA((per * n_swap,)),
            pltpu.SemaphoreType.DMA((2,)),
            pltpu.SemaphoreType.DMA((4 + n_early + per,)),
        ]
        + [pltpu.VMEM(shape, dtype) for shape, dtype in rooms],
        compiler_params=pltpu.CompilerParams(
            collective_id=4, has_side_effects=True, vmem_limit_bytes=60 << 20
        ),
    )(d_query, d_pair, x_all, adapt_all, a_in, picked, dy1, qkv_x, *early)


def as_low(block):
    return (block.astype(BF16),)


def gelu_both(pre):
    square = pre * pre
    bent = jnp.tanh(GELU_COEF * (pre + 0.044715 * square * pre))
    out = 0.5 * pre * (1.0 + bent)
    slope = 0.5 * (1.0 + bent) + 0.5 * pre * (1.0 - bent * bent) * GELU_COEF * (
        1.0 + 3.0 * 0.044715 * square
    )
    return out.astype(BF16), slope.astype(BF16)


def local(
    x_in,
    cotangent,
    lengths,
    adapter_ids,
    w_qkv,
    w_out,
    w_up,
    w_down,
    ln_gain,
    ln_bias,
    a_qkv,
    b_qkv,
    a_out,
    b_out,
    a_up,
    b_up,
    a_down,
    b_down,
):
    n_ctx, n_fsdp = lax.axis_size("ctx"), lax.axis_size("fsdp")
    z, ct = lax.axis_index("fsdp"), lax.axis_index("ctx")
    seqs, piece, width = x_in.shape
    per = seqs // n_fsdp
    loc = n_fsdp * piece
    heads_width = w_qkv.shape[2]
    n_group = GROUPS if per % GROUPS == 0 else 1
    g_per = per // n_group
    g_rows = g_per * loc

    def take(array, start, size, axis=0):
        return lax.dynamic_slice_in_dim(array, start, size, axis)

    units = w_up.shape[1]
    rows_shape = (per, n_fsdp, piece, width)
    zq, zu = w_qkv.shape[1], w_up.shape[0]

    def first_items(ins, outs, z):
        x_ref, w_ref = ins
        rows_ref, whole_ref = outs

        def deal(g):
            return Deal(lambda to: x_ref.at[to * per + g], lambda s: rows_ref.at[g, s])

        def weight(j):
            size = zq // n_ctx
            columns = pl.ds(j * heads_width, heads_width)
            return Weight(
                lambda c: w_ref.at[j, pl.ds(pl.multiple_of(c * size, size), size)],
                lambda o, c: whole_ref.at[
                    pl.ds(pl.multiple_of(o * zq + c * size, size), size), columns
                ],
            )

        stay = [(x_ref.at[z * per + g], rows_ref.at[g, 0]) for g in range(per)]
        for j in range(3):
            own = whole_ref.at[
                pl.ds(pl.multiple_of(z * zq, zq), zq), pl.ds(j * heads_width, heads_width)
            ]
            stay.append((w_ref.at[j], own))
        items = [weight(j) for j in range(3)] + [deal(g) for g in range(per)]
        return items, stay

    x_all, qkv_x = move(
        first_items,
        [Weight] * 3 + [Deal] * per,
        (x_in, w_qkv),
        (rows_shape, (width + 3 * NR, 3 * heads_width)),
        n_fsdp,
        n_ctx,
        ((piece, width),) * per + (w_qkv.shape[1:],) * 3,
        0,
        foot=(b_qkv, lambda outs: outs[1].at[pl.ds(width, 3 * NR)]),
    )

    a_in = a_qkv.transpose(1, 0, 2).reshape(width, 3 * NR)

    my_lengths = take(lengths, z * per, per)
    my_ids = take(adapter_ids, z * per, per)
    picked = (my_ids[:, None] == jnp.arange(NR)[None, :] // RANK).astype(F32)
    steps = lax.rem(z - jnp.arange(n_fsdp) + n_fsdp, n_fsdp)
    ctx_of = ct ^ jnp.array(offsets(n_ctx))
    key_pos = (
        (steps[None, :, None] * n_ctx + ctx_of[:, None, None]) * piece
        + jnp.arange(piece)[None, None, :]
    ).reshape(-1)
    bias_all = jnp.where(key_pos[None, :] < my_lengths[:, None], 0.0, -1e30).astype(F32)
    bias_all = jnp.broadcast_to(bias_all[:, :, None], bias_all.shape + (128,))

    pick_all = jnp.repeat(picked, loc, axis=0)
    x_flat = x_all.reshape(per * loc, width)
    adapt_all = (dot(x_flat, a_in) * jnp.concatenate([pick_all] * 3, axis=1)).astype(BF16)
    proj_all = mm(jnp.concatenate([x_flat, adapt_all], axis=1), qkv_x, False, as_low, 1024)
    kv_own = jnp.stack([proj_all[:, heads_width : 2 * heads_width], proj_all[:, 2 * heads_width :]])
    kv_own = kv_own.reshape(2, per, loc, heads_width)
    moved = forward_and_gather(
        proj_all[:, :heads_width].reshape(per, loc, heads_width),
        kv_own,
        bias_all,
        (cotangent, w_out, w_up, w_down),
        (a_out, b_up, a_down),
        n_fsdp,
        n_ctx,
    )
    kv_all = [kv_own] + list(moved[: n_ctx - 1])
    cot_all, out_x, up_x, down_x, context, log_total, part_out, other_out = moved[n_ctx - 1 :]

    groups = range(n_group)
    picks = [jnp.repeat(take(picked, g * g_per, g_per), loc, axis=0) for g in groups]
    part = [slice(g * g_rows, (g + 1) * g_rows) for g in groups]
    x_rows = [x_flat[part[g]] for g in groups]

    (wide_h, gelu_out, acts, wide_d, d_pre, dy1, wide_a, adapt_out, adapt_down, dadapt_up, d_context) = middle(
        x_all.reshape(per, loc, width),
        part_out,
        other_out,
        cot_all.reshape(per, loc, width),
        picked[:, None, :],
        ln_gain,
        ln_bias,
        (out_x, up_x, down_x),
        (a_up, b_out, b_down, a_down, b_up),
    )
    d_query, d_pair, activations = attend_back(
        proj_all[:, :heads_width].reshape(per, loc, heads_width),
        kv_own,
        kv_all[1:],
        bias_all,
        d_context,
        log_total,
        acts.reshape(per, n_fsdp, piece, width),
        n_fsdp,
        n_ctx,
    )
    code, row, unit = (0, NR), (0, width), (0, units)
    tail = (width, NR)
    early_pairs = [
        ((0,) + code, (1,) + row),
        ((1,) + tail, (2,) + unit),
        ((3,) + tail, (4,) + unit),
        ((5,) + code, (3,) + row),
        ((6,) + code, (7,) + row),
        ((7,) + tail, (8, 0, heads_width)),
    ]
    early_in = (
        adapt_down, wide_d, gelu_out, wide_h, d_pre, dadapt_up, adapt_out, wide_a, context,
    )
    input_grad, early, late = last(
        d_query,
        d_pair,
        x_all.reshape(per, loc, width),
        adapt_all.reshape(per, loc, 3 * NR),
        dy1,
        qkv_x,
        a_in,
        picked[:, None, :],
        early_in,
        early_pairs,
        n_fsdp,
        n_ctx,
    )
    codes = (adapter_ids[:, None] * RANK + jnp.arange(RANK)[None, :]).reshape(-1)
    chosen = (codes[:, None] == jnp.arange(NR)[None, :]).astype(BF16)
    e = combine(
        early,
        chosen,
        [
            (NR, width), (units, NR), (NR, units), (width, NR), (NR, width), (heads_width, NR),
            (3, NR, heads_width),
        ],
    )
    (a_qkv_grad,) = combine(late, chosen, [(3, width, NR)])
    return activations, input_grad, a_qkv_grad, e[6], e[5], e[4], e[3], e[2], e[1], e[0]


def solution(mesh):
    rows = P(None, ("fsdp", "ctx"), None)
    return jax.shard_map(
        local,
        mesh=mesh,
        in_specs=(
            rows,
            rows,
            P(),
            P(),
            P(None, "fsdp", "tp"),
            P("tp", "fsdp"),
            P("fsdp", "tp"),
            P("tp", "fsdp"),
            P(),
            P(),
            P(),
            P(None, None, "tp"),
            P("tp", None),
            P(),
            P(),
            P(None, "tp"),
            P("tp", None),
            P(),
        ),
        out_specs=(
            rows,
            rows,
            P(),
            P(None, None, "tp"),
            P("tp", None),
            P(),
            P(),
            P(None, "tp"),
            P("tp", None),
            P(),
        ),
        check_vma=False,
    )
```

```python
import math

import jax
import jax.numpy as jnp
from jax import lax
from jax.experimental import pallas as pl
from jax.experimental.pallas import tpu as pltpu
from jax.sharding import PartitionSpec as P

HEAD_DIM = 128
RANK = 16
ADAPTERS = 8
NR = RANK * ADAPTERS
NORM_EPS = 1e-06
GELU_COEF = 0.7978845608028654
SCALE = 1.0 / math.sqrt(HEAD_DIM)
F32 = jnp.float32
BF16 = jnp.bfloat16


def dot(left, right):
    return jnp.dot(left, right, preferred_element_type=F32)


def dot_nt(left, right):
    return lax.dot_general(left, right, (((1,), (1,)), ((), ())), preferred_element_type=F32)


def dot_tn(left, right):
    return lax.dot_general(left, right, (((0,), (0,)), ((), ())), preferred_element_type=F32)


def masks_of(n):
    out = []
    while n > 1:
        n //= 2
        out.append(n)
    return out


def offsets(n):
    out = [0]
    for mask in masks_of(n):
        out = out + [o ^ mask for o in out]
    return out


def attend_head(query, keys, values, biases):
    scores = [dot_nt(k, query) * SCALE + bias for k, bias in zip(keys, biases)]
    top = scores[0].max(axis=0, keepdims=True)
    for s in scores[1:]:
        top = jnp.maximum(top, s.max(axis=0, keepdims=True))
    total = jnp.zeros_like(top)
    mixed = None
    for s, v in zip(scores, values):
        probs = jnp.exp(s - top)
        total = total + probs.sum(axis=0, keepdims=True)
        term = dot_tn(v, probs.astype(BF16))
        mixed = term if mixed is None else mixed + term
    return (mixed / total).T.astype(BF16), top + jnp.log(total)


def attend_back_head(query, grad, log_total, keys, values, biases):
    probs, dprobs, dvalues = [], [], []
    delta = jnp.zeros_like(log_total)
    for k, v, bias in zip(keys, values, biases):
        p = jnp.exp(dot_nt(k, query) * SCALE + bias - log_total)
        dp = dot_nt(v, grad)
        dvalues.append(dot(p.astype(BF16), grad).astype(BF16))
        delta = delta + (p * dp).sum(axis=0, keepdims=True)
        probs.append(p)
        dprobs.append(dp)
    dquery, dkeys = None, []
    for k, p, dp in zip(keys, probs, dprobs):
        ds = (p * (dp - delta)).astype(BF16)
        dkeys.append((dot(ds, query) * SCALE).astype(BF16))
        term = dot_tn(k, ds)
        dquery = term if dquery is None else dquery + term
    return (dquery * SCALE).T.astype(BF16), dkeys, dvalues


def ds(start, size):
    return pl.ds(pl.multiple_of(start, size), size)


def flip(ct, offset):
    mask = 1
    while mask <= offset:
        if offset & mask:
            ct = ct + mask - 2 * mask * lax.rem(ct // mask, 2)
        mask *= 2
    return ct


class Weight:
    def __init__(self, shard_at, whole_at, own=None, skip=0):
        self.shard_at, self.whole_at, self.own, self.skip = shard_at, whole_at, own, skip


class Deal:
    def __init__(self, source_at, rows_at):
        self.source_at, self.rows_at = source_at, rows_at


class Pair:
    def __init__(self, slot_at):
        self.slot_at = slot_at


class Mover:
    def __init__(self, n_fsdp, n_ctx, send, recv):
        self.n_fsdp, self.n_ctx = n_fsdp, n_ctx
        self.z, self.ct = lax.axis_index("fsdp"), lax.axis_index("ctx")
        self.send, self.recv = send, recv
        self.used = 0
        self.open = []
        self.masks = masks_of(n_ctx)
        self.offsets = offsets(n_ctx)
        self.came, self.waiting, self.done = {}, {}, {}

    def skip(self, item):
        return item.skip if isinstance(item, Weight) else 0

    def part(self, item):
        return lax.rem(self.ct, self.n_ctx >> item.skip) if item.skip else self.ct

    def greet(self, tp=False):
        barrier = pltpu.get_barrier_semaphore()
        others = [{"fsdp": lax.rem(self.z + s, self.n_fsdp)} for s in range(1, self.n_fsdp)]
        others += [{"ctx": flip(self.ct, mask)} for mask in self.masks]
        if tp:
            others.append({"tp": 1 - lax.axis_index("tp")})
        for other in others:
            pl.semaphore_signal(
                barrier, inc=1, device_id=other, device_id_type=pl.DeviceIdType.MESH
            )
        pl.semaphore_wait(barrier, len(others))

    def copy(self, source, target, device, at=None):
        if at is None:
            at = self.used
            self.used += 1
        return pltpu.make_async_remote_copy(
            src_ref=source,
            dst_ref=target,
            send_sem=self.send.at[at],
            recv_sem=self.recv.at[at],
            device_id=device,
            device_id_type=pl.DeviceIdType.MESH,
        )

    def go(self, source, target, device):
        copy = self.copy(source, target, device)
        copy.start()
        self.open.append((None, copy))
        return copy

    def along(self, item, owner, right, ok, source, slot):
        target = item.whole_at(owner, self.part(item))
        device = {"fsdp": lax.rem(self.z + (1 if right else self.n_fsdp - 1), self.n_fsdp)}
        copy = self.copy(source, target, device, self.came[item] + slot - 1)
        pl.when(ok)(copy.start)
        self.open.append((ok, copy))

    def begin(self, item):
        if isinstance(item, Pair):
            self.waiting[item] = [[] for _ in self.masks]
            self.cast(item, item.slot_at, lambda k, level: item.slot_at(k + 2**level), 0, 0)
            return
        if isinstance(item, Weight):
            self.came[item] = self.used
            self.used += self.n_fsdp - 1
            source = item.shard_at(self.part(item))
            self.along(item, self.z, True, self.z < self.n_fsdp - 1, source, 1)
            self.along(item, self.z, False, self.z > 0, source, self.n_fsdp - 1)
            return
        self.came[item] = [
            self.go(
                item.source_at(lax.rem(self.z + s, self.n_fsdp)),
                item.rows_at(s),
                {"fsdp": lax.rem(self.z + s, self.n_fsdp)},
            )
            for s in range(1, self.n_fsdp)
        ]

    def cast(self, item, source_at, target_at, k, first):
        skip = self.skip(item)
        for level in range(first, len(self.masks) - skip):
            device = {"ctx": flip(self.ct, self.masks[level + skip])}
            copy = self.go(source_at(k), target_at(k, level), device)
            self.waiting[item][level].append((copy, k + 2**level, source_at, target_at))

    def relay(self, item):
        if isinstance(item, Deal):
            for copy in self.came[item]:
                copy.wait_recv()
            return
        self.waiting[item] = [[] for _ in self.masks[item.skip :]]
        n, part = self.n_fsdp, self.part(item)
        others = offsets(self.n_ctx >> item.skip)
        if item.own is not None:

            def mine(k):
                return item.own if k == 0 else item.whole_at(self.z, flip(part, others[k]))

            def lands(k, level):
                return item.whole_at(self.z, flip(part, others[k]))

            self.cast(item, mine, lands, 0, 0)
        for i in range(n - 1):
            s = i // 2 + 1 if i % 2 == 0 else n - 1 - i // 2
            owner = lax.rem(self.z - s + n, n)
            here = item.whole_at(owner, part)
            self.copy(here, here, {"fsdp": owner}, self.came[item] + s - 1).wait_recv()
            if s < n - 1:
                ok = (self.z >= s) & (self.z < n - 1)
                self.along(item, owner, True, ok, here, s + 1)
            if s > 1:
                ok = (self.z < s) & (self.z > 0)
                self.along(item, owner, False, ok, here, s - 1)

            def at(k, owner=owner):
                return item.whole_at(owner, flip(part, others[k]))

            self.cast(item, at, lambda k, level, at=at: at(k), 0, 0)

    def finish(self, item, level):
        if isinstance(item, Deal) or level != self.done.get(item, 0):
            return
        if level == len(self.waiting[item]):
            return
        for copy, k, source_at, target_at in self.waiting[item][level]:
            copy.wait_recv()
            self.cast(item, source_at, target_at, k, level + 1)
        self.done[item] = level + 1

    def complete(self, item):
        while self.done.get(item, 0) < len(self.waiting[item]):
            self.finish(item, self.done.get(item, 0))

    def close(self):
        for ok, copy in self.open:
            if ok is None:
                copy.wait_send()
            else:
                pl.when(ok)(copy.wait_send)


def copies_of(items, n_fsdp, n_ctx):
    total = 0
    for item in items:
        total += {Weight: (n_fsdp - 1) * n_ctx, Deal: n_fsdp - 1, Pair: n_ctx - 1}[item]
    return total


def keep(stay, room, sems):
    out = []
    for k, (source, target) in enumerate(stay):
        first = pltpu.make_async_copy(source, room[k], sems.at[2 * k])
        first.start()
        out.append((first, pltpu.make_async_copy(room[k], target, sems.at[2 * k + 1])))
    return out


def move(make, kinds, inputs, outputs, n_fsdp, n_ctx, local_shapes, ident, ahead=2, foot=None):
    n_in = len(inputs)
    n_copy = copies_of(kinds, n_fsdp, n_ctx)

    def kernel(*refs):
        ins, outs = refs[:n_in], refs[n_in : n_in + len(outputs)]
        send, recv, here = refs[n_in + len(outputs) : n_in + len(outputs) + 3]
        room = refs[n_in + len(outputs) + 3 :]
        if foot is not None:
            blocks_ref, ins = ins[-1], ins[:-1]
            strip = room[-1]
        mover = Mover(n_fsdp, n_ctx, send, recv)
        items, stay = make(ins, outs, mover.z)
        mover.greet()
        for item in items[:ahead]:
            mover.begin(item)
        kept = keep(stay, room, here)
        levels = len(mover.masks)
        for i in range(len(items) + levels):
            if i < len(items):
                mover.relay(items[i])
                if i + ahead < len(items):
                    mover.begin(items[i + ahead])
            if i == 0 and foot is not None:
                strip[...] = jnp.zeros_like(strip)
                high, wide = blocks_ref.shape[1:]
                for j in range(blocks_ref.shape[0]):
                    strip[j * high : (j + 1) * high, j * wide : (j + 1) * wide] = blocks_ref[j]
                set_foot = pltpu.make_async_copy(strip, foot[1](outs), here.at[2 * len(local_shapes)])
                set_foot.start()
                kept.append((None, set_foot))
            if i == 0:
                for first, second in kept:
                    if first is not None:
                        first.wait()
                        second.start()
            for level in range(levels):
                if 0 <= i - 1 - level < len(items):
                    mover.finish(items[i - 1 - level], level)
        for _, second in kept:
            second.wait()
        mover.close()

    spaces = [pl.BlockSpec(memory_space=pl.ANY)] * n_in
    room_shapes = list(local_shapes)
    if foot is not None:
        blocks = foot[0]
        inputs = inputs + (blocks,)
        n_in += 1
        spaces.append(pl.BlockSpec(memory_space=pltpu.VMEM))
        room_shapes.append((blocks.shape[0] * blocks.shape[1], blocks.shape[0] * blocks.shape[2]))
    return pl.pallas_call(
        kernel,
        in_specs=spaces,
        out_specs=[pl.BlockSpec(memory_space=pl.ANY)] * len(outputs),
        out_shape=[jax.ShapeDtypeStruct(shape, BF16) for shape in outputs],
        scratch_shapes=[
            pltpu.SemaphoreType.DMA((n_copy,)),
            pltpu.SemaphoreType.DMA((n_copy,)),
            pltpu.SemaphoreType.DMA((2 * len(local_shapes) + 1,)),
        ]
        + [pltpu.VMEM(shape, BF16) for shape in room_shapes],
        compiler_params=pltpu.CompilerParams(
            collective_id=ident, has_side_effects=True, vmem_limit_bytes=60 << 20
        ),
    )(*inputs)


def forward_and_gather(x_rows, qkv_x, a_qkv, picked, bias, shards, maps, n_fsdp, n_ctx):
    per, loc, width = x_rows.shape
    w_out, w_up, w_down = shards
    width_here = qkv_x.shape[1] // 3
    heads, units = width_here // HEAD_DIM, w_up.shape[1]
    zu, zo = w_up.shape[0], w_out.shape[1]
    n_part = n_ctx // 2 if n_ctx > 1 else 1
    so, su, sd = w_out.shape[0] // n_ctx, zu // n_ctx, w_down.shape[0] // n_ctx
    wide = width + NR
    wide_x = width + 3 * NR
    cuts = 4
    paired = cuts // 2 if n_ctx > 1 else 0
    tile = 512
    per_kind = width_here // tile
    n_tile = 3 * per_kind
    n_copy = (n_fsdp - 1) * n_ctx * (1 + 2 * cuts) + 2 * per * (n_ctx - 1) + 6 + per
    lag = 4

    def kernel(*refs):
        bias_ref, a_ref, pick_ref, x_ref, w_ref = refs[:5]
        wo_ref, wu_ref, wd_ref, ao_ref, bu_ref, ad_ref = refs[5:11]
        slots = refs[11 : 10 + n_ctx]
        q_ref, kv_ref, adapt_ref, out_ref, up_ref, down_ref, ctx_ref, log_ref, part_ref, other_ref = refs[
            10 + n_ctx : 20 + n_ctx
        ]
        send, recv, here, load, ring_sem, x_room, w_room, proj, kv_room, out_room = refs[20 + n_ctx :]
        mover = Mover(n_fsdp, n_ctx, send, recv)
        ring = Ring(
            w_room,
            ring_sem,
            0,
            lambda t: w_ref.at[:, ds(lax.rem(t + per_kind, n_tile) * tile, tile)],
        )
        z = mover.z
        rows = [pl.ds(g * loc, loc) for g in range(per)]

        def columns(j):
            return pl.ds(j * width_here, width_here)

        out_item = Weight(
            lambda c: wo_ref.at[ds(c * so, so)],
            lambda o, c: out_ref.at[ds(c * so, so), ds(o * zo, zo)],
        )

        def up_item(h):
            at = pl.ds(h * (units // cuts), units // cuts)
            return Weight(
                lambda c: wu_ref.at[ds(c * su, su), at],
                lambda o, c: up_ref.at[ds(o * zu + c * su, su), at],
            )

        def down_item(h):
            size = sd // cuts
            return Weight(
                lambda c: wd_ref.at[ds(c * sd + h * size, size)],
                lambda o, c: down_ref.at[ds(c * sd + h * size, size), ds(o * zo, zo)],
            )

        def down_pair(h):
            size = sd // cuts

            def at(c, p):
                return ds((c + p * n_part) * sd + h * size, size)

            def half(p):
                return Weight(
                    lambda c: wd_ref.at[at(c, p)],
                    lambda o, c: down_ref.at[at(c, p), ds(o * zo, zo)],
                    skip=1,
                )

            return [half(p) for p in range(2)]

        def pair(g, j):
            return Pair(
                lambda k: proj.at[rows[g], columns(1 + j)] if k == 0 else slots[k - 1].at[j, g]
            )

        pairs = [pair(g, j) for g in range(per) for j in range(2)]
        items = [out_item] + [up_item(h) for h in range(cuts)]
        items += [down_item(h) for h in range(cuts - paired)]
        for h in range(cuts - paired, cuts):
            items += down_pair(h)
        used = [0]

        def move(source, target):
            copy = pltpu.make_async_copy(source, target, here.at[used[0]])
            used[0] += 1
            copy.start()
            return copy

        def attend(g):
            for j in range(2):
                mover.complete(pairs[2 * g + j])
            loads = []
            for k in range(1, n_ctx):
                copy = pltpu.make_async_copy(slots[k - 1].at[:, g], kv_room.at[k], load.at[k])
                copy.start()
                loads.append(copy)
            for j in range(2):
                kv_room[0, j] = proj[g * loc : (g + 1) * loc, (1 + j) * width_here : (2 + j) * width_here]
            for copy in loads:
                copy.wait()

            def one(h, carry):
                at = ds(h * HEAD_DIM, HEAD_DIM)
                biases = []
                for k in range(n_ctx):
                    block = bias_ref[g, k * loc : (k + 1) * loc, :]
                    biases.append(jnp.concatenate([block] * (loc // 128), axis=1))
                context, log = attend_head(
                    proj[g * loc : (g + 1) * loc, at],
                    [kv_room[k, 0, :, at] for k in range(n_ctx)],
                    [kv_room[k, 1, :, at] for k in range(n_ctx)],
                    biases,
                )
                ctx_ref[g, :, at] = context
                log_ref[g, h] = log
                return carry

            lax.fori_loop(0, heads, one, 0)

        def project():
            mover.complete(out_item)
            own[0].wait_recv()
            own[3].wait_recv()
            copy = pltpu.make_async_copy(out_ref, out_room, load.at[0])
            copy.start()
            copy.wait()
            for g in range(per):
                for start in range(0, wide, 1024):
                    at = slice(start, min(start + 1024, wide))
                    part_ref[g, :, at] = dot(ctx_ref[g], out_room[:, at]).astype(BF16)
                swapped.append(
                    mover.go(
                        part_ref.at[g], other_ref.at[g], {"tp": 1 - lax.axis_index("tp")}
                    )
                )

        def tiles(t, room):
            at = ds(lax.rem(t + per_kind, n_tile) * tile, tile)
            proj[:, at] = dot(x_room[...], room[...]).astype(BF16)

        swapped, outward = [], []
        tasks = {1 + g: (lambda g=g: attend(g)) for g in range(per)}
        tasks[per + 2] = project
        ring.prefetch()
        loads = [move(x_ref.at[g], x_room.at[rows[g], pl.ds(0, width)]) for g in range(per)]
        mover.greet(tp=True)
        ahead = 3
        for item in items[:ahead]:
            mover.begin(item)
        sibling = {"ctx": flip(mover.ct, 1)}
        own = [
            mover.go(source, target, sibling)
            for source, target in (
                (wo_ref, out_ref.at[:, ds(z * zo, zo)]),
                (wu_ref, up_ref.at[ds(z * zu, zu)]),
                (wd_ref, down_ref.at[:, ds(z * zo, zo)]),
                (ao_ref, out_ref.at[:, pl.ds(width, NR)]),
                (bu_ref, up_ref.at[pl.ds(width, NR)]),
                (ad_ref, down_ref.at[:, pl.ds(width, NR)]),
            )
        ]
        for g in range(per):
            loads[g].wait()
            pick = pick_ref[g]
            for j in range(3):
                code = dot(x_room[g * loc : (g + 1) * loc, :width], a_ref[j]) * pick
                x_room[g * loc : (g + 1) * loc, width + j * NR : width + (j + 1) * NR] = code.astype(BF16)
            outward.append(move(x_room.at[rows[g], pl.ds(width, 3 * NR)], adapt_ref.at[g]))
        ring.run(2 * per_kind, tiles, 0, n_tile)
        for item in pairs:
            mover.begin(item)
        for g in range(per):
            for j in range(2):
                outward.append(move(proj.at[rows[g], columns(1 + j)], kv_ref.at[j, g]))
        for i in range(len(items) + lag + 2):
            if i < len(items):
                mover.relay(items[i])
                if i + ahead < len(items):
                    mover.begin(items[i + ahead])
            if i == 0:
                ring.run(n_tile, tiles, 2 * per_kind, n_tile)
                for g in range(per):
                    outward.append(move(proj.at[rows[g], columns(0)], q_ref.at[g]))
            for level in range(len(mover.masks)):
                if 0 <= i - lag - level < len(items):
                    mover.finish(items[i - lag - level], level)
            if i in tasks:
                tasks[i]()
        for item in items:
            mover.complete(item)
        for copy in own[1:3] + own[4:] + swapped:
            copy.wait_recv()
        for copy in outward:
            copy.wait()
        mover.close()

    row = (per, loc, width_here)
    pair_shape = (2,) + row
    vmem, anywhere = pl.BlockSpec(memory_space=pltpu.VMEM), pl.BlockSpec(memory_space=pl.ANY)
    outputs = [(pair_shape, BF16, anywhere)] * (n_ctx - 1) + [
        (row, BF16, anywhere),
        (pair_shape, BF16, anywhere),
        ((per, loc, 3 * NR), BF16, anywhere),
        ((width_here, wide), BF16, anywhere),
        ((wide, units), BF16, anywhere),
        ((units, wide), BF16, anywhere),
        (row, BF16, vmem),
        ((per, heads, 1, loc), F32, vmem),
        ((per, loc, wide), BF16, vmem),
        ((per, loc, wide), BF16, anywhere),
    ]
    return pl.pallas_call(
        kernel,
        in_specs=[vmem] * 3 + [anywhere] * 8,
        out_specs=[space for _, _, space in outputs],
        out_shape=[jax.ShapeDtypeStruct(shape, dtype) for shape, dtype, _ in outputs],
        scratch_shapes=[
            pltpu.SemaphoreType.DMA((n_copy,)),
            pltpu.SemaphoreType.DMA((n_copy,)),
            pltpu.SemaphoreType.DMA((5 * per,)),
            pltpu.SemaphoreType.DMA((n_ctx,)),
            pltpu.SemaphoreType.DMA((2,)),
            pltpu.VMEM((per * loc, wide_x), BF16),
            pltpu.VMEM((2, wide_x, tile), BF16),
            pltpu.VMEM((per * loc, 3 * width_here), BF16),
            pltpu.VMEM((n_ctx, 2, loc, width_here), BF16),
            pltpu.VMEM((width_here, wide), BF16),
        ],
        compiler_params=pltpu.CompilerParams(
            collective_id=1, has_side_effects=True, vmem_limit_bytes=60 << 20
        ),
    )(bias, a_qkv, picked, x_rows, qkv_x, w_out, w_up, w_down, *maps)


def attend_back(query, kv_own, slots, bias, grad, log_total, acts, n_fsdp, n_ctx):
    per, loc, width_here = query.shape
    piece, width = acts.shape[2:]
    heads = width_here // HEAD_DIM
    cuts = 4
    high = heads // cuts
    columns = high * HEAD_DIM
    masks = masks_of(n_ctx)
    units = [(g, c) for g in range(per) for c in range(cuts)]
    n_copy = per * (n_fsdp - 1) + len(units) * (n_ctx - 1)

    def kernel(*refs):
        q_ref, bias_ref, g_ref, log_ref, acts_ref, kv_ref = refs[:6]
        slot_refs = refs[6 : 5 + n_ctx]
        dq_ref, dkv_ref, out_ref = refs[5 + n_ctx : 8 + n_ctx]
        send, recv, load, kv_room, own, came, act_room = refs[8 + n_ctx :]
        mover = Mover(n_fsdp, n_ctx, send, recv)
        z, ct = mover.z, mover.ct
        loads = []
        for g in range(per):
            loads.append([])
            for k in range(n_ctx):
                source = kv_ref if k == 0 else slot_refs[k - 1]
                copy = pltpu.make_async_copy(
                    source.at[:, g], kv_room.at[g, k], load.at[g * n_ctx + k]
                )
                copy.start()
                loads[g].append(copy)
        kept = []
        for g in range(per):
            at = per * n_ctx + 2 * g
            first = pltpu.make_async_copy(acts_ref.at[g, 0], act_room.at[g], load.at[at])
            first.start()
            second = pltpu.make_async_copy(
                act_room.at[g], out_ref.at[z * per + g], load.at[at + 1]
            )
            kept.append((first, second))
        mover.greet()
        dealt = []
        for g in range(per):
            for s in range(1, n_fsdp):
                to = lax.rem(z - s + n_fsdp, n_fsdp)
                dealt.append(
                    mover.go(acts_ref.at[g, s], out_ref.at[z * per + g], {"fsdp": to})
                )
        flying = {}

        def compute(u):
            g, c = units[u]
            if c == 0:
                for copy in loads[g]:
                    copy.wait()

            def one(h, carry):
                at = ds(c * columns + h * HEAD_DIM, HEAD_DIM)
                to = ds(h * HEAD_DIM, HEAD_DIM)
                biases = []
                for k in range(n_ctx):
                    block = bias_ref[g, k * loc : (k + 1) * loc, :]
                    biases.append(jnp.concatenate([block] * (loc // 128), axis=1))
                dquery, dkeys, dvalues = attend_back_head(
                    q_ref[g, :, at],
                    g_ref[g, :, at],
                    log_ref[g, c * high + h],
                    [kv_room[g, k, 0, :, at] for k in range(n_ctx)],
                    [kv_room[g, k, 1, :, at] for k in range(n_ctx)],
                    biases,
                )
                dq_ref[g, :, at] = dquery
                for k in range(n_ctx):
                    own[u, k, 0, :, to] = dkeys[k]
                    own[u, k, 1, :, to] = dvalues[k]
                return carry

            lax.fori_loop(0, high, one, 0)

        def hand(u, level):
            half = 2**level
            device = {"ctx": flip(ct, masks[level])}
            flying[u, level] = [
                mover.go(own.at[u, half + i], came.at[u, half - 1 + i], device) for i in range(half)
            ]

        def take_in(u, level):
            half = 2**level
            for i, copy in enumerate(flying[u, level]):
                copy.wait_recv()
                for j in range(2):
                    total = own[u, i, j].astype(F32) + came[u, half - 1 + i, j].astype(F32)
                    if level:
                        own[u, i, j] = total.astype(BF16)
                    else:
                        g, c = units[u]
                        dkv_ref[j, g, :, c * columns : (c + 1) * columns] = total.astype(BF16)

        last = len(masks) - 1
        for t in range(len(units) + last + 1):
            if t < len(units):
                compute(t)
                hand(t, last)
            if t == 0:
                for first, second in kept:
                    first.wait()
                    second.start()
            for k in range(last + 1):
                u, level = t - 1 - k, last - k
                if 0 <= u < len(units):
                    take_in(u, level)
                    if level:
                        hand(u, level - 1)
        for _, second in kept:
            second.wait()
        for copy in dealt:
            copy.wait_recv()
        mover.close()

    vmem, anywhere = pl.BlockSpec(memory_space=pltpu.VMEM), pl.BlockSpec(memory_space=pl.ANY)
    return pl.pallas_call(
        kernel,
        in_specs=[vmem] * 4 + [anywhere] * (1 + n_ctx),
        out_specs=[vmem, vmem, anywhere],
        out_shape=[
            jax.ShapeDtypeStruct(query.shape, BF16),
            jax.ShapeDtypeStruct(kv_own.shape, BF16),
            jax.ShapeDtypeStruct((per * n_fsdp, piece, width), BF16),
        ],
        scratch_shapes=[
            pltpu.SemaphoreType.DMA((n_copy,)),
            pltpu.SemaphoreType.DMA((n_copy,)),
            pltpu.SemaphoreType.DMA((per * (n_ctx + 2),)),
            pltpu.VMEM((per, n_ctx, 2, loc, width_here), BF16),
            pltpu.VMEM((len(units), n_ctx, 2, loc, columns), BF16),
            pltpu.VMEM((len(units), n_ctx - 1, 2, loc, columns), BF16),
            pltpu.VMEM((per, piece, width), BF16),
        ],
        compiler_params=pltpu.CompilerParams(
            collective_id=2, has_side_effects=True, vmem_limit_bytes=56 << 20
        ),
    )(query, bias, grad, log_total, acts, kv_own, *slots)


class Ring:
    def __init__(self, room, sems, at, tile_at):
        self.room, self.sems, self.at, self.tile_at = room, sems, at, tile_at

    def copy(self, t):
        slot = lax.rem(t, 2)
        return pltpu.make_async_copy(
            self.tile_at(t), self.room.at[slot], self.sems.at[self.at + slot]
        )

    def prefetch(self):
        self.copy(0).start()
        self.copy(1).start()

    def run(self, n, body, first=0, total=None):
        total = n if total is None else total

        def step(t, carry):
            self.copy(t).wait()
            body(t, self.room.at[lax.rem(t, 2)])

            @pl.when(t + 2 < total)
            def _():
                self.copy(t + 2).start()

            return carry

        lax.fori_loop(first, n, step, 0)


def norm_parts(values):
    center = values - jnp.mean(values, axis=-1, keepdims=True)
    rstd = lax.rsqrt(jnp.mean(center * center, axis=-1, keepdims=True) + NORM_EPS)
    return center * rstd, rstd


def norm_back(hat, rstd, dhat):
    first = jnp.mean(dhat, axis=-1, keepdims=True)
    second = jnp.mean(dhat * hat, axis=-1, keepdims=True)
    return rstd * (dhat - first - hat * second)


def gelu_both(pre):
    square = pre * pre
    bent = jnp.tanh(GELU_COEF * (pre + 0.044715 * square * pre))
    out = 0.5 * pre * (1.0 + bent)
    slope = 0.5 * (1.0 + bent) + 0.5 * pre * (1.0 - bent * bent) * GELU_COEF * (
        1.0 + 3.0 * 0.044715 * square
    )
    return out.astype(BF16), slope.astype(BF16)


def middle(x_all, part_out, other_out, cot, picked, gain, shift_by, weights, maps, n_fsdp, n_ctx):
    per, loc, width = x_all.shape
    out_x, up_x, down_x = weights
    a_up, b_out, b_down, a_down, b_up = maps
    wide, units = up_x.shape
    width_here = out_x.shape[0]
    tile = 512
    chunk = 32
    n_wide = width // tile
    n_swap = n_wide + 1

    def kernel(*refs):
        pick_ref, gain_ref, shift_ref, a_up_ref, b_out_ref, b_down_ref, a_down_ref, b_up_ref = refs[:8]
        x_ref, first_ref, second_ref, cot_ref, out_ref, up_ref, down_ref = refs[8:15]
        h_out, gelu_out, acts_out, dd_out, dpre_out, dy1_out, da_out, cot_rows = refs[15:23]
        adapt_out_ref, adapt_down_ref, dadapt_up_ref, ctx_ref = refs[23:27]
        (send, recv, deal_send, deal_recv, ring_sem, sems) = refs[27:33]
        (up_room, down_room, down_rows, up_rows) = refs[33:37]
        (stage, part, got, hat1, rstd1, keep32, slope, gelu, wide_v, turned, dpre_t) = refs[37:]
        mover = Mover(n_fsdp, n_ctx, deal_send, deal_recv)
        partner = {"tp": 1 - lax.axis_index("tp")}

        up = Ring(up_room, ring_sem, 0, lambda t: up_ref.at[:, ds(t * tile, tile)])
        down = Ring(down_room, ring_sem, 2, lambda t: down_ref.at[:, ds(t * tile, tile)])
        down_r = Ring(down_rows, ring_sem, 4, lambda t: down_ref.at[ds(t * tile, tile)])
        up_r = Ring(up_rows, ring_sem, 6, lambda t: up_ref.at[ds(t * tile, tile)])
        out_r = Ring(down_rows, ring_sem, 4, lambda t: out_ref.at[ds(t * tile, tile)])

        busy = {}
        used = [0]

        def move(source, target, key):
            copy = pltpu.make_async_copy(source, target, sems.at[used[0]])
            used[0] += 1
            copy.start()
            busy.setdefault(key, []).append(copy)

        def free(*keys):
            for key in keys:
                for copy in busy.pop(key, []):
                    copy.wait()

        def swap_copy(turn, g, t, size):
            at = ds(t * tile, size)
            sem = (turn * per + g) * n_swap + t
            return pltpu.make_async_remote_copy(
                src_ref=part.at[g, :, at],
                dst_ref=got.at[turn, g, :, at],
                send_sem=send.at[sem],
                recv_sem=recv.at[sem],
                device_id=partner,
                device_id_type=pl.DeviceIdType.MESH,
            )

        def swapped(turn, g):
            for t in range(n_swap):
                copy = swap_copy(turn, g, t, tile if t < n_wide else NR)
                copy.wait_recv()
                copy.wait_send()

        def by_rows(body):
            def step(r, carry):
                body(pl.ds(pl.multiple_of(r * chunk, chunk), chunk))
                return carry

            lax.fori_loop(0, loc // chunk, step, 0)

        def deal(g):
            return Deal(lambda to: cot_ref.at[to * per + g], lambda s: cot_rows.at[g, s])

        deals = [deal(g) for g in range(per)]
        for g in range(per):
            move(x_ref.at[g], stage.at[g], ("stage", g))
            move(cot_ref.at[mover.z * per + g], cot_rows.at[g, 0], ("cot", g))
            move(first_ref.at[g], part.at[g], ("part", g))
            move(second_ref.at[g], slope.at[g, :, pl.ds(0, wide)], ("slope", g))
        up.prefetch()
        down.prefetch()
        mover.greet(tp=True)
        for item in deals:
            mover.begin(item)

        for g in range(per):
            free(("stage", g), ("part", g), ("slope", g), "wide", "gelu")
            pick = pick_ref[g]

            def first_norm(rows, g=g, pick=pick):
                total = part[g, rows, :].astype(F32) + slope[g, rows, :wide].astype(F32)
                code = (total[:, width:] * pick).astype(BF16)
                adapt_out_ref[g, rows, :] = code
                y1 = stage[g, rows, :].astype(F32) + total[:, :width] + dot(code, b_out_ref[...])
                hat, rstd = norm_parts(y1)
                hat1[g, rows, :] = hat
                rstd1[g, rows, :] = jnp.broadcast_to(rstd, (chunk, 128))
                low = (hat * gain_ref[0:1, :] + shift_ref[0:1, :]).astype(BF16)
                wide_v[rows, :width] = low
                wide_v[rows, width:] = (dot(low, a_up_ref[...]) * pick).astype(BF16)

            by_rows(first_norm)
            move(wide_v, h_out.at[g], "wide")

            def up_tile(t, room, g=g):
                at = ds(t * tile, tile)
                value, factor = gelu_both(dot(wide_v[...], room[...]))
                gelu[:, at] = value
                slope[g, :, at] = factor

            up.run(units // tile, up_tile)
            if g + 1 < per:
                up.prefetch()
            else:
                down_r.prefetch()
            move(gelu, gelu_out.at[g], "gelu")

            def down_tile(t, room, g=g):
                part[g, :, ds(t * tile, tile)] = dot(gelu[...], room[...]).astype(BF16)
                swap_copy(0, g, t, tile).start()

            down.run(n_wide, down_tile)
            if g + 1 < per:
                down.prefetch()
            else:
                up_r.prefetch()
            part[g, :, width:] = dot(gelu[...], a_down_ref[...]).astype(BF16)
            swap_copy(0, g, n_wide, NR).start()

        for g in range(per):
            mover.relay(deals[g])
            free(("cot", g))
            for s in range(n_fsdp):
                at = pl.ds(s * cot.shape[1], cot.shape[1])
                move(cot_rows.at[g, s], stage.at[g, at], ("stage", g))
            swapped(0, g)
            free(("stage", g), "wide")
            pick = pick_ref[g]

            def second_norm(rows, g=g, pick=pick):
                total = part[g, rows, :].astype(F32) + got[0, g, rows, :].astype(F32)
                code = (total[:, width:] * pick).astype(BF16)
                adapt_down_ref[g, rows, :] = code
                hidden = hat1[g, rows, :] * gain_ref[0:1, :] + shift_ref[0:1, :]
                hat, rstd = norm_parts(hidden + total[:, :width] + dot(code, b_down_ref[...]))
                part[g, rows, :width] = (hat * gain_ref[1:2, :] + shift_ref[1:2, :]).astype(BF16)
                dy2 = norm_back(hat, rstd, stage[g, rows, :].astype(F32) * gain_ref[1:2, :])
                keep32[g, rows, :] = dy2
                low = dy2.astype(BF16)
                wide_v[rows, :width] = low
                wide_v[rows, width:] = (dot_nt(low, b_down_ref[...]) * pick).astype(BF16)

            by_rows(second_norm)
            move(part.at[g, :, pl.ds(0, width)], acts_out.at[g], ("part", g))
            move(wide_v, dd_out.at[g], "wide")
            turned[...] = wide_v[...].T

            def down_back(t, room, g=g):
                at = ds(t * tile, tile)
                block = dot(room[...], turned[...]).T
                low = (block * slope[g, :, at].astype(F32)).astype(BF16)
                slope[g, :, at] = low
                dpre_t[at, :] = low.T

            down_r.run(units // tile, down_back)
            (down_r if g + 1 < per else out_r).prefetch()
            move(slope.at[g], dpre_out.at[g], ("slope", g))
            free(("part", g))

            def up_back(t, room, g=g):
                part[g, :, ds(t * tile, tile)] = dot(room[...], dpre_t[...]).T.astype(BF16)
                swap_copy(1, g, t, tile).start()

            up_r.run(n_wide, up_back)
            if g + 1 < per:
                up_r.prefetch()
            part[g, :, width:] = dot(b_up_ref[...], dpre_t[...]).T.astype(BF16)
            swap_copy(1, g, n_wide, NR).start()

        for g in range(per):
            swapped(1, g)
            free("wide")
            pick = pick_ref[g]

            def first_back(rows, g=g, pick=pick):
                total = part[g, rows, :].astype(F32) + got[1, g, rows, :].astype(F32)
                code = (total[:, width:] * pick).astype(BF16)
                dadapt_up_ref[g, rows, :] = code
                dh1 = keep32[g, rows, :] + total[:, :width] + dot_nt(code, a_up_ref[...])
                rstd = rstd1[g, rows, 0:1]
                dy1 = norm_back(hat1[g, rows, :], rstd, dh1 * gain_ref[0:1, :])
                keep32[g, rows, :] = dy1
                low = dy1.astype(BF16)
                wide_v[rows, :width] = low
                wide_v[rows, width:] = (dot_nt(low, b_out_ref[...]) * pick).astype(BF16)

            by_rows(first_back)
            move(keep32.at[g], dy1_out.at[g], "dy1")
            move(wide_v, da_out.at[g], "wide")
            turned[...] = wide_v[...].T

            def out_back(t, room, g=g):
                ctx_ref[g, :, ds(t * tile, tile)] = dot(room[...], turned[...]).T.astype(BF16)

            out_r.run(width_here // tile, out_back)
            if g + 1 < per:
                out_r.prefetch()
        free(*list(busy))
        mover.close()

    vmem, anywhere = pl.BlockSpec(memory_space=pltpu.VMEM), pl.BlockSpec(memory_space=pl.ANY)
    row = (per, loc)
    outputs = [
        (row + (wide,), BF16, anywhere),
        (row + (units,), BF16, anywhere),
        (row + (width,), BF16, anywhere),
        (row + (wide,), BF16, anywhere),
        (row + (units,), BF16, anywhere),
        (row + (width,), F32, anywhere),
        (row + (wide,), BF16, anywhere),
        ((per, n_fsdp) + cot.shape[1:], BF16, anywhere),
        (row + (NR,), BF16, vmem),
        (row + (NR,), BF16, vmem),
        (row + (NR,), BF16, vmem),
        (row + (width_here,), BF16, vmem),
    ]
    n_copy = 2 * per * n_swap
    return pl.pallas_call(
        kernel,
        in_specs=[vmem] * 8 + [anywhere] * 7,
        out_specs=[space for _, _, space in outputs],
        out_shape=[jax.ShapeDtypeStruct(shape, dtype) for shape, dtype, _ in outputs],
        scratch_shapes=[
            pltpu.SemaphoreType.DMA((n_copy,)),
            pltpu.SemaphoreType.DMA((n_copy,)),
            pltpu.SemaphoreType.DMA((per * (n_fsdp - 1),)),
            pltpu.SemaphoreType.DMA((per * (n_fsdp - 1),)),
            pltpu.SemaphoreType.DMA((8,)),
            pltpu.SemaphoreType.DMA(((11 + n_fsdp) * per,)),
            pltpu.VMEM((2, wide, tile), BF16),
            pltpu.VMEM((2, units, tile), BF16),
            pltpu.VMEM((2, tile, wide), BF16),
            pltpu.VMEM((2, tile, units), BF16),
            pltpu.VMEM(row + (width,), BF16),
            pltpu.VMEM(row + (wide,), BF16),
            pltpu.VMEM((2,) + row + (wide,), BF16),
            pltpu.VMEM(row + (width,), F32),
            pltpu.VMEM(row + (128,), F32),
            pltpu.VMEM(row + (width,), F32),
            pltpu.VMEM(row + (units,), BF16),
            pltpu.VMEM((loc, units), BF16),
            pltpu.VMEM((loc, wide), BF16),
            pltpu.VMEM((wide, loc), BF16),
            pltpu.VMEM((units, loc), BF16),
        ],
        compiler_params=pltpu.CompilerParams(
            collective_id=3, has_side_effects=True, vmem_limit_bytes=62 << 20
        ),
    )(
        picked, gain, shift_by, a_up, b_out, b_down, a_down, b_up,
        x_all, part_out, other_out, cot, out_x, up_x, down_x,
    )


def combine(pieces, chosen, shapes):
    n_part, n_fsdp = pieces.shape[:2]
    flat = []
    for i, shape in enumerate(shapes):
        for lead in range(shape[0] if len(shape) == 3 else 1):
            flat.append((i, lead if len(shape) == 3 else None, shape[-2:]))

    def kernel(chosen_ref, piece_ref, *outs):
        for part in range(n_part):
            ordered = jnp.concatenate([piece_ref[part, a] for a in range(n_fsdp)], axis=0)
            start = 0
            for i, lead, (high, wide) in flat:
                out_ref = outs[i] if lead is None else outs[i].at[lead]
                tall = wide == NR and high != NR
                size = (high if tall else wide) // n_part
                block = ordered[:, start : start + size]
                at = slice(part * size, (part + 1) * size)
                if tall:
                    out_ref[at, :] = dot_tn(block, chosen_ref[...])
                else:
                    out_ref[:, at] = dot_tn(chosen_ref[...], block)
                start += size

    vmem = pl.BlockSpec(memory_space=pltpu.VMEM)
    return pl.pallas_call(
        kernel,
        in_specs=[vmem, vmem],
        out_specs=[vmem] * len(shapes),
        out_shape=[jax.ShapeDtypeStruct(shape, F32) for shape in shapes],
        compiler_params=pltpu.CompilerParams(vmem_limit_bytes=48 << 20),
    )(chosen, pieces)


def last(d_query, d_pair, x_all, adapt_all, dy1, qkv_x, a_qkv, picked, early, pairs, n_fsdp, n_ctx):
    per, loc, width_here = d_query.shape
    piece, width = loc // n_fsdp, x_all.shape[2]
    depth = 3 * width_here
    foot = 3 * NR
    wide = width + foot
    tile, chunk = 512, 32
    n_wide = width // tile
    n_swap = n_wide + 1
    n_early = len(early)
    early_sizes = [values[2] // n_ctx for _, values in pairs] + [width_here // n_ctx] * 3
    late_sizes = [width // n_ctx] * 3
    gathers = 2
    n_copy = per * (n_fsdp - 1) + gathers * ((n_fsdp - 1) * n_ctx + 2 * (n_ctx - 1))

    def kernel(*refs):
        dq_ref, dkv_ref, x_ref, adapt_ref, a_ref, pick_ref = refs[:6]
        dy1_ref, w_ref = refs[6:8]
        early_refs = refs[8 : 8 + n_early]
        in_ref, early_out, late_out = refs[8 + n_early : 11 + n_early]
        send, recv, swap_send, swap_recv, ring_sem, sems = refs[11 + n_early : 17 + n_early]
        rows_room, foot_room, dy1_room, turned, part, got, codes_in, dx = refs[
            17 + n_early : 25 + n_early
        ]
        early_part, early_came, late_part, late_came = refs[25 + n_early : 29 + n_early]
        staged = refs[29 + n_early :]
        mover = Mover(n_fsdp, n_ctx, send, recv)
        z, ct, masks = mover.z, mover.ct, mover.masks
        partner = {"tp": 1 - lax.axis_index("tp")}
        ring = Ring(rows_room, ring_sem, 0, lambda t: w_ref.at[ds(t * tile, tile)])
        used = [0]

        def move(source, target):
            copy = pltpu.make_async_copy(source, target, sems.at[used[0]])
            used[0] += 1
            copy.start()
            return copy

        def swap_copy(g, t, size):
            at = ds(t * tile, tile) if size == tile else pl.ds(width, size)
            sem = g * n_swap + t
            return pltpu.make_async_remote_copy(
                src_ref=part.at[g, :, at],
                dst_ref=got.at[g, :, at],
                send_sem=swap_send.at[sem],
                recv_sem=swap_recv.at[sem],
                device_id=partner,
                device_id_type=pl.DeviceIdType.MESH,
            )

        def compact(out_ref, n, entries, sizes):
            column = lax.broadcasted_iota(jnp.int32, (NR, RANK), 0)
            rank = lax.broadcasted_iota(jnp.int32, (NR, RANK), 1)
            used_columns = jnp.where(lax.rem(column, RANK) == rank, 1.0, 0.0).astype(BF16)
            start = 0
            for (code, value), size in zip(entries, sizes):
                short = dot(code(), used_columns).astype(BF16)
                block = dot_tn(short, value()).astype(BF16)
                for k in range(n_ctx):
                    out_ref[k, n * RANK : (n + 1) * RANK, start : start + size] = block[
                        :, k * size : (k + 1) * size
                    ]
                start += size

        class Fold:
            def __init__(self, parts, came):
                self.parts, self.came, self.flying = parts, came, {}

            def at(self, k):
                return flip(ct, mover.offsets[k])

            def hand(self, level):
                half = 2**level
                self.flying[level] = [
                    mover.go(
                        self.parts.at[self.at(half + i)],
                        self.came.at[half - 1 + i],
                        {"ctx": flip(ct, masks[level])},
                    )
                    for i in range(half)
                ]

            def take(self, level):
                for i, copy in enumerate(self.flying[level]):
                    copy.wait_recv()
                    total = self.parts[self.at(i)].astype(F32) + self.came[2**level - 1 + i].astype(F32)
                    self.parts[self.at(i)] = total.astype(BF16)

        lasting = len(masks) - 1
        load_foot = move(w_ref.at[pl.ds(width, foot)], foot_room)
        ring.prefetch()
        loads = [move(ref, room) for ref, room in zip(early_refs, staged)]
        load_dy1 = move(dy1_ref, dy1_room)
        mover.greet(tp=True)
        folds = [Fold(early_part, early_came), Fold(late_part, late_came)]
        for g in range(per):
            turned[0:width_here, :] = dq_ref[g].T
            turned[width_here : 2 * width_here, :] = dkv_ref[0, g].T
            turned[2 * width_here :, :] = dkv_ref[1, g].T
            if g == 0:
                load_foot.wait()
            part[g, :, width:] = dot(foot_room[...], turned[...]).T.astype(BF16)
            swap_copy(g, n_wide, foot).start()

            def back(t, room, g=g):
                part[g, :, ds(t * tile, tile)] = dot(room[...], turned[...]).T.astype(BF16)
                swap_copy(g, t, tile).start()

            ring.run(n_wide, back)
            if g + 1 < per:
                ring.prefetch()
            if g == 0:
                for copy in loads:
                    copy.wait()
                for n in range(per):
                    entries = []
                    for (i, first, size), (j, start, count) in pairs:
                        entries.append(
                            (
                                lambda n=n, i=i, f=first, c=size: staged[i][n, :, f : f + c],
                                lambda n=n, i=j, f=start, c=count: staged[i][n, :, f : f + c],
                            )
                        )
                    values = [
                        lambda n=n: dq_ref[n],
                        lambda n=n: dkv_ref[0, n],
                        lambda n=n: dkv_ref[1, n],
                    ]
                    for j in range(3):
                        entries.append(
                            (lambda n=n, j=j: adapt_ref[n, :, j * NR : (j + 1) * NR], values[j])
                        )
                    compact(early_part, n, entries, early_sizes)
                folds[0].hand(lasting)
        for level in range(lasting, -1, -1):
            folds[0].take(level)
            if level:
                folds[0].hand(level - 1)

        def gather(parts, out_ref):
            own = parts.at[ct]
            kept.append(move(own, out_ref.at[ct, z]))
            item = Weight(lambda c: parts.at[c], lambda o, c: out_ref.at[c, o], own)
            mover.begin(item)
            return item

        kept = []
        first = gather(early_part, early_out)
        load_dy1.wait()
        dealt = []

        def finish_rows(g):
            for t in range(n_swap):
                copy = swap_copy(g, t, tile if t < n_wide else foot)
                copy.wait_recv()
                copy.wait_send()
            pick = jnp.concatenate([pick_ref[g]] * 3, axis=1)

            def step(r, carry):
                rows = ds(r * chunk, chunk)
                total = part[g, rows, :].astype(F32) + got[g, rows, :].astype(F32)
                code = (total[:, width:] * pick).astype(BF16)
                codes_in[g, rows, :] = code
                value = dy1_room[g, rows, :] + total[:, :width]
                for j in range(3):
                    value = value + dot_nt(code[:, j * NR : (j + 1) * NR], a_ref[j])
                dx[g, rows, :] = value.astype(BF16)
                return carry

            lax.fori_loop(0, loc // chunk, step, 0)
            kept.append(move(dx.at[g, pl.ds(0, piece)], in_ref.at[z * per + g]))
            for s in range(1, n_fsdp):
                to = lax.rem(z - s + n_fsdp, n_fsdp)
                dealt.append(
                    mover.go(
                        dx.at[g, pl.ds(s * piece, piece)], in_ref.at[z * per + g], {"fsdp": to}
                    )
                )

        for g in range(per):
            finish_rows(g)
            if g == 0:
                mover.relay(first)
        for n in range(per):
            entries = []
            for j in range(3):
                entries.append(
                    (
                        lambda n=n, j=j: codes_in[n, :, j * NR : (j + 1) * NR],
                        lambda n=n: x_ref[n],
                    )
                )
            compact(late_part, n, entries, late_sizes)
        folds[1].hand(lasting)
        for level in range(lasting, -1, -1):
            folds[1].take(level)
            if level:
                folds[1].hand(level - 1)
        second = gather(late_part, late_out)
        for level in range(len(masks)):
            mover.finish(first, level)
        mover.relay(second)
        for level in range(len(masks)):
            mover.finish(second, level)
        for copy in dealt:
            copy.wait_recv()
        for copy in kept:
            copy.wait()
        mover.close()

    vmem, anywhere = pl.BlockSpec(memory_space=pltpu.VMEM), pl.BlockSpec(memory_space=pl.ANY)
    parts = [(n_ctx, per * RANK, sum(early_sizes)), (n_ctx, per * RANK, sum(late_sizes))]
    rooms = [
        ((2, tile, depth), BF16),
        ((foot, depth), BF16),
        (dy1.shape, F32),
        ((depth, loc), BF16),
        ((per, loc, wide), BF16),
        ((per, loc, wide), BF16),
        ((per, loc, foot), BF16),
        ((per, loc, width), BF16),
    ]
    for shape in parts:
        rooms += [(shape, BF16), ((n_ctx - 1,) + shape[1:], BF16)]
    rooms += [(x.shape, BF16) for x in early]
    return pl.pallas_call(
        kernel,
        in_specs=[vmem] * 6 + [anywhere] * (2 + n_early),
        out_specs=[anywhere] * 3,
        out_shape=[jax.ShapeDtypeStruct((per * n_fsdp, piece, width), BF16)]
        + [jax.ShapeDtypeStruct((n_ctx, n_fsdp) + shape[1:], BF16) for shape in parts],
        scratch_shapes=[
            pltpu.SemaphoreType.DMA((n_copy,)),
            pltpu.SemaphoreType.DMA((n_copy,)),
            pltpu.SemaphoreType.DMA((per * n_swap,)),
            pltpu.SemaphoreType.DMA((per * n_swap,)),
            pltpu.SemaphoreType.DMA((2,)),
            pltpu.SemaphoreType.DMA((4 + n_early + per,)),
        ]
        + [pltpu.VMEM(shape, dtype) for shape, dtype in rooms],
        compiler_params=pltpu.CompilerParams(
            collective_id=4, has_side_effects=True, vmem_limit_bytes=60 << 20
        ),
    )(d_query, d_pair, x_all, adapt_all, a_qkv, picked, dy1, qkv_x, *early)


def gelu_both(pre):
    square = pre * pre
    bent = jnp.tanh(GELU_COEF * (pre + 0.044715 * square * pre))
    out = 0.5 * pre * (1.0 + bent)
    slope = 0.5 * (1.0 + bent) + 0.5 * pre * (1.0 - bent * bent) * GELU_COEF * (
        1.0 + 3.0 * 0.044715 * square
    )
    return out.astype(BF16), slope.astype(BF16)


def local(
    x_in,
    cotangent,
    lengths,
    adapter_ids,
    w_qkv,
    w_out,
    w_up,
    w_down,
    ln_gain,
    ln_bias,
    a_qkv,
    b_qkv,
    a_out,
    b_out,
    a_up,
    b_up,
    a_down,
    b_down,
):
    n_ctx, n_fsdp = lax.axis_size("ctx"), lax.axis_size("fsdp")
    z, ct = lax.axis_index("fsdp"), lax.axis_index("ctx")
    seqs, piece, width = x_in.shape
    per = seqs // n_fsdp
    loc = n_fsdp * piece
    heads_width = w_qkv.shape[2]
    def take(array, start, size, axis=0):
        return lax.dynamic_slice_in_dim(array, start, size, axis)

    units = w_up.shape[1]
    rows_shape = (per, n_fsdp, piece, width)
    zq = w_qkv.shape[1]

    def first_items(ins, outs, z):
        x_ref, w_ref = ins
        rows_ref, whole_ref = outs

        def deal(g):
            return Deal(lambda to: x_ref.at[to * per + g], lambda s: rows_ref.at[g, s])

        def weight(j):
            size = zq // n_ctx
            columns = pl.ds(j * heads_width, heads_width)
            return Weight(
                lambda c: w_ref.at[j, pl.ds(pl.multiple_of(c * size, size), size)],
                lambda o, c: whole_ref.at[
                    pl.ds(pl.multiple_of(o * zq + c * size, size), size), columns
                ],
            )

        stay = [(x_ref.at[z * per + g], rows_ref.at[g, 0]) for g in range(per)]
        for j in range(3):
            own = whole_ref.at[
                pl.ds(pl.multiple_of(z * zq, zq), zq), pl.ds(j * heads_width, heads_width)
            ]
            stay.append((w_ref.at[j], own))
        items = [weight(j) for j in range(3)] + [deal(g) for g in range(per)]
        return items, stay

    x_all, qkv_x = move(
        first_items,
        [Weight] * 3 + [Deal] * per,
        (x_in, w_qkv),
        (rows_shape, (width + 3 * NR, 3 * heads_width)),
        n_fsdp,
        n_ctx,
        ((piece, width),) * per + (w_qkv.shape[1:],) * 3,
        0,
        foot=(b_qkv, lambda outs: outs[1].at[pl.ds(width, 3 * NR)]),
    )

    my_lengths = take(lengths, z * per, per)
    my_ids = take(adapter_ids, z * per, per)
    picked = (my_ids[:, None] == jnp.arange(NR)[None, :] // RANK).astype(F32)
    steps = lax.rem(z - jnp.arange(n_fsdp) + n_fsdp, n_fsdp)
    ctx_of = ct ^ jnp.array(offsets(n_ctx))
    key_pos = (
        (steps[None, :, None] * n_ctx + ctx_of[:, None, None]) * piece
        + jnp.arange(piece)[None, None, :]
    ).reshape(-1)
    bias_all = jnp.where(key_pos[None, :] < my_lengths[:, None], 0.0, -1e30).astype(F32)
    bias_all = jnp.broadcast_to(bias_all[:, :, None], bias_all.shape + (128,))

    picked = picked[:, None, :]
    x_rows = x_all.reshape(per, loc, width)
    moved = forward_and_gather(
        x_rows, qkv_x, a_qkv, picked, bias_all, (w_out, w_up, w_down), (a_out, b_up, a_down), n_fsdp, n_ctx
    )
    slots = moved[: n_ctx - 1]
    (query, kv_own, adapt_all, out_x, up_x, down_x, context, log_total, part_out, other_out) = moved[
        n_ctx - 1 :
    ]
    (
        wide_h, gelu_out, acts, wide_d, d_pre, dy1, wide_a, _, adapt_out, adapt_down, dadapt_up, d_context,
    ) = middle(
        x_rows,
        part_out,
        other_out,
        cotangent,
        picked,
        ln_gain,
        ln_bias,
        (out_x, up_x, down_x),
        (a_up, b_out, b_down, a_down, b_up),
        n_fsdp,
        n_ctx,
    )
    d_query, d_pair, activations = attend_back(
        query,
        kv_own,
        slots,
        bias_all,
        d_context,
        log_total,
        acts.reshape(per, n_fsdp, piece, width),
        n_fsdp,
        n_ctx,
    )
    code, row, unit = (0, NR), (0, width), (0, units)
    tail = (width, NR)
    early_pairs = [
        ((0,) + code, (1,) + row),
        ((1,) + tail, (2,) + unit),
        ((3,) + tail, (4,) + unit),
        ((5,) + code, (3,) + row),
        ((6,) + code, (7,) + row),
        ((7,) + tail, (8, 0, heads_width)),
    ]
    early_in = (
        adapt_down, wide_d, gelu_out, wide_h, d_pre, dadapt_up, adapt_out, wide_a, context,
    )
    input_grad, early, late = last(
        d_query,
        d_pair,
        x_rows,
        adapt_all,
        dy1,
        qkv_x,
        a_qkv,
        picked,
        early_in,
        early_pairs,
        n_fsdp,
        n_ctx,
    )
    codes = (adapter_ids[:, None] * RANK + jnp.arange(RANK)[None, :]).reshape(-1)
    chosen = (codes[:, None] == jnp.arange(NR)[None, :]).astype(BF16)
    e = combine(
        early,
        chosen,
        [
            (NR, width), (units, NR), (NR, units), (width, NR), (NR, width), (heads_width, NR),
            (3, NR, heads_width),
        ],
    )
    (a_qkv_grad,) = combine(late, chosen, [(3, width, NR)])
    return activations, input_grad, a_qkv_grad, e[6], e[5], e[4], e[3], e[2], e[1], e[0]


def solution(mesh):
    rows = P(None, ("fsdp", "ctx"), None)
    return jax.shard_map(
        local,
        mesh=mesh,
        in_specs=(
            rows,
            rows,
            P(),
            P(),
            P(None, "fsdp", "tp"),
            P("tp", "fsdp"),
            P("fsdp", "tp"),
            P("tp", "fsdp"),
            P(),
            P(),
            P(),
            P(None, None, "tp"),
            P("tp", None),
            P(),
            P(),
            P(None, "tp"),
            P("tp", None),
            P(),
        ),
        out_specs=(
            rows,
            rows,
            P(),
            P(None, None, "tp"),
            P("tp", None),
            P(),
            P(),
            P(None, "tp"),
            P("tp", None),
            P(),
        ),
        check_vma=False,
    )
```

```python
import math

import jax
import jax.numpy as jnp
from jax import lax
from jax.experimental import pallas as pl
from jax.experimental.pallas import tpu as pltpu
from jax.sharding import PartitionSpec as P

HEAD_DIM = 128
RANK = 16
ADAPTERS = 8
NR = RANK * ADAPTERS
NORM_EPS = 1e-06
GELU_COEF = 0.7978845608028654
SCALE = 1.0 / math.sqrt(HEAD_DIM)
F32 = jnp.float32
BF16 = jnp.bfloat16


def dot(left, right):
    return jnp.dot(left, right, preferred_element_type=F32)


def dot_nt(left, right):
    return lax.dot_general(left, right, (((1,), (1,)), ((), ())), preferred_element_type=F32)


def dot_tn(left, right):
    return lax.dot_general(left, right, (((0,), (0,)), ((), ())), preferred_element_type=F32)


def masks_of(n):
    out = []
    while n > 1:
        n //= 2
        out.append(n)
    return out


def offsets(n):
    out = [0]
    for mask in masks_of(n):
        out = out + [o ^ mask for o in out]
    return out


def attend_head(query, keys, values, biases):
    scores = [dot_nt(k, query) * SCALE + bias for k, bias in zip(keys, biases)]
    top = scores[0].max(axis=0, keepdims=True)
    for s in scores[1:]:
        top = jnp.maximum(top, s.max(axis=0, keepdims=True))
    total = jnp.zeros_like(top)
    mixed = None
    for s, v in zip(scores, values):
        probs = jnp.exp(s - top)
        total = total + probs.sum(axis=0, keepdims=True)
        term = dot_tn(v, probs.astype(BF16))
        mixed = term if mixed is None else mixed + term
    return (mixed / total).T.astype(BF16), top + jnp.log(total)


def attend_back_head(query, grad, log_total, keys, values, biases):
    probs, dprobs, dvalues = [], [], []
    delta = jnp.zeros_like(log_total)
    for k, v, bias in zip(keys, values, biases):
        p = jnp.exp(dot_nt(k, query) * SCALE + bias - log_total)
        dp = dot_nt(v, grad)
        dvalues.append(dot(p.astype(BF16), grad).astype(BF16))
        delta = delta + (p * dp).sum(axis=0, keepdims=True)
        probs.append(p)
        dprobs.append(dp)
    dquery, dkeys = None, []
    for k, p, dp in zip(keys, probs, dprobs):
        ds = (p * (dp - delta)).astype(BF16)
        dkeys.append((dot(ds, query) * SCALE).astype(BF16))
        term = dot_tn(k, ds)
        dquery = term if dquery is None else dquery + term
    return (dquery * SCALE).T.astype(BF16), dkeys, dvalues


def ds(start, size):
    return pl.ds(pl.multiple_of(start, size), size)


def flip(ct, offset):
    mask = 1
    while mask <= offset:
        if offset & mask:
            ct = ct + mask - 2 * mask * lax.rem(ct // mask, 2)
        mask *= 2
    return ct


class Weight:
    def __init__(self, shard_at, whole_at, own=None, skip=0):
        self.shard_at, self.whole_at, self.own, self.skip = shard_at, whole_at, own, skip


class Deal:
    def __init__(self, source_at, rows_at):
        self.source_at, self.rows_at = source_at, rows_at


class Pair:
    def __init__(self, slot_at):
        self.slot_at = slot_at


class Mover:
    def __init__(self, n_fsdp, n_ctx, send, recv):
        self.n_fsdp, self.n_ctx = n_fsdp, n_ctx
        self.z, self.ct = lax.axis_index("fsdp"), lax.axis_index("ctx")
        self.send, self.recv = send, recv
        self.used = 0
        self.open = []
        self.masks = masks_of(n_ctx)
        self.offsets = offsets(n_ctx)
        self.came, self.waiting, self.done = {}, {}, {}

    def skip(self, item):
        return item.skip if isinstance(item, Weight) else 0

    def part(self, item):
        return lax.rem(self.ct, self.n_ctx >> item.skip) if item.skip else self.ct

    def greet(self, tp=False):
        barrier = pltpu.get_barrier_semaphore()
        others = [{"fsdp": lax.rem(self.z + s, self.n_fsdp)} for s in range(1, self.n_fsdp)]
        others += [{"ctx": flip(self.ct, mask)} for mask in self.masks]
        if tp:
            others.append({"tp": 1 - lax.axis_index("tp")})
        for other in others:
            pl.semaphore_signal(
                barrier, inc=1, device_id=other, device_id_type=pl.DeviceIdType.MESH
            )
        pl.semaphore_wait(barrier, len(others))

    def copy(self, source, target, device, at=None):
        if at is None:
            at = self.used
            self.used += 1
        return pltpu.make_async_remote_copy(
            src_ref=source,
            dst_ref=target,
            send_sem=self.send.at[at],
            recv_sem=self.recv.at[at],
            device_id=device,
            device_id_type=pl.DeviceIdType.MESH,
        )

    def go(self, source, target, device):
        copy = self.copy(source, target, device)
        copy.start()
        self.open.append((None, copy))
        return copy

    def along(self, item, owner, right, ok, source, slot):
        target = item.whole_at(owner, self.part(item))
        device = {"fsdp": lax.rem(self.z + (1 if right else self.n_fsdp - 1), self.n_fsdp)}
        copy = self.copy(source, target, device, self.came[item] + slot - 1)
        pl.when(ok)(copy.start)
        self.open.append((ok, copy))

    def begin(self, item):
        if isinstance(item, Pair):
            self.waiting[item] = [[] for _ in self.masks]
            self.cast(item, item.slot_at, lambda k, level: item.slot_at(k + 2**level), 0, 0)
            return
        if isinstance(item, Weight):
            self.came[item] = self.used
            self.used += self.n_fsdp - 1
            source = item.shard_at(self.part(item))
            self.along(item, self.z, True, self.z < self.n_fsdp - 1, source, 1)
            self.along(item, self.z, False, self.z > 0, source, self.n_fsdp - 1)
            return
        self.came[item] = [
            self.go(
                item.source_at(lax.rem(self.z + s, self.n_fsdp)),
                item.rows_at(s),
                {"fsdp": lax.rem(self.z + s, self.n_fsdp)},
            )
            for s in range(1, self.n_fsdp)
        ]

    def cast(self, item, source_at, target_at, k, first):
        skip = self.skip(item)
        for level in range(first, len(self.masks) - skip):
            device = {"ctx": flip(self.ct, self.masks[level + skip])}
            copy = self.go(source_at(k), target_at(k, level), device)
            self.waiting[item][level].append((copy, k + 2**level, source_at, target_at))

    def relay(self, item):
        if isinstance(item, Deal):
            for copy in self.came[item]:
                copy.wait_recv()
            return
        self.waiting[item] = [[] for _ in self.masks[item.skip :]]
        n, part = self.n_fsdp, self.part(item)
        others = offsets(self.n_ctx >> item.skip)
        if item.own is not None:

            def mine(k):
                return item.own if k == 0 else item.whole_at(self.z, flip(part, others[k]))

            def lands(k, level):
                return item.whole_at(self.z, flip(part, others[k]))

            self.cast(item, mine, lands, 0, 0)
        for i in range(n - 1):
            s = i // 2 + 1 if i % 2 == 0 else n - 1 - i // 2
            owner = lax.rem(self.z - s + n, n)
            here = item.whole_at(owner, part)
            self.copy(here, here, {"fsdp": owner}, self.came[item] + s - 1).wait_recv()
            if s < n - 1:
                ok = (self.z >= s) & (self.z < n - 1)
                self.along(item, owner, True, ok, here, s + 1)
            if s > 1:
                ok = (self.z < s) & (self.z > 0)
                self.along(item, owner, False, ok, here, s - 1)

            def at(k, owner=owner):
                return item.whole_at(owner, flip(part, others[k]))

            self.cast(item, at, lambda k, level, at=at: at(k), 0, 0)

    def finish(self, item, level):
        if isinstance(item, Deal) or level != self.done.get(item, 0):
            return
        if level == len(self.waiting[item]):
            return
        for copy, k, source_at, target_at in self.waiting[item][level]:
            copy.wait_recv()
            self.cast(item, source_at, target_at, k, level + 1)
        self.done[item] = level + 1

    def complete(self, item):
        while self.done.get(item, 0) < len(self.waiting[item]):
            self.finish(item, self.done.get(item, 0))

    def close(self):
        for ok, copy in self.open:
            if ok is None:
                copy.wait_send()
            else:
                pl.when(ok)(copy.wait_send)


def copies_of(items, n_fsdp, n_ctx):
    total = 0
    for item in items:
        total += {Weight: (n_fsdp - 1) * n_ctx, Deal: n_fsdp - 1, Pair: n_ctx - 1}[item]
    return total


def keep(stay, room, sems):
    out = []
    for k, (source, target) in enumerate(stay):
        first = pltpu.make_async_copy(source, room[k], sems.at[2 * k])
        first.start()
        out.append((first, pltpu.make_async_copy(room[k], target, sems.at[2 * k + 1])))
    return out


def move(make, kinds, inputs, outputs, n_fsdp, n_ctx, local_shapes, ident, ahead=2, foot=None):
    n_in = len(inputs)
    n_copy = copies_of(kinds, n_fsdp, n_ctx)

    def kernel(*refs):
        ins, outs = refs[:n_in], refs[n_in : n_in + len(outputs)]
        send, recv, here = refs[n_in + len(outputs) : n_in + len(outputs) + 3]
        room = refs[n_in + len(outputs) + 3 :]
        if foot is not None:
            blocks_ref, ins = ins[-1], ins[:-1]
            strip = room[-1]
        mover = Mover(n_fsdp, n_ctx, send, recv)
        items, stay = make(ins, outs, mover.z)
        mover.greet()
        for item in items[:ahead]:
            mover.begin(item)
        kept = keep(stay, room, here)
        levels = len(mover.masks)
        for i in range(len(items) + levels):
            if i < len(items):
                mover.relay(items[i])
                if i + ahead < len(items):
                    mover.begin(items[i + ahead])
            if i == 0 and foot is not None:
                strip[...] = jnp.zeros_like(strip)
                high, wide = blocks_ref.shape[1:]
                for j in range(blocks_ref.shape[0]):
                    strip[j * high : (j + 1) * high, j * wide : (j + 1) * wide] = blocks_ref[j]
                set_foot = pltpu.make_async_copy(strip, foot[1](outs), here.at[2 * len(local_shapes)])
                set_foot.start()
                kept.append((None, set_foot))
            if i == 0:
                for first, second in kept:
                    if first is not None:
                        first.wait()
                        second.start()
            for level in range(levels):
                if 0 <= i - 1 - level < len(items):
                    mover.finish(items[i - 1 - level], level)
        for _, second in kept:
            second.wait()
        mover.close()

    spaces = [pl.BlockSpec(memory_space=pl.ANY)] * n_in
    room_shapes = list(local_shapes)
    if foot is not None:
        blocks = foot[0]
        inputs = inputs + (blocks,)
        n_in += 1
        spaces.append(pl.BlockSpec(memory_space=pltpu.VMEM))
        room_shapes.append((blocks.shape[0] * blocks.shape[1], blocks.shape[0] * blocks.shape[2]))
    return pl.pallas_call(
        kernel,
        in_specs=spaces,
        out_specs=[pl.BlockSpec(memory_space=pl.ANY)] * len(outputs),
        out_shape=[jax.ShapeDtypeStruct(shape, BF16) for shape in outputs],
        scratch_shapes=[
            pltpu.SemaphoreType.DMA((n_copy,)),
            pltpu.SemaphoreType.DMA((n_copy,)),
            pltpu.SemaphoreType.DMA((2 * len(local_shapes) + 1,)),
        ]
        + [pltpu.VMEM(shape, BF16) for shape in room_shapes],
        compiler_params=pltpu.CompilerParams(
            collective_id=ident, has_side_effects=True, vmem_limit_bytes=60 << 20
        ),
    )(*inputs)


def forward_and_gather(
    x_rows, qkv_x, a_qkv, picked, bias, gain, shift_by, first_maps, shards, maps, n_fsdp, n_ctx
):
    per, loc, width = x_rows.shape
    w_out, w_up, w_down = shards
    width_here = qkv_x.shape[1] // 3
    heads, units = width_here // HEAD_DIM, w_up.shape[1]
    zu, zo = w_up.shape[0], w_out.shape[1]
    n_part = n_ctx // 2 if n_ctx > 1 else 1
    so, su, sd = w_out.shape[0] // n_ctx, zu // n_ctx, w_down.shape[0] // n_ctx
    wide = width + NR
    wide_x = width + 3 * NR
    cuts = 4
    paired = cuts // 2 if n_ctx > 1 else 0
    tile = 512
    per_kind = width_here // tile
    chunk = 32
    n_tile = 3 * per_kind
    n_copy = (n_fsdp - 1) * n_ctx * (1 + 2 * cuts) + 2 * per * (n_ctx - 1) + 6 + per
    lag = 4

    def kernel(*refs):
        bias_ref, a_ref, pick_ref, gain_ref, shift_ref, a_up_ref, b_out_ref, x_ref, w_ref = refs[:9]
        wo_ref, wu_ref, wd_ref, ao_ref, bu_ref, ad_ref = refs[9:15]
        slots = refs[15 : 14 + n_ctx]
        q_ref, kv_ref, adapt_ref, out_ref, up_ref, down_ref, ctx_ref, log_ref = refs[
            14 + n_ctx : 22 + n_ctx
        ]
        h_ref, gelu_ref, slope_ref, hat_ref, rstd_ref, adapt_out_ref, adapt_up_ref = refs[
            22 + n_ctx : 29 + n_ctx
        ]
        send, recv, here, load, ring_sem, x_room, w_room, proj, kv_room, out_room = refs[
            29 + n_ctx : 39 + n_ctx
        ]
        part_ref, other_ref, up_room, wide_v, hat1, gelu, slope = refs[39 + n_ctx :]
        mover = Mover(n_fsdp, n_ctx, send, recv)
        ring = Ring(
            w_room,
            ring_sem,
            0,
            lambda t: w_ref.at[:, ds(lax.rem(t + per_kind, n_tile) * tile, tile)],
        )
        z = mover.z
        rows = [pl.ds(g * loc, loc) for g in range(per)]

        def columns(j):
            return pl.ds(j * width_here, width_here)

        out_item = Weight(
            lambda c: wo_ref.at[ds(c * so, so)],
            lambda o, c: out_ref.at[ds(c * so, so), ds(o * zo, zo)],
        )

        def up_item(h):
            at = pl.ds(h * (units // cuts), units // cuts)
            return Weight(
                lambda c: wu_ref.at[ds(c * su, su), at],
                lambda o, c: up_ref.at[ds(o * zu + c * su, su), at],
            )

        def down_item(h):
            size = sd // cuts
            return Weight(
                lambda c: wd_ref.at[ds(c * sd + h * size, size)],
                lambda o, c: down_ref.at[ds(c * sd + h * size, size), ds(o * zo, zo)],
            )

        def down_pair(h):
            size = sd // cuts

            def at(c, p):
                return ds((c + p * n_part) * sd + h * size, size)

            def half(p):
                return Weight(
                    lambda c: wd_ref.at[at(c, p)],
                    lambda o, c: down_ref.at[at(c, p), ds(o * zo, zo)],
                    skip=1,
                )

            return [half(p) for p in range(2)]

        def pair(g, j):
            return Pair(
                lambda k: proj.at[rows[g], columns(1 + j)] if k == 0 else slots[k - 1].at[j, g]
            )

        pairs = [pair(g, j) for g in range(per) for j in range(2)]
        items = [out_item] + [up_item(h) for h in range(cuts)]
        items += [down_item(h) for h in range(cuts - paired)]
        for h in range(cuts - paired, cuts):
            items += down_pair(h)
        used = [0]

        def move(source, target):
            copy = pltpu.make_async_copy(source, target, here.at[used[0]])
            used[0] += 1
            copy.start()
            return copy

        def attend(g):
            for j in range(2):
                mover.complete(pairs[2 * g + j])
            loads = []
            for k in range(1, n_ctx):
                copy = pltpu.make_async_copy(slots[k - 1].at[:, g], kv_room.at[k], load.at[k])
                copy.start()
                loads.append(copy)
            for j in range(2):
                kv_room[0, j] = proj[g * loc : (g + 1) * loc, (1 + j) * width_here : (2 + j) * width_here]
            for copy in loads:
                copy.wait()

            def one(h, carry):
                at = ds(h * HEAD_DIM, HEAD_DIM)
                biases = []
                for k in range(n_ctx):
                    block = bias_ref[g, k * loc : (k + 1) * loc, :]
                    biases.append(jnp.concatenate([block] * (loc // 128), axis=1))
                context, log = attend_head(
                    proj[g * loc : (g + 1) * loc, at],
                    [kv_room[k, 0, :, at] for k in range(n_ctx)],
                    [kv_room[k, 1, :, at] for k in range(n_ctx)],
                    biases,
                )
                ctx_ref[g, :, at] = context
                log_ref[g, h] = log
                return carry

            lax.fori_loop(0, heads, one, 0)

        def project():
            mover.complete(out_item)
            own[0].wait_recv()
            own[3].wait_recv()
            copy = pltpu.make_async_copy(out_ref, out_room, load.at[0])
            copy.start()
            copy.wait()
            for g in range(per):
                for start in range(0, wide, 1024):
                    at = slice(start, min(start + 1024, wide))
                    part_ref[g, :, at] = dot(ctx_ref[g], out_room[:, at]).astype(BF16)
                swapped.append(
                    mover.go(
                        part_ref.at[g], other_ref.at[g], {"tp": 1 - lax.axis_index("tp")}
                    )
                )

        def tiles(t, room):
            at = ds(lax.rem(t + per_kind, n_tile) * tile, tile)
            proj[:, at] = dot(x_room[...], room[...]).astype(BF16)

        up_ring = Ring(up_room, ring_sem, 2, lambda t: up_ref.at[:, ds(t * tile, tile)])

        def first_norm(g):
            swapped[g].wait_recv()
            pick = pick_ref[g]

            def step(r, carry):
                rows_r = ds(r * chunk, chunk)
                total = part_ref[g, rows_r, :].astype(F32) + other_ref[g, rows_r, :].astype(F32)
                code = (total[:, width:] * pick).astype(BF16)
                adapt_out_ref[g, rows_r, :] = code
                x = x_room[ds(g * loc + r * chunk, chunk), :width].astype(F32)
                hat, rstd = norm_parts(x + total[:, :width] + dot(code, b_out_ref[...]))
                hat1[g, rows_r, :] = hat
                rstd_ref[g, rows_r, :] = jnp.broadcast_to(rstd, (chunk, 128))
                low = (hat * gain_ref[0:1, :] + shift_ref[0:1, :]).astype(BF16)
                wide_v[g, rows_r, :width] = low
                code = (dot(low, a_up_ref[...]) * pick).astype(BF16)
                wide_v[g, rows_r, width:] = code
                adapt_up_ref[g, rows_r, :] = code
                return carry

            lax.fori_loop(0, loc // chunk, step, 0)
            outward.append(move(hat1.at[g], hat_ref.at[g]))
            outward.append(move(wide_v.at[g], h_ref.at[g]))

        def feed(g):
            if g == 0:
                for item in items[1 : 1 + cuts]:
                    mover.complete(item)
                own[1].wait_recv()
                own[4].wait_recv()
                up_ring.prefetch()

            def up_tile(t, room):
                at = ds(t * tile, tile)
                value, factor = gelu_both(dot(wide_v[g], room[...]))
                gelu[g, :, at] = value
                slope[g, :, at] = factor

            up_ring.run(units // tile, up_tile)
            if g + 1 < per:
                up_ring.prefetch()
            outward.append(move(gelu.at[g], gelu_ref.at[g]))
            outward.append(move(slope.at[g], slope_ref.at[g]))

        swapped, outward = [], []
        tasks = {1 + g: (lambda g=g: attend(g)) for g in range(per)}
        tasks[per + 2] = project
        tasks[per + 5] = lambda: [first_norm(g) for g in range(per)]
        for g in range(per):
            tasks[per + 6 + g] = lambda g=g: feed(g)
        ring.prefetch()
        loads = [move(x_ref.at[g], x_room.at[rows[g], pl.ds(0, width)]) for g in range(per)]
        mover.greet(tp=True)
        ahead = 3
        for item in items[:ahead]:
            mover.begin(item)
        sibling = {"ctx": flip(mover.ct, 1)}
        own = [
            mover.go(source, target, sibling)
            for source, target in (
                (wo_ref, out_ref.at[:, ds(z * zo, zo)]),
                (wu_ref, up_ref.at[ds(z * zu, zu)]),
                (wd_ref, down_ref.at[:, ds(z * zo, zo)]),
                (ao_ref, out_ref.at[:, pl.ds(width, NR)]),
                (bu_ref, up_ref.at[pl.ds(width, NR)]),
                (ad_ref, down_ref.at[:, pl.ds(width, NR)]),
            )
        ]
        for g in range(per):
            loads[g].wait()
            pick = pick_ref[g]
            for j in range(3):
                code = dot(x_room[g * loc : (g + 1) * loc, :width], a_ref[j]) * pick
                x_room[g * loc : (g + 1) * loc, width + j * NR : width + (j + 1) * NR] = code.astype(BF16)
            outward.append(move(x_room.at[rows[g], pl.ds(width, 3 * NR)], adapt_ref.at[g]))
        ring.run(2 * per_kind, tiles, 0, n_tile)
        for item in pairs:
            mover.begin(item)
        for g in range(per):
            for j in range(2):
                outward.append(move(proj.at[rows[g], columns(1 + j)], kv_ref.at[j, g]))
        for i in range(len(items) + lag + 2):
            if i < len(items):
                mover.relay(items[i])
                if i + ahead < len(items):
                    mover.begin(items[i + ahead])
            if i == 0:
                ring.run(n_tile, tiles, 2 * per_kind, n_tile)
                for g in range(per):
                    outward.append(move(proj.at[rows[g], columns(0)], q_ref.at[g]))
            for level in range(len(mover.masks)):
                if 0 <= i - lag - level < len(items):
                    mover.finish(items[i - lag - level], level)
            if i in tasks:
                tasks[i]()
        for item in items:
            mover.complete(item)
        for copy in (own[2], own[5]):
            copy.wait_recv()
        for copy in outward:
            copy.wait()
        mover.close()

    row = (per, loc, width_here)
    pair_shape = (2,) + row
    vmem, anywhere = pl.BlockSpec(memory_space=pltpu.VMEM), pl.BlockSpec(memory_space=pl.ANY)
    outputs = [(pair_shape, BF16, anywhere)] * (n_ctx - 1) + [
        (row, BF16, anywhere),
        (pair_shape, BF16, anywhere),
        ((per, loc, 3 * NR), BF16, anywhere),
        ((width_here, wide), BF16, anywhere),
        ((wide, units), BF16, anywhere),
        ((units, wide), BF16, anywhere),
        (row, BF16, vmem),
        ((per, heads, 1, loc), F32, vmem),
        ((per, loc, wide), BF16, anywhere),
        ((per, loc, units), BF16, anywhere),
        ((per, loc, units), BF16, anywhere),
        ((per, loc, width), F32, anywhere),
        ((per, loc, 128), F32, vmem),
        ((per, loc, NR), BF16, vmem),
        ((per, loc, NR), BF16, vmem),
    ]
    return pl.pallas_call(
        kernel,
        in_specs=[vmem] * 7 + [anywhere] * 8,
        out_specs=[space for _, _, space in outputs],
        out_shape=[jax.ShapeDtypeStruct(shape, dtype) for shape, dtype, _ in outputs],
        scratch_shapes=[
            pltpu.SemaphoreType.DMA((n_copy,)),
            pltpu.SemaphoreType.DMA((n_copy,)),
            pltpu.SemaphoreType.DMA((9 * per,)),
            pltpu.SemaphoreType.DMA((n_ctx,)),
            pltpu.SemaphoreType.DMA((4,)),
            pltpu.VMEM((per * loc, wide_x), BF16),
            pltpu.VMEM((2, wide_x, tile), BF16),
            pltpu.VMEM((per * loc, 3 * width_here), BF16),
            pltpu.VMEM((n_ctx, 2, loc, width_here), BF16),
            pltpu.VMEM((width_here, wide), BF16),
            pltpu.VMEM((per, loc, wide), BF16),
            pltpu.VMEM((per, loc, wide), BF16),
            pltpu.VMEM((2, wide, tile), BF16),
            pltpu.VMEM((per, loc, wide), BF16),
            pltpu.VMEM((per, loc, width), F32),
            pltpu.VMEM((per, loc, units), BF16),
            pltpu.VMEM((per, loc, units), BF16),
        ],
        compiler_params=pltpu.CompilerParams(
            collective_id=1, has_side_effects=True, vmem_limit_bytes=60 << 20
        ),
    )(bias, a_qkv, picked, gain, shift_by, *first_maps, x_rows, qkv_x, w_out, w_up, w_down, *maps)


def attend_back(query, kv_own, slots, bias, grad, log_total, acts, n_fsdp, n_ctx):
    per, loc, width_here = query.shape
    piece, width = acts.shape[2:]
    heads = width_here // HEAD_DIM
    cuts = 4
    high = heads // cuts
    columns = high * HEAD_DIM
    masks = masks_of(n_ctx)
    units = [(g, c) for g in range(per) for c in range(cuts)]
    n_copy = per * (n_fsdp - 1) + len(units) * (n_ctx - 1)

    def kernel(*refs):
        q_ref, bias_ref, g_ref, log_ref, acts_ref, kv_ref = refs[:6]
        slot_refs = refs[6 : 5 + n_ctx]
        dq_ref, dkv_ref, out_ref = refs[5 + n_ctx : 8 + n_ctx]
        send, recv, load, kv_room, own, came, act_room = refs[8 + n_ctx :]
        mover = Mover(n_fsdp, n_ctx, send, recv)
        z, ct = mover.z, mover.ct
        loads = []
        for g in range(per):
            loads.append([])
            for k in range(n_ctx):
                source = kv_ref if k == 0 else slot_refs[k - 1]
                copy = pltpu.make_async_copy(
                    source.at[:, g], kv_room.at[g, k], load.at[g * n_ctx + k]
                )
                copy.start()
                loads[g].append(copy)
        kept = []
        for g in range(per):
            at = per * n_ctx + 2 * g
            first = pltpu.make_async_copy(acts_ref.at[g, 0], act_room.at[g], load.at[at])
            first.start()
            second = pltpu.make_async_copy(
                act_room.at[g], out_ref.at[z * per + g], load.at[at + 1]
            )
            kept.append((first, second))
        mover.greet()
        dealt = []
        for g in range(per):
            for s in range(1, n_fsdp):
                to = lax.rem(z - s + n_fsdp, n_fsdp)
                dealt.append(
                    mover.go(acts_ref.at[g, s], out_ref.at[z * per + g], {"fsdp": to})
                )
        flying = {}

        def compute(u):
            g, c = units[u]
            if c == 0:
                for copy in loads[g]:
                    copy.wait()

            def one(h, carry):
                at = ds(c * columns + h * HEAD_DIM, HEAD_DIM)
                to = ds(h * HEAD_DIM, HEAD_DIM)
                biases = []
                for k in range(n_ctx):
                    block = bias_ref[g, k * loc : (k + 1) * loc, :]
                    biases.append(jnp.concatenate([block] * (loc // 128), axis=1))
                dquery, dkeys, dvalues = attend_back_head(
                    q_ref[g, :, at],
                    g_ref[g, :, at],
                    log_ref[g, c * high + h],
                    [kv_room[g, k, 0, :, at] for k in range(n_ctx)],
                    [kv_room[g, k, 1, :, at] for k in range(n_ctx)],
                    biases,
                )
                dq_ref[g, :, at] = dquery
                for k in range(n_ctx):
                    own[u, k, 0, :, to] = dkeys[k]
                    own[u, k, 1, :, to] = dvalues[k]
                return carry

            lax.fori_loop(0, high, one, 0)

        def hand(u, level):
            half = 2**level
            device = {"ctx": flip(ct, masks[level])}
            flying[u, level] = [
                mover.go(own.at[u, half + i], came.at[u, half - 1 + i], device) for i in range(half)
            ]

        def take_in(u, level):
            half = 2**level
            for i, copy in enumerate(flying[u, level]):
                copy.wait_recv()
                for j in range(2):
                    total = own[u, i, j].astype(F32) + came[u, half - 1 + i, j].astype(F32)
                    if level:
                        own[u, i, j] = total.astype(BF16)
                    else:
                        g, c = units[u]
                        dkv_ref[j, g, :, c * columns : (c + 1) * columns] = total.astype(BF16)

        last = len(masks) - 1
        for t in range(len(units) + last + 1):
            if t < len(units):
                compute(t)
                hand(t, last)
            if t == 0:
                for first, second in kept:
                    first.wait()
                    second.start()
            for k in range(last + 1):
                u, level = t - 1 - k, last - k
                if 0 <= u < len(units):
                    take_in(u, level)
                    if level:
                        hand(u, level - 1)
        for _, second in kept:
            second.wait()
        for copy in dealt:
            copy.wait_recv()
        mover.close()

    vmem, anywhere = pl.BlockSpec(memory_space=pltpu.VMEM), pl.BlockSpec(memory_space=pl.ANY)
    return pl.pallas_call(
        kernel,
        in_specs=[vmem] * 4 + [anywhere] * (1 + n_ctx),
        out_specs=[vmem, vmem, anywhere],
        out_shape=[
            jax.ShapeDtypeStruct(query.shape, BF16),
            jax.ShapeDtypeStruct(kv_own.shape, BF16),
            jax.ShapeDtypeStruct((per * n_fsdp, piece, width), BF16),
        ],
        scratch_shapes=[
            pltpu.SemaphoreType.DMA((n_copy,)),
            pltpu.SemaphoreType.DMA((n_copy,)),
            pltpu.SemaphoreType.DMA((per * (n_ctx + 2),)),
            pltpu.VMEM((per, n_ctx, 2, loc, width_here), BF16),
            pltpu.VMEM((len(units), n_ctx, 2, loc, columns), BF16),
            pltpu.VMEM((len(units), n_ctx - 1, 2, loc, columns), BF16),
            pltpu.VMEM((per, piece, width), BF16),
        ],
        compiler_params=pltpu.CompilerParams(
            collective_id=2, has_side_effects=True, vmem_limit_bytes=56 << 20
        ),
    )(query, bias, grad, log_total, acts, kv_own, *slots)


class Ring:
    def __init__(self, room, sems, at, tile_at):
        self.room, self.sems, self.at, self.tile_at = room, sems, at, tile_at

    def copy(self, t):
        slot = lax.rem(t, 2)
        return pltpu.make_async_copy(
            self.tile_at(t), self.room.at[slot], self.sems.at[self.at + slot]
        )

    def prefetch(self):
        self.copy(0).start()
        self.copy(1).start()

    def run(self, n, body, first=0, total=None):
        total = n if total is None else total

        def step(t, carry):
            self.copy(t).wait()
            body(t, self.room.at[lax.rem(t, 2)])

            @pl.when(t + 2 < total)
            def _():
                self.copy(t + 2).start()

            return carry

        lax.fori_loop(first, n, step, 0)


def compact(out_ref, n, entries, sizes):
    column = lax.broadcasted_iota(jnp.int32, (NR, RANK), 0)
    rank = lax.broadcasted_iota(jnp.int32, (NR, RANK), 1)
    used = jnp.where(lax.rem(column, RANK) == rank, 1.0, 0.0).astype(BF16)
    start = 0
    for (code, value), size in zip(entries, sizes):
        short = dot(code(), used).astype(BF16)
        block = dot_tn(short, value()).astype(BF16)
        for k in range(out_ref.shape[0]):
            out_ref[k, n * RANK : (n + 1) * RANK, start : start + size] = block[
                :, k * size : (k + 1) * size
            ]
        start += size


class Fold:
    def __init__(self, mover, parts, came, out_ref):
        self.mover, self.parts, self.came, self.out_ref = mover, parts, came, out_ref
        self.flying = {}

    def at(self, k):
        return flip(self.mover.ct, self.mover.offsets[k])

    def hand(self, level):
        half = 2**level
        self.flying[level] = [
            self.mover.go(
                self.parts.at[self.at(half + i)],
                self.came.at[half - 1 + i],
                {"ctx": flip(self.mover.ct, self.mover.masks[level])},
            )
            for i in range(half)
        ]

    def take(self, level):
        for i, copy in enumerate(self.flying[level]):
            copy.wait_recv()
            total = self.parts[self.at(i)].astype(F32) + self.came[2**level - 1 + i].astype(F32)
            self.parts[self.at(i)] = total.astype(BF16)

    def next(self, level):
        self.take(level)
        if level:
            self.hand(level - 1)

    def gather(self):
        own = self.parts.at[self.mover.ct]
        item = Weight(lambda c: self.parts.at[c], lambda o, c: self.out_ref.at[c, o], own)
        self.mover.begin(item)
        return own, self.out_ref.at[self.mover.ct, self.mover.z], item


def norm_parts(values):
    center = values - jnp.mean(values, axis=-1, keepdims=True)
    rstd = lax.rsqrt(jnp.mean(center * center, axis=-1, keepdims=True) + NORM_EPS)
    return center * rstd, rstd


def norm_back(hat, rstd, dhat):
    first = jnp.mean(dhat, axis=-1, keepdims=True)
    second = jnp.mean(dhat * hat, axis=-1, keepdims=True)
    return rstd * (dhat - first - hat * second)


def gelu_both(pre):
    square = pre * pre
    bent = jnp.tanh(GELU_COEF * (pre + 0.044715 * square * pre))
    out = 0.5 * pre * (1.0 + bent)
    slope = 0.5 * (1.0 + bent) + 0.5 * pre * (1.0 - bent * bent) * GELU_COEF * (
        1.0 + 3.0 * 0.044715 * square
    )
    return out.astype(BF16), slope.astype(BF16)


def middle(hats, rstds, gelus, slopes, adapt_up, cot, picked, gain, shift_by, weights, maps, n_fsdp, n_ctx):
    per, loc, width = hats.shape
    out_x, up_x, down_x = weights
    a_up, b_out, b_down, a_down, b_up = maps
    wide, units = up_x.shape
    width_here = out_x.shape[0]
    tile = 512
    chunk = 32
    n_wide = width // tile
    n_swap = n_wide + 1
    sizes = [width // n_ctx, units // n_ctx, units // n_ctx]

    def kernel(*refs):
        pick_ref, gain_ref, shift_ref, rstd1, code_up_ref = refs[:5]
        a_up_ref, b_out_ref, b_down_ref, a_down_ref, b_up_ref = refs[5:10]
        hat_ref, gelu_ref, slope_ref, cot_ref, out_ref, up_ref, down_ref = refs[10:17]
        acts_out, dy1_out, da_out, cot_rows, grads_out = refs[17:22]
        dadapt_up_ref, ctx_ref = refs[22:24]
        (send, recv, deal_send, deal_recv, ring_sem, sems) = refs[24:30]
        (down_room, down_rows, up_rows) = refs[30:33]
        (stage, part, got, hat1, keep32, slope, gelu, wide_v, turned, dpre_t) = refs[33:43]
        codes_down, grads_part, grads_came = refs[43:]
        mover = Mover(n_fsdp, n_ctx, deal_send, deal_recv)
        partner = {"tp": 1 - lax.axis_index("tp")}

        down = Ring(down_room, ring_sem, 0, lambda t: down_ref.at[:, ds(t * tile, tile)])
        down_r = Ring(down_rows, ring_sem, 4, lambda t: down_ref.at[ds(t * tile, tile)])
        up_r = Ring(up_rows, ring_sem, 6, lambda t: up_ref.at[ds(t * tile, tile)])
        out_r = Ring(down_rows, ring_sem, 4, lambda t: out_ref.at[ds(t * tile, tile)])

        busy = {}
        used = [0]

        def move(source, target, key):
            copy = pltpu.make_async_copy(source, target, sems.at[used[0]])
            used[0] += 1
            copy.start()
            busy.setdefault(key, []).append(copy)

        def free(*keys):
            for key in keys:
                for copy in busy.pop(key, []):
                    copy.wait()

        def swap_copy(turn, g, t, size):
            at = ds(t * tile, size)
            sem = (turn * per + g) * n_swap + t
            return pltpu.make_async_remote_copy(
                src_ref=part.at[g, :, at],
                dst_ref=got.at[turn, g, :, at],
                send_sem=send.at[sem],
                recv_sem=recv.at[sem],
                device_id=partner,
                device_id_type=pl.DeviceIdType.MESH,
            )

        def swapped(turn, g):
            for t in range(n_swap):
                copy = swap_copy(turn, g, t, tile if t < n_wide else NR)
                copy.wait_recv()
                copy.wait_send()

        def by_rows(body):
            def step(r, carry):
                body(pl.ds(pl.multiple_of(r * chunk, chunk), chunk))
                return carry

            lax.fori_loop(0, loc // chunk, step, 0)

        def deal(g):
            return Deal(lambda to: cot_ref.at[to * per + g], lambda s: cot_rows.at[g, s])

        deals = [deal(g) for g in range(per)]
        for g in range(per):
            move(gelu_ref.at[g], gelu.at[g], ("gelu", g))
            if g == 0:
                down.prefetch()
            move(cot_ref.at[mover.z * per + g], cot_rows.at[g, 0], ("cot", g))
        for g in range(per):
            move(hat_ref.at[g], hat1.at[g], ("hat", g))
            move(slope_ref.at[g], slope.at[g], ("slope", g))
        mover.greet(tp=True)
        mover.begin(deals[0])

        for g in range(per):
            if g + 1 == per:
                down_r.prefetch()
            free(("gelu", g))

            def down_tile(t, room, g=g):
                part[g, :, ds(t * tile, tile)] = dot(gelu[g], room[...]).astype(BF16)
                swap_copy(0, g, t, tile).start()

            down.run(n_wide, down_tile)
            if g + 1 < per:
                down.prefetch()
            else:
                up_r.prefetch()
            part[g, :, width:] = dot(gelu[g], a_down_ref[...]).astype(BF16)
            swap_copy(0, g, n_wide, NR).start()

        for g in range(per):
            mover.relay(deals[g])
            if g + 1 < per:
                mover.begin(deals[g + 1])
            free(("cot", g))
            for s in range(n_fsdp):
                at = pl.ds(s * cot.shape[1], cot.shape[1])
                move(cot_rows.at[g, s], stage.at[g, at], ("stage", g))
            swapped(0, g)
            free(("stage", g), ("hat", g), ("slope", g))
            pick = pick_ref[g]

            def second_norm(rows, g=g, pick=pick):
                total = part[g, rows, :].astype(F32) + got[0, g, rows, :].astype(F32)
                code = (total[:, width:] * pick).astype(BF16)
                codes_down[g, rows, :] = code
                hidden = hat1[g, rows, :] * gain_ref[0:1, :] + shift_ref[0:1, :]
                hat, rstd = norm_parts(hidden + total[:, :width] + dot(code, b_down_ref[...]))
                part[g, rows, :width] = (hat * gain_ref[1:2, :] + shift_ref[1:2, :]).astype(BF16)
                dy2 = norm_back(hat, rstd, stage[g, rows, :].astype(F32) * gain_ref[1:2, :])
                keep32[g, rows, :] = dy2
                low = dy2.astype(BF16)
                wide_v[g, rows, :width] = low
                wide_v[g, rows, width:] = (dot_nt(low, b_down_ref[...]) * pick).astype(BF16)

            by_rows(second_norm)
            move(part.at[g, :, pl.ds(0, width)], acts_out.at[g], ("part", g))
            turned[...] = wide_v[g].T

            def down_back(t, room, g=g):
                at = ds(t * tile, tile)
                block = dot(room[...], turned[...]).T
                low = (block * slope[g, :, at].astype(F32)).astype(BF16)
                slope[g, :, at] = low
                dpre_t[at, :] = low.T

            down_r.run(units // tile, down_back)
            (down_r if g + 1 < per else out_r).prefetch()
            free(("part", g))

            def up_back(t, room, g=g):
                part[g, :, ds(t * tile, tile)] = dot(room[...], dpre_t[...]).T.astype(BF16)
                swap_copy(1, g, t, tile).start()

            up_r.run(n_wide, up_back)
            if g + 1 < per:
                up_r.prefetch()
            part[g, :, width:] = dot(b_up_ref[...], dpre_t[...]).T.astype(BF16)
            swap_copy(1, g, n_wide, NR).start()

        for g in range(per):
            entries = [
                (lambda g=g: codes_down[g], lambda g=g: wide_v[g, :, :width]),
                (lambda g=g: wide_v[g, :, width:], lambda g=g: gelu[g]),
                (lambda g=g: code_up_ref[g], lambda g=g: slope[g]),
            ]
            compact(grads_part, g, entries, sizes)

        fold = Fold(mover, grads_part, grads_came, grads_out)
        lasting = len(mover.masks) - 1
        fold.hand(lasting)
        for g in range(per):
            swapped(1, g)
            pick = pick_ref[g]

            def first_back(rows, g=g, pick=pick):
                total = part[g, rows, :].astype(F32) + got[1, g, rows, :].astype(F32)
                code = (total[:, width:] * pick).astype(BF16)
                dadapt_up_ref[g, rows, :] = code
                dh1 = keep32[g, rows, :] + total[:, :width] + dot_nt(code, a_up_ref[...])
                rstd = rstd1[g, rows, 0:1]
                dy1 = norm_back(hat1[g, rows, :], rstd, dh1 * gain_ref[0:1, :])
                keep32[g, rows, :] = dy1
                low = dy1.astype(BF16)
                wide_v[g, rows, :width] = low
                wide_v[g, rows, width:] = (dot_nt(low, b_out_ref[...]) * pick).astype(BF16)

            by_rows(first_back)
            if g == 0:
                fold.next(lasting)
            move(keep32.at[g], dy1_out.at[g], "dy1")
            move(wide_v.at[g], da_out.at[g], "wide")
            turned[...] = wide_v[g].T

            def out_back(t, room, g=g):
                ctx_ref[g, :, ds(t * tile, tile)] = dot(room[...], turned[...]).T.astype(BF16)

            out_r.run(width_here // tile, out_back)
            if g + 1 < per:
                out_r.prefetch()
            if g == 0:
                for level in range(lasting - 1, -1, -1):
                    fold.next(level)
                source, target, item = fold.gather()
                move(source, target, "grads")
                mover.relay(item)
        mover.complete(item)
        free(*list(busy))
        mover.close()

    vmem, anywhere = pl.BlockSpec(memory_space=pltpu.VMEM), pl.BlockSpec(memory_space=pl.ANY)
    row = (per, loc)
    grads_shape = (n_ctx, per * RANK, sum(sizes))
    outputs = [
        (row + (width,), BF16, anywhere),
        (row + (width,), F32, anywhere),
        (row + (wide,), BF16, anywhere),
        ((per, n_fsdp) + cot.shape[1:], BF16, anywhere),
        ((n_ctx, n_fsdp) + grads_shape[1:], BF16, anywhere),
        (row + (NR,), BF16, vmem),
        (row + (width_here,), BF16, vmem),
    ]
    n_copy = 2 * per * n_swap
    n_deal = per * (n_fsdp - 1) + (n_fsdp - 1) * n_ctx + 2 * (n_ctx - 1)
    return pl.pallas_call(
        kernel,
        in_specs=[vmem] * 10 + [anywhere] * 7,
        out_specs=[space for _, _, space in outputs],
        out_shape=[jax.ShapeDtypeStruct(shape, dtype) for shape, dtype, _ in outputs],
        scratch_shapes=[
            pltpu.SemaphoreType.DMA((n_copy,)),
            pltpu.SemaphoreType.DMA((n_copy,)),
            pltpu.SemaphoreType.DMA((n_deal,)),
            pltpu.SemaphoreType.DMA((n_deal,)),
            pltpu.SemaphoreType.DMA((8,)),
            pltpu.SemaphoreType.DMA(((7 + n_fsdp) * per + 1,)),
            pltpu.VMEM((2, units, tile), BF16),
            pltpu.VMEM((2, tile, wide), BF16),
            pltpu.VMEM((2, tile, units), BF16),
            pltpu.VMEM(row + (width,), BF16),
            pltpu.VMEM(row + (wide,), BF16),
            pltpu.VMEM((2,) + row + (wide,), BF16),
            pltpu.VMEM(row + (width,), F32),
            pltpu.VMEM(row + (width,), F32),
            pltpu.VMEM(row + (units,), BF16),
            pltpu.VMEM(row + (units,), BF16),
            pltpu.VMEM(row + (wide,), BF16),
            pltpu.VMEM((wide, loc), BF16),
            pltpu.VMEM((units, loc), BF16),
            pltpu.VMEM(row + (NR,), BF16),
            pltpu.VMEM(grads_shape, BF16),
            pltpu.VMEM((n_ctx - 1,) + grads_shape[1:], BF16),
        ],
        compiler_params=pltpu.CompilerParams(
            collective_id=3, has_side_effects=True, vmem_limit_bytes=62 << 20
        ),
    )(
        picked, gain, shift_by, rstds, adapt_up, a_up, b_out, b_down, a_down, b_up,
        hats, gelus, slopes, cot, out_x, up_x, down_x,
    )


def combine(pieces, chosen, shapes):
    n_part, n_fsdp, rows, columns = pieces.shape
    flat, specs = [], []
    for i, shape in enumerate(shapes):
        high, wide = shape[-2:]
        tall = wide == NR and high != NR
        size = (high if tall else wide) // n_part
        block = (size, NR) if tall else (NR, size)
        lead = shape[0] if len(shape) == 3 else None
        for j in range(lead or 1):
            flat.append((i, None if lead is None else j, tall, size))
        if lead is None:
            specs.append(pl.BlockSpec(block, (lambda c: (c, 0)) if tall else (lambda c: (0, c))))
        else:
            specs.append(
                pl.BlockSpec(
                    (lead,) + block, (lambda c: (0, c, 0)) if tall else (lambda c: (0, 0, c))
                )
            )

    def kernel(chosen_ref, piece_ref, *outs):
        ordered = jnp.concatenate([piece_ref[0, a] for a in range(n_fsdp)], axis=0)
        start = 0
        for i, lead, tall, size in flat:
            block = ordered[:, start : start + size]
            value = dot_tn(block, chosen_ref[...]) if tall else dot_tn(chosen_ref[...], block)
            if lead is None:
                outs[i][...] = value
            else:
                outs[i][lead] = value
            start += size

    return pl.pallas_call(
        kernel,
        grid=(n_part,),
        in_specs=[
            pl.BlockSpec(chosen.shape, lambda c: (0, 0)),
            pl.BlockSpec((1, n_fsdp, rows, columns), lambda c: (c, 0, 0, 0)),
        ],
        out_specs=specs,
        out_shape=[jax.ShapeDtypeStruct(shape, F32) for shape in shapes],
        compiler_params=pltpu.CompilerParams(vmem_limit_bytes=48 << 20),
    )(chosen, pieces)


def last(d_query, d_pair, x_all, adapt_all, dy1, qkv_x, a_qkv, picked, early, pairs, n_fsdp, n_ctx):
    per, loc, width_here = d_query.shape
    piece, width = loc // n_fsdp, x_all.shape[2]
    depth = 3 * width_here
    foot = 3 * NR
    wide = width + foot
    tile, chunk = 512, 32
    n_wide = width // tile
    n_swap = n_wide + 1
    n_early = len(early)
    early_sizes = [values[2] // n_ctx for _, values in pairs] + [width_here // n_ctx] * 3
    late_sizes = [width // n_ctx] * 3
    gathers = 2
    n_copy = per * (n_fsdp - 1) + gathers * ((n_fsdp - 1) * n_ctx + 2 * (n_ctx - 1))

    def kernel(*refs):
        dq_ref, dkv_ref, x_ref, adapt_ref, a_ref, pick_ref = refs[:6]
        dy1_ref, w_ref = refs[6:8]
        early_refs = refs[8 : 8 + n_early]
        in_ref, early_out, late_out = refs[8 + n_early : 11 + n_early]
        send, recv, swap_send, swap_recv, ring_sem, sems = refs[11 + n_early : 17 + n_early]
        rows_room, foot_room, dy1_room, turned, part, got, codes_in, dx = refs[
            17 + n_early : 25 + n_early
        ]
        early_part, early_came, late_part, late_came = refs[25 + n_early : 29 + n_early]
        staged = refs[29 + n_early :]
        mover = Mover(n_fsdp, n_ctx, send, recv)
        z, ct, masks = mover.z, mover.ct, mover.masks
        partner = {"tp": 1 - lax.axis_index("tp")}
        ring = Ring(rows_room, ring_sem, 0, lambda t: w_ref.at[ds(t * tile, tile)])
        used = [0]

        def move(source, target):
            copy = pltpu.make_async_copy(source, target, sems.at[used[0]])
            used[0] += 1
            copy.start()
            return copy

        def swap_copy(g, t, size):
            at = ds(t * tile, tile) if size == tile else pl.ds(width, size)
            sem = g * n_swap + t
            return pltpu.make_async_remote_copy(
                src_ref=part.at[g, :, at],
                dst_ref=got.at[g, :, at],
                send_sem=swap_send.at[sem],
                recv_sem=swap_recv.at[sem],
                device_id=partner,
                device_id_type=pl.DeviceIdType.MESH,
            )

        lasting = len(masks) - 1
        load_foot = move(w_ref.at[pl.ds(width, foot)], foot_room)
        ring.prefetch()
        loads = [move(ref, room) for ref, room in zip(early_refs, staged)]
        load_dy1 = move(dy1_ref, dy1_room)
        mover.greet(tp=True)
        folds = [
            Fold(mover, early_part, early_came, early_out),
            Fold(mover, late_part, late_came, late_out),
        ]
        for g in range(per):
            turned[0:width_here, :] = dq_ref[g].T
            turned[width_here : 2 * width_here, :] = dkv_ref[0, g].T
            turned[2 * width_here :, :] = dkv_ref[1, g].T
            if g == 0:
                load_foot.wait()
            part[g, :, width:] = dot(foot_room[...], turned[...]).T.astype(BF16)
            swap_copy(g, n_wide, foot).start()

            def back(t, room, g=g):
                part[g, :, ds(t * tile, tile)] = dot(room[...], turned[...]).T.astype(BF16)
                swap_copy(g, t, tile).start()

            ring.run(n_wide, back)
            if g + 1 < per:
                ring.prefetch()
            if g == 0:
                for copy in loads:
                    copy.wait()
                for n in range(per):
                    entries = []
                    for (i, first, size), (j, start, count) in pairs:
                        entries.append(
                            (
                                lambda n=n, i=i, f=first, c=size: staged[i][n, :, f : f + c],
                                lambda n=n, i=j, f=start, c=count: staged[i][n, :, f : f + c],
                            )
                        )
                    values = [
                        lambda n=n: dq_ref[n],
                        lambda n=n: dkv_ref[0, n],
                        lambda n=n: dkv_ref[1, n],
                    ]
                    for j in range(3):
                        entries.append(
                            (lambda n=n, j=j: adapt_ref[n, :, j * NR : (j + 1) * NR], values[j])
                        )
                    compact(early_part, n, entries, early_sizes)
                folds[0].hand(lasting)
        for level in range(lasting, -1, -1):
            folds[0].next(level)
        kept = []
        source, target, first = folds[0].gather()
        kept.append(move(source, target))
        for g in range(per):
            swap_copy(g, n_wide, foot).wait_recv()
            pick = jnp.concatenate([pick_ref[g]] * 3, axis=1)
            total = part[g, :, width:].astype(F32) + got[g, :, width:].astype(F32)
            codes_in[g] = (total * pick).astype(BF16)
        for n in range(per):
            entries = []
            for j in range(3):
                entries.append(
                    (
                        lambda n=n, j=j: codes_in[n, :, j * NR : (j + 1) * NR],
                        lambda n=n: x_ref[n],
                    )
                )
            compact(late_part, n, entries, late_sizes)
        folds[1].hand(lasting)
        mover.relay(first)
        load_dy1.wait()
        dealt = []

        def finish_rows(g):
            for t in range(n_swap):
                copy = swap_copy(g, t, tile if t < n_wide else foot)
                if t < n_wide:
                    copy.wait_recv()
                copy.wait_send()

            def step(r, carry):
                rows = ds(r * chunk, chunk)
                code = codes_in[g, rows, :]
                total = part[g, rows, :width].astype(F32) + got[g, rows, :width].astype(F32)
                value = dy1_room[g, rows, :] + total
                for j in range(3):
                    value = value + dot_nt(code[:, j * NR : (j + 1) * NR], a_ref[j])
                dx[g, rows, :] = value.astype(BF16)
                return carry

            lax.fori_loop(0, loc // chunk, step, 0)
            kept.append(move(dx.at[g, pl.ds(0, piece)], in_ref.at[z * per + g]))
            for s in range(1, n_fsdp):
                to = lax.rem(z - s + n_fsdp, n_fsdp)
                dealt.append(
                    mover.go(
                        dx.at[g, pl.ds(s * piece, piece)], in_ref.at[z * per + g], {"fsdp": to}
                    )
                )

        for g in range(per):
            finish_rows(g)
            if g == 0:
                for level in range(lasting, -1, -1):
                    folds[1].next(level)
                source, target, second = folds[1].gather()
                kept.append(move(source, target))
                mover.relay(second)
                mover.complete(first)
        mover.complete(second)
        for copy in dealt:
            copy.wait_recv()
        for copy in kept:
            copy.wait()
        mover.close()

    vmem, anywhere = pl.BlockSpec(memory_space=pltpu.VMEM), pl.BlockSpec(memory_space=pl.ANY)
    parts = [(n_ctx, per * RANK, sum(early_sizes)), (n_ctx, per * RANK, sum(late_sizes))]
    rooms = [
        ((2, tile, depth), BF16),
        ((foot, depth), BF16),
        (dy1.shape, F32),
        ((depth, loc), BF16),
        ((per, loc, wide), BF16),
        ((per, loc, wide), BF16),
        ((per, loc, foot), BF16),
        ((per, loc, width), BF16),
    ]
    for shape in parts:
        rooms += [(shape, BF16), ((n_ctx - 1,) + shape[1:], BF16)]
    rooms += [(x.shape, BF16) for x in early]
    return pl.pallas_call(
        kernel,
        in_specs=[vmem] * 6 + [anywhere] * (2 + n_early),
        out_specs=[anywhere] * 3,
        out_shape=[jax.ShapeDtypeStruct((per * n_fsdp, piece, width), BF16)]
        + [jax.ShapeDtypeStruct((n_ctx, n_fsdp) + shape[1:], BF16) for shape in parts],
        scratch_shapes=[
            pltpu.SemaphoreType.DMA((n_copy,)),
            pltpu.SemaphoreType.DMA((n_copy,)),
            pltpu.SemaphoreType.DMA((per * n_swap,)),
            pltpu.SemaphoreType.DMA((per * n_swap,)),
            pltpu.SemaphoreType.DMA((2,)),
            pltpu.SemaphoreType.DMA((4 + n_early + per,)),
        ]
        + [pltpu.VMEM(shape, dtype) for shape, dtype in rooms],
        compiler_params=pltpu.CompilerParams(
            collective_id=4, has_side_effects=True, vmem_limit_bytes=60 << 20
        ),
    )(d_query, d_pair, x_all, adapt_all, a_qkv, picked, dy1, qkv_x, *early)


def gelu_both(pre):
    square = pre * pre
    bent = jnp.tanh(GELU_COEF * (pre + 0.044715 * square * pre))
    out = 0.5 * pre * (1.0 + bent)
    slope = 0.5 * (1.0 + bent) + 0.5 * pre * (1.0 - bent * bent) * GELU_COEF * (
        1.0 + 3.0 * 0.044715 * square
    )
    return out.astype(BF16), slope.astype(BF16)


def local(
    x_in,
    cotangent,
    lengths,
    adapter_ids,
    w_qkv,
    w_out,
    w_up,
    w_down,
    ln_gain,
    ln_bias,
    a_qkv,
    b_qkv,
    a_out,
    b_out,
    a_up,
    b_up,
    a_down,
    b_down,
):
    n_ctx, n_fsdp = lax.axis_size("ctx"), lax.axis_size("fsdp")
    z, ct = lax.axis_index("fsdp"), lax.axis_index("ctx")
    seqs, piece, width = x_in.shape
    per = seqs // n_fsdp
    loc = n_fsdp * piece
    heads_width = w_qkv.shape[2]
    def take(array, start, size, axis=0):
        return lax.dynamic_slice_in_dim(array, start, size, axis)

    units = w_up.shape[1]
    rows_shape = (per, n_fsdp, piece, width)
    zq = w_qkv.shape[1]

    def first_items(ins, outs, z):
        x_ref, w_ref = ins
        rows_ref, whole_ref = outs

        def deal(g):
            return Deal(lambda to: x_ref.at[to * per + g], lambda s: rows_ref.at[g, s])

        def weight(j):
            size = zq // n_ctx
            columns = pl.ds(j * heads_width, heads_width)
            return Weight(
                lambda c: w_ref.at[j, pl.ds(pl.multiple_of(c * size, size), size)],
                lambda o, c: whole_ref.at[
                    pl.ds(pl.multiple_of(o * zq + c * size, size), size), columns
                ],
            )

        stay = [(x_ref.at[z * per + g], rows_ref.at[g, 0]) for g in range(per)]
        for j in range(3):
            own = whole_ref.at[
                pl.ds(pl.multiple_of(z * zq, zq), zq), pl.ds(j * heads_width, heads_width)
            ]
            stay.append((w_ref.at[j], own))
        items = [weight(j) for j in range(3)] + [deal(g) for g in range(per)]
        return items, stay

    x_all, qkv_x = move(
        first_items,
        [Weight] * 3 + [Deal] * per,
        (x_in, w_qkv),
        (rows_shape, (width + 3 * NR, 3 * heads_width)),
        n_fsdp,
        n_ctx,
        ((piece, width),) * per + (w_qkv.shape[1:],) * 3,
        0,
        foot=(b_qkv, lambda outs: outs[1].at[pl.ds(width, 3 * NR)]),
    )

    my_lengths = take(lengths, z * per, per)
    my_ids = take(adapter_ids, z * per, per)
    picked = (my_ids[:, None] == jnp.arange(NR)[None, :] // RANK).astype(F32)
    steps = lax.rem(z - jnp.arange(n_fsdp) + n_fsdp, n_fsdp)
    ctx_of = ct ^ jnp.array(offsets(n_ctx))
    key_pos = (
        (steps[None, :, None] * n_ctx + ctx_of[:, None, None]) * piece
        + jnp.arange(piece)[None, None, :]
    ).reshape(-1)
    bias_all = jnp.where(key_pos[None, :] < my_lengths[:, None], 0.0, -1e30).astype(F32)
    bias_all = jnp.broadcast_to(bias_all[:, :, None], bias_all.shape + (128,))

    picked = picked[:, None, :]
    x_rows = x_all.reshape(per, loc, width)
    moved = forward_and_gather(
        x_rows, qkv_x, a_qkv, picked, bias_all, ln_gain, ln_bias, (a_up, b_out), (w_out, w_up, w_down),
        (a_out, b_up, a_down), n_fsdp, n_ctx,
    )
    slots = moved[: n_ctx - 1]
    (
        query, kv_own, adapt_all, out_x, up_x, down_x, context, log_total, wide_h, gelus, slopes, hats, rstds,
        adapt_out, adapt_up,
    ) = moved[n_ctx - 1 :]
    acts, dy1, wide_a, _, grads, dadapt_up, d_context = middle(
        hats, rstds, gelus, slopes, adapt_up, cotangent, picked, ln_gain, ln_bias, (out_x, up_x, down_x),
        (a_up, b_out, b_down, a_down, b_up), n_fsdp, n_ctx,
    )
    d_query, d_pair, activations = attend_back(
        query,
        kv_own,
        slots,
        bias_all,
        d_context,
        log_total,
        acts.reshape(per, n_fsdp, piece, width),
        n_fsdp,
        n_ctx,
    )
    early_in = (dadapt_up, wide_h, adapt_out, wide_a, context)
    early_pairs = [
        ((0, 0, NR), (1, 0, width)),
        ((2, 0, NR), (3, 0, width)),
        ((3, width, NR), (4, 0, heads_width)),
    ]
    input_grad, early, late = last(
        d_query,
        d_pair,
        x_rows,
        adapt_all,
        dy1,
        qkv_x,
        a_qkv,
        picked,
        early_in,
        early_pairs,
        n_fsdp,
        n_ctx,
    )
    codes = (adapter_ids[:, None] * RANK + jnp.arange(RANK)[None, :]).reshape(-1)
    chosen = (codes[:, None] == jnp.arange(NR)[None, :]).astype(BF16)
    b_down_grad, a_down_grad, b_up_grad = combine(
        grads, chosen, [(NR, width), (units, NR), (NR, units)]
    )
    a_up_grad, b_out_grad, a_out_grad, b_qkv_grad = combine(
        early, chosen, [(width, NR), (NR, width), (heads_width, NR), (3, NR, heads_width)]
    )
    (a_qkv_grad,) = combine(late, chosen, [(3, width, NR)])
    return (
        activations, input_grad, a_qkv_grad, b_qkv_grad, a_out_grad, b_out_grad, a_up_grad, b_up_grad,
        a_down_grad, b_down_grad,
    )


def solution(mesh):
    rows = P(None, ("fsdp", "ctx"), None)
    return jax.shard_map(
        local,
        mesh=mesh,
        in_specs=(
            rows,
            rows,
            P(),
            P(),
            P(None, "fsdp", "tp"),
            P("tp", "fsdp"),
            P("fsdp", "tp"),
            P("tp", "fsdp"),
            P(),
            P(),
            P(),
            P(None, None, "tp"),
            P("tp", None),
            P(),
            P(),
            P(None, "tp"),
            P("tp", None),
            P(),
        ),
        out_specs=(
            rows,
            rows,
            P(),
            P(None, None, "tp"),
            P("tp", None),
            P(),
            P(),
            P(None, "tp"),
            P("tp", None),
            P(),
        ),
        check_vma=False,
    )
```

```python
import math

import jax
import jax.numpy as jnp
from jax import lax
from jax.experimental import pallas as pl
from jax.experimental.pallas import tpu as pltpu
from jax.sharding import PartitionSpec as P

HEAD_DIM = 128
RANK = 16
ADAPTERS = 8
NR = RANK * ADAPTERS
NORM_EPS = 1e-06
GELU_COEF = 0.7978845608028654
SCALE = 1.0 / math.sqrt(HEAD_DIM)
F32 = jnp.float32
BF16 = jnp.bfloat16


def dot(left, right):
    return jnp.dot(left, right, preferred_element_type=F32)


def dot_nt(left, right):
    return lax.dot_general(left, right, (((1,), (1,)), ((), ())), preferred_element_type=F32)


def dot_tn(left, right):
    return lax.dot_general(left, right, (((0,), (0,)), ((), ())), preferred_element_type=F32)


def masks_of(n):
    out = []
    while n > 1:
        n //= 2
        out.append(n)
    return out


def offsets(n):
    out = [0]
    for mask in masks_of(n):
        out = out + [o ^ mask for o in out]
    return out


def attend_head(query, keys, values, biases):
    scores = [dot_nt(k, query) * SCALE + bias for k, bias in zip(keys, biases)]
    top = scores[0].max(axis=0, keepdims=True)
    for s in scores[1:]:
        top = jnp.maximum(top, s.max(axis=0, keepdims=True))
    total = jnp.zeros_like(top)
    mixed = None
    for s, v in zip(scores, values):
        probs = jnp.exp(s - top)
        total = total + probs.sum(axis=0, keepdims=True)
        term = dot_tn(v, probs.astype(BF16))
        mixed = term if mixed is None else mixed + term
    return (mixed / total).T.astype(BF16), top + jnp.log(total)


def attend_back_head(query, grad, log_total, keys, values, biases):
    probs, dprobs, dvalues = [], [], []
    delta = jnp.zeros_like(log_total)
    for k, v, bias in zip(keys, values, biases):
        p = jnp.exp(dot_nt(k, query) * SCALE + bias - log_total)
        dp = dot_nt(v, grad)
        dvalues.append(dot(p.astype(BF16), grad).astype(BF16))
        delta = delta + (p * dp).sum(axis=0, keepdims=True)
        probs.append(p)
        dprobs.append(dp)
    dquery, dkeys = None, []
    for k, p, dp in zip(keys, probs, dprobs):
        ds = (p * (dp - delta)).astype(BF16)
        dkeys.append((dot(ds, query) * SCALE).astype(BF16))
        term = dot_tn(k, ds)
        dquery = term if dquery is None else dquery + term
    return (dquery * SCALE).T.astype(BF16), dkeys, dvalues


def ds(start, size):
    return pl.ds(pl.multiple_of(start, size), size)


def flip(ct, offset):
    mask = 1
    while mask <= offset:
        if offset & mask:
            ct = ct + mask - 2 * mask * lax.rem(ct // mask, 2)
        mask *= 2
    return ct


class Weight:
    def __init__(self, shard_at, whole_at, own=None, skip=0):
        self.shard_at, self.whole_at, self.own, self.skip = shard_at, whole_at, own, skip


class Deal:
    def __init__(self, source_at, rows_at):
        self.source_at, self.rows_at = source_at, rows_at


class Pair:
    def __init__(self, slot_at):
        self.slot_at = slot_at


class Mover:
    def __init__(self, n_fsdp, n_ctx, send, recv):
        self.n_fsdp, self.n_ctx = n_fsdp, n_ctx
        self.z, self.ct = lax.axis_index("fsdp"), lax.axis_index("ctx")
        self.send, self.recv = send, recv
        self.used = 0
        self.open = []
        self.masks = masks_of(n_ctx)
        self.offsets = offsets(n_ctx)
        self.came, self.waiting, self.done = {}, {}, {}

    def skip(self, item):
        return item.skip if isinstance(item, Weight) else 0

    def part(self, item):
        return lax.rem(self.ct, self.n_ctx >> item.skip) if item.skip else self.ct

    def greet(self, tp=False):
        barrier = pltpu.get_barrier_semaphore()
        others = [{"fsdp": lax.rem(self.z + s, self.n_fsdp)} for s in range(1, self.n_fsdp)]
        others += [{"ctx": flip(self.ct, mask)} for mask in self.masks]
        if tp:
            others.append({"tp": 1 - lax.axis_index("tp")})
        for other in others:
            pl.semaphore_signal(
                barrier, inc=1, device_id=other, device_id_type=pl.DeviceIdType.MESH
            )
        pl.semaphore_wait(barrier, len(others))

    def copy(self, source, target, device, at=None):
        if at is None:
            at = self.used
            self.used += 1
        return pltpu.make_async_remote_copy(
            src_ref=source,
            dst_ref=target,
            send_sem=self.send.at[at],
            recv_sem=self.recv.at[at],
            device_id=device,
            device_id_type=pl.DeviceIdType.MESH,
        )

    def go(self, source, target, device):
        copy = self.copy(source, target, device)
        copy.start()
        self.open.append((None, copy))
        return copy

    def along(self, item, owner, right, ok, source, slot):
        target = item.whole_at(owner, self.part(item))
        device = {"fsdp": lax.rem(self.z + (1 if right else self.n_fsdp - 1), self.n_fsdp)}
        copy = self.copy(source, target, device, self.came[item] + slot - 1)
        pl.when(ok)(copy.start)
        self.open.append((ok, copy))

    def begin(self, item):
        if isinstance(item, Pair):
            self.waiting[item] = [[] for _ in self.masks]
            self.cast(item, item.slot_at, lambda k, level: item.slot_at(k + 2**level), 0, 0)
            return
        if isinstance(item, Weight):
            self.came[item] = self.used
            self.used += self.n_fsdp - 1
            source = item.shard_at(self.part(item))
            self.along(item, self.z, True, self.z < self.n_fsdp - 1, source, 1)
            self.along(item, self.z, False, self.z > 0, source, self.n_fsdp - 1)
            return
        self.came[item] = [
            self.go(
                item.source_at(lax.rem(self.z + s, self.n_fsdp)),
                item.rows_at(s),
                {"fsdp": lax.rem(self.z + s, self.n_fsdp)},
            )
            for s in range(1, self.n_fsdp)
        ]

    def cast(self, item, source_at, target_at, k, first):
        skip = self.skip(item)
        for level in range(first, len(self.masks) - skip):
            device = {"ctx": flip(self.ct, self.masks[level + skip])}
            copy = self.go(source_at(k), target_at(k, level), device)
            self.waiting[item][level].append((copy, k + 2**level, source_at, target_at))

    def relay(self, item):
        if isinstance(item, Deal):
            for copy in self.came[item]:
                copy.wait_recv()
            return
        self.waiting[item] = [[] for _ in self.masks[item.skip :]]
        n, part = self.n_fsdp, self.part(item)
        others = offsets(self.n_ctx >> item.skip)
        if item.own is not None:

            def mine(k):
                return item.own if k == 0 else item.whole_at(self.z, flip(part, others[k]))

            def lands(k, level):
                return item.whole_at(self.z, flip(part, others[k]))

            self.cast(item, mine, lands, 0, 0)
        for i in range(n - 1):
            s = i // 2 + 1 if i % 2 == 0 else n - 1 - i // 2
            owner = lax.rem(self.z - s + n, n)
            here = item.whole_at(owner, part)
            self.copy(here, here, {"fsdp": owner}, self.came[item] + s - 1).wait_recv()
            if s < n - 1:
                ok = (self.z >= s) & (self.z < n - 1)
                self.along(item, owner, True, ok, here, s + 1)
            if s > 1:
                ok = (self.z < s) & (self.z > 0)
                self.along(item, owner, False, ok, here, s - 1)

            def at(k, owner=owner):
                return item.whole_at(owner, flip(part, others[k]))

            self.cast(item, at, lambda k, level, at=at: at(k), 0, 0)

    def finish(self, item, level):
        if isinstance(item, Deal) or level != self.done.get(item, 0):
            return
        if level == len(self.waiting[item]):
            return
        for copy, k, source_at, target_at in self.waiting[item][level]:
            copy.wait_recv()
            self.cast(item, source_at, target_at, k, level + 1)
        self.done[item] = level + 1

    def complete(self, item):
        while self.done.get(item, 0) < len(self.waiting[item]):
            self.finish(item, self.done.get(item, 0))

    def close(self):
        for ok, copy in self.open:
            if ok is None:
                copy.wait_send()
            else:
                pl.when(ok)(copy.wait_send)


def copies_of(items, n_fsdp, n_ctx):
    total = 0
    for item in items:
        total += {Weight: (n_fsdp - 1) * n_ctx, Deal: n_fsdp - 1, Pair: n_ctx - 1}[item]
    return total


def keep(stay, room, sems):
    out = []
    for k, (source, target) in enumerate(stay):
        first = pltpu.make_async_copy(source, room[k], sems.at[2 * k])
        first.start()
        out.append((first, pltpu.make_async_copy(room[k], target, sems.at[2 * k + 1])))
    return out


def move(make, kinds, inputs, outputs, n_fsdp, n_ctx, local_shapes, ident, ahead=2, foot=None):
    n_in = len(inputs)
    n_copy = copies_of(kinds, n_fsdp, n_ctx)

    def kernel(*refs):
        ins, outs = refs[:n_in], refs[n_in : n_in + len(outputs)]
        send, recv, here = refs[n_in + len(outputs) : n_in + len(outputs) + 3]
        room = refs[n_in + len(outputs) + 3 :]
        if foot is not None:
            blocks_ref, ins = ins[-1], ins[:-1]
            strip = room[-1]
        mover = Mover(n_fsdp, n_ctx, send, recv)
        items, stay = make(ins, outs, mover.z)
        mover.greet()
        for item in items[:ahead]:
            mover.begin(item)
        kept = keep(stay, room, here)
        levels = len(mover.masks)
        for i in range(len(items) + levels):
            if i < len(items):
                mover.relay(items[i])
                if i + ahead < len(items):
                    mover.begin(items[i + ahead])
            if i == 0 and foot is not None:
                strip[...] = jnp.zeros_like(strip)
                high, wide = blocks_ref.shape[1:]
                for j in range(blocks_ref.shape[0]):
                    strip[j * high : (j + 1) * high, j * wide : (j + 1) * wide] = blocks_ref[j]
                set_foot = pltpu.make_async_copy(strip, foot[1](outs), here.at[2 * len(local_shapes)])
                set_foot.start()
                kept.append((None, set_foot))
            if i == 0:
                for first, second in kept:
                    if first is not None:
                        first.wait()
                        second.start()
            for level in range(levels):
                if 0 <= i - 1 - level < len(items):
                    mover.finish(items[i - 1 - level], level)
        for _, second in kept:
            second.wait()
        mover.close()

    spaces = [pl.BlockSpec(memory_space=pl.ANY)] * n_in
    room_shapes = list(local_shapes)
    if foot is not None:
        blocks = foot[0]
        inputs = inputs + (blocks,)
        n_in += 1
        spaces.append(pl.BlockSpec(memory_space=pltpu.VMEM))
        room_shapes.append((blocks.shape[0] * blocks.shape[1], blocks.shape[0] * blocks.shape[2]))
    return pl.pallas_call(
        kernel,
        in_specs=spaces,
        out_specs=[pl.BlockSpec(memory_space=pl.ANY)] * len(outputs),
        out_shape=[jax.ShapeDtypeStruct(shape, BF16) for shape in outputs],
        scratch_shapes=[
            pltpu.SemaphoreType.DMA((n_copy,)),
            pltpu.SemaphoreType.DMA((n_copy,)),
            pltpu.SemaphoreType.DMA((2 * len(local_shapes) + 1,)),
        ]
        + [pltpu.VMEM(shape, BF16) for shape in room_shapes],
        compiler_params=pltpu.CompilerParams(
            collective_id=ident, has_side_effects=True, vmem_limit_bytes=60 << 20
        ),
    )(*inputs)


def forward_and_gather(
    x_rows, qkv_x, a_qkv, picked, bias, gain, shift_by, first_maps, shards, maps, n_fsdp, n_ctx
):
    per, loc, width = x_rows.shape
    w_out, w_up, w_down = shards
    width_here = qkv_x.shape[1] // 3
    heads, units = width_here // HEAD_DIM, w_up.shape[1]
    zu, zo = w_up.shape[0], w_out.shape[1]
    n_part = n_ctx // 2 if n_ctx > 1 else 1
    so, su, sd = w_out.shape[0] // n_ctx, zu // n_ctx, w_down.shape[0] // n_ctx
    wide = width + NR
    wide_x = width + 3 * NR
    cuts = 4
    paired = cuts // 2 if n_ctx > 1 else 0
    tile = 512
    per_kind = width_here // tile
    chunk = 32
    n_tile = 3 * per_kind
    n_copy = (n_fsdp - 1) * n_ctx * (1 + 2 * cuts) + 2 * per * (n_ctx - 1) + 6 + per
    lag = 4

    def kernel(*refs):
        bias_ref, a_ref, pick_ref, gain_ref, shift_ref, a_up_ref, b_out_ref, x_ref, w_ref = refs[:9]
        wo_ref, wu_ref, wd_ref, ao_ref, bu_ref, ad_ref = refs[9:15]
        slots = refs[15 : 14 + n_ctx]
        q_ref, kv_ref, adapt_ref, out_ref, up_ref, down_ref, ctx_ref, log_ref = refs[
            14 + n_ctx : 22 + n_ctx
        ]
        h_ref, gelu_ref, slope_ref, hat_ref, rstd_ref, adapt_out_ref, adapt_up_ref = refs[
            22 + n_ctx : 29 + n_ctx
        ]
        send, recv, here, load, ring_sem, x_room, w_room, proj, kv_room, out_room = refs[
            29 + n_ctx : 39 + n_ctx
        ]
        part_ref, other_ref, up_room, wide_v, hat1, gelu, slope = refs[39 + n_ctx :]
        mover = Mover(n_fsdp, n_ctx, send, recv)
        ring = Ring(
            w_room,
            ring_sem,
            0,
            lambda t: w_ref.at[:, ds(lax.rem(t + per_kind, n_tile) * tile, tile)],
        )
        z = mover.z
        rows = [pl.ds(g * loc, loc) for g in range(per)]

        def columns(j):
            return pl.ds(j * width_here, width_here)

        out_item = Weight(
            lambda c: wo_ref.at[ds(c * so, so)],
            lambda o, c: out_ref.at[ds(c * so, so), ds(o * zo, zo)],
        )

        def up_item(h):
            at = pl.ds(h * (units // cuts), units // cuts)
            return Weight(
                lambda c: wu_ref.at[ds(c * su, su), at],
                lambda o, c: up_ref.at[ds(o * zu + c * su, su), at],
            )

        def down_item(h):
            size = sd // cuts
            return Weight(
                lambda c: wd_ref.at[ds(c * sd + h * size, size)],
                lambda o, c: down_ref.at[ds(c * sd + h * size, size), ds(o * zo, zo)],
            )

        def down_pair(h):
            size = sd // cuts

            def at(c, p):
                return ds((c + p * n_part) * sd + h * size, size)

            def half(p):
                return Weight(
                    lambda c: wd_ref.at[at(c, p)],
                    lambda o, c: down_ref.at[at(c, p), ds(o * zo, zo)],
                    skip=1,
                )

            return [half(p) for p in range(2)]

        def pair(g, j):
            return Pair(
                lambda k: proj.at[rows[g], columns(1 + j)] if k == 0 else slots[k - 1].at[j, g]
            )

        pairs = [pair(g, j) for g in range(per) for j in range(2)]
        items = [out_item] + [up_item(h) for h in range(cuts)]
        items += [down_item(h) for h in range(cuts - paired)]
        for h in range(cuts - paired, cuts):
            items += down_pair(h)
        used = [0]

        def move(source, target):
            copy = pltpu.make_async_copy(source, target, here.at[used[0]])
            used[0] += 1
            copy.start()
            return copy

        def attend(g):
            for j in range(2):
                mover.complete(pairs[2 * g + j])
            loads = []
            for k in range(1, n_ctx):
                copy = pltpu.make_async_copy(slots[k - 1].at[:, g], kv_room.at[k], load.at[k])
                copy.start()
                loads.append(copy)
            for j in range(2):
                kv_room[0, j] = proj[g * loc : (g + 1) * loc, (1 + j) * width_here : (2 + j) * width_here]
            for copy in loads:
                copy.wait()

            def one(h, carry):
                at = ds(h * HEAD_DIM, HEAD_DIM)
                biases = []
                for k in range(n_ctx):
                    block = bias_ref[g, k * loc : (k + 1) * loc, :]
                    biases.append(jnp.concatenate([block] * (loc // 128), axis=1))
                context, log = attend_head(
                    proj[g * loc : (g + 1) * loc, at],
                    [kv_room[k, 0, :, at] for k in range(n_ctx)],
                    [kv_room[k, 1, :, at] for k in range(n_ctx)],
                    biases,
                )
                ctx_ref[g, :, at] = context
                log_ref[g, h] = log
                return carry

            lax.fori_loop(0, heads, one, 0)

        def project():
            mover.complete(out_item)
            own[0].wait_recv()
            own[3].wait_recv()
            copy = pltpu.make_async_copy(out_ref, out_room, load.at[0])
            copy.start()
            copy.wait()
            for g in range(per):
                for start in range(0, wide, 1024):
                    at = slice(start, min(start + 1024, wide))
                    part_ref[g, :, at] = dot(ctx_ref[g], out_room[:, at]).astype(BF16)
                swapped.append(
                    mover.go(
                        part_ref.at[g], other_ref.at[g], {"tp": 1 - lax.axis_index("tp")}
                    )
                )

        def tiles(t, room):
            at = ds(lax.rem(t + per_kind, n_tile) * tile, tile)
            proj[:, at] = dot(x_room[...], room[...]).astype(BF16)

        up_ring = Ring(up_room, ring_sem, 2, lambda t: up_ref.at[:, ds(t * tile, tile)])

        def first_norm(g):
            swapped[g].wait_recv()
            pick = pick_ref[g]

            def step(r, carry):
                rows_r = ds(r * chunk, chunk)
                total = part_ref[g, rows_r, :].astype(F32) + other_ref[g, rows_r, :].astype(F32)
                code = (total[:, width:] * pick).astype(BF16)
                adapt_out_ref[g, rows_r, :] = code
                x = x_room[ds(g * loc + r * chunk, chunk), :width].astype(F32)
                hat, rstd = norm_parts(x + total[:, :width] + dot(code, b_out_ref[...]))
                hat1[g, rows_r, :] = hat
                rstd_ref[g, rows_r, :] = jnp.broadcast_to(rstd, (chunk, 128))
                low = (hat * gain_ref[0:1, :] + shift_ref[0:1, :]).astype(BF16)
                wide_v[g, rows_r, :width] = low
                code = (dot(low, a_up_ref[...]) * pick).astype(BF16)
                wide_v[g, rows_r, width:] = code
                adapt_up_ref[g, rows_r, :] = code
                return carry

            lax.fori_loop(0, loc // chunk, step, 0)
            outward.append(move(hat1.at[g], hat_ref.at[g]))
            outward.append(move(wide_v.at[g], h_ref.at[g]))

        def feed(g):
            if g == 0:
                for item in items[1 : 1 + cuts]:
                    mover.complete(item)
                own[1].wait_recv()
                own[4].wait_recv()
                up_ring.prefetch()

            def up_tile(t, room):
                at = ds(t * tile, tile)
                value, factor = gelu_both(dot(wide_v[g], room[...]))
                gelu[g, :, at] = value
                slope[g, :, at] = factor

            up_ring.run(units // tile, up_tile)
            if g + 1 < per:
                up_ring.prefetch()
            outward.append(move(gelu.at[g], gelu_ref.at[g]))
            outward.append(move(slope.at[g], slope_ref.at[g]))

        swapped, outward = [], []
        tasks = {1 + g: (lambda g=g: attend(g)) for g in range(per)}
        tasks[per + 2] = project
        tasks[per + 5] = lambda: [first_norm(g) for g in range(per)]
        for g in range(per):
            tasks[per + 6 + g] = lambda g=g: feed(g)
        ring.prefetch()
        loads = [move(x_ref.at[g], x_room.at[rows[g], pl.ds(0, width)]) for g in range(per)]
        mover.greet(tp=True)
        ahead = 3
        for item in items[:ahead]:
            mover.begin(item)
        sibling = {"ctx": flip(mover.ct, 1)}
        own = [
            mover.go(source, target, sibling)
            for source, target in (
                (wo_ref, out_ref.at[:, ds(z * zo, zo)]),
                (wu_ref, up_ref.at[ds(z * zu, zu)]),
                (wd_ref, down_ref.at[:, ds(z * zo, zo)]),
                (ao_ref, out_ref.at[:, pl.ds(width, NR)]),
                (bu_ref, up_ref.at[pl.ds(width, NR)]),
                (ad_ref, down_ref.at[:, pl.ds(width, NR)]),
            )
        ]
        for g in range(per):
            loads[g].wait()
            pick = pick_ref[g]
            for j in range(3):
                code = dot(x_room[g * loc : (g + 1) * loc, :width], a_ref[j]) * pick
                x_room[g * loc : (g + 1) * loc, width + j * NR : width + (j + 1) * NR] = code.astype(BF16)
            outward.append(move(x_room.at[rows[g], pl.ds(width, 3 * NR)], adapt_ref.at[g]))
        ring.run(2 * per_kind, tiles, 0, n_tile)
        for item in pairs:
            mover.begin(item)
        for g in range(per):
            for j in range(2):
                outward.append(move(proj.at[rows[g], columns(1 + j)], kv_ref.at[j, g]))
        for i in range(len(items) + lag + 2):
            if i < len(items):
                mover.relay(items[i])
                if i + ahead < len(items):
                    mover.begin(items[i + ahead])
            if i == 0:
                ring.run(n_tile, tiles, 2 * per_kind, n_tile)
                for g in range(per):
                    outward.append(move(proj.at[rows[g], columns(0)], q_ref.at[g]))
            for level in range(len(mover.masks)):
                if 0 <= i - lag - level < len(items):
                    mover.finish(items[i - lag - level], level)
            if i in tasks:
                tasks[i]()
        for item in items:
            mover.complete(item)
        for copy in (own[2], own[5]):
            copy.wait_recv()
        for copy in outward:
            copy.wait()
        mover.close()

    row = (per, loc, width_here)
    pair_shape = (2,) + row
    vmem, anywhere = pl.BlockSpec(memory_space=pltpu.VMEM), pl.BlockSpec(memory_space=pl.ANY)
    outputs = [(pair_shape, BF16, anywhere)] * (n_ctx - 1) + [
        (row, BF16, anywhere),
        (pair_shape, BF16, anywhere),
        ((per, loc, 3 * NR), BF16, anywhere),
        ((width_here, wide), BF16, anywhere),
        ((wide, units), BF16, anywhere),
        ((units, wide), BF16, anywhere),
        (row, BF16, vmem),
        ((per, heads, 1, loc), F32, vmem),
        ((per, loc, wide), BF16, anywhere),
        ((per, loc, units), BF16, anywhere),
        ((per, loc, units), BF16, anywhere),
        ((per, loc, width), F32, anywhere),
        ((per, loc, 128), F32, vmem),
        ((per, loc, NR), BF16, vmem),
        ((per, loc, NR), BF16, vmem),
    ]
    return pl.pallas_call(
        kernel,
        in_specs=[vmem] * 7 + [anywhere] * 8,
        out_specs=[space for _, _, space in outputs],
        out_shape=[jax.ShapeDtypeStruct(shape, dtype) for shape, dtype, _ in outputs],
        scratch_shapes=[
            pltpu.SemaphoreType.DMA((n_copy,)),
            pltpu.SemaphoreType.DMA((n_copy,)),
            pltpu.SemaphoreType.DMA((9 * per,)),
            pltpu.SemaphoreType.DMA((n_ctx,)),
            pltpu.SemaphoreType.DMA((4,)),
            pltpu.VMEM((per * loc, wide_x), BF16),
            pltpu.VMEM((2, wide_x, tile), BF16),
            pltpu.VMEM((per * loc, 3 * width_here), BF16),
            pltpu.VMEM((n_ctx, 2, loc, width_here), BF16),
            pltpu.VMEM((width_here, wide), BF16),
            pltpu.VMEM((per, loc, wide), BF16),
            pltpu.VMEM((per, loc, wide), BF16),
            pltpu.VMEM((2, wide, tile), BF16),
            pltpu.VMEM((per, loc, wide), BF16),
            pltpu.VMEM((per, loc, width), F32),
            pltpu.VMEM((per, loc, units), BF16),
            pltpu.VMEM((per, loc, units), BF16),
        ],
        compiler_params=pltpu.CompilerParams(
            collective_id=1, has_side_effects=True, vmem_limit_bytes=60 << 20
        ),
    )(bias, a_qkv, picked, gain, shift_by, *first_maps, x_rows, qkv_x, w_out, w_up, w_down, *maps)


class Ring:
    def __init__(self, room, sems, at, tile_at):
        self.room, self.sems, self.at, self.tile_at = room, sems, at, tile_at

    def copy(self, t):
        slot = lax.rem(t, 2)
        return pltpu.make_async_copy(
            self.tile_at(t), self.room.at[slot], self.sems.at[self.at + slot]
        )

    def prefetch(self):
        self.copy(0).start()
        self.copy(1).start()

    def run(self, n, body, first=0, total=None):
        total = n if total is None else total

        def step(t, carry):
            self.copy(t).wait()
            body(t, self.room.at[lax.rem(t, 2)])

            @pl.when(t + 2 < total)
            def _():
                self.copy(t + 2).start()

            return carry

        lax.fori_loop(first, n, step, 0)


def compact(out_ref, n, entries, sizes):
    column = lax.broadcasted_iota(jnp.int32, (NR, RANK), 0)
    rank = lax.broadcasted_iota(jnp.int32, (NR, RANK), 1)
    used = jnp.where(lax.rem(column, RANK) == rank, 1.0, 0.0).astype(BF16)
    start = 0
    for (code, value), size in zip(entries, sizes):
        short = dot(code(), used).astype(BF16)
        block = dot_tn(short, value()).astype(BF16)
        for k in range(out_ref.shape[0]):
            out_ref[k, n * RANK : (n + 1) * RANK, start : start + size] = block[
                :, k * size : (k + 1) * size
            ]
        start += size


class Fold:
    def __init__(self, mover, parts, came, out_ref):
        self.mover, self.parts, self.came, self.out_ref = mover, parts, came, out_ref
        self.flying = {}

    def at(self, k):
        return flip(self.mover.ct, self.mover.offsets[k])

    def hand(self, level):
        half = 2**level
        self.flying[level] = [
            self.mover.go(
                self.parts.at[self.at(half + i)],
                self.came.at[half - 1 + i],
                {"ctx": flip(self.mover.ct, self.mover.masks[level])},
            )
            for i in range(half)
        ]

    def take(self, level):
        for i, copy in enumerate(self.flying[level]):
            copy.wait_recv()
            total = self.parts[self.at(i)].astype(F32) + self.came[2**level - 1 + i].astype(F32)
            self.parts[self.at(i)] = total.astype(BF16)

    def next(self, level):
        self.take(level)
        if level:
            self.hand(level - 1)

    def gather(self):
        own = self.parts.at[self.mover.ct]
        item = Weight(lambda c: self.parts.at[c], lambda o, c: self.out_ref.at[c, o], own)
        self.mover.begin(item)
        return own, self.out_ref.at[self.mover.ct, self.mover.z], item


def norm_parts(values):
    center = values - jnp.mean(values, axis=-1, keepdims=True)
    rstd = lax.rsqrt(jnp.mean(center * center, axis=-1, keepdims=True) + NORM_EPS)
    return center * rstd, rstd


def norm_back(hat, rstd, dhat):
    first = jnp.mean(dhat, axis=-1, keepdims=True)
    second = jnp.mean(dhat * hat, axis=-1, keepdims=True)
    return rstd * (dhat - first - hat * second)


def gelu_both(pre):
    square = pre * pre
    bent = jnp.tanh(GELU_COEF * (pre + 0.044715 * square * pre))
    out = 0.5 * pre * (1.0 + bent)
    slope = 0.5 * (1.0 + bent) + 0.5 * pre * (1.0 - bent * bent) * GELU_COEF * (
        1.0 + 3.0 * 0.044715 * square
    )
    return out.astype(BF16), slope.astype(BF16)


def middle(hats, rstds, gelus, slopes, adapt_up, cot, picked, gain, shift_by, weights, maps, n_fsdp, n_ctx):
    per, loc, width = hats.shape
    piece = cot.shape[1]
    out_x, up_x, down_x = weights
    a_up, b_out, b_down, a_down, b_up = maps
    wide, units = up_x.shape
    width_here = out_x.shape[0]
    tile = 512
    chunk = 32
    n_wide = width // tile
    n_swap = n_wide + 1
    sizes = [width // n_ctx, units // n_ctx, units // n_ctx]

    def kernel(*refs):
        pick_ref, gain_ref, shift_ref, rstd1, code_up_ref = refs[:5]
        a_up_ref, b_out_ref, b_down_ref, a_down_ref, b_up_ref = refs[5:10]
        hat_ref, gelu_ref, slope_ref, cot_ref, out_ref, up_ref, down_ref = refs[10:17]
        acts_out, dy1_out, da_out, cot_rows, grads_out, back_out = refs[17:23]
        dadapt_up_ref, ctx_ref = refs[23:25]
        (send, recv, deal_send, deal_recv, ring_sem, sems) = refs[25:31]
        (down_room, down_rows, up_rows) = refs[31:34]
        (stage, part, got, hat1, keep32, slope, gelu, wide_v, turned, dpre_t) = refs[34:44]
        codes_down, grads_part, grads_came = refs[44:]
        mover = Mover(n_fsdp, n_ctx, deal_send, deal_recv)
        partner = {"tp": 1 - lax.axis_index("tp")}

        down = Ring(down_room, ring_sem, 0, lambda t: down_ref.at[:, ds(t * tile, tile)])
        down_r = Ring(down_rows, ring_sem, 4, lambda t: down_ref.at[ds(t * tile, tile)])
        up_r = Ring(up_rows, ring_sem, 6, lambda t: up_ref.at[ds(t * tile, tile)])
        out_r = Ring(down_rows, ring_sem, 4, lambda t: out_ref.at[ds(t * tile, tile)])

        busy = {}
        used = [0]

        def move(source, target, key):
            copy = pltpu.make_async_copy(source, target, sems.at[used[0]])
            used[0] += 1
            copy.start()
            busy.setdefault(key, []).append(copy)

        def free(*keys):
            for key in keys:
                for copy in busy.pop(key, []):
                    copy.wait()

        def swap_copy(turn, g, t, size):
            at = ds(t * tile, size)
            sem = (turn * per + g) * n_swap + t
            return pltpu.make_async_remote_copy(
                src_ref=part.at[g, :, at],
                dst_ref=got.at[turn, g, :, at],
                send_sem=send.at[sem],
                recv_sem=recv.at[sem],
                device_id=partner,
                device_id_type=pl.DeviceIdType.MESH,
            )

        def swapped(turn, g):
            for t in range(n_swap):
                copy = swap_copy(turn, g, t, tile if t < n_wide else NR)
                copy.wait_recv()
                copy.wait_send()

        def by_rows(body):
            def step(r, carry):
                body(pl.ds(pl.multiple_of(r * chunk, chunk), chunk))
                return carry

            lax.fori_loop(0, loc // chunk, step, 0)

        def deal(g):
            return Deal(lambda to: cot_ref.at[to * per + g], lambda s: cot_rows.at[g, s])

        deals = [deal(g) for g in range(per)]
        dealt = []
        for g in range(per):
            move(gelu_ref.at[g], gelu.at[g], ("gelu", g))
            if g == 0:
                down.prefetch()
            move(cot_ref.at[mover.z * per + g], cot_rows.at[g, 0], ("cot", g))
        for g in range(per):
            move(hat_ref.at[g], hat1.at[g], ("hat", g))
            move(slope_ref.at[g], slope.at[g], ("slope", g))
        mover.greet(tp=True)
        mover.begin(deals[0])

        for g in range(per):
            if g + 1 == per:
                down_r.prefetch()
            free(("gelu", g))

            def down_tile(t, room, g=g):
                part[g, :, ds(t * tile, tile)] = dot(gelu[g], room[...]).astype(BF16)
                swap_copy(0, g, t, tile).start()

            down.run(n_wide, down_tile)
            if g + 1 < per:
                down.prefetch()
            else:
                up_r.prefetch()
            part[g, :, width:] = dot(gelu[g], a_down_ref[...]).astype(BF16)
            swap_copy(0, g, n_wide, NR).start()

        for g in range(per):
            mover.relay(deals[g])
            if g + 1 < per:
                mover.begin(deals[g + 1])
            free(("cot", g))
            for s in range(n_fsdp):
                at = pl.ds(s * cot.shape[1], cot.shape[1])
                move(cot_rows.at[g, s], stage.at[g, at], ("stage", g))
            swapped(0, g)
            free(("stage", g), ("hat", g), ("slope", g))
            pick = pick_ref[g]

            def second_norm(rows, g=g, pick=pick):
                total = part[g, rows, :].astype(F32) + got[0, g, rows, :].astype(F32)
                code = (total[:, width:] * pick).astype(BF16)
                codes_down[g, rows, :] = code
                hidden = hat1[g, rows, :] * gain_ref[0:1, :] + shift_ref[0:1, :]
                hat, rstd = norm_parts(hidden + total[:, :width] + dot(code, b_down_ref[...]))
                part[g, rows, :width] = (hat * gain_ref[1:2, :] + shift_ref[1:2, :]).astype(BF16)
                dy2 = norm_back(hat, rstd, stage[g, rows, :].astype(F32) * gain_ref[1:2, :])
                keep32[g, rows, :] = dy2
                low = dy2.astype(BF16)
                wide_v[g, rows, :width] = low
                wide_v[g, rows, width:] = (dot_nt(low, b_down_ref[...]) * pick).astype(BF16)

            by_rows(second_norm)
            move(part.at[g, :, pl.ds(0, width)], acts_out.at[g], ("part", g))
            own = part.at[g, pl.ds(0, piece), pl.ds(0, width)]
            move(own, back_out.at[mover.z * per + g], ("part", g))
            turned[...] = wide_v[g].T

            def down_back(t, room, g=g):
                at = ds(t * tile, tile)
                block = dot(room[...], turned[...]).T
                low = (block * slope[g, :, at].astype(F32)).astype(BF16)
                slope[g, :, at] = low
                dpre_t[at, :] = low.T

            down_r.run(units // tile, down_back)
            (down_r if g + 1 < per else out_r).prefetch()
            free(("part", g))
            for s in range(1, n_fsdp):
                to = lax.rem(mover.z - s + n_fsdp, n_fsdp)
                rows_s = acts_out.at[g, pl.ds(s * piece, piece)]
                dealt.append(mover.go(rows_s, back_out.at[mover.z * per + g], {"fsdp": to}))

            def up_back(t, room, g=g):
                part[g, :, ds(t * tile, tile)] = dot(room[...], dpre_t[...]).T.astype(BF16)
                swap_copy(1, g, t, tile).start()

            up_r.run(n_wide, up_back)
            if g + 1 < per:
                up_r.prefetch()
            part[g, :, width:] = dot(b_up_ref[...], dpre_t[...]).T.astype(BF16)
            swap_copy(1, g, n_wide, NR).start()

        for g in range(per):
            entries = [
                (lambda g=g: codes_down[g], lambda g=g: wide_v[g, :, :width]),
                (lambda g=g: wide_v[g, :, width:], lambda g=g: gelu[g]),
                (lambda g=g: code_up_ref[g], lambda g=g: slope[g]),
            ]
            compact(grads_part, g, entries, sizes)

        fold = Fold(mover, grads_part, grads_came, grads_out)
        lasting = len(mover.masks) - 1
        fold.hand(lasting)
        for g in range(per):
            swapped(1, g)
            pick = pick_ref[g]

            def first_back(rows, g=g, pick=pick):
                total = part[g, rows, :].astype(F32) + got[1, g, rows, :].astype(F32)
                code = (total[:, width:] * pick).astype(BF16)
                dadapt_up_ref[g, rows, :] = code
                dh1 = keep32[g, rows, :] + total[:, :width] + dot_nt(code, a_up_ref[...])
                rstd = rstd1[g, rows, 0:1]
                dy1 = norm_back(hat1[g, rows, :], rstd, dh1 * gain_ref[0:1, :])
                keep32[g, rows, :] = dy1
                low = dy1.astype(BF16)
                wide_v[g, rows, :width] = low
                wide_v[g, rows, width:] = (dot_nt(low, b_out_ref[...]) * pick).astype(BF16)

            by_rows(first_back)
            if g == 0:
                fold.next(lasting)
            move(keep32.at[g], dy1_out.at[g], "dy1")
            move(wide_v.at[g], da_out.at[g], "wide")
            turned[...] = wide_v[g].T

            def out_back(t, room, g=g):
                ctx_ref[g, :, ds(t * tile, tile)] = dot(room[...], turned[...]).T.astype(BF16)

            out_r.run(width_here // tile, out_back)
            if g + 1 < per:
                out_r.prefetch()
            if g == 0:
                for level in range(lasting - 1, -1, -1):
                    fold.next(level)
                source, target, item = fold.gather()
                move(source, target, "grads")
                mover.relay(item)
        mover.complete(item)
        for copy in dealt:
            copy.wait_recv()
        free(*list(busy))
        mover.close()

    vmem, anywhere = pl.BlockSpec(memory_space=pltpu.VMEM), pl.BlockSpec(memory_space=pl.ANY)
    row = (per, loc)
    grads_shape = (n_ctx, per * RANK, sum(sizes))
    outputs = [
        (row + (width,), BF16, anywhere),
        (row + (width,), F32, anywhere),
        (row + (wide,), BF16, anywhere),
        ((per, n_fsdp) + cot.shape[1:], BF16, anywhere),
        ((n_ctx, n_fsdp) + grads_shape[1:], BF16, anywhere),
        (cot.shape, BF16, anywhere),
        (row + (NR,), BF16, vmem),
        (row + (width_here,), BF16, vmem),
    ]
    n_copy = 2 * per * n_swap
    n_deal = 2 * per * (n_fsdp - 1) + (n_fsdp - 1) * n_ctx + 2 * (n_ctx - 1)
    return pl.pallas_call(
        kernel,
        in_specs=[vmem] * 10 + [anywhere] * 7,
        out_specs=[space for _, _, space in outputs],
        out_shape=[jax.ShapeDtypeStruct(shape, dtype) for shape, dtype, _ in outputs],
        scratch_shapes=[
            pltpu.SemaphoreType.DMA((n_copy,)),
            pltpu.SemaphoreType.DMA((n_copy,)),
            pltpu.SemaphoreType.DMA((n_deal,)),
            pltpu.SemaphoreType.DMA((n_deal,)),
            pltpu.SemaphoreType.DMA((8,)),
            pltpu.SemaphoreType.DMA(((8 + n_fsdp) * per + 1,)),
            pltpu.VMEM((2, units, tile), BF16),
            pltpu.VMEM((2, tile, wide), BF16),
            pltpu.VMEM((2, tile, units), BF16),
            pltpu.VMEM(row + (width,), BF16),
            pltpu.VMEM(row + (wide,), BF16),
            pltpu.VMEM((2,) + row + (wide,), BF16),
            pltpu.VMEM(row + (width,), F32),
            pltpu.VMEM(row + (width,), F32),
            pltpu.VMEM(row + (units,), BF16),
            pltpu.VMEM(row + (units,), BF16),
            pltpu.VMEM(row + (wide,), BF16),
            pltpu.VMEM((wide, loc), BF16),
            pltpu.VMEM((units, loc), BF16),
            pltpu.VMEM(row + (NR,), BF16),
            pltpu.VMEM(grads_shape, BF16),
            pltpu.VMEM((n_ctx - 1,) + grads_shape[1:], BF16),
        ],
        compiler_params=pltpu.CompilerParams(
            collective_id=3, has_side_effects=True, vmem_limit_bytes=62 << 20
        ),
    )(
        picked, gain, shift_by, rstds, adapt_up, a_up, b_out, b_down, a_down, b_up,
        hats, gelus, slopes, cot, out_x, up_x, down_x,
    )


def combine(pieces, chosen, shapes):
    n_part, n_fsdp, rows, columns = pieces.shape
    flat, specs = [], []
    for i, shape in enumerate(shapes):
        high, wide = shape[-2:]
        tall = wide == NR and high != NR
        size = (high if tall else wide) // n_part
        block = (size, NR) if tall else (NR, size)
        lead = shape[0] if len(shape) == 3 else None
        for j in range(lead or 1):
            flat.append((i, None if lead is None else j, tall, size))
        if lead is None:
            specs.append(pl.BlockSpec(block, (lambda c: (c, 0)) if tall else (lambda c: (0, c))))
        else:
            specs.append(
                pl.BlockSpec(
                    (lead,) + block, (lambda c: (0, c, 0)) if tall else (lambda c: (0, 0, c))
                )
            )

    def kernel(chosen_ref, piece_ref, *outs):
        ordered = jnp.concatenate([piece_ref[0, a] for a in range(n_fsdp)], axis=0)
        start = 0
        for i, lead, tall, size in flat:
            block = ordered[:, start : start + size]
            value = dot_tn(block, chosen_ref[...]) if tall else dot_tn(chosen_ref[...], block)
            if lead is None:
                outs[i][...] = value
            else:
                outs[i][lead] = value
            start += size

    return pl.pallas_call(
        kernel,
        grid=(n_part,),
        in_specs=[
            pl.BlockSpec(chosen.shape, lambda c: (0, 0)),
            pl.BlockSpec((1, n_fsdp, rows, columns), lambda c: (c, 0, 0, 0)),
        ],
        out_specs=specs,
        out_shape=[jax.ShapeDtypeStruct(shape, F32) for shape in shapes],
        compiler_params=pltpu.CompilerParams(vmem_limit_bytes=48 << 20),
    )(chosen, pieces)


def finish(
    query, kv_own, slots, bias, grad, log_total, x_rows, adapt_in, dy1, qkv_x, a_qkv, picked, early, pairs, n_fsdp, n_ctx
):
    per, loc, width_here = query.shape
    piece, width = loc // n_fsdp, x_rows.shape[2]
    heads = width_here // HEAD_DIM
    cuts = 4
    high = heads // cuts
    columns = high * HEAD_DIM
    masks = masks_of(n_ctx)
    units = [(g, c) for g in range(per) for c in range(cuts)]
    depth = 3 * width_here
    foot = 3 * NR
    wide = width + foot
    tile = 512
    n_wide = width // tile
    n_swap = n_wide + 1
    n_early = len(early)
    early_sizes = [values[2] // n_ctx for _, values in pairs]
    late_sizes = [width_here // n_ctx] * 3 + [width // n_ctx] * 3
    n_copy = len(units) * (n_ctx - 1) + per * n_wide * (n_fsdp - 1)
    n_copy += 2 * ((n_fsdp - 1) * n_ctx + 2 * (n_ctx - 1))

    def kernel(*refs):
        q_ref, bias_ref, g_ref, log_ref, x_ref, adapt_ref, a_ref, pick_ref = refs[:8]
        dy1_ref, w_ref, kv_ref = refs[8:11]
        slot_refs = refs[11 : 10 + n_ctx]
        early_refs = refs[10 + n_ctx : 10 + n_ctx + n_early]
        at = 10 + n_ctx + n_early
        in_ref, early_out, late_out = refs[at : at + 3]
        send, recv, swap_send, swap_recv, ring_sem, load, sems = refs[at + 3 : at + 10]
        kv_room, own, came, dq, dkv = refs[at + 10 : at + 15]
        tiles, foot_room, dy1_room, turned, part, got, codes_in, dx = refs[at + 15 : at + 23]
        early_part, early_came, late_part, late_came = refs[at + 23 : at + 27]
        staged = refs[at + 27 :]
        mover = Mover(n_fsdp, n_ctx, send, recv)
        z, ct = mover.z, mover.ct
        partner = {"tp": 1 - lax.axis_index("tp")}
        ring = Ring(tiles, ring_sem, 0, lambda t: w_ref.at[ds(t * tile, tile)])
        used = [0]
        kept, dealt, flying = [], [], {}

        def move(source, target):
            copy = pltpu.make_async_copy(source, target, sems.at[used[0]])
            used[0] += 1
            copy.start()
            return copy

        loads = []
        for g in range(per):
            loads.append([])
            for k in range(n_ctx):
                source = kv_ref if k == 0 else slot_refs[k - 1]
                copy = pltpu.make_async_copy(
                    source.at[:, g], kv_room.at[g, k], load.at[g * n_ctx + k]
                )
                copy.start()
                loads[g].append(copy)
        staging = [move(ref, room) for ref, room in zip(early_refs, staged)]
        load_foot = move(w_ref.at[pl.ds(width, foot)], foot_room)
        ring.prefetch()
        load_dy1 = move(dy1_ref, dy1_room)
        mover.greet(tp=True)

        def compute(u):
            g, c = units[u]
            if c == 0:
                for copy in loads[g]:
                    copy.wait()

            def one(h, carry):
                at = ds(c * columns + h * HEAD_DIM, HEAD_DIM)
                to = ds(h * HEAD_DIM, HEAD_DIM)
                biases = []
                for k in range(n_ctx):
                    block = bias_ref[g, k * loc : (k + 1) * loc, :]
                    biases.append(jnp.concatenate([block] * (loc // 128), axis=1))
                dquery, dkeys, dvalues = attend_back_head(
                    q_ref[g, :, at],
                    g_ref[g, :, at],
                    log_ref[g, c * high + h],
                    [kv_room[g, k, 0, :, at] for k in range(n_ctx)],
                    [kv_room[g, k, 1, :, at] for k in range(n_ctx)],
                    biases,
                )
                dq[g, :, at] = dquery
                for k in range(n_ctx):
                    own[u, k, 0, :, to] = dkeys[k]
                    own[u, k, 1, :, to] = dvalues[k]
                return carry

            lax.fori_loop(0, high, one, 0)

        def hand(u, level):
            half = 2**level
            device = {"ctx": flip(ct, masks[level])}
            flying[u, level] = [
                mover.go(own.at[u, half + i], came.at[u, half - 1 + i], device) for i in range(half)
            ]

        def take_in(u, level):
            half = 2**level
            g, c = units[u]
            for i, copy in enumerate(flying[u, level]):
                copy.wait_recv()
                for j in range(2):
                    total = own[u, i, j].astype(F32) + came[u, half - 1 + i, j].astype(F32)
                    if level:
                        own[u, i, j] = total.astype(BF16)
                    else:
                        dkv[j, g, :, c * columns : (c + 1) * columns] = total.astype(BF16)
            if level:
                hand(u, level - 1)

        def swap_copy(g, t):
            at = pl.ds(width, foot) if isinstance(t, int) and t == n_wide else ds(t * tile, tile)
            sem = g * n_swap + t
            return pltpu.make_async_remote_copy(
                src_ref=part.at[g, :, at],
                dst_ref=got.at[g, :, at],
                send_sem=swap_send.at[sem],
                recv_sem=swap_recv.at[sem],
                device_id=partner,
                device_id_type=pl.DeviceIdType.MESH,
            )

        def project_back(g):
            turned[0:width_here, :] = dq[g].T
            turned[width_here : 2 * width_here, :] = dkv[0, g].T
            turned[2 * width_here :, :] = dkv[1, g].T
            if g == 0:
                load_foot.wait()
            part[g, :, width:] = dot(foot_room[...], turned[...]).T.astype(BF16)
            swap_copy(g, n_wide).start()

            def back(t, room):
                part[g, :, ds(t * tile, tile)] = dot(room[...], turned[...]).T.astype(BF16)
                swap_copy(g, t).start()

            ring.run(n_wide, back)
            if g + 1 < per:
                ring.prefetch()

        def take_codes(g):
            swap_copy(g, n_wide).wait_recv()
            pick = jnp.concatenate([pick_ref[g]] * 3, axis=1)
            total = part[g, :, width:].astype(F32) + got[g, :, width:].astype(F32)
            codes_in[g] = (total * pick).astype(BF16)

        def finish_tile(g, t):
            swap_copy(g, t).wait_recv()
            at = slice(t * tile, (t + 1) * tile)
            value = part[g, :, at].astype(F32) + got[g, :, at].astype(F32) + dy1_room[g, :, at]
            for j in range(3):
                value = value + dot_nt(codes_in[g, :, j * NR : (j + 1) * NR], a_ref[j, at, :])
            dx[g, :, at] = value.astype(BF16)
            to_at = pl.ds(t * tile, tile)
            kept.append(move(dx.at[g, pl.ds(0, piece), to_at], in_ref.at[z * per + g, :, to_at]))
            for s in range(1, n_fsdp):
                to = lax.rem(z - s + n_fsdp, n_fsdp)
                dealt.append(
                    mover.go(
                        dx.at[g, pl.ds(s * piece, piece), to_at],
                        in_ref.at[z * per + g, :, to_at],
                        {"fsdp": to},
                    )
                )

        last = len(masks) - 1
        for t in range(len(units) + last):
            if t < len(units):
                compute(t)
                hand(t, last)
            for k in range(last):
                if 0 <= t - 1 - k < len(units):
                    take_in(t - 1 - k, last - k)
        for copy in staging:
            copy.wait()
        for n in range(per):
            entries = []
            for (i, first, size), (j, start, count) in pairs:
                entries.append(
                    (
                        lambda n=n, i=i, f=first, c=size: staged[i][n, :, f : f + c],
                        lambda n=n, i=j, f=start, c=count: staged[i][n, :, f : f + c],
                    )
                )
            compact(early_part, n, entries, early_sizes)
        early_fold = Fold(mover, early_part, early_came, early_out)
        late_fold = Fold(mover, late_part, late_came, late_out)
        early_fold.hand(last)
        done = set()
        for g in range(per):
            for u, (owner, _) in enumerate(units):
                if owner == g:
                    take_in(u, 0)
            project_back(g)
            take_codes(g)
            if g == 0:
                for level in range(last, -1, -1):
                    early_fold.next(level)
                source, target, first = early_fold.gather()
                kept.append(move(source, target))
                load_dy1.wait()
            if g + 1 < per:
                for t in range(n_wide // 2):
                    finish_tile(g, t)
                    done.add((g, t))
            if g == 0:
                mover.relay(first)
        for n in range(per):
            values = [
                lambda n=n: dq[n],
                lambda n=n: dkv[0, n],
                lambda n=n: dkv[1, n],
            ]
            entries = [
                (lambda n=n, j=j: adapt_ref[n, :, j * NR : (j + 1) * NR], values[j]) for j in range(3)
            ]
            entries += [
                (lambda n=n, j=j: codes_in[n, :, j * NR : (j + 1) * NR], lambda n=n: x_ref[n])
                for j in range(3)
            ]
            compact(late_part, n, entries, late_sizes)
        late_fold.hand(last)
        rest = [(g, t) for g in range(per) for t in range(n_wide) if (g, t) not in done]
        cut = len(rest) - 2
        for i, (g, t) in enumerate(rest):
            finish_tile(g, t)
            if i == cut - 2:
                for level in range(last, 0, -1):
                    late_fold.next(level)
            if i == cut - 1:
                late_fold.next(0)
                source, target, second = late_fold.gather()
                kept.append(move(source, target))
                mover.complete(first)
            if i == cut:
                mover.relay(second)
        mover.complete(second)
        for g in range(per):
            for t in range(n_swap):
                swap_copy(g, t).wait_send()
        for copy in dealt:
            copy.wait_recv()
        for copy in kept:
            copy.wait()
        mover.close()

    vmem, anywhere = pl.BlockSpec(memory_space=pltpu.VMEM), pl.BlockSpec(memory_space=pl.ANY)
    parts = [(n_ctx, per * RANK, sum(early_sizes)), (n_ctx, per * RANK, sum(late_sizes))]
    row = (per, loc)
    rooms = [
        ((per, n_ctx, 2, loc, width_here), BF16),
        ((len(units), n_ctx, 2, loc, columns), BF16),
        ((len(units), n_ctx - 1, 2, loc, columns), BF16),
        (row + (width_here,), BF16),
        ((2,) + row + (width_here,), BF16),
        ((2, tile, depth), BF16),
        ((foot, depth), BF16),
        (dy1.shape, F32),
        ((depth, loc), BF16),
        (row + (wide,), BF16),
        (row + (wide,), BF16),
        (row + (foot,), BF16),
        (row + (width,), BF16),
    ]
    for shape in parts:
        rooms += [(shape, BF16), ((n_ctx - 1,) + shape[1:], BF16)]
    rooms += [(x.shape, BF16) for x in early]
    return pl.pallas_call(
        kernel,
        in_specs=[vmem] * 8 + [anywhere] * (2 + n_ctx + n_early),
        out_specs=[anywhere] * 3,
        out_shape=[jax.ShapeDtypeStruct((per * n_fsdp, piece, width), BF16)]
        + [jax.ShapeDtypeStruct((n_ctx, n_fsdp) + shape[1:], BF16) for shape in parts],
        scratch_shapes=[
            pltpu.SemaphoreType.DMA((n_copy,)),
            pltpu.SemaphoreType.DMA((n_copy,)),
            pltpu.SemaphoreType.DMA((per * n_swap,)),
            pltpu.SemaphoreType.DMA((per * n_swap,)),
            pltpu.SemaphoreType.DMA((2,)),
            pltpu.SemaphoreType.DMA((per * n_ctx,)),
            pltpu.SemaphoreType.DMA((4 + n_early + per * n_wide,)),
        ]
        + [pltpu.VMEM(shape, dtype) for shape, dtype in rooms],
        compiler_params=pltpu.CompilerParams(
            collective_id=4, has_side_effects=True, vmem_limit_bytes=63 << 20
        ),
    )(
        query, bias, grad, log_total, x_rows, adapt_in, a_qkv, picked, dy1, qkv_x, kv_own, *slots, *early,
    )


def gelu_both(pre):
    square = pre * pre
    bent = jnp.tanh(GELU_COEF * (pre + 0.044715 * square * pre))
    out = 0.5 * pre * (1.0 + bent)
    slope = 0.5 * (1.0 + bent) + 0.5 * pre * (1.0 - bent * bent) * GELU_COEF * (
        1.0 + 3.0 * 0.044715 * square
    )
    return out.astype(BF16), slope.astype(BF16)


def local(
    x_in,
    cotangent,
    lengths,
    adapter_ids,
    w_qkv,
    w_out,
    w_up,
    w_down,
    ln_gain,
    ln_bias,
    a_qkv,
    b_qkv,
    a_out,
    b_out,
    a_up,
    b_up,
    a_down,
    b_down,
):
    n_ctx, n_fsdp = lax.axis_size("ctx"), lax.axis_size("fsdp")
    z, ct = lax.axis_index("fsdp"), lax.axis_index("ctx")
    seqs, piece, width = x_in.shape
    per = seqs // n_fsdp
    loc = n_fsdp * piece
    heads_width = w_qkv.shape[2]
    def take(array, start, size, axis=0):
        return lax.dynamic_slice_in_dim(array, start, size, axis)

    units = w_up.shape[1]
    rows_shape = (per, n_fsdp, piece, width)
    zq = w_qkv.shape[1]

    def first_items(ins, outs, z):
        x_ref, w_ref = ins
        rows_ref, whole_ref = outs

        def deal(g):
            return Deal(lambda to: x_ref.at[to * per + g], lambda s: rows_ref.at[g, s])

        def weight(j):
            size = zq // n_ctx
            columns = pl.ds(j * heads_width, heads_width)
            return Weight(
                lambda c: w_ref.at[j, pl.ds(pl.multiple_of(c * size, size), size)],
                lambda o, c: whole_ref.at[
                    pl.ds(pl.multiple_of(o * zq + c * size, size), size), columns
                ],
            )

        stay = [(x_ref.at[z * per + g], rows_ref.at[g, 0]) for g in range(per)]
        for j in range(3):
            own = whole_ref.at[
                pl.ds(pl.multiple_of(z * zq, zq), zq), pl.ds(j * heads_width, heads_width)
            ]
            stay.append((w_ref.at[j], own))
        items = [weight(j) for j in range(3)] + [deal(g) for g in range(per)]
        return items, stay

    x_all, qkv_x = move(
        first_items,
        [Weight] * 3 + [Deal] * per,
        (x_in, w_qkv),
        (rows_shape, (width + 3 * NR, 3 * heads_width)),
        n_fsdp,
        n_ctx,
        ((piece, width),) * per + (w_qkv.shape[1:],) * 3,
        0,
        foot=(b_qkv, lambda outs: outs[1].at[pl.ds(width, 3 * NR)]),
    )

    my_lengths = take(lengths, z * per, per)
    my_ids = take(adapter_ids, z * per, per)
    picked = (my_ids[:, None] == jnp.arange(NR)[None, :] // RANK).astype(F32)
    steps = lax.rem(z - jnp.arange(n_fsdp) + n_fsdp, n_fsdp)
    ctx_of = ct ^ jnp.array(offsets(n_ctx))
    key_pos = (
        (steps[None, :, None] * n_ctx + ctx_of[:, None, None]) * piece
        + jnp.arange(piece)[None, None, :]
    ).reshape(-1)
    bias_all = jnp.where(key_pos[None, :] < my_lengths[:, None], 0.0, -1e30).astype(F32)
    bias_all = jnp.broadcast_to(bias_all[:, :, None], bias_all.shape + (128,))

    picked = picked[:, None, :]
    x_rows = x_all.reshape(per, loc, width)
    moved = forward_and_gather(
        x_rows, qkv_x, a_qkv, picked, bias_all, ln_gain, ln_bias, (a_up, b_out), (w_out, w_up, w_down),
        (a_out, b_up, a_down), n_fsdp, n_ctx,
    )
    slots = moved[: n_ctx - 1]
    (
        query, kv_own, adapt_all, out_x, up_x, down_x, context, log_total, wide_h, gelus, slopes, hats, rstds,
        adapt_out, adapt_up,
    ) = moved[n_ctx - 1 :]
    _, dy1, wide_a, _, grads, activations, dadapt_up, d_context = middle(
        hats, rstds, gelus, slopes, adapt_up, cotangent, picked, ln_gain, ln_bias, (out_x, up_x, down_x),
        (a_up, b_out, b_down, a_down, b_up), n_fsdp, n_ctx,
    )
    early_in = (dadapt_up, wide_h, adapt_out, wide_a, context)
    early_pairs = [
        ((0, 0, NR), (1, 0, width)),
        ((2, 0, NR), (3, 0, width)),
        ((3, width, NR), (4, 0, heads_width)),
    ]
    input_grad, early, late = finish(
        query, kv_own, slots, bias_all, d_context, log_total, x_rows, adapt_all, dy1, qkv_x, a_qkv, picked,
        early_in, early_pairs, n_fsdp, n_ctx,
    )

    codes = (adapter_ids[:, None] * RANK + jnp.arange(RANK)[None, :]).reshape(-1)
    chosen = (codes[:, None] == jnp.arange(NR)[None, :]).astype(BF16)
    b_down_grad, a_down_grad, b_up_grad = combine(
        grads, chosen, [(NR, width), (units, NR), (NR, units)]
    )
    a_up_grad, b_out_grad, a_out_grad = combine(
        early, chosen, [(width, NR), (NR, width), (heads_width, NR)]
    )
    b_qkv_grad, a_qkv_grad = combine(late, chosen, [(3, NR, heads_width), (3, width, NR)])
    return (
        activations, input_grad, a_qkv_grad, b_qkv_grad, a_out_grad, b_out_grad, a_up_grad, b_up_grad,
        a_down_grad, b_down_grad,
    )


def solution(mesh):
    rows = P(None, ("fsdp", "ctx"), None)
    return jax.shard_map(
        local,
        mesh=mesh,
        in_specs=(
            rows,
            rows,
            P(),
            P(),
            P(None, "fsdp", "tp"),
            P("tp", "fsdp"),
            P("fsdp", "tp"),
            P("tp", "fsdp"),
            P(),
            P(),
            P(),
            P(None, None, "tp"),
            P("tp", None),
            P(),
            P(),
            P(None, "tp"),
            P("tp", None),
            P(),
        ),
        out_specs=(
            rows,
            rows,
            P(),
            P(None, None, "tp"),
            P("tp", None),
            P(),
            P(),
            P(None, "tp"),
            P("tp", None),
            P(),
        ),
        check_vma=False,
    )
```

```python
import math

import jax
import jax.numpy as jnp
from jax import lax
from jax.experimental import pallas as pl
from jax.experimental.pallas import tpu as pltpu
from jax.sharding import PartitionSpec as P

HEAD_DIM = 128
RANK = 16
ADAPTERS = 8
NR = RANK * ADAPTERS
NORM_EPS = 1e-06
GELU_COEF = 0.7978845608028654
SCALE = 1.0 / math.sqrt(HEAD_DIM)
F32 = jnp.float32
BF16 = jnp.bfloat16


def dot(left, right):
    return jnp.dot(left, right, preferred_element_type=F32)


def dot_nt(left, right):
    return lax.dot_general(left, right, (((1,), (1,)), ((), ())), preferred_element_type=F32)


def dot_tn(left, right):
    return lax.dot_general(left, right, (((0,), (0,)), ((), ())), preferred_element_type=F32)


def masks_of(n):
    out = []
    while n > 1:
        n //= 2
        out.append(n)
    return out


def offsets(n):
    out = [0]
    for mask in masks_of(n):
        out = out + [o ^ mask for o in out]
    return out


def attend_head(query, keys, values, biases):
    scores = [dot_nt(k, query) * SCALE + bias for k, bias in zip(keys, biases)]
    top = scores[0].max(axis=0, keepdims=True)
    for s in scores[1:]:
        top = jnp.maximum(top, s.max(axis=0, keepdims=True))
    total = jnp.zeros_like(top)
    mixed = None
    for s, v in zip(scores, values):
        probs = jnp.exp(s - top)
        total = total + probs.sum(axis=0, keepdims=True)
        term = dot_tn(v, probs.astype(BF16))
        mixed = term if mixed is None else mixed + term
    return (mixed / total).T.astype(BF16), top + jnp.log(total)


def attend_back_head(query, grad, log_total, keys, values, biases):
    probs, dprobs, dvalues = [], [], []
    delta = jnp.zeros_like(log_total)
    for k, v, bias in zip(keys, values, biases):
        p = jnp.exp(dot_nt(k, query) * SCALE + bias - log_total)
        dp = dot_nt(v, grad)
        dvalues.append(dot(p.astype(BF16), grad).astype(BF16))
        delta = delta + (p * dp).sum(axis=0, keepdims=True)
        probs.append(p)
        dprobs.append(dp)
    dquery, dkeys = None, []
    for k, p, dp in zip(keys, probs, dprobs):
        ds = (p * (dp - delta)).astype(BF16)
        dkeys.append((dot(ds, query) * SCALE).astype(BF16))
        term = dot_tn(k, ds)
        dquery = term if dquery is None else dquery + term
    return (dquery * SCALE).T.astype(BF16), dkeys, dvalues


def ds(start, size):
    return pl.ds(pl.multiple_of(start, size), size)


def flip(ct, offset):
    mask = 1
    while mask <= offset:
        if offset & mask:
            ct = ct + mask - 2 * mask * lax.rem(ct // mask, 2)
        mask *= 2
    return ct


class Weight:
    def __init__(self, shard_at, whole_at, own=None, skip=0, direct=False):
        self.shard_at, self.whole_at, self.own, self.skip = shard_at, whole_at, own, skip
        self.direct = direct


class Deal:
    def __init__(self, source_at, rows_at):
        self.source_at, self.rows_at = source_at, rows_at


class Pair:
    def __init__(self, slot_at):
        self.slot_at = slot_at


class Mover:
    def __init__(self, n_fsdp, n_ctx, send, recv):
        self.n_fsdp, self.n_ctx = n_fsdp, n_ctx
        self.z, self.ct = lax.axis_index("fsdp"), lax.axis_index("ctx")
        self.send, self.recv = send, recv
        self.used = 0
        self.open = []
        self.masks = masks_of(n_ctx)
        self.offsets = offsets(n_ctx)
        self.came, self.waiting, self.done = {}, {}, {}

    def skip(self, item):
        return item.skip if isinstance(item, Weight) else 0

    def part(self, item):
        return lax.rem(self.ct, self.n_ctx >> item.skip) if item.skip else self.ct

    def greet(self, tp=False):
        barrier = pltpu.get_barrier_semaphore()
        others = [{"fsdp": lax.rem(self.z + s, self.n_fsdp)} for s in range(1, self.n_fsdp)]
        others += [{"ctx": flip(self.ct, mask)} for mask in self.masks]
        if tp:
            others.append({"tp": 1 - lax.axis_index("tp")})
        for other in others:
            pl.semaphore_signal(
                barrier, inc=1, device_id=other, device_id_type=pl.DeviceIdType.MESH
            )
        pl.semaphore_wait(barrier, len(others))

    def copy(self, source, target, device, at=None):
        if at is None:
            at = self.used
            self.used += 1
        return pltpu.make_async_remote_copy(
            src_ref=source,
            dst_ref=target,
            send_sem=self.send.at[at],
            recv_sem=self.recv.at[at],
            device_id=device,
            device_id_type=pl.DeviceIdType.MESH,
        )

    def go(self, source, target, device):
        copy = self.copy(source, target, device)
        copy.start()
        self.open.append((None, copy))
        return copy

    def along(self, item, owner, right, ok, source, slot):
        target = item.whole_at(owner, self.part(item))
        device = {"fsdp": lax.rem(self.z + (1 if right else self.n_fsdp - 1), self.n_fsdp)}
        copy = self.copy(source, target, device, self.came[item] + slot - 1)
        pl.when(ok)(copy.start)
        self.open.append((ok, copy))

    def begin(self, item):
        if isinstance(item, Pair):
            self.waiting[item] = [[] for _ in self.masks]
            self.cast(item, item.slot_at, lambda k, level: item.slot_at(k + 2**level), 0, 0)
            return
        if isinstance(item, Weight) and item.direct:
            part = self.part(item)
            self.came[item] = [
                self.go(
                    item.shard_at(part),
                    item.whole_at(self.z, part),
                    {"fsdp": lax.rem(self.z + s, self.n_fsdp)},
                )
                for s in range(1, self.n_fsdp)
            ]
            return
        if isinstance(item, Weight):
            self.came[item] = self.used
            self.used += self.n_fsdp - 1
            source = item.shard_at(self.part(item))
            self.along(item, self.z, True, self.z < self.n_fsdp - 1, source, 1)
            self.along(item, self.z, False, self.z > 0, source, self.n_fsdp - 1)
            return
        self.came[item] = [
            self.go(
                item.source_at(lax.rem(self.z + s, self.n_fsdp)),
                item.rows_at(s),
                {"fsdp": lax.rem(self.z + s, self.n_fsdp)},
            )
            for s in range(1, self.n_fsdp)
        ]

    def cast(self, item, source_at, target_at, k, first):
        skip = self.skip(item)
        for level in range(first, len(self.masks) - skip):
            device = {"ctx": flip(self.ct, self.masks[level + skip])}
            copy = self.go(source_at(k), target_at(k, level), device)
            self.waiting[item][level].append((copy, k + 2**level, source_at, target_at))

    def relay(self, item):
        if isinstance(item, Deal):
            for copy in self.came[item]:
                copy.wait_recv()
            return
        self.waiting[item] = [[] for _ in self.masks[item.skip :]]
        n, part = self.n_fsdp, self.part(item)
        others = offsets(self.n_ctx >> item.skip)
        if item.own is not None:

            def mine(k):
                return item.own if k == 0 else item.whole_at(self.z, flip(part, others[k]))

            def lands(k, level):
                return item.whole_at(self.z, flip(part, others[k]))

            self.cast(item, mine, lands, 0, 0)
        for i in range(n - 1):
            s = i // 2 + 1 if i % 2 == 0 else n - 1 - i // 2
            owner = lax.rem(self.z - s + n, n)
            here = item.whole_at(owner, part)
            if item.direct:
                self.came[item][s - 1].wait_recv()
            else:
                self.copy(here, here, {"fsdp": owner}, self.came[item] + s - 1).wait_recv()
                if s < n - 1:
                    ok = (self.z >= s) & (self.z < n - 1)
                    self.along(item, owner, True, ok, here, s + 1)
                if s > 1:
                    ok = (self.z < s) & (self.z > 0)
                    self.along(item, owner, False, ok, here, s - 1)

            def at(k, owner=owner):
                return item.whole_at(owner, flip(part, others[k]))

            self.cast(item, at, lambda k, level, at=at: at(k), 0, 0)

    def finish(self, item, level):
        if isinstance(item, Deal) or level != self.done.get(item, 0):
            return
        if level == len(self.waiting[item]):
            return
        for copy, k, source_at, target_at in self.waiting[item][level]:
            copy.wait_recv()
            self.cast(item, source_at, target_at, k, level + 1)
        self.done[item] = level + 1

    def complete(self, item):
        while self.done.get(item, 0) < len(self.waiting[item]):
            self.finish(item, self.done.get(item, 0))

    def close(self):
        for ok, copy in self.open:
            if ok is None:
                copy.wait_send()
            else:
                pl.when(ok)(copy.wait_send)


def copies_of(items, n_fsdp, n_ctx):
    total = 0
    for item in items:
        total += {Weight: (n_fsdp - 1) * n_ctx, Deal: n_fsdp - 1, Pair: n_ctx - 1}[item]
    return total


def keep(stay, room, sems):
    out = []
    for k, (source, target) in enumerate(stay):
        first = pltpu.make_async_copy(source, room[k], sems.at[2 * k])
        first.start()
        out.append((first, pltpu.make_async_copy(room[k], target, sems.at[2 * k + 1])))
    return out


def move(make, kinds, inputs, outputs, n_fsdp, n_ctx, local_shapes, ident, ahead=2, foot=None):
    n_in = len(inputs)
    n_copy = copies_of(kinds, n_fsdp, n_ctx)

    def kernel(*refs):
        ins, outs = refs[:n_in], refs[n_in : n_in + len(outputs)]
        send, recv, here = refs[n_in + len(outputs) : n_in + len(outputs) + 3]
        room = refs[n_in + len(outputs) + 3 :]
        if foot is not None:
            blocks_ref, ins = ins[-1], ins[:-1]
            strip = room[-1]
        mover = Mover(n_fsdp, n_ctx, send, recv)
        items, stay = make(ins, outs, mover.z)
        mover.greet()
        for item in items[:ahead]:
            mover.begin(item)
        kept = keep(stay, room, here)
        levels = len(mover.masks)
        for i in range(len(items) + levels):
            if i < len(items):
                mover.relay(items[i])
                if i + ahead < len(items):
                    mover.begin(items[i + ahead])
            if i == 0 and foot is not None:
                strip[...] = jnp.zeros_like(strip)
                high, wide = blocks_ref.shape[1:]
                for j in range(blocks_ref.shape[0]):
                    strip[j * high : (j + 1) * high, j * wide : (j + 1) * wide] = blocks_ref[j]
                set_foot = pltpu.make_async_copy(strip, foot[1](outs), here.at[2 * len(local_shapes)])
                set_foot.start()
                kept.append((None, set_foot))
            if i == 0:
                for first, second in kept:
                    if first is not None:
                        first.wait()
                        second.start()
            for level in range(levels):
                if 0 <= i - 1 - level < len(items):
                    mover.finish(items[i - 1 - level], level)
        for _, second in kept:
            second.wait()
        mover.close()

    spaces = [pl.BlockSpec(memory_space=pl.ANY)] * n_in
    room_shapes = list(local_shapes)
    if foot is not None:
        blocks = foot[0]
        inputs = inputs + (blocks,)
        n_in += 1
        spaces.append(pl.BlockSpec(memory_space=pltpu.VMEM))
        room_shapes.append((blocks.shape[0] * blocks.shape[1], blocks.shape[0] * blocks.shape[2]))
    return pl.pallas_call(
        kernel,
        in_specs=spaces,
        out_specs=[pl.BlockSpec(memory_space=pl.ANY)] * len(outputs),
        out_shape=[jax.ShapeDtypeStruct(shape, BF16) for shape in outputs],
        scratch_shapes=[
            pltpu.SemaphoreType.DMA((n_copy,)),
            pltpu.SemaphoreType.DMA((n_copy,)),
            pltpu.SemaphoreType.DMA((2 * len(local_shapes) + 1,)),
        ]
        + [pltpu.VMEM(shape, BF16) for shape in room_shapes],
        compiler_params=pltpu.CompilerParams(
            collective_id=ident, has_side_effects=True, vmem_limit_bytes=60 << 20
        ),
    )(*inputs)


def forward_and_gather(
    x_rows, qkv_x, a_qkv, picked, bias, gain, shift_by, first_maps, shards, maps, n_fsdp, n_ctx
):
    per, loc, width = x_rows.shape
    w_out, w_up, w_down = shards
    width_here = qkv_x.shape[1] // 3
    heads, units = width_here // HEAD_DIM, w_up.shape[1]
    zu, zo = w_up.shape[0], w_out.shape[1]
    n_part = n_ctx // 2 if n_ctx > 1 else 1
    so, su, sd = w_out.shape[0] // n_ctx, zu // n_ctx, w_down.shape[0] // n_ctx
    wide = width + NR
    wide_x = width + 3 * NR
    cuts = 4
    paired = cuts // 2 if n_ctx > 1 else 0
    tile = 512
    per_kind = width_here // tile
    chunk = 32
    n_tile = 3 * per_kind
    n_copy = (n_fsdp - 1) * n_ctx * (1 + 2 * cuts) + 2 * per * (n_ctx - 1) + 6 + per
    lag = 4

    def kernel(*refs):
        bias_ref, a_ref, pick_ref, gain_ref, shift_ref, a_up_ref, b_out_ref, x_ref, w_ref = refs[:9]
        wo_ref, wu_ref, wd_ref, ao_ref, bu_ref, ad_ref = refs[9:15]
        slots = refs[15 : 14 + n_ctx]
        q_ref, kv_ref, adapt_ref, out_ref, up_ref, down_ref, ctx_ref, log_ref = refs[
            14 + n_ctx : 22 + n_ctx
        ]
        h_ref, gelu_ref, slope_ref, hat_ref, rstd_ref, adapt_out_ref, adapt_up_ref = refs[
            22 + n_ctx : 29 + n_ctx
        ]
        send, recv, here, load, ring_sem, x_room, w_room, proj, kv_room, out_room = refs[
            29 + n_ctx : 39 + n_ctx
        ]
        part_ref, other_ref, up_room, wide_v, hat1, gelu, slope = refs[39 + n_ctx :]
        mover = Mover(n_fsdp, n_ctx, send, recv)
        ring = Ring(
            w_room,
            ring_sem,
            0,
            lambda t: w_ref.at[:, ds(lax.rem(t + per_kind, n_tile) * tile, tile)],
        )
        z = mover.z
        rows = [pl.ds(g * loc, loc) for g in range(per)]

        def columns(j):
            return pl.ds(j * width_here, width_here)

        out_item = Weight(
            lambda c: wo_ref.at[ds(c * so, so)],
            lambda o, c: out_ref.at[ds(c * so, so), ds(o * zo, zo)],
        )

        def up_item(h):
            at = pl.ds(h * (units // cuts), units // cuts)
            return Weight(
                lambda c: wu_ref.at[ds(c * su, su), at],
                lambda o, c: up_ref.at[ds(o * zu + c * su, su), at],
            )

        def down_item(h):
            size = sd // cuts
            return Weight(
                lambda c: wd_ref.at[ds(c * sd + h * size, size)],
                lambda o, c: down_ref.at[ds(c * sd + h * size, size), ds(o * zo, zo)],
            )

        def down_pair(h):
            size = sd // cuts

            def at(c, p):
                return ds((c + p * n_part) * sd + h * size, size)

            def half(p):
                return Weight(
                    lambda c: wd_ref.at[at(c, p)],
                    lambda o, c: down_ref.at[at(c, p), ds(o * zo, zo)],
                    skip=1,
                )

            return [half(p) for p in range(2)]

        def pair(g, j):
            return Pair(
                lambda k: proj.at[rows[g], columns(1 + j)] if k == 0 else slots[k - 1].at[j, g]
            )

        pairs = [pair(g, j) for g in range(per) for j in range(2)]
        items = [out_item] + [up_item(h) for h in range(cuts)]
        items += [down_item(h) for h in range(cuts - paired)]
        for h in range(cuts - paired, cuts):
            items += down_pair(h)
        used = [0]

        def move(source, target):
            copy = pltpu.make_async_copy(source, target, here.at[used[0]])
            used[0] += 1
            copy.start()
            return copy

        def attend(g):
            for j in range(2):
                mover.complete(pairs[2 * g + j])
            loads = []
            for k in range(1, n_ctx):
                copy = pltpu.make_async_copy(slots[k - 1].at[:, g], kv_room.at[k], load.at[k])
                copy.start()
                loads.append(copy)
            for j in range(2):
                kv_room[0, j] = proj[g * loc : (g + 1) * loc, (1 + j) * width_here : (2 + j) * width_here]
            for copy in loads:
                copy.wait()

            def one(h, carry):
                at = ds(h * HEAD_DIM, HEAD_DIM)
                biases = []
                for k in range(n_ctx):
                    block = bias_ref[g, k * loc : (k + 1) * loc, :]
                    biases.append(jnp.concatenate([block] * (loc // 128), axis=1))
                context, log = attend_head(
                    proj[g * loc : (g + 1) * loc, at],
                    [kv_room[k, 0, :, at] for k in range(n_ctx)],
                    [kv_room[k, 1, :, at] for k in range(n_ctx)],
                    biases,
                )
                ctx_ref[g, :, at] = context
                log_ref[g, h] = log
                return carry

            lax.fori_loop(0, heads, one, 0)

        def project():
            mover.complete(out_item)
            own[0].wait_recv()
            own[3].wait_recv()
            copy = pltpu.make_async_copy(out_ref, out_room, load.at[0])
            copy.start()
            copy.wait()
            for g in range(per):
                for start in range(0, wide, 1024):
                    at = slice(start, min(start + 1024, wide))
                    part_ref[g, :, at] = dot(ctx_ref[g], out_room[:, at]).astype(BF16)
                swapped.append(
                    mover.go(
                        part_ref.at[g], other_ref.at[g], {"tp": 1 - lax.axis_index("tp")}
                    )
                )

        def tiles(t, room):
            at = ds(lax.rem(t + per_kind, n_tile) * tile, tile)
            proj[:, at] = dot(x_room[...], room[...]).astype(BF16)

        up_ring = Ring(up_room, ring_sem, 2, lambda t: up_ref.at[:, ds(t * tile, tile)])

        def first_norm(g):
            swapped[g].wait_recv()
            pick = pick_ref[g]

            def step(r, carry):
                rows_r = ds(r * chunk, chunk)
                total = part_ref[g, rows_r, :].astype(F32) + other_ref[g, rows_r, :].astype(F32)
                code = (total[:, width:] * pick).astype(BF16)
                adapt_out_ref[g, rows_r, :] = code
                x = x_room[ds(g * loc + r * chunk, chunk), :width].astype(F32)
                hat, rstd = norm_parts(x + total[:, :width] + dot(code, b_out_ref[...]))
                hat1[g, rows_r, :] = hat
                rstd_ref[g, rows_r, :] = jnp.broadcast_to(rstd, (chunk, 128))
                low = (hat * gain_ref[0:1, :] + shift_ref[0:1, :]).astype(BF16)
                wide_v[g, rows_r, :width] = low
                code = (dot(low, a_up_ref[...]) * pick).astype(BF16)
                wide_v[g, rows_r, width:] = code
                adapt_up_ref[g, rows_r, :] = code
                return carry

            lax.fori_loop(0, loc // chunk, step, 0)
            outward.append(move(hat1.at[g], hat_ref.at[g]))
            outward.append(move(wide_v.at[g], h_ref.at[g]))

        def feed(g):
            if g == 0:
                for item in items[1 : 1 + cuts]:
                    mover.complete(item)
                own[1].wait_recv()
                own[4].wait_recv()
                up_ring.prefetch()

            def up_tile(t, room):
                at = ds(t * tile, tile)
                value, factor = gelu_both(dot(wide_v[g], room[...]))
                gelu[g, :, at] = value
                slope[g, :, at] = factor

            up_ring.run(units // tile, up_tile)
            if g + 1 < per:
                up_ring.prefetch()
            outward.append(move(gelu.at[g], gelu_ref.at[g]))
            outward.append(move(slope.at[g], slope_ref.at[g]))

        swapped, outward = [], []
        tasks = {1 + g: (lambda g=g: attend(g)) for g in range(per)}
        tasks[per + 2] = project
        tasks[per + 5] = lambda: [first_norm(g) for g in range(per)]
        for g in range(per):
            tasks[per + 6 + g] = lambda g=g: feed(g)
        ring.prefetch()
        loads = [move(x_ref.at[g], x_room.at[rows[g], pl.ds(0, width)]) for g in range(per)]
        mover.greet(tp=True)
        ahead = 3
        for item in items[:ahead]:
            mover.begin(item)
        sibling = {"ctx": flip(mover.ct, 1)}
        own = [
            mover.go(source, target, sibling)
            for source, target in (
                (wo_ref, out_ref.at[:, ds(z * zo, zo)]),
                (wu_ref, up_ref.at[ds(z * zu, zu)]),
                (wd_ref, down_ref.at[:, ds(z * zo, zo)]),
                (ao_ref, out_ref.at[:, pl.ds(width, NR)]),
                (bu_ref, up_ref.at[pl.ds(width, NR)]),
                (ad_ref, down_ref.at[:, pl.ds(width, NR)]),
            )
        ]
        for g in range(per):
            loads[g].wait()
            pick = pick_ref[g]
            for j in range(3):
                code = dot(x_room[g * loc : (g + 1) * loc, :width], a_ref[j]) * pick
                x_room[g * loc : (g + 1) * loc, width + j * NR : width + (j + 1) * NR] = code.astype(BF16)
            outward.append(move(x_room.at[rows[g], pl.ds(width, 3 * NR)], adapt_ref.at[g]))
        ring.run(2 * per_kind, tiles, 0, n_tile)
        for item in pairs:
            mover.begin(item)
        for g in range(per):
            for j in range(2):
                outward.append(move(proj.at[rows[g], columns(1 + j)], kv_ref.at[j, g]))
        for i in range(len(items) + lag + 2):
            if i < len(items):
                mover.relay(items[i])
                if i + ahead < len(items):
                    mover.begin(items[i + ahead])
            if i == 0:
                ring.run(n_tile, tiles, 2 * per_kind, n_tile)
                for g in range(per):
                    outward.append(move(proj.at[rows[g], columns(0)], q_ref.at[g]))
            for level in range(len(mover.masks)):
                if 0 <= i - lag - level < len(items):
                    mover.finish(items[i - lag - level], level)
            if i in tasks:
                tasks[i]()
        for item in items:
            mover.complete(item)
        for copy in (own[2], own[5]):
            copy.wait_recv()
        for copy in outward:
            copy.wait()
        mover.close()

    row = (per, loc, width_here)
    pair_shape = (2,) + row
    vmem, anywhere = pl.BlockSpec(memory_space=pltpu.VMEM), pl.BlockSpec(memory_space=pl.ANY)
    outputs = [(pair_shape, BF16, anywhere)] * (n_ctx - 1) + [
        (row, BF16, anywhere),
        (pair_shape, BF16, anywhere),
        ((per, loc, 3 * NR), BF16, anywhere),
        ((width_here, wide), BF16, anywhere),
        ((wide, units), BF16, anywhere),
        ((units, wide), BF16, anywhere),
        (row, BF16, vmem),
        ((per, heads, 1, loc), F32, vmem),
        ((per, loc, wide), BF16, anywhere),
        ((per, loc, units), BF16, anywhere),
        ((per, loc, units), BF16, anywhere),
        ((per, loc, width), F32, anywhere),
        ((per, loc, 128), F32, vmem),
        ((per, loc, NR), BF16, vmem),
        ((per, loc, NR), BF16, vmem),
    ]
    return pl.pallas_call(
        kernel,
        in_specs=[vmem] * 7 + [anywhere] * 8,
        out_specs=[space for _, _, space in outputs],
        out_shape=[jax.ShapeDtypeStruct(shape, dtype) for shape, dtype, _ in outputs],
        scratch_shapes=[
            pltpu.SemaphoreType.DMA((n_copy,)),
            pltpu.SemaphoreType.DMA((n_copy,)),
            pltpu.SemaphoreType.DMA((9 * per,)),
            pltpu.SemaphoreType.DMA((n_ctx,)),
            pltpu.SemaphoreType.DMA((4,)),
            pltpu.VMEM((per * loc, wide_x), BF16),
            pltpu.VMEM((2, wide_x, tile), BF16),
            pltpu.VMEM((per * loc, 3 * width_here), BF16),
            pltpu.VMEM((n_ctx, 2, loc, width_here), BF16),
            pltpu.VMEM((width_here, wide), BF16),
            pltpu.VMEM((per, loc, wide), BF16),
            pltpu.VMEM((per, loc, wide), BF16),
            pltpu.VMEM((2, wide, tile), BF16),
            pltpu.VMEM((per, loc, wide), BF16),
            pltpu.VMEM((per, loc, width), F32),
            pltpu.VMEM((per, loc, units), BF16),
            pltpu.VMEM((per, loc, units), BF16),
        ],
        compiler_params=pltpu.CompilerParams(
            collective_id=1, has_side_effects=True, vmem_limit_bytes=60 << 20
        ),
    )(bias, a_qkv, picked, gain, shift_by, *first_maps, x_rows, qkv_x, w_out, w_up, w_down, *maps)


class Ring:
    def __init__(self, room, sems, at, tile_at):
        self.room, self.sems, self.at, self.tile_at = room, sems, at, tile_at

    def copy(self, t):
        slot = lax.rem(t, 2)
        return pltpu.make_async_copy(
            self.tile_at(t), self.room.at[slot], self.sems.at[self.at + slot]
        )

    def prefetch(self):
        self.copy(0).start()
        self.copy(1).start()

    def run(self, n, body, first=0, total=None):
        total = n if total is None else total

        def step(t, carry):
            self.copy(t).wait()
            body(t, self.room.at[lax.rem(t, 2)])

            @pl.when(t + 2 < total)
            def _():
                self.copy(t + 2).start()

            return carry

        lax.fori_loop(first, n, step, 0)


def compact(out_ref, n, entries, sizes, start=0):
    column = lax.broadcasted_iota(jnp.int32, (NR, RANK), 0)
    rank = lax.broadcasted_iota(jnp.int32, (NR, RANK), 1)
    used = jnp.where(lax.rem(column, RANK) == rank, 1.0, 0.0).astype(BF16)
    for (code, value), size in zip(entries, sizes):
        short = dot(code(), used).astype(BF16)
        block = dot_tn(short, value()).astype(BF16)
        for k in range(out_ref.shape[0]):
            out_ref[k, n * RANK : (n + 1) * RANK, start : start + size] = block[
                :, k * size : (k + 1) * size
            ]
        start += size


class Fold:
    def __init__(self, mover, parts, came, out_ref):
        self.mover, self.parts, self.came, self.out_ref = mover, parts, came, out_ref
        self.flying = {}

    def at(self, k):
        return flip(self.mover.ct, self.mover.offsets[k])

    def hand(self, level):
        half = 2**level
        self.flying[level] = [
            self.mover.go(
                self.parts.at[self.at(half + i)],
                self.came.at[half - 1 + i],
                {"ctx": flip(self.mover.ct, self.mover.masks[level])},
            )
            for i in range(half)
        ]

    def take(self, level):
        for i, copy in enumerate(self.flying[level]):
            copy.wait_recv()
            total = self.parts[self.at(i)].astype(F32) + self.came[2**level - 1 + i].astype(F32)
            self.parts[self.at(i)] = total.astype(BF16)

    def next(self, level):
        self.take(level)
        if level:
            self.hand(level - 1)

    def gather(self):
        own = self.parts.at[self.mover.ct]
        item = Weight(
            lambda c: self.parts.at[c], lambda o, c: self.out_ref.at[c, o], own, direct=True
        )
        self.mover.begin(item)
        return own, self.out_ref.at[self.mover.ct, self.mover.z], item


def norm_parts(values):
    center = values - jnp.mean(values, axis=-1, keepdims=True)
    rstd = lax.rsqrt(jnp.mean(center * center, axis=-1, keepdims=True) + NORM_EPS)
    return center * rstd, rstd


def norm_back(hat, rstd, dhat):
    first = jnp.mean(dhat, axis=-1, keepdims=True)
    second = jnp.mean(dhat * hat, axis=-1, keepdims=True)
    return rstd * (dhat - first - hat * second)


def gelu_both(pre):
    square = pre * pre
    bent = jnp.tanh(GELU_COEF * (pre + 0.044715 * square * pre))
    out = 0.5 * pre * (1.0 + bent)
    slope = 0.5 * (1.0 + bent) + 0.5 * pre * (1.0 - bent * bent) * GELU_COEF * (
        1.0 + 3.0 * 0.044715 * square
    )
    return out.astype(BF16), slope.astype(BF16)


def middle(hats, rstds, gelus, slopes, adapt_up, cot, picked, gain, shift_by, weights, maps, n_fsdp, n_ctx):
    per, loc, width = hats.shape
    piece = cot.shape[1]
    out_x, up_x, down_x = weights
    a_up, b_out, b_down, a_down, b_up = maps
    wide, units = up_x.shape
    width_here = out_x.shape[0]
    tile = 512
    chunk = 32
    n_wide = width // tile
    n_swap = n_wide + 1
    sizes = [width // n_ctx, units // n_ctx, units // n_ctx]

    def kernel(*refs):
        pick_ref, gain_ref, shift_ref, rstd1, code_up_ref = refs[:5]
        a_up_ref, b_out_ref, b_down_ref, a_down_ref, b_up_ref = refs[5:10]
        hat_ref, gelu_ref, slope_ref, cot_ref, out_ref, up_ref, down_ref = refs[10:17]
        acts_out, dy1_out, da_out, cot_rows, grads_part, back_out = refs[17:23]
        dadapt_up_ref, ctx_ref = refs[23:25]
        (send, recv, deal_send, deal_recv, ring_sem, sems) = refs[25:31]
        (down_room, down_rows, up_rows) = refs[31:34]
        (stage, part, got, hat1, keep32, slope, gelu, wide_v, turned, dpre_t) = refs[34:44]
        (codes_down,) = refs[44:]
        mover = Mover(n_fsdp, n_ctx, deal_send, deal_recv)
        partner = {"tp": 1 - lax.axis_index("tp")}

        down = Ring(down_room, ring_sem, 0, lambda t: down_ref.at[:, ds(t * tile, tile)])
        down_r = Ring(down_rows, ring_sem, 4, lambda t: down_ref.at[ds(t * tile, tile)])
        up_r = Ring(up_rows, ring_sem, 6, lambda t: up_ref.at[ds(t * tile, tile)])
        out_r = Ring(down_rows, ring_sem, 4, lambda t: out_ref.at[ds(t * tile, tile)])

        busy = {}
        used = [0]

        def move(source, target, key):
            copy = pltpu.make_async_copy(source, target, sems.at[used[0]])
            used[0] += 1
            copy.start()
            busy.setdefault(key, []).append(copy)

        def free(*keys):
            for key in keys:
                for copy in busy.pop(key, []):
                    copy.wait()

        def swap_copy(turn, g, t, size):
            at = ds(t * tile, size)
            sem = (turn * per + g) * n_swap + t
            return pltpu.make_async_remote_copy(
                src_ref=part.at[g, :, at],
                dst_ref=got.at[turn, g, :, at],
                send_sem=send.at[sem],
                recv_sem=recv.at[sem],
                device_id=partner,
                device_id_type=pl.DeviceIdType.MESH,
            )

        def swapped(turn, g):
            for t in range(n_swap):
                copy = swap_copy(turn, g, t, tile if t < n_wide else NR)
                copy.wait_recv()
                copy.wait_send()

        def by_rows(body):
            def step(r, carry):
                body(pl.ds(pl.multiple_of(r * chunk, chunk), chunk))
                return carry

            lax.fori_loop(0, loc // chunk, step, 0)

        def deal(g):
            return Deal(lambda to: cot_ref.at[to * per + g], lambda s: cot_rows.at[g, s])

        deals = [deal(g) for g in range(per)]
        dealt = []
        for g in range(per):
            move(gelu_ref.at[g], gelu.at[g], ("gelu", g))
            if g == 0:
                down.prefetch()
            move(cot_ref.at[mover.z * per + g], cot_rows.at[g, 0], ("cot", g))
        for g in range(per):
            move(hat_ref.at[g], hat1.at[g], ("hat", g))
            move(slope_ref.at[g], slope.at[g], ("slope", g))
        mover.greet(tp=True)
        mover.begin(deals[0])

        for g in range(per):
            if g + 1 == per:
                down_r.prefetch()
            free(("gelu", g))

            def down_tile(t, room, g=g):
                part[g, :, ds(t * tile, tile)] = dot(gelu[g], room[...]).astype(BF16)
                swap_copy(0, g, t, tile).start()

            down.run(n_wide, down_tile)
            if g + 1 < per:
                down.prefetch()
            else:
                up_r.prefetch()
            part[g, :, width:] = dot(gelu[g], a_down_ref[...]).astype(BF16)
            swap_copy(0, g, n_wide, NR).start()

        for g in range(per):
            mover.relay(deals[g])
            if g + 1 < per:
                mover.begin(deals[g + 1])
            free(("cot", g))
            for s in range(n_fsdp):
                at = pl.ds(s * cot.shape[1], cot.shape[1])
                move(cot_rows.at[g, s], stage.at[g, at], ("stage", g))
            swapped(0, g)
            free(("stage", g), ("hat", g), ("slope", g))
            pick = pick_ref[g]

            def second_norm(rows, g=g, pick=pick):
                total = part[g, rows, :].astype(F32) + got[0, g, rows, :].astype(F32)
                code = (total[:, width:] * pick).astype(BF16)
                codes_down[g, rows, :] = code
                hidden = hat1[g, rows, :] * gain_ref[0:1, :] + shift_ref[0:1, :]
                hat, rstd = norm_parts(hidden + total[:, :width] + dot(code, b_down_ref[...]))
                part[g, rows, :width] = (hat * gain_ref[1:2, :] + shift_ref[1:2, :]).astype(BF16)
                dy2 = norm_back(hat, rstd, stage[g, rows, :].astype(F32) * gain_ref[1:2, :])
                keep32[g, rows, :] = dy2
                low = dy2.astype(BF16)
                wide_v[g, rows, :width] = low
                wide_v[g, rows, width:] = (dot_nt(low, b_down_ref[...]) * pick).astype(BF16)

            by_rows(second_norm)
            move(part.at[g, :, pl.ds(0, width)], acts_out.at[g], ("part", g))
            own = part.at[g, pl.ds(0, piece), pl.ds(0, width)]
            move(own, back_out.at[mover.z * per + g], ("part", g))
            turned[...] = wide_v[g].T

            def down_back(t, room, g=g):
                at = ds(t * tile, tile)
                block = dot(room[...], turned[...]).T
                low = (block * slope[g, :, at].astype(F32)).astype(BF16)
                slope[g, :, at] = low
                dpre_t[at, :] = low.T

            down_r.run(units // tile, down_back)
            (down_r if g + 1 < per else out_r).prefetch()
            free(("part", g))
            for s in range(1, n_fsdp):
                to = lax.rem(mover.z - s + n_fsdp, n_fsdp)
                rows_s = acts_out.at[g, pl.ds(s * piece, piece)]
                dealt.append(mover.go(rows_s, back_out.at[mover.z * per + g], {"fsdp": to}))

            def up_back(t, room, g=g):
                part[g, :, ds(t * tile, tile)] = dot(room[...], dpre_t[...]).T.astype(BF16)
                swap_copy(1, g, t, tile).start()

            up_r.run(n_wide, up_back)
            if g + 1 < per:
                up_r.prefetch()
            part[g, :, width:] = dot(b_up_ref[...], dpre_t[...]).T.astype(BF16)
            swap_copy(1, g, n_wide, NR).start()

        for g in range(per):
            entries = [
                (lambda g=g: codes_down[g], lambda g=g: wide_v[g, :, :width]),
                (lambda g=g: wide_v[g, :, width:], lambda g=g: gelu[g]),
                (lambda g=g: code_up_ref[g], lambda g=g: slope[g]),
            ]
            compact(grads_part, g, entries, sizes)
        for g in range(per):
            swapped(1, g)
            pick = pick_ref[g]

            def first_back(rows, g=g, pick=pick):
                total = part[g, rows, :].astype(F32) + got[1, g, rows, :].astype(F32)
                code = (total[:, width:] * pick).astype(BF16)
                dadapt_up_ref[g, rows, :] = code
                dh1 = keep32[g, rows, :] + total[:, :width] + dot_nt(code, a_up_ref[...])
                rstd = rstd1[g, rows, 0:1]
                dy1 = norm_back(hat1[g, rows, :], rstd, dh1 * gain_ref[0:1, :])
                keep32[g, rows, :] = dy1
                low = dy1.astype(BF16)
                wide_v[g, rows, :width] = low
                wide_v[g, rows, width:] = (dot_nt(low, b_out_ref[...]) * pick).astype(BF16)

            by_rows(first_back)
            move(keep32.at[g], dy1_out.at[g], "dy1")
            move(wide_v.at[g], da_out.at[g], "wide")
            turned[...] = wide_v[g].T

            def out_back(t, room, g=g):
                ctx_ref[g, :, ds(t * tile, tile)] = dot(room[...], turned[...]).T.astype(BF16)

            out_r.run(width_here // tile, out_back)
            if g + 1 < per:
                out_r.prefetch()
        for copy in dealt:
            copy.wait_recv()
        free(*list(busy))
        mover.close()

    vmem, anywhere = pl.BlockSpec(memory_space=pltpu.VMEM), pl.BlockSpec(memory_space=pl.ANY)
    row = (per, loc)
    grads_shape = (n_ctx, per * RANK, sum(sizes))
    outputs = [
        (row + (width,), BF16, anywhere),
        (row + (width,), F32, anywhere),
        (row + (wide,), BF16, anywhere),
        ((per, n_fsdp) + cot.shape[1:], BF16, anywhere),
        (grads_shape, BF16, vmem),
        (cot.shape, BF16, anywhere),
        (row + (NR,), BF16, vmem),
        (row + (width_here,), BF16, vmem),
    ]
    n_copy = 2 * per * n_swap
    n_deal = 2 * per * (n_fsdp - 1)
    return pl.pallas_call(
        kernel,
        in_specs=[vmem] * 10 + [anywhere] * 7,
        out_specs=[space for _, _, space in outputs],
        out_shape=[jax.ShapeDtypeStruct(shape, dtype) for shape, dtype, _ in outputs],
        scratch_shapes=[
            pltpu.SemaphoreType.DMA((n_copy,)),
            pltpu.SemaphoreType.DMA((n_copy,)),
            pltpu.SemaphoreType.DMA((n_deal,)),
            pltpu.SemaphoreType.DMA((n_deal,)),
            pltpu.SemaphoreType.DMA((8,)),
            pltpu.SemaphoreType.DMA(((8 + n_fsdp) * per,)),
            pltpu.VMEM((2, units, tile), BF16),
            pltpu.VMEM((2, tile, wide), BF16),
            pltpu.VMEM((2, tile, units), BF16),
            pltpu.VMEM(row + (width,), BF16),
            pltpu.VMEM(row + (wide,), BF16),
            pltpu.VMEM((2,) + row + (wide,), BF16),
            pltpu.VMEM(row + (width,), F32),
            pltpu.VMEM(row + (width,), F32),
            pltpu.VMEM(row + (units,), BF16),
            pltpu.VMEM(row + (units,), BF16),
            pltpu.VMEM(row + (wide,), BF16),
            pltpu.VMEM((wide, loc), BF16),
            pltpu.VMEM((units, loc), BF16),
            pltpu.VMEM(row + (NR,), BF16),
        ],
        compiler_params=pltpu.CompilerParams(
            collective_id=3, has_side_effects=True, vmem_limit_bytes=62 << 20
        ),
    )(
        picked, gain, shift_by, rstds, adapt_up, a_up, b_out, b_down, a_down, b_up,
        hats, gelus, slopes, cot, out_x, up_x, down_x,
    )


def combine(pieces, chosen, shapes):
    n_part, n_fsdp, rows, columns = pieces.shape
    flat, specs = [], []
    for i, shape in enumerate(shapes):
        high, wide = shape[-2:]
        tall = wide == NR and high != NR
        size = (high if tall else wide) // n_part
        block = (size, NR) if tall else (NR, size)
        lead = shape[0] if len(shape) == 3 else None
        for j in range(lead or 1):
            flat.append((i, None if lead is None else j, tall, size))
        if lead is None:
            specs.append(pl.BlockSpec(block, (lambda c: (c, 0)) if tall else (lambda c: (0, c))))
        else:
            specs.append(
                pl.BlockSpec(
                    (lead,) + block, (lambda c: (0, c, 0)) if tall else (lambda c: (0, 0, c))
                )
            )

    def kernel(chosen_ref, piece_ref, *outs):
        ordered = jnp.concatenate([piece_ref[0, a] for a in range(n_fsdp)], axis=0)
        start = 0
        for i, lead, tall, size in flat:
            block = ordered[:, start : start + size]
            value = dot_tn(block, chosen_ref[...]) if tall else dot_tn(chosen_ref[...], block)
            if lead is None:
                outs[i][...] = value
            else:
                outs[i][lead] = value
            start += size

    return pl.pallas_call(
        kernel,
        grid=(n_part,),
        in_specs=[
            pl.BlockSpec(chosen.shape, lambda c: (0, 0)),
            pl.BlockSpec((1, n_fsdp, rows, columns), lambda c: (c, 0, 0, 0)),
        ],
        out_specs=specs,
        out_shape=[jax.ShapeDtypeStruct(shape, F32) for shape in shapes],
        compiler_params=pltpu.CompilerParams(vmem_limit_bytes=48 << 20),
    )(chosen, pieces)


def finish(
    query, kv_own, slots, bias, grad, log_total, x_rows, adapt_in, dy1, qkv_x, a_qkv, picked, grads, early, pairs, n_fsdp, n_ctx
):
    per, loc, width_here = query.shape
    piece, width = loc // n_fsdp, x_rows.shape[2]
    heads = width_here // HEAD_DIM
    cuts = 4
    high = heads // cuts
    columns = high * HEAD_DIM
    masks = masks_of(n_ctx)
    units = [(g, c) for g in range(per) for c in range(cuts)]
    depth = 3 * width_here
    foot = 3 * NR
    wide = width + foot
    tile = 512
    n_wide = width // tile
    n_swap = n_wide + 1
    n_early = len(early)
    early_sizes = [values[2] // n_ctx for _, values in pairs]
    before = grads.shape[2]
    late_sizes = [width_here // n_ctx] * 3 + [width // n_ctx] * 3
    n_copy = len(units) * (n_ctx - 1) + per * n_wide * (n_fsdp - 1)
    n_copy += 2 * ((n_fsdp - 1) * n_ctx + 2 * (n_ctx - 1))

    def kernel(*refs):
        q_ref, bias_ref, g_ref, log_ref, x_ref, adapt_ref, a_ref, pick_ref = refs[:8]
        dy1_ref, w_ref, grads_ref, kv_ref = refs[8:12]
        slot_refs = refs[12 : 11 + n_ctx]
        early_refs = refs[11 + n_ctx : 11 + n_ctx + n_early]
        at = 11 + n_ctx + n_early
        in_ref, early_out, late_out = refs[at : at + 3]
        send, recv, swap_send, swap_recv, ring_sem, load, sems = refs[at + 3 : at + 10]
        kv_room, own, came, dq, dkv = refs[at + 10 : at + 15]
        tiles, foot_room, dy1_room, turned, part, got, codes_in = refs[at + 15 : at + 22]
        early_part, early_came, late_part, late_came = refs[at + 22 : at + 26]
        staged = refs[at + 26 :]
        mover = Mover(n_fsdp, n_ctx, send, recv)
        z, ct = mover.z, mover.ct
        partner = {"tp": 1 - lax.axis_index("tp")}
        ring = Ring(tiles, ring_sem, 0, lambda t: w_ref.at[ds(t * tile, tile)])
        used = [0]
        kept, dealt, flying = [], [], {}

        def move(source, target):
            copy = pltpu.make_async_copy(source, target, sems.at[used[0]])
            used[0] += 1
            copy.start()
            return copy

        loads = []
        for g in range(per):
            loads.append([])
            for k in range(n_ctx):
                source = kv_ref if k == 0 else slot_refs[k - 1]
                copy = pltpu.make_async_copy(
                    source.at[:, g], kv_room.at[g, k], load.at[g * n_ctx + k]
                )
                copy.start()
                loads[g].append(copy)
        staging = [move(ref, room) for ref, room in zip(early_refs, staged)]
        staging.append(move(grads_ref, early_part.at[:, :, pl.ds(0, before)]))
        load_foot = move(w_ref.at[pl.ds(width, foot)], foot_room)
        ring.prefetch()
        load_dy1 = move(dy1_ref, dy1_room)
        mover.greet(tp=True)

        def compute(u):
            g, c = units[u]
            if c == 0:
                for copy in loads[g]:
                    copy.wait()

            def one(h, carry):
                at = ds(c * columns + h * HEAD_DIM, HEAD_DIM)
                to = ds(h * HEAD_DIM, HEAD_DIM)
                biases = []
                for k in range(n_ctx):
                    block = bias_ref[g, k * loc : (k + 1) * loc, :]
                    biases.append(jnp.concatenate([block] * (loc // 128), axis=1))
                dquery, dkeys, dvalues = attend_back_head(
                    q_ref[g, :, at],
                    g_ref[g, :, at],
                    log_ref[g, c * high + h],
                    [kv_room[g, k, 0, :, at] for k in range(n_ctx)],
                    [kv_room[g, k, 1, :, at] for k in range(n_ctx)],
                    biases,
                )
                dq[g, :, at] = dquery
                for k in range(n_ctx):
                    own[u, k, 0, :, to] = dkeys[k]
                    own[u, k, 1, :, to] = dvalues[k]
                return carry

            lax.fori_loop(0, high, one, 0)

        def hand(u, level):
            half = 2**level
            device = {"ctx": flip(ct, masks[level])}
            flying[u, level] = [
                mover.go(own.at[u, half + i], came.at[u, half - 1 + i], device) for i in range(half)
            ]

        def take_in(u, level):
            half = 2**level
            g, c = units[u]
            for i, copy in enumerate(flying[u, level]):
                copy.wait_recv()
                for j in range(2):
                    total = own[u, i, j].astype(F32) + came[u, half - 1 + i, j].astype(F32)
                    if level:
                        own[u, i, j] = total.astype(BF16)
                    else:
                        dkv[j, g, :, c * columns : (c + 1) * columns] = total.astype(BF16)
            if level:
                hand(u, level - 1)

        def swap_copy(g, t):
            at = pl.ds(width, foot) if isinstance(t, int) and t == n_wide else ds(t * tile, tile)
            sem = g * n_swap + t
            return pltpu.make_async_remote_copy(
                src_ref=part.at[g, :, at],
                dst_ref=got.at[g, :, at],
                send_sem=swap_send.at[sem],
                recv_sem=swap_recv.at[sem],
                device_id=partner,
                device_id_type=pl.DeviceIdType.MESH,
            )

        def project_back(g):
            turned[0:width_here, :] = dq[g].T
            turned[width_here : 2 * width_here, :] = dkv[0, g].T
            turned[2 * width_here :, :] = dkv[1, g].T
            if g == 0:
                load_foot.wait()
            part[g, :, width:] = dot(foot_room[...], turned[...]).T.astype(BF16)
            swap_copy(g, n_wide).start()

            def back(t, room):
                part[g, :, ds(t * tile, tile)] = dot(room[...], turned[...]).T.astype(BF16)
                swap_copy(g, t).start()

            ring.run(n_wide, back)
            if g + 1 < per:
                ring.prefetch()

        def take_codes(g):
            swap_copy(g, n_wide).wait_recv()
            pick = jnp.concatenate([pick_ref[g]] * 3, axis=1)
            total = part[g, :, width:].astype(F32) + got[g, :, width:].astype(F32)
            codes_in[g] = (total * pick).astype(BF16)

        def finish_tile(g, t):
            swap_copy(g, t).wait_recv()
            swap_copy(g, t).wait_send()
            at = slice(t * tile, (t + 1) * tile)
            value = part[g, :, at].astype(F32) + got[g, :, at].astype(F32) + dy1_room[g, :, at]
            for j in range(3):
                value = value + dot_nt(codes_in[g, :, j * NR : (j + 1) * NR], a_ref[j, at, :])
            part[g, :, at] = value.astype(BF16)
            to_at = pl.ds(t * tile, tile)
            kept.append(move(part.at[g, pl.ds(0, piece), to_at], in_ref.at[z * per + g, :, to_at]))
            for s in range(1, n_fsdp):
                to = lax.rem(z - s + n_fsdp, n_fsdp)
                dealt.append(
                    mover.go(
                        part.at[g, pl.ds(s * piece, piece), to_at],
                        in_ref.at[z * per + g, :, to_at],
                        {"fsdp": to},
                    )
                )

        early_fold = Fold(mover, early_part, early_came, early_out)
        late_fold = Fold(mover, late_part, late_came, late_out)

        def known():
            for copy in staging:
                copy.wait()
            for n in range(per):
                entries = []
                for (i, first, size), (j, start, count) in pairs:
                    entries.append(
                        (
                            lambda n=n, i=i, f=first, c=size: staged[i][n, :, f : f + c],
                            lambda n=n, i=j, f=start, c=count: staged[i][n, :, f : f + c],
                        )
                    )
                compact(early_part, n, entries, early_sizes, before)
            early_fold.hand(last)

        last = len(masks) - 1
        for t in range(len(units) + last):
            if t < len(units):
                compute(t)
                hand(t, last)
            for k in range(last):
                if 0 <= t - 1 - k < len(units):
                    take_in(t - 1 - k, last - k)
            if t == 1:
                known()
            if t == 3:
                for level in range(last, 0, -1):
                    early_fold.next(level)
            if t == 6:
                early_fold.next(0)
                source, target, first = early_fold.gather()
                kept.append(move(source, target))
        done = set()
        for g in range(per):
            for u, (owner, _) in enumerate(units):
                if owner == g:
                    take_in(u, 0)
            if g + 1 == per:
                mover.relay(first)
            project_back(g)
            take_codes(g)
            if g == 0:
                load_dy1.wait()
            if g + 1 < per:
                for t in range(n_wide // 2):
                    finish_tile(g, t)
                    done.add((g, t))
        for n in range(per):
            values = [
                lambda n=n: dq[n],
                lambda n=n: dkv[0, n],
                lambda n=n: dkv[1, n],
            ]
            entries = [
                (lambda n=n, j=j: adapt_ref[n, :, j * NR : (j + 1) * NR], values[j]) for j in range(3)
            ]
            entries += [
                (lambda n=n, j=j: codes_in[n, :, j * NR : (j + 1) * NR], lambda n=n: x_ref[n])
                for j in range(3)
            ]
            compact(late_part, n, entries, late_sizes)
        late_fold.hand(last)
        rest = [(g, t) for g in range(per) for t in range(n_wide) if (g, t) not in done]
        for i, (g, t) in enumerate(rest):
            finish_tile(g, t)
            if i == 0:
                for level in range(last, 0, -1):
                    late_fold.next(level)
            if i == 1:
                late_fold.next(0)
                source, target, second = late_fold.gather()
                kept.append(move(source, target))
            if i == len(rest) - 3:
                mover.complete(first)
            if i == len(rest) - 2:
                mover.relay(second)
        mover.complete(second)
        for g in range(per):
            swap_copy(g, n_wide).wait_send()
        for copy in dealt:
            copy.wait_recv()
        for copy in kept:
            copy.wait()
        mover.close()

    vmem, anywhere = pl.BlockSpec(memory_space=pltpu.VMEM), pl.BlockSpec(memory_space=pl.ANY)
    parts = [(n_ctx, per * RANK, before + sum(early_sizes)), (n_ctx, per * RANK, sum(late_sizes))]
    row = (per, loc)
    rooms = [
        ((per, n_ctx, 2, loc, width_here), BF16),
        ((len(units), n_ctx, 2, loc, columns), BF16),
        ((len(units), n_ctx - 1, 2, loc, columns), BF16),
        (row + (width_here,), BF16),
        ((2,) + row + (width_here,), BF16),
        ((2, tile, depth), BF16),
        ((foot, depth), BF16),
        (dy1.shape, F32),
        ((depth, loc), BF16),
        (row + (wide,), BF16),
        (row + (wide,), BF16),
        (row + (foot,), BF16),
    ]
    for shape in parts:
        rooms += [(shape, BF16), ((n_ctx - 1,) + shape[1:], BF16)]
    rooms += [(x.shape, BF16) for x in early]
    return pl.pallas_call(
        kernel,
        in_specs=[vmem] * 8 + [anywhere] * (3 + n_ctx + n_early),
        out_specs=[anywhere] * 3,
        out_shape=[jax.ShapeDtypeStruct((per * n_fsdp, piece, width), BF16)]
        + [jax.ShapeDtypeStruct((n_ctx, n_fsdp) + shape[1:], BF16) for shape in parts],
        scratch_shapes=[
            pltpu.SemaphoreType.DMA((n_copy,)),
            pltpu.SemaphoreType.DMA((n_copy,)),
            pltpu.SemaphoreType.DMA((per * n_swap,)),
            pltpu.SemaphoreType.DMA((per * n_swap,)),
            pltpu.SemaphoreType.DMA((2,)),
            pltpu.SemaphoreType.DMA((per * n_ctx,)),
            pltpu.SemaphoreType.DMA((5 + n_early + per * n_wide,)),
        ]
        + [pltpu.VMEM(shape, dtype) for shape, dtype in rooms],
        compiler_params=pltpu.CompilerParams(
            collective_id=4, has_side_effects=True, vmem_limit_bytes=63 << 20
        ),
    )(
        query, bias, grad, log_total, x_rows, adapt_in, a_qkv, picked, dy1, qkv_x, grads, kv_own, *slots, *early,
    )


def gelu_both(pre):
    square = pre * pre
    bent = jnp.tanh(GELU_COEF * (pre + 0.044715 * square * pre))
    out = 0.5 * pre * (1.0 + bent)
    slope = 0.5 * (1.0 + bent) + 0.5 * pre * (1.0 - bent * bent) * GELU_COEF * (
        1.0 + 3.0 * 0.044715 * square
    )
    return out.astype(BF16), slope.astype(BF16)


def local(
    x_in,
    cotangent,
    lengths,
    adapter_ids,
    w_qkv,
    w_out,
    w_up,
    w_down,
    ln_gain,
    ln_bias,
    a_qkv,
    b_qkv,
    a_out,
    b_out,
    a_up,
    b_up,
    a_down,
    b_down,
):
    n_ctx, n_fsdp = lax.axis_size("ctx"), lax.axis_size("fsdp")
    z, ct = lax.axis_index("fsdp"), lax.axis_index("ctx")
    seqs, piece, width = x_in.shape
    per = seqs // n_fsdp
    loc = n_fsdp * piece
    heads_width = w_qkv.shape[2]
    def take(array, start, size, axis=0):
        return lax.dynamic_slice_in_dim(array, start, size, axis)

    units = w_up.shape[1]
    rows_shape = (per, n_fsdp, piece, width)
    zq = w_qkv.shape[1]

    def first_items(ins, outs, z):
        x_ref, w_ref = ins
        rows_ref, whole_ref = outs

        def deal(g):
            return Deal(lambda to: x_ref.at[to * per + g], lambda s: rows_ref.at[g, s])

        def weight(j):
            size = zq // n_ctx
            columns = pl.ds(j * heads_width, heads_width)
            return Weight(
                lambda c: w_ref.at[j, pl.ds(pl.multiple_of(c * size, size), size)],
                lambda o, c: whole_ref.at[
                    pl.ds(pl.multiple_of(o * zq + c * size, size), size), columns
                ],
            )

        stay = [(x_ref.at[z * per + g], rows_ref.at[g, 0]) for g in range(per)]
        for j in range(3):
            own = whole_ref.at[
                pl.ds(pl.multiple_of(z * zq, zq), zq), pl.ds(j * heads_width, heads_width)
            ]
            stay.append((w_ref.at[j], own))
        items = [weight(j) for j in range(3)] + [deal(g) for g in range(per)]
        return items, stay

    x_all, qkv_x = move(
        first_items,
        [Weight] * 3 + [Deal] * per,
        (x_in, w_qkv),
        (rows_shape, (width + 3 * NR, 3 * heads_width)),
        n_fsdp,
        n_ctx,
        ((piece, width),) * per + (w_qkv.shape[1:],) * 3,
        0,
        foot=(b_qkv, lambda outs: outs[1].at[pl.ds(width, 3 * NR)]),
    )

    my_lengths = take(lengths, z * per, per)
    my_ids = take(adapter_ids, z * per, per)
    picked = (my_ids[:, None] == jnp.arange(NR)[None, :] // RANK).astype(F32)
    steps = lax.rem(z - jnp.arange(n_fsdp) + n_fsdp, n_fsdp)
    ctx_of = ct ^ jnp.array(offsets(n_ctx))
    key_pos = (
        (steps[None, :, None] * n_ctx + ctx_of[:, None, None]) * piece
        + jnp.arange(piece)[None, None, :]
    ).reshape(-1)
    bias_all = jnp.where(key_pos[None, :] < my_lengths[:, None], 0.0, -1e30).astype(F32)
    bias_all = jnp.broadcast_to(bias_all[:, :, None], bias_all.shape + (128,))

    picked = picked[:, None, :]
    x_rows = x_all.reshape(per, loc, width)
    moved = forward_and_gather(
        x_rows, qkv_x, a_qkv, picked, bias_all, ln_gain, ln_bias, (a_up, b_out), (w_out, w_up, w_down),
        (a_out, b_up, a_down), n_fsdp, n_ctx,
    )
    slots = moved[: n_ctx - 1]
    (
        query, kv_own, adapt_all, out_x, up_x, down_x, context, log_total, wide_h, gelus, slopes, hats, rstds,
        adapt_out, adapt_up,
    ) = moved[n_ctx - 1 :]
    _, dy1, wide_a, _, grads, activations, dadapt_up, d_context = middle(
        hats, rstds, gelus, slopes, adapt_up, cotangent, picked, ln_gain, ln_bias, (out_x, up_x, down_x),
        (a_up, b_out, b_down, a_down, b_up), n_fsdp, n_ctx,
    )
    early_in = (dadapt_up, wide_h, adapt_out, wide_a, context)
    early_pairs = [
        ((0, 0, NR), (1, 0, width)),
        ((2, 0, NR), (3, 0, width)),
        ((3, width, NR), (4, 0, heads_width)),
    ]
    input_grad, early, late = finish(
        query, kv_own, slots, bias_all, d_context, log_total, x_rows, adapt_all, dy1, qkv_x, a_qkv, picked,
        grads, early_in, early_pairs, n_fsdp, n_ctx,
    )

    codes = (adapter_ids[:, None] * RANK + jnp.arange(RANK)[None, :]).reshape(-1)
    chosen = (codes[:, None] == jnp.arange(NR)[None, :]).astype(BF16)
    b_down_grad, a_down_grad, b_up_grad, a_up_grad, b_out_grad, a_out_grad = combine(
        early,
        chosen,
        [(NR, width), (units, NR), (NR, units), (width, NR), (NR, width), (heads_width, NR)],
    )
    b_qkv_grad, a_qkv_grad = combine(late, chosen, [(3, NR, heads_width), (3, width, NR)])
    return (
        activations, input_grad, a_qkv_grad, b_qkv_grad, a_out_grad, b_out_grad, a_up_grad, b_up_grad,
        a_down_grad, b_down_grad,
    )


def solution(mesh):
    rows = P(None, ("fsdp", "ctx"), None)
    return jax.shard_map(
        local,
        mesh=mesh,
        in_specs=(
            rows,
            rows,
            P(),
            P(),
            P(None, "fsdp", "tp"),
            P("tp", "fsdp"),
            P("fsdp", "tp"),
            P("tp", "fsdp"),
            P(),
            P(),
            P(),
            P(None, None, "tp"),
            P("tp", None),
            P(),
            P(),
            P(None, "tp"),
            P("tp", None),
            P(),
        ),
        out_specs=(
            rows,
            rows,
            P(),
            P(None, None, "tp"),
            P("tp", None),
            P(),
            P(),
            P(None, "tp"),
            P("tp", None),
            P(),
        ),
        check_vma=False,
    )
```

```python
import math

import jax
import jax.numpy as jnp
from jax import lax
from jax.experimental import pallas as pl
from jax.experimental.pallas import tpu as pltpu
from jax.sharding import PartitionSpec as P

HEAD_DIM = 128
RANK = 16
ADAPTERS = 8
NR = RANK * ADAPTERS
NORM_EPS = 1e-06
GELU_COEF = 0.7978845608028654
SCALE = 1.0 / math.sqrt(HEAD_DIM)
F32 = jnp.float32
BF16 = jnp.bfloat16


def dot(left, right):
    return jnp.dot(left, right, preferred_element_type=F32)


def dot_nt(left, right):
    return lax.dot_general(left, right, (((1,), (1,)), ((), ())), preferred_element_type=F32)


def dot_tn(left, right):
    return lax.dot_general(left, right, (((0,), (0,)), ((), ())), preferred_element_type=F32)


def masks_of(n):
    out = []
    while n > 1:
        n //= 2
        out.append(n)
    return out


def offsets(n):
    out = [0]
    for mask in masks_of(n):
        out = out + [o ^ mask for o in out]
    return out


def attend_head(query, keys, values, biases):
    scores = [dot_nt(k, query) * SCALE + bias for k, bias in zip(keys, biases)]
    top = scores[0].max(axis=0, keepdims=True)
    for s in scores[1:]:
        top = jnp.maximum(top, s.max(axis=0, keepdims=True))
    total = jnp.zeros_like(top)
    mixed = None
    for s, v in zip(scores, values):
        probs = jnp.exp(s - top)
        total = total + probs.sum(axis=0, keepdims=True)
        term = dot_tn(v, probs.astype(BF16))
        mixed = term if mixed is None else mixed + term
    return (mixed / total).T.astype(BF16), top + jnp.log(total)


def attend_back_head(query, grad, log_total, keys, values, biases):
    probs, dprobs, dvalues = [], [], []
    delta = jnp.zeros_like(log_total)
    for k, v, bias in zip(keys, values, biases):
        p = jnp.exp(dot_nt(k, query) * SCALE + bias - log_total)
        dp = dot_nt(v, grad)
        dvalues.append(dot(p.astype(BF16), grad).astype(BF16))
        delta = delta + (p * dp).sum(axis=0, keepdims=True)
        probs.append(p)
        dprobs.append(dp)
    dquery, dkeys = None, []
    for k, p, dp in zip(keys, probs, dprobs):
        ds = (p * (dp - delta)).astype(BF16)
        dkeys.append((dot(ds, query) * SCALE).astype(BF16))
        term = dot_tn(k, ds)
        dquery = term if dquery is None else dquery + term
    return (dquery * SCALE).T.astype(BF16), dkeys, dvalues


def ds(start, size):
    return pl.ds(pl.multiple_of(start, size), size)


def flip(ct, offset):
    mask = 1
    while mask <= offset:
        if offset & mask:
            ct = ct + mask - 2 * mask * lax.rem(ct // mask, 2)
        mask *= 2
    return ct


class Weight:
    def __init__(self, shard_at, whole_at, own=None, skip=0, direct=False):
        self.shard_at, self.whole_at, self.own, self.skip = shard_at, whole_at, own, skip
        self.direct = direct


class Deal:
    def __init__(self, source_at, rows_at):
        self.source_at, self.rows_at = source_at, rows_at


class Pair:
    def __init__(self, slot_at):
        self.slot_at = slot_at


class Mover:
    def __init__(self, n_fsdp, n_ctx, send, recv):
        self.n_fsdp, self.n_ctx = n_fsdp, n_ctx
        self.z, self.ct = lax.axis_index("fsdp"), lax.axis_index("ctx")
        self.send, self.recv = send, recv
        self.used = 0
        self.open = []
        self.masks = masks_of(n_ctx)
        self.offsets = offsets(n_ctx)
        self.came, self.waiting, self.done = {}, {}, {}

    def skip(self, item):
        return item.skip if isinstance(item, Weight) else 0

    def part(self, item):
        return lax.rem(self.ct, self.n_ctx >> item.skip) if item.skip else self.ct

    def greet(self, tp=False):
        barrier = pltpu.get_barrier_semaphore()
        others = [{"fsdp": lax.rem(self.z + s, self.n_fsdp)} for s in range(1, self.n_fsdp)]
        others += [{"ctx": flip(self.ct, mask)} for mask in self.masks]
        if tp:
            others.append({"tp": 1 - lax.axis_index("tp")})
        for other in others:
            pl.semaphore_signal(
                barrier, inc=1, device_id=other, device_id_type=pl.DeviceIdType.MESH
            )
        pl.semaphore_wait(barrier, len(others))

    def copy(self, source, target, device, at=None):
        if at is None:
            at = self.used
            self.used += 1
        return pltpu.make_async_remote_copy(
            src_ref=source,
            dst_ref=target,
            send_sem=self.send.at[at],
            recv_sem=self.recv.at[at],
            device_id=device,
            device_id_type=pl.DeviceIdType.MESH,
        )

    def go(self, source, target, device):
        copy = self.copy(source, target, device)
        copy.start()
        self.open.append((None, copy))
        return copy

    def along(self, item, owner, right, ok, source, slot):
        target = item.whole_at(owner, self.part(item))
        device = {"fsdp": lax.rem(self.z + (1 if right else self.n_fsdp - 1), self.n_fsdp)}
        copy = self.copy(source, target, device, self.came[item] + slot - 1)
        pl.when(ok)(copy.start)
        self.open.append((ok, copy))

    def begin(self, item):
        if isinstance(item, Pair):
            self.waiting[item] = [[] for _ in self.masks]
            self.cast(item, item.slot_at, lambda k, level: item.slot_at(k + 2**level), 0, 0)
            return
        if isinstance(item, Weight) and item.direct:
            part = self.part(item)
            self.came[item] = [
                self.go(
                    item.shard_at(part),
                    item.whole_at(self.z, part),
                    {"fsdp": lax.rem(self.z + s, self.n_fsdp)},
                )
                for s in range(1, self.n_fsdp)
            ]
            return
        if isinstance(item, Weight):
            self.came[item] = self.used
            self.used += self.n_fsdp - 1
            source = item.shard_at(self.part(item))
            self.along(item, self.z, True, self.z < self.n_fsdp - 1, source, 1)
            self.along(item, self.z, False, self.z > 0, source, self.n_fsdp - 1)
            return
        self.came[item] = [
            self.go(
                item.source_at(lax.rem(self.z + s, self.n_fsdp)),
                item.rows_at(s),
                {"fsdp": lax.rem(self.z + s, self.n_fsdp)},
            )
            for s in range(1, self.n_fsdp)
        ]

    def cast(self, item, source_at, target_at, k, first):
        skip = self.skip(item)
        for level in range(first, len(self.masks) - skip):
            device = {"ctx": flip(self.ct, self.masks[level + skip])}
            copy = self.go(source_at(k), target_at(k, level), device)
            self.waiting[item][level].append((copy, k + 2**level, source_at, target_at))

    def relay(self, item):
        if isinstance(item, Deal):
            for copy in self.came[item]:
                copy.wait_recv()
            return
        self.waiting[item] = [[] for _ in self.masks[item.skip :]]
        n, part = self.n_fsdp, self.part(item)
        others = offsets(self.n_ctx >> item.skip)
        if item.own is not None:

            def mine(k):
                return item.own if k == 0 else item.whole_at(self.z, flip(part, others[k]))

            def lands(k, level):
                return item.whole_at(self.z, flip(part, others[k]))

            self.cast(item, mine, lands, 0, 0)
        for i in range(n - 1):
            s = i // 2 + 1 if i % 2 == 0 else n - 1 - i // 2
            owner = lax.rem(self.z - s + n, n)
            here = item.whole_at(owner, part)
            if item.direct:
                self.came[item][s - 1].wait_recv()
            else:
                self.copy(here, here, {"fsdp": owner}, self.came[item] + s - 1).wait_recv()
                if s < n - 1:
                    ok = (self.z >= s) & (self.z < n - 1)
                    self.along(item, owner, True, ok, here, s + 1)
                if s > 1:
                    ok = (self.z < s) & (self.z > 0)
                    self.along(item, owner, False, ok, here, s - 1)

            def at(k, owner=owner):
                return item.whole_at(owner, flip(part, others[k]))

            self.cast(item, at, lambda k, level, at=at: at(k), 0, 0)

    def finish(self, item, level):
        if isinstance(item, Deal) or level != self.done.get(item, 0):
            return
        if level == len(self.waiting[item]):
            return
        for copy, k, source_at, target_at in self.waiting[item][level]:
            copy.wait_recv()
            self.cast(item, source_at, target_at, k, level + 1)
        self.done[item] = level + 1

    def complete(self, item):
        while self.done.get(item, 0) < len(self.waiting[item]):
            self.finish(item, self.done.get(item, 0))

    def close(self):
        for ok, copy in self.open:
            if ok is None:
                copy.wait_send()
            else:
                pl.when(ok)(copy.wait_send)


def copies_of(items, n_fsdp, n_ctx):
    total = 0
    for item in items:
        total += {Weight: (n_fsdp - 1) * n_ctx, Deal: n_fsdp - 1, Pair: n_ctx - 1}[item]
    return total


def keep(stay, room, sems):
    out = []
    for k, (source, target) in enumerate(stay):
        first = pltpu.make_async_copy(source, room[k], sems.at[2 * k])
        first.start()
        out.append((first, pltpu.make_async_copy(room[k], target, sems.at[2 * k + 1])))
    return out


def move(make, kinds, inputs, outputs, n_fsdp, n_ctx, local_shapes, ident, ahead=2, foot=None):
    n_in = len(inputs)
    n_copy = copies_of(kinds, n_fsdp, n_ctx)

    def kernel(*refs):
        ins, outs = refs[:n_in], refs[n_in : n_in + len(outputs)]
        send, recv, here = refs[n_in + len(outputs) : n_in + len(outputs) + 3]
        room = refs[n_in + len(outputs) + 3 :]
        if foot is not None:
            blocks_ref, ins = ins[-1], ins[:-1]
            strip = room[-1]
        mover = Mover(n_fsdp, n_ctx, send, recv)
        items, stay = make(ins, outs, mover.z)
        mover.greet()
        for item in items[:ahead]:
            mover.begin(item)
        kept = keep(stay, room, here)
        levels = len(mover.masks)
        for i in range(len(items) + levels):
            if i < len(items):
                mover.relay(items[i])
                if i + ahead < len(items):
                    mover.begin(items[i + ahead])
            if i == 0 and foot is not None:
                strip[...] = jnp.zeros_like(strip)
                high, wide = blocks_ref.shape[1:]
                for j in range(blocks_ref.shape[0]):
                    strip[j * high : (j + 1) * high, j * wide : (j + 1) * wide] = blocks_ref[j]
                set_foot = pltpu.make_async_copy(strip, foot[1](outs), here.at[2 * len(local_shapes)])
                set_foot.start()
                kept.append((None, set_foot))
            if i == 0:
                for first, second in kept:
                    if first is not None:
                        first.wait()
                        second.start()
            for level in range(levels):
                if 0 <= i - 1 - level < len(items):
                    mover.finish(items[i - 1 - level], level)
        for _, second in kept:
            second.wait()
        mover.close()

    spaces = [pl.BlockSpec(memory_space=pl.ANY)] * n_in
    room_shapes = list(local_shapes)
    if foot is not None:
        blocks = foot[0]
        inputs = inputs + (blocks,)
        n_in += 1
        spaces.append(pl.BlockSpec(memory_space=pltpu.VMEM))
        room_shapes.append((blocks.shape[0] * blocks.shape[1], blocks.shape[0] * blocks.shape[2]))
    return pl.pallas_call(
        kernel,
        in_specs=spaces,
        out_specs=[pl.BlockSpec(memory_space=pl.ANY)] * len(outputs),
        out_shape=[jax.ShapeDtypeStruct(shape, BF16) for shape in outputs],
        scratch_shapes=[
            pltpu.SemaphoreType.DMA((n_copy,)),
            pltpu.SemaphoreType.DMA((n_copy,)),
            pltpu.SemaphoreType.DMA((2 * len(local_shapes) + 1,)),
        ]
        + [pltpu.VMEM(shape, BF16) for shape in room_shapes],
        compiler_params=pltpu.CompilerParams(
            collective_id=ident, has_side_effects=True, vmem_limit_bytes=60 << 20
        ),
    )(*inputs)


def forward_and_gather(
    x_rows, qkv_x, a_qkv, picked, bias, gain, shift_by, first_maps, shards, maps, n_fsdp, n_ctx
):
    per, loc, width = x_rows.shape
    w_out, w_up, w_down = shards
    width_here = qkv_x.shape[1] // 3
    heads, units = width_here // HEAD_DIM, w_up.shape[1]
    zu, zo = w_up.shape[0], w_out.shape[1]
    n_part = n_ctx // 2 if n_ctx > 1 else 1
    so, su, sd = w_out.shape[0] // n_ctx, zu // n_ctx, w_down.shape[0] // n_ctx
    wide = width + NR
    wide_x = width + 3 * NR
    cuts = 4
    paired = cuts // 2 if n_ctx > 1 else 0
    tile = 512
    per_kind = width_here // tile
    chunk = 64
    n_tile = 3 * per_kind
    n_copy = (n_fsdp - 1) * n_ctx * (1 + 2 * cuts) + 2 * per * (n_ctx - 1) + 6 + per
    lag = 4

    def kernel(*refs):
        bias_ref, a_ref, pick_ref, gain_ref, shift_ref, a_up_ref, b_out_ref, x_ref, w_ref = refs[:9]
        wo_ref, wu_ref, wd_ref, ao_ref, bu_ref, ad_ref = refs[9:15]
        slots = refs[15 : 14 + n_ctx]
        q_ref, kv_ref, adapt_ref, out_ref, up_ref, down_ref, ctx_ref, log_ref = refs[
            14 + n_ctx : 22 + n_ctx
        ]
        h_ref, gelu_ref, slope_ref, hat_ref, rstd_ref, adapt_out_ref, adapt_up_ref = refs[
            22 + n_ctx : 29 + n_ctx
        ]
        send, recv, here, load, ring_sem, x_room, w_room, proj, kv_room, out_room = refs[
            29 + n_ctx : 39 + n_ctx
        ]
        part_ref, other_ref, up_room, wide_v, hat1, gelu, slope = refs[39 + n_ctx :]
        mover = Mover(n_fsdp, n_ctx, send, recv)
        ring = Ring(
            w_room,
            ring_sem,
            0,
            lambda t: w_ref.at[:, ds(lax.rem(t + per_kind, n_tile) * tile, tile)],
        )
        z = mover.z
        rows = [pl.ds(g * loc, loc) for g in range(per)]

        def columns(j):
            return pl.ds(j * width_here, width_here)

        out_item = Weight(
            lambda c: wo_ref.at[ds(c * so, so)],
            lambda o, c: out_ref.at[ds(c * so, so), ds(o * zo, zo)],
        )

        def up_item(h):
            at = pl.ds(h * (units // cuts), units // cuts)
            return Weight(
                lambda c: wu_ref.at[ds(c * su, su), at],
                lambda o, c: up_ref.at[ds(o * zu + c * su, su), at],
            )

        def down_item(h):
            size = sd // cuts
            return Weight(
                lambda c: wd_ref.at[ds(c * sd + h * size, size)],
                lambda o, c: down_ref.at[ds(c * sd + h * size, size), ds(o * zo, zo)],
            )

        def down_pair(h):
            size = sd // cuts

            def at(c, p):
                return ds((c + p * n_part) * sd + h * size, size)

            def half(p):
                return Weight(
                    lambda c: wd_ref.at[at(c, p)],
                    lambda o, c: down_ref.at[at(c, p), ds(o * zo, zo)],
                    skip=1,
                )

            return [half(p) for p in range(2)]

        def pair(g, j):
            return Pair(
                lambda k: proj.at[rows[g], columns(1 + j)] if k == 0 else slots[k - 1].at[j, g]
            )

        pairs = [pair(g, j) for g in range(per) for j in range(2)]
        items = [out_item] + [up_item(h) for h in range(cuts)]
        items += [down_item(h) for h in range(cuts - paired)]
        for h in range(cuts - paired, cuts):
            items += down_pair(h)
        used = [0]

        def move(source, target):
            copy = pltpu.make_async_copy(source, target, here.at[used[0]])
            used[0] += 1
            copy.start()
            return copy

        def attend(g):
            for j in range(2):
                mover.complete(pairs[2 * g + j])
            loads = []
            for k in range(1, n_ctx):
                copy = pltpu.make_async_copy(slots[k - 1].at[:, g], kv_room.at[k], load.at[k])
                copy.start()
                loads.append(copy)
            for j in range(2):
                kv_room[0, j] = proj[g * loc : (g + 1) * loc, (1 + j) * width_here : (2 + j) * width_here]
            for copy in loads:
                copy.wait()

            def one(h, carry):
                at = ds(h * HEAD_DIM, HEAD_DIM)
                biases = []
                for k in range(n_ctx):
                    block = bias_ref[g, k * loc : (k + 1) * loc, :]
                    biases.append(jnp.concatenate([block] * (loc // 128), axis=1))
                context, log = attend_head(
                    proj[g * loc : (g + 1) * loc, at],
                    [kv_room[k, 0, :, at] for k in range(n_ctx)],
                    [kv_room[k, 1, :, at] for k in range(n_ctx)],
                    biases,
                )
                ctx_ref[g, :, at] = context
                log_ref[g, h] = log
                return carry

            lax.fori_loop(0, heads, one, 0)

        def project():
            mover.complete(out_item)
            own[0].wait_recv()
            own[3].wait_recv()
            copy = pltpu.make_async_copy(out_ref, out_room, load.at[0])
            copy.start()
            copy.wait()
            for g in range(per):
                for start in range(0, wide, 1024):
                    at = slice(start, min(start + 1024, wide))
                    part_ref[g, :, at] = dot(ctx_ref[g], out_room[:, at]).astype(BF16)
                swapped.append(
                    mover.go(
                        part_ref.at[g], other_ref.at[g], {"tp": 1 - lax.axis_index("tp")}
                    )
                )

        def tiles(t, room):
            at = ds(lax.rem(t + per_kind, n_tile) * tile, tile)
            proj[:, at] = dot(x_room[...], room[...]).astype(BF16)

        up_ring = Ring(up_room, ring_sem, 2, lambda t: up_ref.at[:, ds(t * tile, tile)])

        def first_norm(g):
            swapped[g].wait_recv()
            pick = pick_ref[g]

            def step(r, carry):
                rows_r = ds(r * chunk, chunk)
                total = part_ref[g, rows_r, :].astype(F32) + other_ref[g, rows_r, :].astype(F32)
                code = (total[:, width:] * pick).astype(BF16)
                adapt_out_ref[g, rows_r, :] = code
                x = x_room[ds(g * loc + r * chunk, chunk), :width].astype(F32)
                hat, rstd = norm_parts(x + total[:, :width] + dot(code, b_out_ref[...]))
                hat1[g, rows_r, :] = hat
                rstd_ref[g, rows_r, :] = jnp.broadcast_to(rstd, (chunk, 128))
                low = (hat * gain_ref[0:1, :] + shift_ref[0:1, :]).astype(BF16)
                wide_v[g, rows_r, :width] = low
                code = (dot(low, a_up_ref[...]) * pick).astype(BF16)
                wide_v[g, rows_r, width:] = code
                adapt_up_ref[g, rows_r, :] = code
                return carry

            lax.fori_loop(0, loc // chunk, step, 0)
            outward.append(move(hat1.at[g], hat_ref.at[g]))
            outward.append(move(wide_v.at[g], h_ref.at[g]))

        def feed(g):
            if g == 0:
                for item in items[1 : 1 + cuts]:
                    mover.complete(item)
                own[1].wait_recv()
                own[4].wait_recv()
                up_ring.prefetch()

            def up_tile(t, room):
                at = ds(t * tile, tile)
                value, factor = gelu_both(dot(wide_v[g], room[...]))
                gelu[g, :, at] = value
                slope[g, :, at] = factor

            up_ring.run(units // tile, up_tile)
            if g + 1 < per:
                up_ring.prefetch()
            outward.append(move(gelu.at[g], gelu_ref.at[g]))
            outward.append(move(slope.at[g], slope_ref.at[g]))

        swapped, outward = [], []
        tasks = {1 + g: (lambda g=g: attend(g)) for g in range(per)}
        tasks[per + 2] = project
        tasks[per + 5] = lambda: [first_norm(g) for g in range(per)]
        for g in range(per):
            tasks[per + 6 + g] = lambda g=g: feed(g)
        ring.prefetch()
        loads = [move(x_ref.at[g], x_room.at[rows[g], pl.ds(0, width)]) for g in range(per)]
        mover.greet(tp=True)
        ahead = 3
        for item in items[:ahead]:
            mover.begin(item)
        sibling = {"ctx": flip(mover.ct, 1)}
        own = [
            mover.go(source, target, sibling)
            for source, target in (
                (wo_ref, out_ref.at[:, ds(z * zo, zo)]),
                (wu_ref, up_ref.at[ds(z * zu, zu)]),
                (wd_ref, down_ref.at[:, ds(z * zo, zo)]),
                (ao_ref, out_ref.at[:, pl.ds(width, NR)]),
                (bu_ref, up_ref.at[pl.ds(width, NR)]),
                (ad_ref, down_ref.at[:, pl.ds(width, NR)]),
            )
        ]
        for g in range(per):
            loads[g].wait()
            pick = pick_ref[g]
            for j in range(3):
                code = dot(x_room[g * loc : (g + 1) * loc, :width], a_ref[j]) * pick
                x_room[g * loc : (g + 1) * loc, width + j * NR : width + (j + 1) * NR] = code.astype(BF16)
            outward.append(move(x_room.at[rows[g], pl.ds(width, 3 * NR)], adapt_ref.at[g]))
        ring.run(2 * per_kind, tiles, 0, n_tile)
        for item in pairs:
            mover.begin(item)
        for g in range(per):
            for j in range(2):
                outward.append(move(proj.at[rows[g], columns(1 + j)], kv_ref.at[j, g]))
        for i in range(len(items) + lag + 2):
            if i < len(items):
                mover.relay(items[i])
                if i + ahead < len(items):
                    mover.begin(items[i + ahead])
            if i == 0:
                ring.run(n_tile, tiles, 2 * per_kind, n_tile)
                for g in range(per):
                    outward.append(move(proj.at[rows[g], columns(0)], q_ref.at[g]))
            for level in range(len(mover.masks)):
                if 0 <= i - lag - level < len(items):
                    mover.finish(items[i - lag - level], level)
            if i in tasks:
                tasks[i]()
        for item in items:
            mover.complete(item)
        for copy in (own[2], own[5]):
            copy.wait_recv()
        for copy in outward:
            copy.wait()
        mover.close()

    row = (per, loc, width_here)
    pair_shape = (2,) + row
    vmem, anywhere = pl.BlockSpec(memory_space=pltpu.VMEM), pl.BlockSpec(memory_space=pl.ANY)
    outputs = [(pair_shape, BF16, anywhere)] * (n_ctx - 1) + [
        (row, BF16, anywhere),
        (pair_shape, BF16, anywhere),
        ((per, loc, 3 * NR), BF16, anywhere),
        ((width_here, wide), BF16, anywhere),
        ((wide, units), BF16, anywhere),
        ((units, wide), BF16, anywhere),
        (row, BF16, vmem),
        ((per, heads, 1, loc), F32, vmem),
        ((per, loc, wide), BF16, anywhere),
        ((per, loc, units), BF16, anywhere),
        ((per, loc, units), BF16, anywhere),
        ((per, loc, width), F32, anywhere),
        ((per, loc, 128), F32, vmem),
        ((per, loc, NR), BF16, vmem),
        ((per, loc, NR), BF16, vmem),
    ]
    return pl.pallas_call(
        kernel,
        in_specs=[vmem] * 7 + [anywhere] * 8,
        out_specs=[space for _, _, space in outputs],
        out_shape=[jax.ShapeDtypeStruct(shape, dtype) for shape, dtype, _ in outputs],
        scratch_shapes=[
            pltpu.SemaphoreType.DMA((n_copy,)),
            pltpu.SemaphoreType.DMA((n_copy,)),
            pltpu.SemaphoreType.DMA((9 * per,)),
            pltpu.SemaphoreType.DMA((n_ctx,)),
            pltpu.SemaphoreType.DMA((4,)),
            pltpu.VMEM((per * loc, wide_x), BF16),
            pltpu.VMEM((2, wide_x, tile), BF16),
            pltpu.VMEM((per * loc, 3 * width_here), BF16),
            pltpu.VMEM((n_ctx, 2, loc, width_here), BF16),
            pltpu.VMEM((width_here, wide), BF16),
            pltpu.VMEM((per, loc, wide), BF16),
            pltpu.VMEM((per, loc, wide), BF16),
            pltpu.VMEM((2, wide, tile), BF16),
            pltpu.VMEM((per, loc, wide), BF16),
            pltpu.VMEM((per, loc, width), F32),
            pltpu.VMEM((per, loc, units), BF16),
            pltpu.VMEM((per, loc, units), BF16),
        ],
        compiler_params=pltpu.CompilerParams(
            collective_id=1, has_side_effects=True, vmem_limit_bytes=60 << 20
        ),
    )(bias, a_qkv, picked, gain, shift_by, *first_maps, x_rows, qkv_x, w_out, w_up, w_down, *maps)


class Ring:
    def __init__(self, room, sems, at, tile_at):
        self.room, self.sems, self.at, self.tile_at = room, sems, at, tile_at

    def copy(self, t):
        slot = lax.rem(t, 2)
        return pltpu.make_async_copy(
            self.tile_at(t), self.room.at[slot], self.sems.at[self.at + slot]
        )

    def prefetch(self):
        self.copy(0).start()
        self.copy(1).start()

    def run(self, n, body, first=0, total=None):
        total = n if total is None else total

        def step(t, carry):
            self.copy(t).wait()
            body(t, self.room.at[lax.rem(t, 2)])

            @pl.when(t + 2 < total)
            def _():
                self.copy(t + 2).start()

            return carry

        lax.fori_loop(first, n, step, 0)


def compact(out_ref, n, entries, sizes, start=0):
    column = lax.broadcasted_iota(jnp.int32, (NR, RANK), 0)
    rank = lax.broadcasted_iota(jnp.int32, (NR, RANK), 1)
    used = jnp.where(lax.rem(column, RANK) == rank, 1.0, 0.0).astype(BF16)
    for (code, value), size in zip(entries, sizes):
        short = dot(code(), used).astype(BF16)
        block = dot_tn(short, value()).astype(BF16)
        for k in range(out_ref.shape[0]):
            out_ref[k, n * RANK : (n + 1) * RANK, start : start + size] = block[
                :, k * size : (k + 1) * size
            ]
        start += size


class Fold:
    def __init__(self, mover, parts, came, out_ref):
        self.mover, self.parts, self.came, self.out_ref = mover, parts, came, out_ref
        self.flying = {}

    def at(self, k):
        return flip(self.mover.ct, self.mover.offsets[k])

    def hand(self, level):
        half = 2**level
        self.flying[level] = [
            self.mover.go(
                self.parts.at[self.at(half + i)],
                self.came.at[half - 1 + i],
                {"ctx": flip(self.mover.ct, self.mover.masks[level])},
            )
            for i in range(half)
        ]

    def take(self, level):
        for i, copy in enumerate(self.flying[level]):
            copy.wait_recv()
            total = self.parts[self.at(i)].astype(F32) + self.came[2**level - 1 + i].astype(F32)
            self.parts[self.at(i)] = total.astype(BF16)

    def next(self, level):
        self.take(level)
        if level:
            self.hand(level - 1)

    def gather(self):
        own = self.parts.at[self.mover.ct]
        item = Weight(
            lambda c: self.parts.at[c], lambda o, c: self.out_ref.at[c, o], own, direct=True
        )
        self.mover.begin(item)
        return own, self.out_ref.at[self.mover.ct, self.mover.z], item


def norm_parts(values):
    center = values - jnp.mean(values, axis=-1, keepdims=True)
    rstd = lax.rsqrt(jnp.mean(center * center, axis=-1, keepdims=True) + NORM_EPS)
    return center * rstd, rstd


def norm_back(hat, rstd, dhat):
    first = jnp.mean(dhat, axis=-1, keepdims=True)
    second = jnp.mean(dhat * hat, axis=-1, keepdims=True)
    return rstd * (dhat - first - hat * second)


def gelu_both(pre):
    square = pre * pre
    bent = jnp.tanh(GELU_COEF * (pre + 0.044715 * square * pre))
    out = 0.5 * pre * (1.0 + bent)
    slope = 0.5 * (1.0 + bent) + 0.5 * pre * (1.0 - bent * bent) * GELU_COEF * (
        1.0 + 3.0 * 0.044715 * square
    )
    return out.astype(BF16), slope.astype(BF16)


def middle(hats, rstds, gelus, slopes, adapt_up, cot, picked, gain, shift_by, weights, maps, n_fsdp, n_ctx):
    per, loc, width = hats.shape
    piece = cot.shape[1]
    out_x, up_x, down_x = weights
    a_up, b_out, b_down, a_down, b_up = maps
    wide, units = up_x.shape
    width_here = out_x.shape[0]
    tile = 512
    chunk = 128
    n_wide = width // tile
    n_swap = n_wide + 1
    sizes = [width // n_ctx, units // n_ctx, units // n_ctx]

    def kernel(*refs):
        pick_ref, gain_ref, shift_ref, rstd1, code_up_ref = refs[:5]
        a_up_ref, b_out_ref, b_down_ref, a_down_ref, b_up_ref = refs[5:10]
        hat_ref, gelu_ref, slope_ref, cot_ref, out_ref, up_ref, down_ref = refs[10:17]
        acts_out, dy1_out, da_out, cot_rows, grads_part, back_out = refs[17:23]
        dadapt_up_ref, ctx_ref = refs[23:25]
        (send, recv, deal_send, deal_recv, ring_sem, sems) = refs[25:31]
        (down_room, down_rows, up_rows) = refs[31:34]
        (stage, part, got, hat1, keep32, slope, gelu, wide_v, turned, dpre_t) = refs[34:44]
        (codes_down,) = refs[44:]
        mover = Mover(n_fsdp, n_ctx, deal_send, deal_recv)
        partner = {"tp": 1 - lax.axis_index("tp")}

        down = Ring(down_room, ring_sem, 0, lambda t: down_ref.at[:, ds(t * tile, tile)])
        down_r = Ring(down_rows, ring_sem, 4, lambda t: down_ref.at[ds(t * tile, tile)])
        up_r = Ring(up_rows, ring_sem, 6, lambda t: up_ref.at[ds(t * tile, tile)])
        out_r = Ring(down_rows, ring_sem, 4, lambda t: out_ref.at[ds(t * tile, tile)])

        busy = {}
        used = [0]

        def move(source, target, key):
            copy = pltpu.make_async_copy(source, target, sems.at[used[0]])
            used[0] += 1
            copy.start()
            busy.setdefault(key, []).append(copy)

        def free(*keys):
            for key in keys:
                for copy in busy.pop(key, []):
                    copy.wait()

        def swap_copy(turn, g, t, size):
            at = ds(t * tile, size)
            sem = (turn * per + g) * n_swap + t
            return pltpu.make_async_remote_copy(
                src_ref=part.at[g, :, at],
                dst_ref=got.at[turn, g, :, at],
                send_sem=send.at[sem],
                recv_sem=recv.at[sem],
                device_id=partner,
                device_id_type=pl.DeviceIdType.MESH,
            )

        def swapped(turn, g):
            for t in range(n_swap):
                copy = swap_copy(turn, g, t, tile if t < n_wide else NR)
                copy.wait_recv()
                copy.wait_send()

        def by_rows(body):
            def step(r, carry):
                body(pl.ds(pl.multiple_of(r * chunk, chunk), chunk))
                return carry

            lax.fori_loop(0, loc // chunk, step, 0)

        def deal(g):
            return Deal(lambda to: cot_ref.at[to * per + g], lambda s: cot_rows.at[g, s])

        deals = [deal(g) for g in range(per)]
        dealt = []
        for g in range(per):
            move(gelu_ref.at[g], gelu.at[g], ("gelu", g))
            if g == 0:
                down.prefetch()
            move(cot_ref.at[mover.z * per + g], cot_rows.at[g, 0], ("cot", g))

        def load_rest(g):
            move(hat_ref.at[g], hat1.at[g], ("hat", g))
            move(slope_ref.at[g], slope.at[g], ("slope", g))

        mover.greet(tp=True)
        mover.begin(deals[0])

        for g in range(per):
            if g + 1 == per:
                down_r.prefetch()
            free(("gelu", g))

            def down_tile(t, room, g=g):
                part[g, :, ds(t * tile, tile)] = dot(gelu[g], room[...]).astype(BF16)
                swap_copy(0, g, t, tile).start()

            down.run(n_wide, down_tile)
            if g + 1 < per:
                down.prefetch()
            else:
                up_r.prefetch()
            part[g, :, width:] = dot(gelu[g], a_down_ref[...]).astype(BF16)
            swap_copy(0, g, n_wide, NR).start()

        load_rest(0)
        for g in range(per):
            mover.relay(deals[g])
            if g + 1 < per:
                mover.begin(deals[g + 1])
            free(("cot", g))
            for s in range(n_fsdp):
                at = pl.ds(s * cot.shape[1], cot.shape[1])
                move(cot_rows.at[g, s], stage.at[g, at], ("stage", g))
            swapped(0, g)
            free(("stage", g), ("hat", g), ("slope", g))
            pick = pick_ref[g]

            def second_norm(rows, g=g, pick=pick):
                total = part[g, rows, :].astype(F32) + got[0, g, rows, :].astype(F32)
                code = (total[:, width:] * pick).astype(BF16)
                codes_down[g, rows, :] = code
                hidden = hat1[g, rows, :] * gain_ref[0:1, :] + shift_ref[0:1, :]
                hat, rstd = norm_parts(hidden + total[:, :width] + dot(code, b_down_ref[...]))
                part[g, rows, :width] = (hat * gain_ref[1:2, :] + shift_ref[1:2, :]).astype(BF16)
                dy2 = norm_back(hat, rstd, stage[g, rows, :].astype(F32) * gain_ref[1:2, :])
                keep32[g, rows, :] = dy2
                low = dy2.astype(BF16)
                wide_v[g, rows, :width] = low
                wide_v[g, rows, width:] = (dot_nt(low, b_down_ref[...]) * pick).astype(BF16)

            if g + 1 < per:
                load_rest(g + 1)
            by_rows(second_norm)
            move(part.at[g, :, pl.ds(0, width)], acts_out.at[g], ("part", g))
            own = part.at[g, pl.ds(0, piece), pl.ds(0, width)]
            move(own, back_out.at[mover.z * per + g], ("part", g))
            turned[...] = wide_v[g].T

            def down_back(t, room, g=g):
                at = ds(t * tile, tile)
                block = dot(room[...], turned[...]).T
                low = (block * slope[g, :, at].astype(F32)).astype(BF16)
                slope[g, :, at] = low
                dpre_t[at, :] = low.T

            down_r.run(units // tile, down_back)
            (down_r if g + 1 < per else out_r).prefetch()
            free(("part", g))
            for s in range(1, n_fsdp):
                to = lax.rem(mover.z - s + n_fsdp, n_fsdp)
                rows_s = acts_out.at[g, pl.ds(s * piece, piece)]
                dealt.append(mover.go(rows_s, back_out.at[mover.z * per + g], {"fsdp": to}))

            def up_back(t, room, g=g):
                part[g, :, ds(t * tile, tile)] = dot(room[...], dpre_t[...]).T.astype(BF16)
                swap_copy(1, g, t, tile).start()

            up_r.run(n_wide, up_back)
            if g + 1 < per:
                up_r.prefetch()
            part[g, :, width:] = dot(b_up_ref[...], dpre_t[...]).T.astype(BF16)
            swap_copy(1, g, n_wide, NR).start()

        for g in range(per):
            entries = [
                (lambda g=g: codes_down[g], lambda g=g: wide_v[g, :, :width]),
                (lambda g=g: wide_v[g, :, width:], lambda g=g: gelu[g]),
                (lambda g=g: code_up_ref[g], lambda g=g: slope[g]),
            ]
            compact(grads_part, g, entries, sizes)
        for g in range(per):
            swapped(1, g)
            pick = pick_ref[g]

            def first_back(rows, g=g, pick=pick):
                total = part[g, rows, :].astype(F32) + got[1, g, rows, :].astype(F32)
                code = (total[:, width:] * pick).astype(BF16)
                dadapt_up_ref[g, rows, :] = code
                dh1 = keep32[g, rows, :] + total[:, :width] + dot_nt(code, a_up_ref[...])
                rstd = rstd1[g, rows, 0:1]
                dy1 = norm_back(hat1[g, rows, :], rstd, dh1 * gain_ref[0:1, :])
                keep32[g, rows, :] = dy1
                low = dy1.astype(BF16)
                wide_v[g, rows, :width] = low
                wide_v[g, rows, width:] = (dot_nt(low, b_out_ref[...]) * pick).astype(BF16)

            by_rows(first_back)
            move(keep32.at[g], dy1_out.at[g], "dy1")
            move(wide_v.at[g], da_out.at[g], "wide")
            turned[...] = wide_v[g].T

            def out_back(t, room, g=g):
                ctx_ref[g, :, ds(t * tile, tile)] = dot(room[...], turned[...]).T.astype(BF16)

            out_r.run(width_here // tile, out_back)
            if g + 1 < per:
                out_r.prefetch()
        for copy in dealt:
            copy.wait_recv()
        free(*list(busy))
        mover.close()

    vmem, anywhere = pl.BlockSpec(memory_space=pltpu.VMEM), pl.BlockSpec(memory_space=pl.ANY)
    row = (per, loc)
    grads_shape = (n_ctx, per * RANK, sum(sizes))
    outputs = [
        (row + (width,), BF16, anywhere),
        (row + (width,), F32, anywhere),
        (row + (wide,), BF16, anywhere),
        ((per, n_fsdp) + cot.shape[1:], BF16, anywhere),
        (grads_shape, BF16, vmem),
        (cot.shape, BF16, anywhere),
        (row + (NR,), BF16, vmem),
        (row + (width_here,), BF16, vmem),
    ]
    n_copy = 2 * per * n_swap
    n_deal = 2 * per * (n_fsdp - 1)
    return pl.pallas_call(
        kernel,
        in_specs=[vmem] * 10 + [anywhere] * 7,
        out_specs=[space for _, _, space in outputs],
        out_shape=[jax.ShapeDtypeStruct(shape, dtype) for shape, dtype, _ in outputs],
        scratch_shapes=[
            pltpu.SemaphoreType.DMA((n_copy,)),
            pltpu.SemaphoreType.DMA((n_copy,)),
            pltpu.SemaphoreType.DMA((n_deal,)),
            pltpu.SemaphoreType.DMA((n_deal,)),
            pltpu.SemaphoreType.DMA((8,)),
            pltpu.SemaphoreType.DMA(((8 + n_fsdp) * per,)),
            pltpu.VMEM((2, units, tile), BF16),
            pltpu.VMEM((2, tile, wide), BF16),
            pltpu.VMEM((2, tile, units), BF16),
            pltpu.VMEM(row + (width,), BF16),
            pltpu.VMEM(row + (wide,), BF16),
            pltpu.VMEM((2,) + row + (wide,), BF16),
            pltpu.VMEM(row + (width,), F32),
            pltpu.VMEM(row + (width,), F32),
            pltpu.VMEM(row + (units,), BF16),
            pltpu.VMEM(row + (units,), BF16),
            pltpu.VMEM(row + (wide,), BF16),
            pltpu.VMEM((wide, loc), BF16),
            pltpu.VMEM((units, loc), BF16),
            pltpu.VMEM(row + (NR,), BF16),
        ],
        compiler_params=pltpu.CompilerParams(
            collective_id=3, has_side_effects=True, vmem_limit_bytes=62 << 20
        ),
    )(
        picked, gain, shift_by, rstds, adapt_up, a_up, b_out, b_down, a_down, b_up,
        hats, gelus, slopes, cot, out_x, up_x, down_x,
    )


def combine(pieces, chosen, shapes):
    n_part, n_fsdp, rows, columns = pieces.shape
    flat, specs = [], []
    for i, shape in enumerate(shapes):
        high, wide = shape[-2:]
        tall = wide == NR and high != NR
        size = (high if tall else wide) // n_part
        block = (size, NR) if tall else (NR, size)
        lead = shape[0] if len(shape) == 3 else None
        for j in range(lead or 1):
            flat.append((i, None if lead is None else j, tall, size))
        if lead is None:
            specs.append(pl.BlockSpec(block, (lambda c: (c, 0)) if tall else (lambda c: (0, c))))
        else:
            specs.append(
                pl.BlockSpec(
                    (lead,) + block, (lambda c: (0, c, 0)) if tall else (lambda c: (0, 0, c))
                )
            )

    def kernel(chosen_ref, piece_ref, *outs):
        ordered = jnp.concatenate([piece_ref[0, a] for a in range(n_fsdp)], axis=0)
        start = 0
        for i, lead, tall, size in flat:
            block = ordered[:, start : start + size]
            value = dot_tn(block, chosen_ref[...]) if tall else dot_tn(chosen_ref[...], block)
            if lead is None:
                outs[i][...] = value
            else:
                outs[i][lead] = value
            start += size

    return pl.pallas_call(
        kernel,
        grid=(n_part,),
        in_specs=[
            pl.BlockSpec(chosen.shape, lambda c: (0, 0)),
            pl.BlockSpec((1, n_fsdp, rows, columns), lambda c: (c, 0, 0, 0)),
        ],
        out_specs=specs,
        out_shape=[jax.ShapeDtypeStruct(shape, F32) for shape in shapes],
        compiler_params=pltpu.CompilerParams(vmem_limit_bytes=48 << 20),
    )(chosen, pieces)


def finish(
    query, kv_own, slots, bias, grad, log_total, x_rows, adapt_in, dy1, qkv_x, a_qkv, picked, grads, early, pairs, n_fsdp, n_ctx
):
    per, loc, width_here = query.shape
    piece, width = loc // n_fsdp, x_rows.shape[2]
    heads = width_here // HEAD_DIM
    cuts = 4
    high = heads // cuts
    columns = high * HEAD_DIM
    masks = masks_of(n_ctx)
    units = [(g, c) for g in range(per) for c in range(cuts)]
    depth = 3 * width_here
    foot = 3 * NR
    wide = width + foot
    tile = 512
    n_wide = width // tile
    n_swap = n_wide + 1
    n_early = len(early)
    early_sizes = [values[2] // n_ctx for _, values in pairs]
    before = grads.shape[2]
    late_sizes = [width_here // n_ctx] * 3 + [width // n_ctx] * 3
    n_copy = len(units) * (n_ctx - 1) + per * n_wide * (n_fsdp - 1)
    n_copy += 2 * ((n_fsdp - 1) * n_ctx + 2 * (n_ctx - 1))

    def kernel(*refs):
        q_ref, bias_ref, g_ref, log_ref, x_ref, adapt_ref, a_ref, pick_ref = refs[:8]
        dy1_ref, w_ref, grads_ref, kv_ref = refs[8:12]
        slot_refs = refs[12 : 11 + n_ctx]
        early_refs = refs[11 + n_ctx : 11 + n_ctx + n_early]
        at = 11 + n_ctx + n_early
        in_ref, early_out, late_out = refs[at : at + 3]
        send, recv, swap_send, swap_recv, ring_sem, load, sems = refs[at + 3 : at + 10]
        kv_room, own, came, dq, dkv = refs[at + 10 : at + 15]
        tiles, foot_room, dy1_room, turned, part, got, codes_in = refs[at + 15 : at + 22]
        early_part, early_came, late_part, late_came = refs[at + 22 : at + 26]
        staged = refs[at + 26 :]
        mover = Mover(n_fsdp, n_ctx, send, recv)
        z, ct = mover.z, mover.ct
        partner = {"tp": 1 - lax.axis_index("tp")}
        ring = Ring(tiles, ring_sem, 0, lambda t: w_ref.at[ds(t * tile, tile)])
        used = [0]
        kept, dealt, flying = [], [], {}

        def move(source, target):
            copy = pltpu.make_async_copy(source, target, sems.at[used[0]])
            used[0] += 1
            copy.start()
            return copy

        loads = []
        for g in range(per):
            loads.append([])
            for k in range(n_ctx):
                source = kv_ref if k == 0 else slot_refs[k - 1]
                copy = pltpu.make_async_copy(
                    source.at[:, g], kv_room.at[g, k], load.at[g * n_ctx + k]
                )
                if g == 0:
                    copy.start()
                loads[g].append(copy)
        mover.greet(tp=True)
        for copy in loads[0]:
            copy.wait()
        staging = [move(ref, room) for ref, room in zip(early_refs, staged)]
        staging.append(move(grads_ref, early_part.at[:, :, pl.ds(0, before)]))
        for group in loads[1:]:
            for copy in group:
                copy.start()
        load_foot = move(w_ref.at[pl.ds(width, foot)], foot_room)
        ring.prefetch()
        load_dy1 = move(dy1_ref, dy1_room)

        def compute(u):
            g, c = units[u]
            if c == 0 and g:
                for copy in loads[g]:
                    copy.wait()

            def one(h, carry):
                at = ds(c * columns + h * HEAD_DIM, HEAD_DIM)
                to = ds(h * HEAD_DIM, HEAD_DIM)
                biases = []
                for k in range(n_ctx):
                    block = bias_ref[g, k * loc : (k + 1) * loc, :]
                    biases.append(jnp.concatenate([block] * (loc // 128), axis=1))
                dquery, dkeys, dvalues = attend_back_head(
                    q_ref[g, :, at],
                    g_ref[g, :, at],
                    log_ref[g, c * high + h],
                    [kv_room[g, k, 0, :, at] for k in range(n_ctx)],
                    [kv_room[g, k, 1, :, at] for k in range(n_ctx)],
                    biases,
                )
                dq[g, :, at] = dquery
                for k in range(n_ctx):
                    own[u, k, 0, :, to] = dkeys[k]
                    own[u, k, 1, :, to] = dvalues[k]
                return carry

            for h in range(high):
                one(h, 0)

        def hand(u, level):
            half = 2**level
            device = {"ctx": flip(ct, masks[level])}
            flying[u, level] = [
                mover.go(own.at[u, half + i], came.at[u, half - 1 + i], device) for i in range(half)
            ]

        def take_in(u, level):
            half = 2**level
            g, c = units[u]
            for i, copy in enumerate(flying[u, level]):
                copy.wait_recv()
                for j in range(2):
                    total = own[u, i, j].astype(F32) + came[u, half - 1 + i, j].astype(F32)
                    if level:
                        own[u, i, j] = total.astype(BF16)
                    else:
                        dkv[j, g, :, c * columns : (c + 1) * columns] = total.astype(BF16)
            if level:
                hand(u, level - 1)

        def swap_copy(g, t):
            at = pl.ds(width, foot) if isinstance(t, int) and t == n_wide else ds(t * tile, tile)
            sem = g * n_swap + t
            return pltpu.make_async_remote_copy(
                src_ref=part.at[g, :, at],
                dst_ref=got.at[g, :, at],
                send_sem=swap_send.at[sem],
                recv_sem=swap_recv.at[sem],
                device_id=partner,
                device_id_type=pl.DeviceIdType.MESH,
            )

        def project_back(g):
            turned[0:width_here, :] = dq[g].T
            turned[width_here : 2 * width_here, :] = dkv[0, g].T
            turned[2 * width_here :, :] = dkv[1, g].T
            if g == 0:
                load_foot.wait()
            part[g, :, width:] = dot(foot_room[...], turned[...]).T.astype(BF16)
            swap_copy(g, n_wide).start()

            def back(t, room):
                part[g, :, ds(t * tile, tile)] = dot(room[...], turned[...]).T.astype(BF16)
                swap_copy(g, t).start()

            ring.run(n_wide, back)
            if g + 1 < per:
                ring.prefetch()

        def take_codes(g):
            swap_copy(g, n_wide).wait_recv()
            pick = jnp.concatenate([pick_ref[g]] * 3, axis=1)
            total = part[g, :, width:].astype(F32) + got[g, :, width:].astype(F32)
            codes_in[g] = (total * pick).astype(BF16)

        def finish_tile(g, t):
            swap_copy(g, t).wait_recv()
            swap_copy(g, t).wait_send()
            at = slice(t * tile, (t + 1) * tile)
            value = part[g, :, at].astype(F32) + got[g, :, at].astype(F32) + dy1_room[g, :, at]
            for j in range(3):
                value = value + dot_nt(codes_in[g, :, j * NR : (j + 1) * NR], a_ref[j, at, :])
            part[g, :, at] = value.astype(BF16)
            to_at = pl.ds(t * tile, tile)
            kept.append(move(part.at[g, pl.ds(0, piece), to_at], in_ref.at[z * per + g, :, to_at]))
            for s in range(1, n_fsdp):
                to = lax.rem(z - s + n_fsdp, n_fsdp)
                dealt.append(
                    mover.go(
                        part.at[g, pl.ds(s * piece, piece), to_at],
                        in_ref.at[z * per + g, :, to_at],
                        {"fsdp": to},
                    )
                )

        early_fold = Fold(mover, early_part, early_came, early_out)
        late_fold = Fold(mover, late_part, late_came, late_out)

        def known():
            for copy in staging:
                copy.wait()
            for n in range(per):
                entries = []
                for (i, first, size), (j, start, count) in pairs:
                    entries.append(
                        (
                            lambda n=n, i=i, f=first, c=size: staged[i][n, :, f : f + c],
                            lambda n=n, i=j, f=start, c=count: staged[i][n, :, f : f + c],
                        )
                    )
                compact(early_part, n, entries, early_sizes, before)
            early_fold.hand(last)

        last = len(masks) - 1
        for t in range(len(units) + last):
            if t < len(units):
                compute(t)
                hand(t, last)
            for k in range(last):
                if 0 <= t - 1 - k < len(units):
                    take_in(t - 1 - k, last - k)
            if t == 1:
                known()
            if t == 3:
                for level in range(last, 0, -1):
                    early_fold.next(level)
            if t == 6:
                early_fold.next(0)
                source, target, first = early_fold.gather()
                kept.append(move(source, target))
        done = set()
        for g in range(per):
            for u, (owner, _) in enumerate(units):
                if owner == g:
                    take_in(u, 0)
            if g + 1 == per:
                mover.relay(first)
            project_back(g)
            take_codes(g)
            if g == 0:
                load_dy1.wait()
            if g + 1 < per:
                for t in range(n_wide - 1):
                    finish_tile(g, t)
                    done.add((g, t))
        for n in range(per):
            values = [
                lambda n=n: dq[n],
                lambda n=n: dkv[0, n],
                lambda n=n: dkv[1, n],
            ]
            entries = [
                (lambda n=n, j=j: adapt_ref[n, :, j * NR : (j + 1) * NR], values[j]) for j in range(3)
            ]
            entries += [
                (lambda n=n, j=j: codes_in[n, :, j * NR : (j + 1) * NR], lambda n=n: x_ref[n])
                for j in range(3)
            ]
            compact(late_part, n, entries, late_sizes)
        late_fold.hand(last)
        rest = [(g, t) for g in range(per) for t in range(n_wide) if (g, t) not in done]
        for i, (g, t) in enumerate(rest):
            finish_tile(g, t)
            if i == 0:
                for level in range(last, 0, -1):
                    late_fold.next(level)
            if i == 1:
                late_fold.next(0)
                source, target, second = late_fold.gather()
                kept.append(move(source, target))
            if i == len(rest) - 3:
                mover.complete(first)
            if i == len(rest) - 2:
                mover.relay(second)
        mover.complete(second)
        for g in range(per):
            swap_copy(g, n_wide).wait_send()
        for copy in dealt:
            copy.wait_recv()
        for copy in kept:
            copy.wait()
        mover.close()

    vmem, anywhere = pl.BlockSpec(memory_space=pltpu.VMEM), pl.BlockSpec(memory_space=pl.ANY)
    parts = [(n_ctx, per * RANK, before + sum(early_sizes)), (n_ctx, per * RANK, sum(late_sizes))]
    row = (per, loc)
    rooms = [
        ((per, n_ctx, 2, loc, width_here), BF16),
        ((len(units), n_ctx, 2, loc, columns), BF16),
        ((len(units), n_ctx - 1, 2, loc, columns), BF16),
        (row + (width_here,), BF16),
        ((2,) + row + (width_here,), BF16),
        ((2, tile, depth), BF16),
        ((foot, depth), BF16),
        (dy1.shape, F32),
        ((depth, loc), BF16),
        (row + (wide,), BF16),
        (row + (wide,), BF16),
        (row + (foot,), BF16),
    ]
    for shape in parts:
        rooms += [(shape, BF16), ((n_ctx - 1,) + shape[1:], BF16)]
    rooms += [(x.shape, BF16) for x in early]
    return pl.pallas_call(
        kernel,
        in_specs=[vmem] * 8 + [anywhere] * (3 + n_ctx + n_early),
        out_specs=[anywhere] * 3,
        out_shape=[jax.ShapeDtypeStruct((per * n_fsdp, piece, width), BF16)]
        + [jax.ShapeDtypeStruct((n_ctx, n_fsdp) + shape[1:], BF16) for shape in parts],
        scratch_shapes=[
            pltpu.SemaphoreType.DMA((n_copy,)),
            pltpu.SemaphoreType.DMA((n_copy,)),
            pltpu.SemaphoreType.DMA((per * n_swap,)),
            pltpu.SemaphoreType.DMA((per * n_swap,)),
            pltpu.SemaphoreType.DMA((2,)),
            pltpu.SemaphoreType.DMA((per * n_ctx,)),
            pltpu.SemaphoreType.DMA((5 + n_early + per * n_wide,)),
        ]
        + [pltpu.VMEM(shape, dtype) for shape, dtype in rooms],
        compiler_params=pltpu.CompilerParams(
            collective_id=4, has_side_effects=True, vmem_limit_bytes=63 << 20
        ),
    )(
        query, bias, grad, log_total, x_rows, adapt_in, a_qkv, picked, dy1, qkv_x, grads, kv_own, *slots, *early,
    )


def gelu_both(pre):
    square = pre * pre
    bent = jnp.tanh(GELU_COEF * (pre + 0.044715 * square * pre))
    out = 0.5 * pre * (1.0 + bent)
    slope = 0.5 * (1.0 + bent) + 0.5 * pre * (1.0 - bent * bent) * GELU_COEF * (
        1.0 + 3.0 * 0.044715 * square
    )
    return out.astype(BF16), slope.astype(BF16)


def local(
    x_in,
    cotangent,
    lengths,
    adapter_ids,
    w_qkv,
    w_out,
    w_up,
    w_down,
    ln_gain,
    ln_bias,
    a_qkv,
    b_qkv,
    a_out,
    b_out,
    a_up,
    b_up,
    a_down,
    b_down,
):
    n_ctx, n_fsdp = lax.axis_size("ctx"), lax.axis_size("fsdp")
    z, ct = lax.axis_index("fsdp"), lax.axis_index("ctx")
    seqs, piece, width = x_in.shape
    per = seqs // n_fsdp
    loc = n_fsdp * piece
    heads_width = w_qkv.shape[2]
    def take(array, start, size, axis=0):
        return lax.dynamic_slice_in_dim(array, start, size, axis)

    units = w_up.shape[1]
    rows_shape = (per, n_fsdp, piece, width)
    zq = w_qkv.shape[1]

    def first_items(ins, outs, z):
        x_ref, w_ref = ins
        rows_ref, whole_ref = outs

        def deal(g):
            return Deal(lambda to: x_ref.at[to * per + g], lambda s: rows_ref.at[g, s])

        def weight(j):
            size = zq // n_ctx
            columns = pl.ds(j * heads_width, heads_width)
            return Weight(
                lambda c: w_ref.at[j, pl.ds(pl.multiple_of(c * size, size), size)],
                lambda o, c: whole_ref.at[
                    pl.ds(pl.multiple_of(o * zq + c * size, size), size), columns
                ],
            )

        stay = [(x_ref.at[z * per + g], rows_ref.at[g, 0]) for g in range(per)]
        for j in range(3):
            own = whole_ref.at[
                pl.ds(pl.multiple_of(z * zq, zq), zq), pl.ds(j * heads_width, heads_width)
            ]
            stay.append((w_ref.at[j], own))
        items = [weight(j) for j in range(3)] + [deal(g) for g in range(per)]
        return items, stay

    x_all, qkv_x = move(
        first_items,
        [Weight] * 3 + [Deal] * per,
        (x_in, w_qkv),
        (rows_shape, (width + 3 * NR, 3 * heads_width)),
        n_fsdp,
        n_ctx,
        ((piece, width),) * per + (w_qkv.shape[1:],) * 3,
        0,
        foot=(b_qkv, lambda outs: outs[1].at[pl.ds(width, 3 * NR)]),
    )

    my_lengths = take(lengths, z * per, per)
    my_ids = take(adapter_ids, z * per, per)
    picked = (my_ids[:, None] == jnp.arange(NR)[None, :] // RANK).astype(F32)
    steps = lax.rem(z - jnp.arange(n_fsdp) + n_fsdp, n_fsdp)
    ctx_of = ct ^ jnp.array(offsets(n_ctx))
    key_pos = (
        (steps[None, :, None] * n_ctx + ctx_of[:, None, None]) * piece
        + jnp.arange(piece)[None, None, :]
    ).reshape(-1)
    bias_all = jnp.where(key_pos[None, :] < my_lengths[:, None], 0.0, -1e30).astype(F32)
    bias_all = jnp.broadcast_to(bias_all[:, :, None], bias_all.shape + (128,))

    picked = picked[:, None, :]
    x_rows = x_all.reshape(per, loc, width)
    moved = forward_and_gather(
        x_rows, qkv_x, a_qkv, picked, bias_all, ln_gain, ln_bias, (a_up, b_out), (w_out, w_up, w_down),
        (a_out, b_up, a_down), n_fsdp, n_ctx,
    )
    slots = moved[: n_ctx - 1]
    (
        query, kv_own, adapt_all, out_x, up_x, down_x, context, log_total, wide_h, gelus, slopes, hats, rstds,
        adapt_out, adapt_up,
    ) = moved[n_ctx - 1 :]
    _, dy1, wide_a, _, grads, activations, dadapt_up, d_context = middle(
        hats, rstds, gelus, slopes, adapt_up, cotangent, picked, ln_gain, ln_bias, (out_x, up_x, down_x),
        (a_up, b_out, b_down, a_down, b_up), n_fsdp, n_ctx,
    )
    early_in = (dadapt_up, wide_h, adapt_out, wide_a, context)
    early_pairs = [
        ((0, 0, NR), (1, 0, width)),
        ((2, 0, NR), (3, 0, width)),
        ((3, width, NR), (4, 0, heads_width)),
    ]
    input_grad, early, late = finish(
        query, kv_own, slots, bias_all, d_context, log_total, x_rows, adapt_all, dy1, qkv_x, a_qkv, picked,
        grads, early_in, early_pairs, n_fsdp, n_ctx,
    )

    codes = (adapter_ids[:, None] * RANK + jnp.arange(RANK)[None, :]).reshape(-1)
    chosen = (codes[:, None] == jnp.arange(NR)[None, :]).astype(BF16)
    b_down_grad, a_down_grad, b_up_grad, a_up_grad, b_out_grad, a_out_grad = combine(
        early,
        chosen,
        [(NR, width), (units, NR), (NR, units), (width, NR), (NR, width), (heads_width, NR)],
    )
    b_qkv_grad, a_qkv_grad = combine(late, chosen, [(3, NR, heads_width), (3, width, NR)])
    return (
        activations, input_grad, a_qkv_grad, b_qkv_grad, a_out_grad, b_out_grad, a_up_grad, b_up_grad,
        a_down_grad, b_down_grad,
    )


def solution(mesh):
    rows = P(None, ("fsdp", "ctx"), None)
    return jax.shard_map(
        local,
        mesh=mesh,
        in_specs=(
            rows,
            rows,
            P(),
            P(),
            P(None, "fsdp", "tp"),
            P("tp", "fsdp"),
            P("fsdp", "tp"),
            P("tp", "fsdp"),
            P(),
            P(),
            P(),
            P(None, None, "tp"),
            P("tp", None),
            P(),
            P(),
            P(None, "tp"),
            P("tp", None),
            P(),
        ),
        out_specs=(
            rows,
            rows,
            P(),
            P(None, None, "tp"),
            P("tp", None),
            P(),
            P(),
            P(None, "tp"),
            P("tp", None),
            P(),
        ),
        check_vma=False,
    )
```

```python
import math

import jax
import jax.numpy as jnp
from jax import lax
from jax.experimental import pallas as pl
from jax.experimental.pallas import tpu as pltpu
from jax.sharding import PartitionSpec as P

HEAD_DIM = 128
RANK = 16
ADAPTERS = 8
NR = RANK * ADAPTERS
NORM_EPS = 1e-06
GELU_COEF = 0.7978845608028654
SCALE = 1.0 / math.sqrt(HEAD_DIM)
F32 = jnp.float32
BF16 = jnp.bfloat16


def dot(left, right):
    return jnp.dot(left, right, preferred_element_type=F32)


def dot_nt(left, right):
    return lax.dot_general(left, right, (((1,), (1,)), ((), ())), preferred_element_type=F32)


def dot_tn(left, right):
    return lax.dot_general(left, right, (((0,), (0,)), ((), ())), preferred_element_type=F32)


def masks_of(n):
    out = []
    while n > 1:
        n //= 2
        out.append(n)
    return out


def offsets(n):
    out = [0]
    for mask in masks_of(n):
        out = out + [o ^ mask for o in out]
    return out


def attend_head(query, keys, values, biases):
    scores = [dot_nt(k, query) * SCALE + bias for k, bias in zip(keys, biases)]
    top = scores[0].max(axis=0, keepdims=True)
    for s in scores[1:]:
        top = jnp.maximum(top, s.max(axis=0, keepdims=True))
    total = jnp.zeros_like(top)
    mixed = None
    for s, v in zip(scores, values):
        probs = jnp.exp(s - top)
        total = total + probs.sum(axis=0, keepdims=True)
        term = dot_tn(v, probs.astype(BF16))
        mixed = term if mixed is None else mixed + term
    return (mixed / total).T.astype(BF16), top + jnp.log(total)


def attend_back_head(query, grad, log_total, keys, values, biases):
    probs, dprobs, dvalues = [], [], []
    delta = jnp.zeros_like(log_total)
    for k, v, bias in zip(keys, values, biases):
        p = jnp.exp(dot_nt(k, query) * SCALE + bias - log_total)
        dp = dot_nt(v, grad)
        dvalues.append(dot(p.astype(BF16), grad).astype(BF16))
        delta = delta + (p * dp).sum(axis=0, keepdims=True)
        probs.append(p)
        dprobs.append(dp)
    dquery, dkeys = None, []
    for k, p, dp in zip(keys, probs, dprobs):
        ds = (p * (dp - delta)).astype(BF16)
        dkeys.append((dot(ds, query) * SCALE).astype(BF16))
        term = dot_tn(k, ds)
        dquery = term if dquery is None else dquery + term
    return (dquery * SCALE).T.astype(BF16), dkeys, dvalues


def ds(start, size):
    return pl.ds(pl.multiple_of(start, size), size)


def flip(ct, offset):
    mask = 1
    while mask <= offset:
        if offset & mask:
            ct = ct + mask - 2 * mask * lax.rem(ct // mask, 2)
        mask *= 2
    return ct


class Weight:
    def __init__(self, shard_at, whole_at, own=None, skip=0, direct=False):
        self.shard_at, self.whole_at, self.own, self.skip = shard_at, whole_at, own, skip
        self.direct = direct


class Deal:
    def __init__(self, source_at, rows_at):
        self.source_at, self.rows_at = source_at, rows_at


class Pair:
    def __init__(self, slot_at):
        self.slot_at = slot_at


class Mover:
    def __init__(self, n_fsdp, n_ctx, send, recv):
        self.n_fsdp, self.n_ctx = n_fsdp, n_ctx
        self.z, self.ct = lax.axis_index("fsdp"), lax.axis_index("ctx")
        self.send, self.recv = send, recv
        self.used = 0
        self.open = []
        self.masks = masks_of(n_ctx)
        self.offsets = offsets(n_ctx)
        self.came, self.waiting, self.done = {}, {}, {}

    def skip(self, item):
        return item.skip if isinstance(item, Weight) else 0

    def part(self, item):
        return lax.rem(self.ct, self.n_ctx >> item.skip) if item.skip else self.ct

    def greet(self, tp=False):
        barrier = pltpu.get_barrier_semaphore()
        others = [{"fsdp": lax.rem(self.z + s, self.n_fsdp)} for s in range(1, self.n_fsdp)]
        others += [{"ctx": flip(self.ct, mask)} for mask in self.masks]
        if tp:
            others.append({"tp": 1 - lax.axis_index("tp")})
        for other in others:
            pl.semaphore_signal(
                barrier, inc=1, device_id=other, device_id_type=pl.DeviceIdType.MESH
            )
        pl.semaphore_wait(barrier, len(others))

    def copy(self, source, target, device, at=None):
        if at is None:
            at = self.used
            self.used += 1
        return pltpu.make_async_remote_copy(
            src_ref=source,
            dst_ref=target,
            send_sem=self.send.at[at],
            recv_sem=self.recv.at[at],
            device_id=device,
            device_id_type=pl.DeviceIdType.MESH,
        )

    def go(self, source, target, device):
        copy = self.copy(source, target, device)
        copy.start()
        self.open.append((None, copy))
        return copy

    def along(self, item, owner, right, ok, source, slot):
        target = item.whole_at(owner, self.part(item))
        device = {"fsdp": lax.rem(self.z + (1 if right else self.n_fsdp - 1), self.n_fsdp)}
        copy = self.copy(source, target, device, self.came[item] + slot - 1)
        pl.when(ok)(copy.start)
        self.open.append((ok, copy))

    def begin(self, item):
        if isinstance(item, Pair):
            self.waiting[item] = [[] for _ in self.masks]
            self.cast(item, item.slot_at, lambda k, level: item.slot_at(k + 2**level), 0, 0)
            return
        if isinstance(item, Weight) and item.direct:
            part = self.part(item)
            self.came[item] = [
                self.go(
                    item.shard_at(part),
                    item.whole_at(self.z, part),
                    {"fsdp": lax.rem(self.z + s, self.n_fsdp)},
                )
                for s in range(1, self.n_fsdp)
            ]
            return
        if isinstance(item, Weight):
            self.came[item] = self.used
            self.used += self.n_fsdp - 1
            source = item.shard_at(self.part(item))
            self.along(item, self.z, True, self.z < self.n_fsdp - 1, source, 1)
            self.along(item, self.z, False, self.z > 0, source, self.n_fsdp - 1)
            return
        self.came[item] = [
            self.go(
                item.source_at(lax.rem(self.z + s, self.n_fsdp)),
                item.rows_at(s),
                {"fsdp": lax.rem(self.z + s, self.n_fsdp)},
            )
            for s in range(1, self.n_fsdp)
        ]

    def cast(self, item, source_at, target_at, k, first):
        skip = self.skip(item)
        for level in range(first, len(self.masks) - skip):
            device = {"ctx": flip(self.ct, self.masks[level + skip])}
            copy = self.go(source_at(k), target_at(k, level), device)
            self.waiting[item][level].append((copy, k + 2**level, source_at, target_at))

    def relay(self, item):
        if isinstance(item, Deal):
            for copy in self.came[item]:
                copy.wait_recv()
            return
        self.waiting[item] = [[] for _ in self.masks[item.skip :]]
        n, part = self.n_fsdp, self.part(item)
        others = offsets(self.n_ctx >> item.skip)
        if item.own is not None:

            def mine(k):
                return item.own if k == 0 else item.whole_at(self.z, flip(part, others[k]))

            def lands(k, level):
                return item.whole_at(self.z, flip(part, others[k]))

            self.cast(item, mine, lands, 0, 0)
        for i in range(n - 1):
            s = i // 2 + 1 if i % 2 == 0 else n - 1 - i // 2
            owner = lax.rem(self.z - s + n, n)
            here = item.whole_at(owner, part)
            if item.direct:
                self.came[item][s - 1].wait_recv()
            else:
                self.copy(here, here, {"fsdp": owner}, self.came[item] + s - 1).wait_recv()
                if s < n - 1:
                    ok = (self.z >= s) & (self.z < n - 1)
                    self.along(item, owner, True, ok, here, s + 1)
                if s > 1:
                    ok = (self.z < s) & (self.z > 0)
                    self.along(item, owner, False, ok, here, s - 1)

            def at(k, owner=owner):
                return item.whole_at(owner, flip(part, others[k]))

            self.cast(item, at, lambda k, level, at=at: at(k), 0, 0)

    def finish(self, item, level):
        if isinstance(item, Deal) or level != self.done.get(item, 0):
            return
        if level == len(self.waiting[item]):
            return
        for copy, k, source_at, target_at in self.waiting[item][level]:
            copy.wait_recv()
            self.cast(item, source_at, target_at, k, level + 1)
        self.done[item] = level + 1

    def complete(self, item):
        while self.done.get(item, 0) < len(self.waiting[item]):
            self.finish(item, self.done.get(item, 0))

    def close(self):
        for ok, copy in self.open:
            if ok is None:
                copy.wait_send()
            else:
                pl.when(ok)(copy.wait_send)


def copies_of(items, n_fsdp, n_ctx):
    total = 0
    for item in items:
        total += {Weight: (n_fsdp - 1) * n_ctx, Deal: n_fsdp - 1, Pair: n_ctx - 1}[item]
    return total


def keep(stay, room, sems):
    out = []
    for k, (source, target) in enumerate(stay):
        first = pltpu.make_async_copy(source, room[k], sems.at[2 * k])
        first.start()
        out.append((first, pltpu.make_async_copy(room[k], target, sems.at[2 * k + 1])))
    return out


def move(make, kinds, inputs, outputs, n_fsdp, n_ctx, local_shapes, ident, ahead=2, foot=None):
    n_in = len(inputs)
    n_copy = copies_of(kinds, n_fsdp, n_ctx)

    def kernel(*refs):
        ins, outs = refs[:n_in], refs[n_in : n_in + len(outputs)]
        send, recv, here = refs[n_in + len(outputs) : n_in + len(outputs) + 3]
        room = refs[n_in + len(outputs) + 3 :]
        if foot is not None:
            blocks_ref, ins = ins[-1], ins[:-1]
            strip = room[-1]
        mover = Mover(n_fsdp, n_ctx, send, recv)
        items, stay = make(ins, outs, mover.z)
        mover.greet()
        for item in items[:ahead]:
            mover.begin(item)
        kept = keep(stay, room, here)
        levels = len(mover.masks)
        for i in range(len(items) + levels):
            if i < len(items):
                mover.relay(items[i])
                if i + ahead < len(items):
                    mover.begin(items[i + ahead])
            if i == 0 and foot is not None:
                strip[...] = jnp.zeros_like(strip)
                high, wide = blocks_ref.shape[1:]
                for j in range(blocks_ref.shape[0]):
                    strip[j * high : (j + 1) * high, j * wide : (j + 1) * wide] = blocks_ref[j]
                set_foot = pltpu.make_async_copy(strip, foot[1](outs), here.at[2 * len(local_shapes)])
                set_foot.start()
                kept.append((None, set_foot))
            if i == 0:
                for first, second in kept:
                    if first is not None:
                        first.wait()
                        second.start()
            for level in range(levels):
                if 0 <= i - 1 - level < len(items):
                    mover.finish(items[i - 1 - level], level)
        for _, second in kept:
            second.wait()
        mover.close()

    spaces = [pl.BlockSpec(memory_space=pl.ANY)] * n_in
    room_shapes = list(local_shapes)
    if foot is not None:
        blocks = foot[0]
        inputs = inputs + (blocks,)
        n_in += 1
        spaces.append(pl.BlockSpec(memory_space=pltpu.VMEM))
        room_shapes.append((blocks.shape[0] * blocks.shape[1], blocks.shape[0] * blocks.shape[2]))
    return pl.pallas_call(
        kernel,
        in_specs=spaces,
        out_specs=[pl.BlockSpec(memory_space=pl.ANY)] * len(outputs),
        out_shape=[jax.ShapeDtypeStruct(shape, BF16) for shape in outputs],
        scratch_shapes=[
            pltpu.SemaphoreType.DMA((n_copy,)),
            pltpu.SemaphoreType.DMA((n_copy,)),
            pltpu.SemaphoreType.DMA((2 * len(local_shapes) + 1,)),
        ]
        + [pltpu.VMEM(shape, BF16) for shape in room_shapes],
        compiler_params=pltpu.CompilerParams(
            collective_id=ident, has_side_effects=True, vmem_limit_bytes=60 << 20
        ),
    )(*inputs)


def forward_and_gather(
    x_rows, qkv_x, a_qkv, picked, bias, gain, shift_by, first_maps, shards, maps, n_fsdp, n_ctx
):
    per, loc, width = x_rows.shape
    w_out, w_up, w_down = shards
    width_here = qkv_x.shape[1] // 3
    heads, units = width_here // HEAD_DIM, w_up.shape[1]
    zu, zo = w_up.shape[0], w_out.shape[1]
    n_part = n_ctx // 2 if n_ctx > 1 else 1
    so, su, sd = w_out.shape[0] // n_ctx, zu // n_ctx, w_down.shape[0] // n_ctx
    wide = width + NR
    wide_x = width + 3 * NR
    cuts = 4
    paired = cuts // 2 if n_ctx > 1 else 0
    tile = 512
    per_kind = width_here // tile
    chunk = 64
    n_tile = 3 * per_kind
    n_copy = (n_fsdp - 1) * n_ctx * (1 + 2 * cuts) + 2 * per * (n_ctx - 1) + 6 + per
    lag = 4

    def kernel(*refs):
        bias_ref, a_ref, pick_ref, gain_ref, shift_ref, a_up_ref, b_out_ref, x_ref, w_ref = refs[:9]
        wo_ref, wu_ref, wd_ref, ao_ref, bu_ref, ad_ref = refs[9:15]
        slots = refs[15 : 14 + n_ctx]
        q_ref, kv_ref, adapt_ref, out_ref, up_ref, down_ref, ctx_ref, log_ref = refs[
            14 + n_ctx : 22 + n_ctx
        ]
        h_ref, gelu_ref, slope_ref, hat_ref, rstd_ref, adapt_out_ref, adapt_up_ref = refs[
            22 + n_ctx : 29 + n_ctx
        ]
        send, recv, here, load, ring_sem, x_room, w_room, proj, kv_room, out_room = refs[
            29 + n_ctx : 39 + n_ctx
        ]
        part_ref, other_ref, up_room, wide_v, hat1, gelu, slope = refs[39 + n_ctx :]
        mover = Mover(n_fsdp, n_ctx, send, recv)
        ring = Ring(
            w_room,
            ring_sem,
            0,
            lambda t: w_ref.at[:, ds(lax.rem(t + per_kind, n_tile) * tile, tile)],
        )
        z = mover.z
        rows = [pl.ds(g * loc, loc) for g in range(per)]

        def columns(j):
            return pl.ds(j * width_here, width_here)

        out_item = Weight(
            lambda c: wo_ref.at[ds(c * so, so)],
            lambda o, c: out_ref.at[ds(c * so, so), ds(o * zo, zo)],
        )

        def up_item(h):
            at = pl.ds(h * (units // cuts), units // cuts)
            return Weight(
                lambda c: wu_ref.at[ds(c * su, su), at],
                lambda o, c: up_ref.at[ds(o * zu + c * su, su), at],
            )

        def down_item(h):
            size = sd // cuts
            return Weight(
                lambda c: wd_ref.at[ds(c * sd + h * size, size)],
                lambda o, c: down_ref.at[ds(c * sd + h * size, size), ds(o * zo, zo)],
            )

        def down_pair(h):
            size = sd // cuts

            def at(c, p):
                return ds((c + p * n_part) * sd + h * size, size)

            def half(p):
                return Weight(
                    lambda c: wd_ref.at[at(c, p)],
                    lambda o, c: down_ref.at[at(c, p), ds(o * zo, zo)],
                    skip=1,
                )

            return [half(p) for p in range(2)]

        def pair(g, j):
            return Pair(
                lambda k: proj.at[rows[g], columns(1 + j)] if k == 0 else slots[k - 1].at[j, g]
            )

        pairs = [pair(g, j) for g in range(per) for j in range(2)]
        items = [out_item] + [up_item(h) for h in range(cuts)]
        items += [down_item(h) for h in range(cuts - paired)]
        for h in range(cuts - paired, cuts):
            items += down_pair(h)
        used = [0]

        def move(source, target):
            copy = pltpu.make_async_copy(source, target, here.at[used[0]])
            used[0] += 1
            copy.start()
            return copy

        def attend(g):
            for j in range(2):
                mover.complete(pairs[2 * g + j])
            loads = []
            for k in range(1, n_ctx):
                copy = pltpu.make_async_copy(slots[k - 1].at[:, g], kv_room.at[k], load.at[k])
                copy.start()
                loads.append(copy)
            for j in range(2):
                kv_room[0, j] = proj[g * loc : (g + 1) * loc, (1 + j) * width_here : (2 + j) * width_here]
            for copy in loads:
                copy.wait()

            def one(h, carry):
                at = ds(h * HEAD_DIM, HEAD_DIM)
                biases = []
                for k in range(n_ctx):
                    block = bias_ref[g, k * loc : (k + 1) * loc, :]
                    biases.append(jnp.concatenate([block] * (loc // 128), axis=1))
                context, log = attend_head(
                    proj[g * loc : (g + 1) * loc, at],
                    [kv_room[k, 0, :, at] for k in range(n_ctx)],
                    [kv_room[k, 1, :, at] for k in range(n_ctx)],
                    biases,
                )
                ctx_ref[g, :, at] = context
                log_ref[g, h] = log
                return carry

            lax.fori_loop(0, heads, one, 0)

        def project():
            mover.complete(out_item)
            own[0].wait_recv()
            own[3].wait_recv()
            copy = pltpu.make_async_copy(out_ref, out_room, load.at[0])
            copy.start()
            copy.wait()
            for g in range(per):
                for start in range(0, wide, 1024):
                    at = slice(start, min(start + 1024, wide))
                    part_ref[g, :, at] = dot(ctx_ref[g], out_room[:, at]).astype(BF16)
                swapped.append(
                    mover.go(
                        part_ref.at[g], other_ref.at[g], {"tp": 1 - lax.axis_index("tp")}
                    )
                )

        def tiles(t, room):
            at = ds(lax.rem(t + per_kind, n_tile) * tile, tile)
            proj[:, at] = dot(x_room[...], room[...]).astype(BF16)

        up_ring = Ring(up_room, ring_sem, 2, lambda t: up_ref.at[:, ds(t * tile, tile)])

        def first_norm(g):
            swapped[g].wait_recv()
            pick = pick_ref[g]

            def step(r, carry):
                rows_r = ds(r * chunk, chunk)
                total = part_ref[g, rows_r, :].astype(F32) + other_ref[g, rows_r, :].astype(F32)
                code = (total[:, width:] * pick).astype(BF16)
                adapt_out_ref[g, rows_r, :] = code
                x = x_room[ds(g * loc + r * chunk, chunk), :width].astype(F32)
                hat, rstd = norm_parts(x + total[:, :width] + dot(code, b_out_ref[...]))
                hat1[g, rows_r, :] = hat
                rstd_ref[g, rows_r, :] = jnp.broadcast_to(rstd, (chunk, 128))
                low = (hat * gain_ref[0:1, :] + shift_ref[0:1, :]).astype(BF16)
                wide_v[g, rows_r, :width] = low
                code = (dot(low, a_up_ref[...]) * pick).astype(BF16)
                wide_v[g, rows_r, width:] = code
                adapt_up_ref[g, rows_r, :] = code
                return carry

            lax.fori_loop(0, loc // chunk, step, 0)
            outward.append(move(hat1.at[g], hat_ref.at[g]))
            outward.append(move(wide_v.at[g], h_ref.at[g]))

        def feed(g):
            if g == 0:
                for item in items[1 : 1 + cuts]:
                    mover.complete(item)
                own[1].wait_recv()
                own[4].wait_recv()
                up_ring.prefetch()

            def up_tile(t, room):
                at = ds(t * tile, tile)
                value, factor = gelu_both(dot(wide_v[g], room[...]))
                gelu[g, :, at] = value
                slope[g, :, at] = factor

            up_ring.run(units // tile, up_tile)
            if g + 1 < per:
                up_ring.prefetch()
            outward.append(move(gelu.at[g], gelu_ref.at[g]))
            outward.append(move(slope.at[g], slope_ref.at[g]))

        swapped, outward = [], []
        tasks = {1 + g: (lambda g=g: attend(g)) for g in range(per)}
        tasks[per + 2] = project
        tasks[per + 5] = lambda: [first_norm(g) for g in range(per)]
        for g in range(per):
            tasks[per + 6 + g] = lambda g=g: feed(g)
        ring.prefetch()
        loads = [move(x_ref.at[g], x_room.at[rows[g], pl.ds(0, width)]) for g in range(per)]
        mover.greet(tp=True)
        ahead = 2
        for item in items[:ahead]:
            mover.begin(item)
        sibling = {"ctx": flip(mover.ct, 1)}
        own = [
            mover.go(source, target, sibling)
            for source, target in (
                (wo_ref, out_ref.at[:, ds(z * zo, zo)]),
                (wu_ref, up_ref.at[ds(z * zu, zu)]),
                (wd_ref, down_ref.at[:, ds(z * zo, zo)]),
                (ao_ref, out_ref.at[:, pl.ds(width, NR)]),
                (bu_ref, up_ref.at[pl.ds(width, NR)]),
                (ad_ref, down_ref.at[:, pl.ds(width, NR)]),
            )
        ]
        for g in range(per):
            loads[g].wait()
            pick = pick_ref[g]
            for j in range(3):
                code = dot(x_room[g * loc : (g + 1) * loc, :width], a_ref[j]) * pick
                x_room[g * loc : (g + 1) * loc, width + j * NR : width + (j + 1) * NR] = code.astype(BF16)
            outward.append(move(x_room.at[rows[g], pl.ds(width, 3 * NR)], adapt_ref.at[g]))
        ring.run(2 * per_kind, tiles, 0, n_tile)
        for item in pairs:
            mover.begin(item)
        for g in range(per):
            for j in range(2):
                outward.append(move(proj.at[rows[g], columns(1 + j)], kv_ref.at[j, g]))
        for i in range(len(items) + lag + 2):
            if i < len(items):
                mover.relay(items[i])
                if i + ahead < len(items):
                    mover.begin(items[i + ahead])
            if i == 0:
                ring.run(n_tile, tiles, 2 * per_kind, n_tile)
                for g in range(per):
                    outward.append(move(proj.at[rows[g], columns(0)], q_ref.at[g]))
            for level in range(len(mover.masks)):
                if 0 <= i - lag - level < len(items):
                    mover.finish(items[i - lag - level], level)
            if i in tasks:
                tasks[i]()
        for item in items:
            mover.complete(item)
        for copy in (own[2], own[5]):
            copy.wait_recv()
        for copy in outward:
            copy.wait()
        mover.close()

    row = (per, loc, width_here)
    pair_shape = (2,) + row
    vmem, anywhere = pl.BlockSpec(memory_space=pltpu.VMEM), pl.BlockSpec(memory_space=pl.ANY)
    outputs = [(pair_shape, BF16, anywhere)] * (n_ctx - 1) + [
        (row, BF16, anywhere),
        (pair_shape, BF16, anywhere),
        ((per, loc, 3 * NR), BF16, anywhere),
        ((width_here, wide), BF16, anywhere),
        ((wide, units), BF16, anywhere),
        ((units, wide), BF16, anywhere),
        (row, BF16, vmem),
        ((per, heads, 1, loc), F32, vmem),
        ((per, loc, wide), BF16, anywhere),
        ((per, loc, units), BF16, anywhere),
        ((per, loc, units), BF16, anywhere),
        ((per, loc, width), F32, anywhere),
        ((per, loc, 128), F32, vmem),
        ((per, loc, NR), BF16, vmem),
        ((per, loc, NR), BF16, vmem),
    ]
    return pl.pallas_call(
        kernel,
        in_specs=[vmem] * 7 + [anywhere] * 8,
        out_specs=[space for _, _, space in outputs],
        out_shape=[jax.ShapeDtypeStruct(shape, dtype) for shape, dtype, _ in outputs],
        scratch_shapes=[
            pltpu.SemaphoreType.DMA((n_copy,)),
            pltpu.SemaphoreType.DMA((n_copy,)),
            pltpu.SemaphoreType.DMA((9 * per,)),
            pltpu.SemaphoreType.DMA((n_ctx,)),
            pltpu.SemaphoreType.DMA((4,)),
            pltpu.VMEM((per * loc, wide_x), BF16),
            pltpu.VMEM((2, wide_x, tile), BF16),
            pltpu.VMEM((per * loc, 3 * width_here), BF16),
            pltpu.VMEM((n_ctx, 2, loc, width_here), BF16),
            pltpu.VMEM((width_here, wide), BF16),
            pltpu.VMEM((per, loc, wide), BF16),
            pltpu.VMEM((per, loc, wide), BF16),
            pltpu.VMEM((2, wide, tile), BF16),
            pltpu.VMEM((per, loc, wide), BF16),
            pltpu.VMEM((per, loc, width), F32),
            pltpu.VMEM((per, loc, units), BF16),
            pltpu.VMEM((per, loc, units), BF16),
        ],
        compiler_params=pltpu.CompilerParams(
            collective_id=1, has_side_effects=True, vmem_limit_bytes=60 << 20
        ),
    )(bias, a_qkv, picked, gain, shift_by, *first_maps, x_rows, qkv_x, w_out, w_up, w_down, *maps)


class Ring:
    def __init__(self, room, sems, at, tile_at):
        self.room, self.sems, self.at, self.tile_at = room, sems, at, tile_at

    def copy(self, t):
        slot = lax.rem(t, 2)
        return pltpu.make_async_copy(
            self.tile_at(t), self.room.at[slot], self.sems.at[self.at + slot]
        )

    def prefetch(self):
        self.copy(0).start()
        self.copy(1).start()

    def run(self, n, body, first=0, total=None):
        total = n if total is None else total

        def step(t, carry):
            self.copy(t).wait()
            body(t, self.room.at[lax.rem(t, 2)])

            @pl.when(t + 2 < total)
            def _():
                self.copy(t + 2).start()

            return carry

        lax.fori_loop(first, n, step, 0)


def compact(out_ref, n, entries, sizes, start=0):
    column = lax.broadcasted_iota(jnp.int32, (NR, RANK), 0)
    rank = lax.broadcasted_iota(jnp.int32, (NR, RANK), 1)
    used = jnp.where(lax.rem(column, RANK) == rank, 1.0, 0.0).astype(BF16)
    for (code, value), size in zip(entries, sizes):
        short = dot(code(), used).astype(BF16)
        block = dot_tn(short, value()).astype(BF16)
        for k in range(out_ref.shape[0]):
            out_ref[k, n * RANK : (n + 1) * RANK, start : start + size] = block[
                :, k * size : (k + 1) * size
            ]
        start += size


class Fold:
    def __init__(self, mover, parts, came, out_ref):
        self.mover, self.parts, self.came, self.out_ref = mover, parts, came, out_ref
        self.flying = {}

    def at(self, k):
        return flip(self.mover.ct, self.mover.offsets[k])

    def hand(self, level):
        half = 2**level
        self.flying[level] = [
            self.mover.go(
                self.parts.at[self.at(half + i)],
                self.came.at[half - 1 + i],
                {"ctx": flip(self.mover.ct, self.mover.masks[level])},
            )
            for i in range(half)
        ]

    def take(self, level):
        for i, copy in enumerate(self.flying[level]):
            copy.wait_recv()
            total = self.parts[self.at(i)].astype(F32) + self.came[2**level - 1 + i].astype(F32)
            self.parts[self.at(i)] = total.astype(BF16)

    def next(self, level):
        self.take(level)
        if level:
            self.hand(level - 1)

    def gather(self):
        own = self.parts.at[self.mover.ct]
        item = Weight(
            lambda c: self.parts.at[c], lambda o, c: self.out_ref.at[c, o], own, direct=True
        )
        self.mover.begin(item)
        return own, self.out_ref.at[self.mover.ct, self.mover.z], item


def norm_parts(values):
    center = values - jnp.mean(values, axis=-1, keepdims=True)
    rstd = lax.rsqrt(jnp.mean(center * center, axis=-1, keepdims=True) + NORM_EPS)
    return center * rstd, rstd


def norm_back(hat, rstd, dhat):
    first = jnp.mean(dhat, axis=-1, keepdims=True)
    second = jnp.mean(dhat * hat, axis=-1, keepdims=True)
    return rstd * (dhat - first - hat * second)


def gelu_both(pre):
    square = pre * pre
    bent = jnp.tanh(GELU_COEF * (pre + 0.044715 * square * pre))
    out = 0.5 * pre * (1.0 + bent)
    slope = 0.5 * (1.0 + bent) + 0.5 * pre * (1.0 - bent * bent) * GELU_COEF * (
        1.0 + 3.0 * 0.044715 * square
    )
    return out.astype(BF16), slope.astype(BF16)


def middle(hats, rstds, gelus, slopes, adapt_up, cot, picked, gain, shift_by, weights, maps, n_fsdp, n_ctx):
    per, loc, width = hats.shape
    piece = cot.shape[1]
    out_x, up_x, down_x = weights
    a_up, b_out, b_down, a_down, b_up = maps
    wide, units = up_x.shape
    width_here = out_x.shape[0]
    tile = 512
    chunk = 128
    n_wide = width // tile
    n_swap = n_wide + 1
    sizes = [width // n_ctx, units // n_ctx, units // n_ctx]

    def kernel(*refs):
        pick_ref, gain_ref, shift_ref, rstd1, code_up_ref = refs[:5]
        a_up_ref, b_out_ref, b_down_ref, a_down_ref, b_up_ref = refs[5:10]
        hat_ref, gelu_ref, slope_ref, cot_ref, out_ref, up_ref, down_ref = refs[10:17]
        acts_out, dy1_out, da_out, cot_rows, grads_part, back_out = refs[17:23]
        dadapt_up_ref, ctx_ref = refs[23:25]
        (send, recv, deal_send, deal_recv, ring_sem, sems) = refs[25:31]
        (down_room, down_rows, up_rows) = refs[31:34]
        (stage, part, got, hat1, keep32, slope, gelu, wide_v, turned, dpre_t) = refs[34:44]
        (codes_down,) = refs[44:]
        mover = Mover(n_fsdp, n_ctx, deal_send, deal_recv)
        partner = {"tp": 1 - lax.axis_index("tp")}

        down = Ring(down_room, ring_sem, 0, lambda t: down_ref.at[:, ds(t * tile, tile)])
        down_r = Ring(down_rows, ring_sem, 4, lambda t: down_ref.at[ds(t * tile, tile)])
        up_r = Ring(up_rows, ring_sem, 6, lambda t: up_ref.at[ds(t * tile, tile)])
        out_r = Ring(down_rows, ring_sem, 4, lambda t: out_ref.at[ds(t * tile, tile)])

        busy = {}
        used = [0]

        def move(source, target, key):
            copy = pltpu.make_async_copy(source, target, sems.at[used[0]])
            used[0] += 1
            copy.start()
            busy.setdefault(key, []).append(copy)

        def free(*keys):
            for key in keys:
                for copy in busy.pop(key, []):
                    copy.wait()

        def swap_copy(turn, g, t, size):
            at = ds(t * tile, size)
            sem = (turn * per + g) * n_swap + t
            return pltpu.make_async_remote_copy(
                src_ref=part.at[g, :, at],
                dst_ref=got.at[turn, g, :, at],
                send_sem=send.at[sem],
                recv_sem=recv.at[sem],
                device_id=partner,
                device_id_type=pl.DeviceIdType.MESH,
            )

        def swapped(turn, g):
            for t in range(n_swap):
                copy = swap_copy(turn, g, t, tile if t < n_wide else NR)
                copy.wait_recv()
                copy.wait_send()

        def by_rows(body):
            def step(r, carry):
                body(pl.ds(pl.multiple_of(r * chunk, chunk), chunk))
                return carry

            lax.fori_loop(0, loc // chunk, step, 0)

        def deal(g):
            return Deal(lambda to: cot_ref.at[to * per + g], lambda s: cot_rows.at[g, s])

        deals = [deal(g) for g in range(per)]
        dealt = []
        for g in range(per):
            move(gelu_ref.at[g], gelu.at[g], ("gelu", g))
            if g == 0:
                down.prefetch()
            move(cot_ref.at[mover.z * per + g], cot_rows.at[g, 0], ("cot", g))

        def load_rest(g):
            move(hat_ref.at[g], hat1.at[g], ("hat", g))
            move(slope_ref.at[g], slope.at[g], ("slope", g))

        mover.greet(tp=True)
        mover.begin(deals[0])

        for g in range(per):
            if g + 1 == per:
                down_r.prefetch()
            free(("gelu", g))

            def down_tile(t, room, g=g):
                part[g, :, ds(t * tile, tile)] = dot(gelu[g], room[...]).astype(BF16)
                swap_copy(0, g, t, tile).start()

            down.run(n_wide, down_tile)
            if g + 1 < per:
                down.prefetch()
            else:
                up_r.prefetch()
            part[g, :, width:] = dot(gelu[g], a_down_ref[...]).astype(BF16)
            swap_copy(0, g, n_wide, NR).start()

        load_rest(0)
        for g in range(per):
            mover.relay(deals[g])
            if g + 1 < per:
                mover.begin(deals[g + 1])
            free(("cot", g))
            for s in range(n_fsdp):
                at = pl.ds(s * cot.shape[1], cot.shape[1])
                move(cot_rows.at[g, s], stage.at[g, at], ("stage", g))
            swapped(0, g)
            free(("stage", g), ("hat", g), ("slope", g))
            pick = pick_ref[g]

            def second_norm(rows, g=g, pick=pick):
                total = part[g, rows, :].astype(F32) + got[0, g, rows, :].astype(F32)
                code = (total[:, width:] * pick).astype(BF16)
                codes_down[g, rows, :] = code
                hidden = hat1[g, rows, :] * gain_ref[0:1, :] + shift_ref[0:1, :]
                hat, rstd = norm_parts(hidden + total[:, :width] + dot(code, b_down_ref[...]))
                part[g, rows, :width] = (hat * gain_ref[1:2, :] + shift_ref[1:2, :]).astype(BF16)
                dy2 = norm_back(hat, rstd, stage[g, rows, :].astype(F32) * gain_ref[1:2, :])
                keep32[g, rows, :] = dy2
                low = dy2.astype(BF16)
                wide_v[g, rows, :width] = low
                wide_v[g, rows, width:] = (dot_nt(low, b_down_ref[...]) * pick).astype(BF16)

            if g + 1 < per:
                load_rest(g + 1)
            by_rows(second_norm)
            move(part.at[g, :, pl.ds(0, width)], acts_out.at[g], ("part", g))
            own = part.at[g, pl.ds(0, piece), pl.ds(0, width)]
            move(own, back_out.at[mover.z * per + g], ("part", g))
            turned[...] = wide_v[g].T

            def down_back(t, room, g=g):
                at = ds(t * tile, tile)
                block = dot(room[...], turned[...]).T
                low = (block * slope[g, :, at].astype(F32)).astype(BF16)
                slope[g, :, at] = low
                dpre_t[at, :] = low.T

            down_r.run(units // tile, down_back)
            (down_r if g + 1 < per else out_r).prefetch()
            free(("part", g))
            for s in range(1, n_fsdp):
                to = lax.rem(mover.z - s + n_fsdp, n_fsdp)
                rows_s = acts_out.at[g, pl.ds(s * piece, piece)]
                dealt.append(mover.go(rows_s, back_out.at[mover.z * per + g], {"fsdp": to}))

            def up_back(t, room, g=g):
                part[g, :, ds(t * tile, tile)] = dot(room[...], dpre_t[...]).T.astype(BF16)
                swap_copy(1, g, t, tile).start()

            up_r.run(n_wide, up_back)
            if g + 1 < per:
                up_r.prefetch()
            part[g, :, width:] = dot(b_up_ref[...], dpre_t[...]).T.astype(BF16)
            swap_copy(1, g, n_wide, NR).start()

        for g in range(per):
            entries = [
                (lambda g=g: codes_down[g], lambda g=g: wide_v[g, :, :width]),
                (lambda g=g: wide_v[g, :, width:], lambda g=g: gelu[g]),
                (lambda g=g: code_up_ref[g], lambda g=g: slope[g]),
            ]
            compact(grads_part, g, entries, sizes)
        for g in range(per):
            swapped(1, g)
            pick = pick_ref[g]

            def first_back(rows, g=g, pick=pick):
                total = part[g, rows, :].astype(F32) + got[1, g, rows, :].astype(F32)
                code = (total[:, width:] * pick).astype(BF16)
                dadapt_up_ref[g, rows, :] = code
                dh1 = keep32[g, rows, :] + total[:, :width] + dot_nt(code, a_up_ref[...])
                rstd = rstd1[g, rows, 0:1]
                dy1 = norm_back(hat1[g, rows, :], rstd, dh1 * gain_ref[0:1, :])
                keep32[g, rows, :] = dy1
                low = dy1.astype(BF16)
                wide_v[g, rows, :width] = low
                wide_v[g, rows, width:] = (dot_nt(low, b_out_ref[...]) * pick).astype(BF16)

            by_rows(first_back)
            move(keep32.at[g], dy1_out.at[g], "dy1")
            move(wide_v.at[g], da_out.at[g], "wide")
            turned[...] = wide_v[g].T

            def out_back(t, room, g=g):
                ctx_ref[g, :, ds(t * tile, tile)] = dot(room[...], turned[...]).T.astype(BF16)

            out_r.run(width_here // tile, out_back)
            if g + 1 < per:
                out_r.prefetch()
        for copy in dealt:
            copy.wait_recv()
        free(*list(busy))
        mover.close()

    vmem, anywhere = pl.BlockSpec(memory_space=pltpu.VMEM), pl.BlockSpec(memory_space=pl.ANY)
    row = (per, loc)
    grads_shape = (n_ctx, per * RANK, sum(sizes))
    outputs = [
        (row + (width,), BF16, anywhere),
        (row + (width,), F32, anywhere),
        (row + (wide,), BF16, anywhere),
        ((per, n_fsdp) + cot.shape[1:], BF16, anywhere),
        (grads_shape, BF16, vmem),
        (cot.shape, BF16, anywhere),
        (row + (NR,), BF16, vmem),
        (row + (width_here,), BF16, vmem),
    ]
    n_copy = 2 * per * n_swap
    n_deal = 2 * per * (n_fsdp - 1)
    return pl.pallas_call(
        kernel,
        in_specs=[vmem] * 10 + [anywhere] * 7,
        out_specs=[space for _, _, space in outputs],
        out_shape=[jax.ShapeDtypeStruct(shape, dtype) for shape, dtype, _ in outputs],
        scratch_shapes=[
            pltpu.SemaphoreType.DMA((n_copy,)),
            pltpu.SemaphoreType.DMA((n_copy,)),
            pltpu.SemaphoreType.DMA((n_deal,)),
            pltpu.SemaphoreType.DMA((n_deal,)),
            pltpu.SemaphoreType.DMA((8,)),
            pltpu.SemaphoreType.DMA(((8 + n_fsdp) * per,)),
            pltpu.VMEM((2, units, tile), BF16),
            pltpu.VMEM((2, tile, wide), BF16),
            pltpu.VMEM((2, tile, units), BF16),
            pltpu.VMEM(row + (width,), BF16),
            pltpu.VMEM(row + (wide,), BF16),
            pltpu.VMEM((2,) + row + (wide,), BF16),
            pltpu.VMEM(row + (width,), F32),
            pltpu.VMEM(row + (width,), F32),
            pltpu.VMEM(row + (units,), BF16),
            pltpu.VMEM(row + (units,), BF16),
            pltpu.VMEM(row + (wide,), BF16),
            pltpu.VMEM((wide, loc), BF16),
            pltpu.VMEM((units, loc), BF16),
            pltpu.VMEM(row + (NR,), BF16),
        ],
        compiler_params=pltpu.CompilerParams(
            collective_id=3, has_side_effects=True, vmem_limit_bytes=62 << 20
        ),
    )(
        picked, gain, shift_by, rstds, adapt_up, a_up, b_out, b_down, a_down, b_up,
        hats, gelus, slopes, cot, out_x, up_x, down_x,
    )


def combine(pieces, chosen, shapes):
    n_part, n_fsdp, rows, columns = pieces.shape
    flat, specs = [], []
    for i, shape in enumerate(shapes):
        high, wide = shape[-2:]
        tall = wide == NR and high != NR
        size = (high if tall else wide) // n_part
        block = (size, NR) if tall else (NR, size)
        lead = shape[0] if len(shape) == 3 else None
        for j in range(lead or 1):
            flat.append((i, None if lead is None else j, tall, size))
        if lead is None:
            specs.append(pl.BlockSpec(block, (lambda c: (c, 0)) if tall else (lambda c: (0, c))))
        else:
            specs.append(
                pl.BlockSpec(
                    (lead,) + block, (lambda c: (0, c, 0)) if tall else (lambda c: (0, 0, c))
                )
            )

    def kernel(chosen_ref, piece_ref, *outs):
        ordered = jnp.concatenate([piece_ref[0, a] for a in range(n_fsdp)], axis=0)
        start = 0
        for i, lead, tall, size in flat:
            block = ordered[:, start : start + size]
            value = dot_tn(block, chosen_ref[...]) if tall else dot_tn(chosen_ref[...], block)
            if lead is None:
                outs[i][...] = value
            else:
                outs[i][lead] = value
            start += size

    return pl.pallas_call(
        kernel,
        grid=(n_part,),
        in_specs=[
            pl.BlockSpec(chosen.shape, lambda c: (0, 0)),
            pl.BlockSpec((1, n_fsdp, rows, columns), lambda c: (c, 0, 0, 0)),
        ],
        out_specs=specs,
        out_shape=[jax.ShapeDtypeStruct(shape, F32) for shape in shapes],
        compiler_params=pltpu.CompilerParams(vmem_limit_bytes=48 << 20),
    )(chosen, pieces)


def finish(
    query, kv_own, slots, bias, grad, log_total, x_rows, adapt_in, dy1, qkv_x, a_qkv, picked, grads, early, pairs, n_fsdp, n_ctx
):
    per, loc, width_here = query.shape
    piece, width = loc // n_fsdp, x_rows.shape[2]
    heads = width_here // HEAD_DIM
    cuts = 4
    high = heads // cuts
    columns = high * HEAD_DIM
    masks = masks_of(n_ctx)
    units = [(g, c) for g in range(per) for c in range(cuts)]
    depth = 3 * width_here
    foot = 3 * NR
    wide = width + foot
    tile = 512
    n_wide = width // tile
    n_swap = n_wide + 1
    n_early = len(early)
    early_sizes = [values[2] // n_ctx for _, values in pairs]
    before = grads.shape[2]
    late_sizes = [width_here // n_ctx] * 3 + [width // n_ctx] * 3
    n_copy = len(units) * (n_ctx - 1) + per * n_wide * (n_fsdp - 1)
    n_copy += 2 * ((n_fsdp - 1) * n_ctx + 2 * (n_ctx - 1))

    def kernel(*refs):
        q_ref, bias_ref, g_ref, log_ref, x_ref, adapt_ref, a_ref, pick_ref = refs[:8]
        dy1_ref, w_ref, grads_ref, kv_ref = refs[8:12]
        slot_refs = refs[12 : 11 + n_ctx]
        early_refs = refs[11 + n_ctx : 11 + n_ctx + n_early]
        at = 11 + n_ctx + n_early
        in_ref, early_out, late_out = refs[at : at + 3]
        send, recv, swap_send, swap_recv, ring_sem, load, sems = refs[at + 3 : at + 10]
        kv_room, own, came, dq, dkv = refs[at + 10 : at + 15]
        tiles, foot_room, dy1_room, turned, part, got, codes_in = refs[at + 15 : at + 22]
        early_part, early_came, late_part, late_came = refs[at + 22 : at + 26]
        staged = refs[at + 26 :]
        mover = Mover(n_fsdp, n_ctx, send, recv)
        z, ct = mover.z, mover.ct
        partner = {"tp": 1 - lax.axis_index("tp")}
        ring = Ring(tiles, ring_sem, 0, lambda t: w_ref.at[ds(t * tile, tile)])
        used = [0]
        kept, dealt, flying = [], [], {}

        def move(source, target):
            copy = pltpu.make_async_copy(source, target, sems.at[used[0]])
            used[0] += 1
            copy.start()
            return copy

        loads = []
        for g in range(per):
            loads.append([])
            for k in range(n_ctx):
                source = kv_ref if k == 0 else slot_refs[k - 1]
                copy = pltpu.make_async_copy(
                    source.at[:, g], kv_room.at[g, k], load.at[g * n_ctx + k]
                )
                if g == 0:
                    copy.start()
                loads[g].append(copy)
        mover.greet(tp=True)
        for copy in loads[0]:
            copy.wait()
        staging = [move(ref, room) for ref, room in zip(early_refs, staged)]
        staging.append(move(grads_ref, early_part.at[:, :, pl.ds(0, before)]))
        for group in loads[1:]:
            for copy in group:
                copy.start()
        load_foot = move(w_ref.at[pl.ds(width, foot)], foot_room)
        ring.prefetch()
        load_dy1 = move(dy1_ref, dy1_room)

        def compute(u):
            g, c = units[u]
            if c == 0 and g:
                for copy in loads[g]:
                    copy.wait()

            def one(h, carry):
                at = ds(c * columns + h * HEAD_DIM, HEAD_DIM)
                to = ds(h * HEAD_DIM, HEAD_DIM)
                biases = []
                for k in range(n_ctx):
                    block = bias_ref[g, k * loc : (k + 1) * loc, :]
                    biases.append(jnp.concatenate([block] * (loc // 128), axis=1))
                dquery, dkeys, dvalues = attend_back_head(
                    q_ref[g, :, at],
                    g_ref[g, :, at],
                    log_ref[g, c * high + h],
                    [kv_room[g, k, 0, :, at] for k in range(n_ctx)],
                    [kv_room[g, k, 1, :, at] for k in range(n_ctx)],
                    biases,
                )
                dq[g, :, at] = dquery
                for k in range(n_ctx):
                    own[u, k, 0, :, to] = dkeys[k]
                    own[u, k, 1, :, to] = dvalues[k]
                return carry

            for h in range(high):
                one(h, 0)

        def hand(u, level):
            half = 2**level
            device = {"ctx": flip(ct, masks[level])}
            flying[u, level] = [
                mover.go(own.at[u, half + i], came.at[u, half - 1 + i], device) for i in range(half)
            ]

        def take_in(u, level):
            half = 2**level
            g, c = units[u]
            for i, copy in enumerate(flying[u, level]):
                copy.wait_recv()
                for j in range(2):
                    total = own[u, i, j].astype(F32) + came[u, half - 1 + i, j].astype(F32)
                    if level:
                        own[u, i, j] = total.astype(BF16)
                    else:
                        dkv[j, g, :, c * columns : (c + 1) * columns] = total.astype(BF16)
            if level:
                hand(u, level - 1)

        def swap_copy(g, t):
            at = pl.ds(width, foot) if isinstance(t, int) and t == n_wide else ds(t * tile, tile)
            sem = g * n_swap + t
            return pltpu.make_async_remote_copy(
                src_ref=part.at[g, :, at],
                dst_ref=got.at[g, :, at],
                send_sem=swap_send.at[sem],
                recv_sem=swap_recv.at[sem],
                device_id=partner,
                device_id_type=pl.DeviceIdType.MESH,
            )

        def project_back(g):
            turned[0:width_here, :] = dq[g].T
            turned[width_here : 2 * width_here, :] = dkv[0, g].T
            turned[2 * width_here :, :] = dkv[1, g].T
            if g == 0:
                load_foot.wait()
            part[g, :, width:] = dot(foot_room[...], turned[...]).T.astype(BF16)
            swap_copy(g, n_wide).start()

            def back(t, room):
                part[g, :, ds(t * tile, tile)] = dot(room[...], turned[...]).T.astype(BF16)
                swap_copy(g, t).start()

            ring.run(n_wide, back)
            if g + 1 < per:
                ring.prefetch()

        def take_codes(g):
            swap_copy(g, n_wide).wait_recv()
            pick = jnp.concatenate([pick_ref[g]] * 3, axis=1)
            total = part[g, :, width:].astype(F32) + got[g, :, width:].astype(F32)
            codes_in[g] = (total * pick).astype(BF16)

        def finish_tile(g, t):
            swap_copy(g, t).wait_recv()
            swap_copy(g, t).wait_send()
            at = slice(t * tile, (t + 1) * tile)
            value = part[g, :, at].astype(F32) + got[g, :, at].astype(F32) + dy1_room[g, :, at]
            for j in range(3):
                value = value + dot_nt(codes_in[g, :, j * NR : (j + 1) * NR], a_ref[j, at, :])
            part[g, :, at] = value.astype(BF16)
            to_at = pl.ds(t * tile, tile)
            kept.append(move(part.at[g, pl.ds(0, piece), to_at], in_ref.at[z * per + g, :, to_at]))
            for s in range(1, n_fsdp):
                to = lax.rem(z - s + n_fsdp, n_fsdp)
                dealt.append(
                    mover.go(
                        part.at[g, pl.ds(s * piece, piece), to_at],
                        in_ref.at[z * per + g, :, to_at],
                        {"fsdp": to},
                    )
                )

        early_fold = Fold(mover, early_part, early_came, early_out)
        late_fold = Fold(mover, late_part, late_came, late_out)

        def known():
            for copy in staging:
                copy.wait()
            for n in range(per):
                entries = []
                for (i, first, size), (j, start, count) in pairs:
                    entries.append(
                        (
                            lambda n=n, i=i, f=first, c=size: staged[i][n, :, f : f + c],
                            lambda n=n, i=j, f=start, c=count: staged[i][n, :, f : f + c],
                        )
                    )
                compact(early_part, n, entries, early_sizes, before)
            early_fold.hand(last)

        last = len(masks) - 1
        for t in range(len(units) + last):
            if t < len(units):
                compute(t)
                hand(t, last)
            for k in range(last):
                if 0 <= t - 1 - k < len(units):
                    take_in(t - 1 - k, last - k)
            if t == 1:
                known()
            if t == 3:
                for level in range(last, 0, -1):
                    early_fold.next(level)
            if t == 6:
                early_fold.next(0)
                source, target, first = early_fold.gather()
                kept.append(move(source, target))
        done = set()
        for g in range(per):
            for u, (owner, _) in enumerate(units):
                if owner == g:
                    take_in(u, 0)
            if g + 1 == per:
                mover.relay(first)
            project_back(g)
            take_codes(g)
            if g == 0:
                load_dy1.wait()
            if g + 1 < per:
                for t in range(n_wide - 1):
                    finish_tile(g, t)
                    done.add((g, t))
        for n in range(per):
            values = [
                lambda n=n: dq[n],
                lambda n=n: dkv[0, n],
                lambda n=n: dkv[1, n],
            ]
            entries = [
                (lambda n=n, j=j: adapt_ref[n, :, j * NR : (j + 1) * NR], values[j]) for j in range(3)
            ]
            entries += [
                (lambda n=n, j=j: codes_in[n, :, j * NR : (j + 1) * NR], lambda n=n: x_ref[n])
                for j in range(3)
            ]
            compact(late_part, n, entries, late_sizes)
        late_fold.hand(last)
        rest = [(g, t) for g in range(per) for t in range(n_wide) if (g, t) not in done]
        for i, (g, t) in enumerate(rest):
            finish_tile(g, t)
            if i == 0:
                for level in range(last, 0, -1):
                    late_fold.next(level)
            if i == 1:
                late_fold.next(0)
                source, target, second = late_fold.gather()
                kept.append(move(source, target))
            if i == len(rest) - 3:
                mover.complete(first)
            if i == len(rest) - 2:
                mover.relay(second)
        mover.complete(second)
        for g in range(per):
            swap_copy(g, n_wide).wait_send()
        for copy in dealt:
            copy.wait_recv()
        for copy in kept:
            copy.wait()
        mover.close()

    vmem, anywhere = pl.BlockSpec(memory_space=pltpu.VMEM), pl.BlockSpec(memory_space=pl.ANY)
    parts = [(n_ctx, per * RANK, before + sum(early_sizes)), (n_ctx, per * RANK, sum(late_sizes))]
    row = (per, loc)
    rooms = [
        ((per, n_ctx, 2, loc, width_here), BF16),
        ((len(units), n_ctx, 2, loc, columns), BF16),
        ((len(units), n_ctx - 1, 2, loc, columns), BF16),
        (row + (width_here,), BF16),
        ((2,) + row + (width_here,), BF16),
        ((2, tile, depth), BF16),
        ((foot, depth), BF16),
        (dy1.shape, F32),
        ((depth, loc), BF16),
        (row + (wide,), BF16),
        (row + (wide,), BF16),
        (row + (foot,), BF16),
    ]
    for shape in parts:
        rooms += [(shape, BF16), ((n_ctx - 1,) + shape[1:], BF16)]
    rooms += [(x.shape, BF16) for x in early]
    return pl.pallas_call(
        kernel,
        in_specs=[vmem] * 8 + [anywhere] * (3 + n_ctx + n_early),
        out_specs=[anywhere] * 3,
        out_shape=[jax.ShapeDtypeStruct((per * n_fsdp, piece, width), BF16)]
        + [jax.ShapeDtypeStruct((n_ctx, n_fsdp) + shape[1:], BF16) for shape in parts],
        scratch_shapes=[
            pltpu.SemaphoreType.DMA((n_copy,)),
            pltpu.SemaphoreType.DMA((n_copy,)),
            pltpu.SemaphoreType.DMA((per * n_swap,)),
            pltpu.SemaphoreType.DMA((per * n_swap,)),
            pltpu.SemaphoreType.DMA((2,)),
            pltpu.SemaphoreType.DMA((per * n_ctx,)),
            pltpu.SemaphoreType.DMA((5 + n_early + per * n_wide,)),
        ]
        + [pltpu.VMEM(shape, dtype) for shape, dtype in rooms],
        compiler_params=pltpu.CompilerParams(
            collective_id=4, has_side_effects=True, vmem_limit_bytes=63 << 20
        ),
    )(
        query, bias, grad, log_total, x_rows, adapt_in, a_qkv, picked, dy1, qkv_x, grads, kv_own, *slots, *early,
    )


def gelu_both(pre):
    square = pre * pre
    bent = jnp.tanh(GELU_COEF * (pre + 0.044715 * square * pre))
    out = 0.5 * pre * (1.0 + bent)
    slope = 0.5 * (1.0 + bent) + 0.5 * pre * (1.0 - bent * bent) * GELU_COEF * (
        1.0 + 3.0 * 0.044715 * square
    )
    return out.astype(BF16), slope.astype(BF16)


def local(
    x_in,
    cotangent,
    lengths,
    adapter_ids,
    w_qkv,
    w_out,
    w_up,
    w_down,
    ln_gain,
    ln_bias,
    a_qkv,
    b_qkv,
    a_out,
    b_out,
    a_up,
    b_up,
    a_down,
    b_down,
):
    n_ctx, n_fsdp = lax.axis_size("ctx"), lax.axis_size("fsdp")
    z, ct = lax.axis_index("fsdp"), lax.axis_index("ctx")
    seqs, piece, width = x_in.shape
    per = seqs // n_fsdp
    loc = n_fsdp * piece
    heads_width = w_qkv.shape[2]
    def take(array, start, size, axis=0):
        return lax.dynamic_slice_in_dim(array, start, size, axis)

    units = w_up.shape[1]
    rows_shape = (per, n_fsdp, piece, width)
    zq = w_qkv.shape[1]

    def first_items(ins, outs, z):
        x_ref, w_ref = ins
        rows_ref, whole_ref = outs

        def deal(g):
            return Deal(lambda to: x_ref.at[to * per + g], lambda s: rows_ref.at[g, s])

        def weight(j):
            size = zq // n_ctx
            columns = pl.ds(j * heads_width, heads_width)
            return Weight(
                lambda c: w_ref.at[j, pl.ds(pl.multiple_of(c * size, size), size)],
                lambda o, c: whole_ref.at[
                    pl.ds(pl.multiple_of(o * zq + c * size, size), size), columns
                ],
            )

        stay = [(x_ref.at[z * per + g], rows_ref.at[g, 0]) for g in range(per)]
        for j in range(3):
            own = whole_ref.at[
                pl.ds(pl.multiple_of(z * zq, zq), zq), pl.ds(j * heads_width, heads_width)
            ]
            stay.append((w_ref.at[j], own))
        items = [weight(j) for j in range(3)] + [deal(g) for g in range(per)]
        return items, stay

    x_all, qkv_x = move(
        first_items,
        [Weight] * 3 + [Deal] * per,
        (x_in, w_qkv),
        (rows_shape, (width + 3 * NR, 3 * heads_width)),
        n_fsdp,
        n_ctx,
        ((piece, width),) * per + (w_qkv.shape[1:],) * 3,
        0,
        foot=(b_qkv, lambda outs: outs[1].at[pl.ds(width, 3 * NR)]),
    )

    my_lengths = take(lengths, z * per, per)
    my_ids = take(adapter_ids, z * per, per)
    picked = (my_ids[:, None] == jnp.arange(NR)[None, :] // RANK).astype(F32)
    steps = lax.rem(z - jnp.arange(n_fsdp) + n_fsdp, n_fsdp)
    ctx_of = ct ^ jnp.array(offsets(n_ctx))
    key_pos = (
        (steps[None, :, None] * n_ctx + ctx_of[:, None, None]) * piece
        + jnp.arange(piece)[None, None, :]
    ).reshape(-1)
    bias_all = jnp.where(key_pos[None, :] < my_lengths[:, None], 0.0, -1e30).astype(F32)
    bias_all = jnp.broadcast_to(bias_all[:, :, None], bias_all.shape + (128,))

    picked = picked[:, None, :]
    x_rows = x_all.reshape(per, loc, width)
    moved = forward_and_gather(
        x_rows, qkv_x, a_qkv, picked, bias_all, ln_gain, ln_bias, (a_up, b_out), (w_out, w_up, w_down),
        (a_out, b_up, a_down), n_fsdp, n_ctx,
    )
    slots = moved[: n_ctx - 1]
    (
        query, kv_own, adapt_all, out_x, up_x, down_x, context, log_total, wide_h, gelus, slopes, hats, rstds,
        adapt_out, adapt_up,
    ) = moved[n_ctx - 1 :]
    _, dy1, wide_a, _, grads, activations, dadapt_up, d_context = middle(
        hats, rstds, gelus, slopes, adapt_up, cotangent, picked, ln_gain, ln_bias, (out_x, up_x, down_x),
        (a_up, b_out, b_down, a_down, b_up), n_fsdp, n_ctx,
    )
    early_in = (dadapt_up, wide_h, adapt_out, wide_a, context)
    early_pairs = [
        ((0, 0, NR), (1, 0, width)),
        ((2, 0, NR), (3, 0, width)),
        ((3, width, NR), (4, 0, heads_width)),
    ]
    input_grad, early, late = finish(
        query, kv_own, slots, bias_all, d_context, log_total, x_rows, adapt_all, dy1, qkv_x, a_qkv, picked,
        grads, early_in, early_pairs, n_fsdp, n_ctx,
    )

    codes = (adapter_ids[:, None] * RANK + jnp.arange(RANK)[None, :]).reshape(-1)
    chosen = (codes[:, None] == jnp.arange(NR)[None, :]).astype(BF16)
    b_down_grad, a_down_grad, b_up_grad, a_up_grad, b_out_grad, a_out_grad = combine(
        early,
        chosen,
        [(NR, width), (units, NR), (NR, units), (width, NR), (NR, width), (heads_width, NR)],
    )
    b_qkv_grad, a_qkv_grad = combine(late, chosen, [(3, NR, heads_width), (3, width, NR)])
    return (
        activations, input_grad, a_qkv_grad, b_qkv_grad, a_out_grad, b_out_grad, a_up_grad, b_up_grad,
        a_down_grad, b_down_grad,
    )


def solution(mesh):
    rows = P(None, ("fsdp", "ctx"), None)
    return jax.shard_map(
        local,
        mesh=mesh,
        in_specs=(
            rows,
            rows,
            P(),
            P(),
            P(None, "fsdp", "tp"),
            P("tp", "fsdp"),
            P("fsdp", "tp"),
            P("tp", "fsdp"),
            P(),
            P(),
            P(),
            P(None, None, "tp"),
            P("tp", None),
            P(),
            P(),
            P(None, "tp"),
            P("tp", None),
            P(),
        ),
        out_specs=(
            rows,
            rows,
            P(),
            P(None, None, "tp"),
            P("tp", None),
            P(),
            P(),
            P(None, "tp"),
            P("tp", None),
            P(),
        ),
        check_vma=False,
    )
```
